32 devices in a mesh: grp: 2 (over core), ctx: 4 (over z), wsh: 4 (over y, x).
Axes of the slice: x: 2, y: 2, z: 4, core: 2. Of those that a mesh axis runs over, the one named last changes fastest.
Arguments:
- tokens: bfloat16 [6144, 1152], P(('grp', 'ctx', 'wsh')), may hold values from -6 to 6
- segment_ids: int32 [6144], P(('grp', 'ctx', 'wsh')), may hold values from 0 to 1, as said below
- positions: int32 [6144], P(('grp', 'ctx', 'wsh')), may hold values from 0 to 3071, as said below
- attend_gain: float32 [1152], replicated, may hold values from 0.5 to 1.5
- query_key_value: bfloat16 [1152, 1920], P('wsh'), may hold values from -0.25 to 0.25
- attend_out: bfloat16 [1152, 1152], P('wsh'), may hold values from -2 to 2
- feed_gain: float32 [1152], replicated, may hold values from 0.5 to 1.5
- gate_up: bfloat16 [1152, 6144], P('wsh'), may hold values from -0.1875 to 0.1875
- down_weight: bfloat16 [3072, 1152], P('wsh'), may hold values from -0.4375 to 0.4375
- upstream: bfloat16 [6144, 1152], P(('grp', 'ctx', 'wsh')), may hold values from -6 to 6
Outputs:
- activations: bfloat16 [6144, 1152], P(('grp', 'ctx', 'wsh'))
- input_grad: float32 [6144, 1152], P(('grp', 'ctx', 'wsh'))
- query_key_value_grad: float32 [1152, 1920], P(('ctx', 'wsh'))
- attend_out_grad: float32 [1152, 1152], P(('ctx', 'wsh'))
- gate_up_grad: float32 [1152, 6144], P(('ctx', 'wsh'))
- down_weight_grad: float32 [3072, 1152], P(('ctx', 'wsh'))
- attend_gain_grad: float32 [1152], P(('ctx', 'wsh'))
- feed_gain_grad: float32 [1152], P(('ctx', 'wsh'))
The draws below stay inside these ranges and needn't reach their ends.
Inputs may be any that keep to these rules, and one draw needn't show every extreme that they name: `segment_ids`: in each group of 3072 rows the aligned runs of 96 rows are the runs of 96 consecutive tokens of that group's token stream, in some order, each once; the stream is the prompt of 2048 tokens (segment 0) followed by 1 continuations of 1024 tokens (segments 1 to 1). `positions`: matching segment_ids: a prompt token's position is its index in the prompt; a continuation token's position is 2048 plus its index in its continuation.
All inputs are finite; a program needn't handle non-finite values.
Results may differ from the reference program's by a relative error of at most 0.02.
Values may be sent and summed in bfloat16 or wider, within the bound.
A program may use at most 256 MiB of HBM per device.

```python
import math
import jax
import jax.numpy as jnp
from jax import lax

D = 1152
HEADS = 18
KV_HEADS = 6
HEAD_DIM = 64
FF = 3072
CONT_LEN = 1024
QW = 1152
KW = 384
GROUPS = 2
GROUP_TOK = 3072
PROMPT = 2048
BLK = 96
TOKENS = 6144


def stream_index(key):
    block_count = GROUP_TOK // BLK

    def one_group(group_index):
        order = jax.random.permutation(jax.random.fold_in(jax.random.fold_in(key, 11), group_index), block_count)
        row_index = jnp.arange(GROUP_TOK, dtype=jnp.int32)
        return (order.astype(jnp.int32)[row_index // BLK] * BLK + row_index % BLK).astype(jnp.int32)
    return jax.vmap(one_group)(jnp.arange(GROUPS, dtype=jnp.int32)).reshape(-1)


def draw_segment_ids(key, part):
    stream = stream_index(key)
    later = jnp.maximum(stream - PROMPT, 0)
    return jnp.where(stream < PROMPT, 0, 1 + later // CONT_LEN).astype(jnp.int32)


def draw_positions(key, part):
    stream = stream_index(key)
    later = jnp.maximum(stream - PROMPT, 0)
    return jnp.where(stream < PROMPT, stream, PROMPT + later % CONT_LEN).astype(jnp.int32)


def block_levels(own_key, dims, shards, smallest, high):
    factor_of, own = 1.0, jax.random.fold_in(own_key, 6)
    for dim, blocks in shards:
        draws = jnp.exp(jax.random.uniform(jax.random.fold_in(own, dim), (blocks,), jnp.float32, smallest / len(shards), high / len(shards)))
        factor_of = factor_of * jnp.repeat(draws, dims[dim] // blocks).reshape([-1 if axis == dim else 1 for axis in range(len(dims))])
    return factor_of


def noise(own_key, dims, spread, limit, cuts=(), kind=jnp.bfloat16):
    factor_of = block_levels(own_key, dims, cuts, -0.22, 0.18) if cuts else 1.0
    entries = jax.random.normal(own_key, dims, jnp.float32) * spread * factor_of
    return jnp.minimum(jnp.maximum(entries, -limit), limit).astype(kind)


def setup_inputs(seed: int = 0) -> dict:
    streams_of = jax.random.split(jax.random.key(seed), 11)
    tokens = noise(streams_of[0], (TOKENS, D), 1.0, 6.0, ((0, 32),))
    segment_ids = draw_segment_ids(jax.random.fold_in(streams_of[10], 71), 0)
    positions = draw_positions(jax.random.fold_in(streams_of[10], 71), 0)
    attend_gain = jnp.clip(1.0 + 0.1 * jax.random.normal(streams_of[3], (D,), jnp.float32), 0.5, 1.5)
    query_key_value = noise(streams_of[4], (D, QW + 2 * KW), (D // 2) ** -0.5, 0.25, ((0, 4),))
    attend_out = noise(streams_of[5], (QW, D), (D // 128) ** -0.5, 2.0, ((0, 4),))
    feed_gain = jnp.clip(1.0 + 0.1 * jax.random.normal(streams_of[6], (D,), jnp.float32), 0.5, 1.5)
    gate_up = noise(streams_of[7], (D, 2 * FF), D ** -0.5, 0.1875, ((0, 4),))
    down_weight = noise(streams_of[8], (FF, D), (FF // 16) ** -0.5, 0.4375, ((0, 4),))
    upstream = noise(streams_of[9], (TOKENS, D), 1.0, 6.0, ((0, 32),))
    return {"tokens": tokens, "segment_ids": segment_ids, "positions": positions, "attend_gain": attend_gain, "query_key_value": query_key_value, "attend_out": attend_out, "feed_gain": feed_gain, "gate_up": gate_up, "down_weight": down_weight, "upstream": upstream}


EPSILON = 1e-05
HIGHEST = lax.Precision.HIGHEST

@jax.custom_vjp
def low(v):
    return lax.optimization_barrier(v.astype(jnp.bfloat16)).astype(jnp.float32)

@jax.custom_vjp
def low_back(v):
    return v

def low_keep(v):
    return (low(v), None)

def low_pass(kept, grad):
    return (grad,)

def back_keep(v):
    return (v, None)

def back_low(kept, grad):
    return (low(grad),)
low.defvjp(low_keep, low_pass)
low_back.defvjp(back_keep, back_low)

def rope_angles(positions):
    halfway = HEAD_DIM // 2
    frequency = jnp.exp(jnp.arange(halfway, dtype=jnp.float32) * (-math.log(10000.0) / halfway))
    angles = positions.astype(jnp.float32)[:, None] * frequency[None, :]
    return (jnp.cos(angles), jnp.sin(angles))

def rotate(tensor, cosine, sine_table):
    halfway = tensor.shape[-1] // 2
    first_half = tensor[..., :halfway]
    second_half = tensor[..., halfway:]
    cos_wide = cosine[:, None, :]
    sin_wide = sine_table[:, None, :]
    return jnp.concatenate([first_half * cos_wide - second_half * sin_wide, second_half * cos_wide + first_half * sin_wide], axis=-1)

def rms_factor(values):
    return lax.rsqrt(lax.optimization_barrier(jnp.mean(values * values, axis=-1, keepdims=True)) + EPSILON)

def group_attention(operands):
    queries, key_rows, value_rows, segment_ids, positions = operands
    span_rows = min(512, GROUP_TOK)
    scale_factor = HEAD_DIM ** (-0.5)

    @jax.checkpoint
    def one_block(pieces):
        query_block, segment_block, position_block = pieces
        allowed = (positions[None, :] <= position_block[:, None]) & ((segment_ids[None, :] == 0) | (segment_ids[None, :] == segment_block[:, None]))
        scores = low_back(jnp.einsum('qhjd,khd->hjqk', query_block, key_rows, precision=HIGHEST) * scale_factor)
        scores = jnp.where(allowed, scores, -1e+30)
        largest = lax.optimization_barrier(jnp.max(scores, axis=-1, keepdims=True))
        expons = jnp.where(allowed, jnp.exp(scores - largest), 0.0)
        weights_all = expons / lax.optimization_barrier(jnp.sum(expons, axis=-1, keepdims=True))
        return jnp.einsum('hjqk,khd->qhjd', low(weights_all), value_rows, precision=HIGHEST)
    shaped = queries.reshape((GROUP_TOK // span_rows, span_rows) + queries.shape[1:])
    result = lax.map(one_block, (shaped, segment_ids.reshape(-1, span_rows), positions.reshape(-1, span_rows)))
    return result.reshape(queries.shape)

def forward(tokens, attend_gain, query_key_value, attend_out, feed_gain, gate_up, down_weight, segment_ids, positions):
    row_count = tokens.shape[0]
    head_ratio = HEADS // KV_HEADS
    normed_one = low(tokens * rms_factor(tokens) * attend_gain)
    projected = low_back(jnp.dot(normed_one, query_key_value, precision=HIGHEST))
    cosine, sine_table = rope_angles(positions)
    queries = low(low_back(rotate(projected[:, :QW].reshape(row_count, HEADS, HEAD_DIM), cosine, sine_table)))
    key_rows = low(low_back(rotate(projected[:, QW:QW + KW].reshape(row_count, KV_HEADS, HEAD_DIM), cosine, sine_table)))
    value_rows = low(low_back(projected[:, QW + KW:].reshape(row_count, KV_HEADS, HEAD_DIM)))
    mixed = lax.map(group_attention, (queries.reshape(GROUPS, GROUP_TOK, KV_HEADS, head_ratio, HEAD_DIM), key_rows.reshape(GROUPS, GROUP_TOK, KV_HEADS, HEAD_DIM), value_rows.reshape(GROUPS, GROUP_TOK, KV_HEADS, HEAD_DIM), segment_ids.reshape(GROUPS, GROUP_TOK), positions.reshape(GROUPS, GROUP_TOK)))
    attended = low(low_back(mixed.reshape(row_count, QW)))
    middle = tokens + low_back(jnp.dot(attended, attend_out, precision=HIGHEST))
    normed_two = low(middle * rms_factor(middle) * feed_gain)
    gate_value = low_back(jnp.dot(normed_two, gate_up, precision=HIGHEST))
    hidden = low(jax.nn.silu(gate_value[:, :FF]) * gate_value[:, FF:])
    return middle + jnp.dot(hidden, down_weight, precision=HIGHEST)

def reference(tokens, segment_ids, positions, attend_gain, query_key_value, attend_out, feed_gain, gate_up, down_weight, upstream):
    floats = (tokens.astype(jnp.float32), attend_gain.astype(jnp.float32), query_key_value.astype(jnp.float32), attend_out.astype(jnp.float32), feed_gain.astype(jnp.float32), gate_up.astype(jnp.float32), down_weight.astype(jnp.float32))

    def run_layer(x_in, gain_one, w_qkv, w_out, gain_two, w_gate_up, w_down):
        return forward(x_in, gain_one, w_qkv, w_out, gain_two, w_gate_up, w_down, segment_ids, positions)
    result, pull_back = jax.vjp(run_layer, *floats)
    grads = pull_back(upstream.astype(jnp.float32))
    return (result.astype(jnp.bfloat16), grads[0], grads[2], grads[3], grads[5], grads[6], grads[1], grads[4])
```

```python
import itertools
import math

import jax
import jax.numpy as jnp
from jax import lax
from jax.experimental import pallas as pl
from jax.experimental.pallas import tpu as pltpu
from jax.sharding import PartitionSpec as P

HEADS = 18
KV_HEADS = 6
HEAD_DIM = 64
FF = 3072
D = 1152
QW = 1152
KW = 384
EPSILON = 1e-05
MESH = pl.DeviceIdType.MESH
F32 = jnp.float32
BF = jnp.bfloat16
VMEM_LIMIT = 56 << 20


def dot_general(a, b, ca, cb):
    return lax.dot_general(a, b, (((ca,), (cb,)), ((), ())), preferred_element_type=F32)


class Exchange:
    def __init__(self, sizes):
        self.sizes = sizes

    def place(self, axes, offset):
        where, index = {}, 0
        for axis, step in zip(axes, offset):
            size = self.sizes[axis]
            spot = lax.axis_index(axis)
            if step:
                spot = lax.rem(spot + step, size)
            where[axis] = spot
            index = index * size + spot
        return where, index

    def offsets(self, axes):
        return list(itertools.product(*[range(self.sizes[axis]) for axis in axes]))

    def gather(self, x, axes):
        count = math.prod(self.sizes[axis] for axis in axes)
        return ("peer", x, axes, lambda ref, p: ref, (count,) + x.shape, x.shape)

    def swap(self, x, axes):
        return ("peer", x, axes, lambda ref, p: ref.at[p], x.shape, x.shape[1:])

    def columns(self, x, axes, start, width):
        count = math.prod(self.sizes[axis] for axis in axes)
        source = lambda ref, p: ref.at[:, pl.ds(pl.multiple_of(start + p * width, 128), width)]
        return ("peer", x, axes, source, (count, x.shape[0], width), (x.shape[0], width))

    def owners(self, x):
        return ("owner", x, None, None, x.shape, x.shape[1:])

    def run(self, name, number, ops):
        ctx, wsh = self.sizes["ctx"], self.sizes["wsh"]
        total = 0
        for kind, x, axes, *_ in ops:
            total += ctx if kind == "owner" else math.prod(self.sizes[a] for a in axes)
        peers = {}
        for kind, x, axes, *_ in ops:
            for offset in self.offsets(axes if kind == "peer" else ("ctx", "wsh")):
                axes_of = axes if kind == "peer" else ("ctx", "wsh")
                key = tuple(sorted((a, o) for a, o in zip(axes_of, offset) if o))
                if key:
                    peers[key] = (axes_of, offset)
        count = len(ops)

        def kernel(*refs):
            ins, outs = refs[:count], refs[count : 2 * count]
            bounce = refs[2 * count : 3 * count]
            send, recv, near = refs[3 * count :]
            barrier = pltpu.get_barrier_semaphore()
            for axes, offset in peers.values():
                where, _ = self.place(axes, offset)
                pl.semaphore_signal(barrier, 1, device_id=where, device_id_type=MESH)
            pl.semaphore_wait(barrier, len(peers))
            first, second, remote, late = [], [], [], []
            slot = 0
            for op, (kind, x, axes, source, _, _) in enumerate(ops):
                if kind == "peer":
                    none = tuple(0 for _ in axes)
                    _, me = self.place(axes, none)
                    for offset in self.offsets(axes):
                        where, index = self.place(axes, offset)
                        if any(offset):
                            copy = pltpu.make_async_remote_copy(
                                source(ins[op], index),
                                outs[op].at[me],
                                send.at[slot],
                                recv.at[slot],
                                device_id=where,
                                device_id_type=MESH,
                            )
                            copy.start()
                            remote.append(copy)
                        else:
                            copy = pltpu.make_async_copy(
                                source(ins[op], me), bounce[op], near.at[op]
                            )
                            copy.start()
                            first.append(copy)
                            second.append(
                                pltpu.make_async_copy(bounce[op], outs[op].at[me], near.at[op])
                            )
                        slot += 1
                else:
                    my_c, my_w = lax.axis_index("ctx"), lax.axis_index("wsh")
                    base = slot
                    for k in range(ctx):
                        shard = my_w * ctx + k
                        to_c, to_w = shard // wsh, lax.rem(shard, wsh)
                        own = jnp.logical_and(to_c == my_c, to_w == my_w)
                        copy = pltpu.make_async_remote_copy(
                            ins[op].at[k],
                            outs[op].at[my_c],
                            send.at[base + k],
                            recv.at[base + my_c],
                            device_id={"ctx": to_c, "wsh": to_w},
                            device_id_type=MESH,
                        )
                        inward = pltpu.make_async_copy(ins[op].at[k], bounce[op], near.at[op])
                        outward = pltpu.make_async_copy(
                            bounce[op], outs[op].at[my_c], near.at[op]
                        )

                        @pl.when(jnp.logical_not(own))
                        def _():
                            copy.start()

                        late.append((own, copy, inward, outward))
                    mine = my_c * wsh + my_w
                    from_w = mine // ctx
                    for c in range(ctx):
                        own = jnp.logical_and(my_c == c, from_w == my_w)
                        arrival = pltpu.make_async_remote_copy(
                            ins[op].at[0],
                            outs[op].at[c],
                            send.at[base + c],
                            recv.at[base + c],
                            device_id={"ctx": my_c, "wsh": my_w},
                            device_id_type=MESH,
                        )
                        late.append((own, arrival, None, None))
                    slot += ctx
            for one, two in zip(first, second):
                one.wait()
                two.start()
            for own, copy, inward, outward in late:
                if inward is not None:

                    @pl.when(own)
                    def _():
                        inward.start()
                        inward.wait()
                        outward.start()
                        outward.wait()

            for copy in second:
                copy.wait()
            for own, copy, inward, outward in late:

                @pl.when(jnp.logical_not(own))
                def _():
                    if inward is None:
                        copy.wait_recv()
                    else:
                        copy.wait_send()

            for copy in remote:
                copy.wait()

        return pl.pallas_call(
            kernel,
            name=name,
            out_shape=[jax.ShapeDtypeStruct(op[4], op[1].dtype) for op in ops],
            in_specs=[pl.BlockSpec(memory_space=pl.ANY)] * count,
            out_specs=[pl.BlockSpec(memory_space=pl.ANY)] * count,
            scratch_shapes=[pltpu.VMEM(op[5], op[1].dtype) for op in ops]
            + [
                pltpu.SemaphoreType.DMA((total,)),
                pltpu.SemaphoreType.DMA((total,)),
                pltpu.SemaphoreType.DMA((count,)),
            ],
            compiler_params=pltpu.CompilerParams(
                collective_id=number, has_side_effects=True, vmem_limit_bytes=VMEM_LIMIT
            ),
        )(*[op[1] for op in ops])


def head_plan(w):
    pair, odd = w // 2, w % 2
    start = 9 * pair + 4 * odd
    if odd:
        f_heads, h_heads = [start + 2, start + 3, start + 4], [start, start + 1]
        f_kv, h_kv = 3 * pair + 2, 3 * pair + 1
    else:
        f_heads, h_heads = [start, start + 1, start + 2], [start + 3, start + 4]
        f_kv, h_kv = 3 * pair, 3 * pair + 1
    q_order = [f_heads[0], h_heads[0], f_heads[1], h_heads[1], f_heads[2], None]
    return q_order, [f_kv, h_kv]


def qkv_columns(weight):
    blank = jnp.zeros((weight.shape[0], HEAD_DIM), weight.dtype)
    parts = []
    for w in range(4):
        q_order, kv_order = head_plan(w)
        pieces = [
            blank if h is None else weight[:, h * HEAD_DIM : (h + 1) * HEAD_DIM] for h in q_order
        ]
        for base in (QW, QW + KW):
            pieces += [
                weight[:, base + h * HEAD_DIM : base + (h + 1) * HEAD_DIM] for h in kv_order
            ]
        parts.append(jnp.concatenate(pieces, axis=1))
    return jnp.stack(parts)


def qkv_restore(parts):
    found = {}
    for w in range(4):
        q_order, kv_order = head_plan(w)
        slots = list(q_order) + [HEADS + h for h in kv_order]
        slots += [HEADS + KV_HEADS + h for h in kv_order]
        for at, head in enumerate(slots):
            if head is not None:
                found.setdefault(head, []).append(
                    parts[w][:, at * HEAD_DIM : (at + 1) * HEAD_DIM]
                )
    pieces = []
    for head in range(HEADS + 2 * KV_HEADS):
        term = found[head][0]
        for other in found[head][1:]:
            term = term + other
        pieces.append(term)
    return jnp.concatenate(pieces, axis=1)


def spread_rows(rows, odd):
    n = rows.shape[1]
    half = jnp.zeros((32, n), rows.dtype)
    blank = jnp.zeros((64, n), rows.dtype)
    even_rows = jnp.concatenate(
        [rows[0:64], rows[192:256], rows[64:128], rows[256:288], half, rows[128:192], blank]
    )
    odd_rows = jnp.concatenate(
        [rows[96:160], half, rows[0:32], rows[160:224], rows[32:96], rows[224:288], blank]
    )
    return jnp.where(odd, odd_rows, even_rows)


def collect_rows(wide, odd):
    f0, h0, f1, h1, f2 = (wide[64 * i : 64 * i + 64] for i in range(5))
    even_rows = jnp.concatenate([f0, f1, f2, h0, h1[:32]])
    odd_rows = jnp.concatenate([h0[32:], h1, f0, f1, f2])
    return jnp.where(odd, odd_rows, even_rows)


def turn(x, cos, sin, lanes):
    swapped = jnp.where(lanes, pltpu.roll(x, 96, 1), pltpu.roll(x, 32, 1))
    return x * cos + swapped * sin


def project(normed, weight, cos, sin):
    rows = normed.shape[0]
    tile = 256

    def kernel(n_ref, w_ref, c_ref, s_ref, q_ref, kv_ref):
        full = jnp.dot(n_ref[...], w_ref[...], preferred_element_type=F32)
        cos_t, sin_t = c_ref[...], s_ref[...]
        low = lax.rem(lax.broadcasted_iota(jnp.int32, (tile, 128), 1), 64) < 32
        for b in range(3):
            block = turn(full[:, 128 * b : 128 * b + 128], cos_t, sin_t, low)
            q_ref[:, 128 * b : 128 * b + 128] = (block.astype(BF).astype(F32) * 0.125).astype(BF)
        kv_ref[:, :128] = turn(full[:, 384:512], cos_t, sin_t, low).astype(BF)
        kv_ref[:, 128:] = full[:, 512:].astype(BF)

    return pl.pallas_call(
        kernel,
        name="project",
        grid=(rows // tile,),
        in_specs=[
            pl.BlockSpec((tile, D), lambda i: (i, 0)),
            pl.BlockSpec((D, 640), lambda i: (0, 0)),
            pl.BlockSpec((tile, 128), lambda i: (i, 0)),
            pl.BlockSpec((tile, 128), lambda i: (i, 0)),
        ],
        out_specs=[
            pl.BlockSpec((tile, 384), lambda i: (i, 0)),
            pl.BlockSpec((tile, 256), lambda i: (i, 0)),
        ],
        out_shape=[
            jax.ShapeDtypeStruct((rows, 384), BF),
            jax.ShapeDtypeStruct((rows, 256), BF),
        ],
        compiler_params=pltpu.CompilerParams(vmem_limit_bytes=VMEM_LIMIT),
    )(normed, weight, cos, sin)


def unproject(q_grad, kv_grad, weight, cos, sin):
    rows = q_grad.shape[0]
    tile = 256

    def kernel(q_ref, kv_ref, w_ref, c_ref, s_ref, pg_ref, dn_ref):
        cos_t, sin_t = c_ref[...], -s_ref[...]
        low = lax.rem(lax.broadcasted_iota(jnp.int32, (tile, 128), 1), 64) < 32
        total = kv_ref[0].astype(F32)
        for c in range(1, kv_ref.shape[0]):
            total += kv_ref[c].astype(F32)
        for b in range(3):
            block = q_ref[:, 128 * b : 128 * b + 128].astype(BF).astype(F32)
            pg_ref[:, 128 * b : 128 * b + 128] = turn(block, cos_t, sin_t, low).astype(BF)
        block = total[:, :128].astype(BF).astype(F32)
        pg_ref[:, 384:512] = turn(block, cos_t, sin_t, low).astype(BF)
        pg_ref[:, 512:] = total[:, 128:].astype(BF)
        dn_ref[...] = dot_general(pg_ref[...], w_ref[...], 1, 1).astype(BF)

    return pl.pallas_call(
        kernel,
        name="unproject",
        grid=(rows // tile,),
        in_specs=[
            pl.BlockSpec((tile, 384), lambda i: (i, 0)),
            pl.BlockSpec((kv_grad.shape[0], tile, 256), lambda i: (0, i, 0)),
            pl.BlockSpec((D, 640), lambda i: (0, 0)),
            pl.BlockSpec((tile, 128), lambda i: (i, 0)),
            pl.BlockSpec((tile, 128), lambda i: (i, 0)),
        ],
        out_specs=[
            pl.BlockSpec((tile, 640), lambda i: (i, 0)),
            pl.BlockSpec((tile, D), lambda i: (i, 0)),
        ],
        out_shape=[
            jax.ShapeDtypeStruct((rows, 640), BF),
            jax.ShapeDtypeStruct((rows, D), BF),
        ],
        compiler_params=pltpu.CompilerParams(vmem_limit_bytes=VMEM_LIMIT),
    )(q_grad, kv_grad, weight, cos, sin)


TQ = 256
TK = 512


def head_block(block, head):
    low = lax.broadcasted_iota(jnp.int32, block.shape, 1) < 64
    return jnp.where(low if head == 0 else jnp.logical_not(low), block, jnp.zeros_like(block))


def visible(kp_ref, ks_ref, qp_ref, qs_ref, start):
    key_pos = kp_ref[pl.ds(start, TK), :]
    key_seg = ks_ref[pl.ds(start, TK), :]
    return (key_pos <= qp_ref[...]) & ((key_seg == 0) | (key_seg == qs_ref[...]))


HEAD_SLOTS = [(0, 0), (0, 1), (1, 0), (1, 1), (2, 0)]


def attend_forward(q, kv, q_pos, q_seg, k_pos, k_seg):
    rows, keys = q.shape[0], kv.shape[0]

    def kernel(q_ref, kv_ref, qp_ref, qs_ref, kp_ref, ks_ref, a_ref, o_ref, lse_ref, acc, top, tot):
        acc[...] = jnp.zeros_like(acc)
        top[...] = jnp.full_like(top, -1e30)
        tot[...] = jnp.zeros_like(tot)
        heads = [head_block(q_ref[:, 128 * b : 128 * b + 128], h) for b, h in HEAD_SLOTS]

        @pl.loop(0, keys // TK)
        def _(t):
            start = pl.multiple_of(t * TK, TK)
            k_tile = kv_ref[pl.ds(start, TK), :128]
            v_tile = kv_ref[pl.ds(start, TK), 128:]
            seen = visible(kp_ref, ks_ref, qp_ref, qs_ref, start)
            for j in range(5):
                scores = dot_general(k_tile, heads[j], 1, 1)
                scores = jnp.where(seen, scores, -1e30)
                old = top[j : j + 1, :]
                new = jnp.maximum(old, jnp.max(scores, axis=0, keepdims=True))
                expons = jnp.exp(scores - new)
                shrink = jnp.exp(old - new)
                tot[j : j + 1, :] = tot[j : j + 1, :] * shrink + jnp.sum(
                    expons, axis=0, keepdims=True
                )
                acc[j] = acc[j] * shrink + dot_general(v_tile, expons.astype(BF), 0, 0)
                top[j : j + 1, :] = new

        for j, (b, h) in enumerate(HEAD_SLOTS):
            out = acc[j] / tot[j : j + 1, :]
            acc[j] = out
        lse_ref[...] = top[...] + jnp.log(jnp.maximum(tot[...], 1e-37))
        low = lax.broadcasted_iota(jnp.int32, (TQ, 128), 1) < 64
        for b in range(3):
            first = acc[2 * b].T
            if b < 2:
                block = jnp.where(low, first, acc[2 * b + 1].T)
            else:
                block = jnp.where(low, first, 0.0)
            o_ref[:, 128 * b : 128 * b + 128] = block
            a_ref[:, 128 * b : 128 * b + 128] = block.astype(BF)

    return pl.pallas_call(
        kernel,
        name="attend_forward",
        grid=(rows // TQ,),
        in_specs=[
            pl.BlockSpec((TQ, 384), lambda i: (i, 0)),
            pl.BlockSpec((keys, 256), lambda i: (0, 0)),
            pl.BlockSpec((1, TQ), lambda i: (0, i)),
            pl.BlockSpec((1, TQ), lambda i: (0, i)),
            pl.BlockSpec((keys, 1), lambda i: (0, 0)),
            pl.BlockSpec((keys, 1), lambda i: (0, 0)),
        ],
        out_specs=[
            pl.BlockSpec((TQ, 384), lambda i: (i, 0)),
            pl.BlockSpec((TQ, 384), lambda i: (i, 0)),
            pl.BlockSpec((8, TQ), lambda i: (0, i)),
        ],
        out_shape=[
            jax.ShapeDtypeStruct((rows, 384), BF),
            jax.ShapeDtypeStruct((rows, 384), F32),
            jax.ShapeDtypeStruct((8, rows), F32),
        ],
        scratch_shapes=[
            pltpu.VMEM((5, 128, TQ), F32),
            pltpu.VMEM((8, TQ), F32),
            pltpu.VMEM((8, TQ), F32),
        ],
        compiler_params=pltpu.CompilerParams(vmem_limit_bytes=VMEM_LIMIT),
    )(q, kv, q_pos, q_seg, k_pos, k_seg)


def attend_backward(q, kv, q_pos, q_seg, k_pos, k_seg, lse, out, out_grad):
    rows, keys = q.shape[0], kv.shape[0]
    steps = rows // TQ

    def kernel(
        q_ref, kv_ref, qp_ref, qs_ref, kp_ref, ks_ref, lse_ref, o_ref, do_ref, dq_ref, dkv_ref,
        acc, kv_acc,
    ):
        @pl.when(pl.program_id(0) == 0)
        def _():
            kv_acc[...] = jnp.zeros_like(kv_acc)

        acc[...] = jnp.zeros_like(acc)
        heads = [head_block(q_ref[:, 128 * b : 128 * b + 128], h) for b, h in HEAD_SLOTS]
        grads = [head_block(do_ref[:, 128 * b : 128 * b + 128], h) for b, h in HEAD_SLOTS]
        delta = []
        for j, (b, h) in enumerate(HEAD_SLOTS):
            product = grads[j].astype(F32) * o_ref[:, 128 * b : 128 * b + 128]
            delta.append(jnp.sum(product.T, axis=0, keepdims=True))

        @pl.loop(0, keys // TK)
        def _(t):
            start = pl.multiple_of(t * TK, TK)
            k_tile = kv_ref[pl.ds(start, TK), :128]
            v_tile = kv_ref[pl.ds(start, TK), 128:]
            seen = visible(kp_ref, ks_ref, qp_ref, qs_ref, start)
            k_sum = jnp.zeros((TK, 128), F32)
            v_sum = jnp.zeros((TK, 128), F32)
            for j in range(5):
                scores = dot_general(k_tile, heads[j], 1, 1)
                probs = jnp.where(seen, jnp.exp(scores - lse_ref[j : j + 1, :]), 0.0)
                prob_grad = dot_general(v_tile, grads[j], 1, 1)
                score_grad = (probs * (prob_grad - delta[j])).astype(BF)
                v_sum += jnp.dot(probs.astype(BF), grads[j], preferred_element_type=F32)
                k_sum += jnp.dot(score_grad, heads[j], preferred_element_type=F32)
                acc[j] += dot_general(k_tile, score_grad, 0, 0)
            kv_acc[pl.ds(start, TK), :128] += k_sum
            kv_acc[pl.ds(start, TK), 128:] += v_sum

        low = lax.broadcasted_iota(jnp.int32, (TQ, 128), 1) < 64
        for b in range(3):
            first = acc[2 * b].T * 0.125
            if b < 2:
                block = jnp.where(low, first, acc[2 * b + 1].T * 0.125)
            else:
                block = jnp.where(low, first, 0.0)
            dq_ref[:, 128 * b : 128 * b + 128] = block.astype(BF)

        @pl.when(pl.program_id(0) == steps - 1)
        def _():
            dkv_ref[...] = kv_acc[...].astype(BF)

    return pl.pallas_call(
        kernel,
        name="attend_backward",
        grid=(steps,),
        in_specs=[
            pl.BlockSpec((TQ, 384), lambda i: (i, 0)),
            pl.BlockSpec((keys, 256), lambda i: (0, 0)),
            pl.BlockSpec((1, TQ), lambda i: (0, i)),
            pl.BlockSpec((1, TQ), lambda i: (0, i)),
            pl.BlockSpec((keys, 1), lambda i: (0, 0)),
            pl.BlockSpec((keys, 1), lambda i: (0, 0)),
            pl.BlockSpec((8, TQ), lambda i: (0, i)),
            pl.BlockSpec((TQ, 384), lambda i: (i, 0)),
            pl.BlockSpec((TQ, 384), lambda i: (i, 0)),
        ],
        out_specs=[
            pl.BlockSpec((TQ, 384), lambda i: (i, 0)),
            pl.BlockSpec((keys, 256), lambda i: (0, 0)),
        ],
        out_shape=[
            jax.ShapeDtypeStruct((rows, 384), BF),
            jax.ShapeDtypeStruct((keys, 256), BF),
        ],
        scratch_shapes=[pltpu.VMEM((5, 128, TQ), F32), pltpu.VMEM((keys, 256), F32)],
        compiler_params=pltpu.CompilerParams(vmem_limit_bytes=VMEM_LIMIT),
    )(q, kv, q_pos, q_seg, k_pos, k_seg, lse, out, out_grad)


def rms_factor(values):
    return lax.rsqrt(jnp.mean(values * values, axis=-1, keepdims=True) + EPSILON)


def norm_back(grad_normed, inputs, factor, gain):
    weighted = grad_normed * gain
    inner_mean = jnp.mean(weighted * inputs, axis=-1, keepdims=True)
    input_part = factor * weighted - inputs * (factor * factor * factor) * inner_mean
    return (input_part, jnp.sum(grad_normed * inputs * factor, axis=0))


def rope_tables(positions):
    frequency = jnp.exp(jnp.arange(32, dtype=F32) * (-math.log(10000.0) / 32))
    angles = positions.astype(F32)[:, None] * jnp.tile(frequency, 4)[None, :]
    sign = jnp.where(jnp.arange(128) % 64 < 32, -1.0, 1.0).astype(F32)
    return jnp.cos(angles), jnp.sin(angles) * sign[None, :]


def build(sizes):
    ctx, wsh = sizes["ctx"], sizes["wsh"]
    shards = ctx * wsh
    link = Exchange(sizes)

    def local(
        tokens,
        segment_ids,
        positions,
        attend_gain,
        query_key_value,
        attend_out,
        feed_gain,
        gate_up,
        down_weight,
        upstream,
    ):
        own = tokens.shape[0]
        plane = own * wsh
        group = plane * ctx
        core = lax.axis_index("grp")
        odd = lax.rem(lax.axis_index("wsh"), 2) == 1
        inputs = tokens.astype(F32)
        factor_one = rms_factor(inputs)
        normed_one = (inputs * factor_one * attend_gain).astype(BF)
        marks = jnp.pad(segment_ids * 65536 + positions, (0, 1024 - own)).reshape(8, 128)

        normed_all, w_qkv, marks_plane = link.run(
            "gather_one",
            1,
            [
                link.gather(normed_one, ("wsh",)),
                link.swap(qkv_columns(query_key_value), ("wsh",)),
                link.gather(marks, ("wsh",)),
            ],
        )
        normed_all = normed_all.reshape(plane, D)
        w_qkv = w_qkv.reshape(D, 640)
        plane_marks = marks_plane.reshape(wsh, 1024)[:, :own].reshape(plane)
        q_pos, q_seg = plane_marks % 65536, plane_marks // 65536
        cos, sin = rope_tables(q_pos)
        queries, kv_own = project(normed_all, w_qkv, cos, sin)

        kv_all, marks_all, dy_all, w_gate, w_up = link.run(
            "gather_keys",
            2,
            [
                link.gather(kv_own, ("ctx",)),
                link.gather(marks_plane, ("ctx",)),
                link.gather(upstream, ("wsh",)),
                link.columns(gate_up, ("wsh",), 0, FF // wsh),
                link.columns(gate_up, ("wsh",), FF, FF // wsh),
            ],
        )
        kv_all = kv_all.reshape(group, 256)
        dy_all = dy_all.reshape(plane, D)
        w_gate, w_up = w_gate.reshape(D, FF // wsh), w_up.reshape(D, FF // wsh)
        marks_all = marks_all.reshape(shards, 1024)[:, :own].reshape(group, 1)
        k_pos, k_seg = marks_all % 65536, marks_all // 65536
        q_pos, q_seg = q_pos.reshape(1, plane), q_seg.reshape(1, plane)
        attended, attended_wide, lse = attend_forward(queries, kv_all, q_pos, q_seg, k_pos, k_seg)

        w_out = spread_rows(attend_out, odd)
        out_part = jnp.dot(attended, w_out, preferred_element_type=F32).astype(BF)
        (out_parts,) = link.run(
            "scatter_out", 3, [link.swap(out_part.reshape(wsh, own, D), ("wsh",))]
        )
        middle = inputs + jnp.sum(out_parts.astype(F32), axis=0)
        factor_two = rms_factor(middle)
        normed_two = (middle * factor_two * feed_gain).astype(BF)
        (normed_two_all,) = link.run("gather_two", 4, [link.gather(normed_two, ("wsh",))])
        normed_two_all = normed_two_all.reshape(plane, D)

        gate_part = jnp.dot(normed_two_all, w_gate, preferred_element_type=F32)
        up_part = jnp.dot(normed_two_all, w_up, preferred_element_type=F32)
        hidden_grad = dot_general(dy_all, down_weight, 1, 1)
        sigmoid_gate = jax.nn.sigmoid(gate_part)
        silu_gate = gate_part * sigmoid_gate
        hidden = (silu_gate * up_part).astype(BF)
        gate_grad = (
            hidden_grad * up_part * sigmoid_gate * (1.0 + gate_part * (1.0 - sigmoid_gate))
        ).astype(BF)
        up_grad = (hidden_grad * silu_gate).astype(BF)
        down_part = jnp.dot(hidden, down_weight, preferred_element_type=F32).astype(BF)
        two_part = (dot_general(gate_grad, w_gate, 1, 1) + dot_general(up_grad, w_up, 1, 1)).astype(
            BF
        )
        two_parts, down_parts = link.run(
            "scatter_feed",
            5,
            [
                link.swap(two_part.reshape(wsh, own, D), ("wsh",)),
                link.swap(down_part.reshape(wsh, own, D), ("wsh",)),
            ],
        )
        activations = (middle + jnp.sum(down_parts.astype(F32), axis=0)).astype(BF)
        normed_two_grad = jnp.sum(two_parts.astype(F32), axis=0)
        middle_part, feed_gain_grad = norm_back(normed_two_grad, middle, factor_two, feed_gain)
        middle_grad = upstream.astype(F32) + middle_part
        branch_grad = middle_grad.astype(BF)

        down_grad = dot_general(hidden, dy_all, 0, 0).astype(BF)
        gate_w_grad = dot_general(normed_two_all, gate_grad, 0, 0).astype(BF)
        up_w_grad = dot_general(normed_two_all, up_grad, 0, 0).astype(BF)
        ffn_rows = FF // shards // 2
        down_halves = down_grad.reshape(ctx, 2, ffn_rows, D).transpose(1, 0, 2, 3)
        gate_halves = jnp.stack([gate_w_grad, up_w_grad]).reshape(2, shards, D // shards, FF // wsh)

        branch_all, down_pair, gate_pair = link.run(
            "gather_branch",
            6,
            [
                link.gather(branch_grad, ("wsh",)),
                link.swap(down_halves, ("grp",)),
                link.swap(gate_halves, ("grp",)),
            ],
        )
        branch_all = branch_all.reshape(plane, D)
        down_send = (down_pair[0].astype(F32) + down_pair[1].astype(F32)).astype(BF)
        gate_send = (gate_pair[0].astype(F32) + gate_pair[1].astype(F32)).astype(BF)
        attended_grad = dot_general(branch_all, w_out, 1, 1).astype(BF)
        q_grad, kv_grad = attend_backward(
            queries, kv_all, q_pos, q_seg, k_pos, k_seg, lse, attended_wide, attended_grad
        )
        kv_parts, down_got, gate_got = link.run(
            "scatter_keys",
            7,
            [
                link.swap(kv_grad.reshape(ctx, plane, 256), ("ctx",)),
                link.owners(down_send),
                link.swap(gate_send, ("ctx", "wsh")),
            ],
        )
        projected_grad, one_part = unproject(q_grad, kv_parts, w_qkv, cos, sin)
        qkv_grad = dot_general(normed_all, projected_grad, 0, 0).astype(BF)
        out_grad = collect_rows(dot_general(attended, branch_all, 0, 0), odd).astype(BF)
        qkv_halves = qkv_grad.reshape(shards, D // shards, 2, 320).transpose(2, 0, 1, 3)
        out_halves = out_grad.reshape(ctx, D // shards, 2, 576).transpose(2, 0, 1, 3)
        one_parts, qkv_pair, out_pair = link.run(
            "scatter_one",
            8,
            [
                link.swap(one_part.reshape(wsh, own, D), ("wsh",)),
                link.swap(qkv_halves, ("grp",)),
                link.swap(out_halves, ("grp",)),
            ],
        )
        normed_one_grad = jnp.sum(one_parts.astype(F32), axis=0)
        input_part, attend_gain_grad = norm_back(normed_one_grad, inputs, factor_one, attend_gain)
        input_grad = middle_grad + input_part
        qkv_send = (qkv_pair[0].astype(F32) + qkv_pair[1].astype(F32)).astype(BF)
        out_send = (out_pair[0].astype(F32) + out_pair[1].astype(F32)).astype(BF)
        gains = jnp.stack([attend_gain_grad, feed_gain_grad]).reshape(2, shards, D // shards)
        gains = jnp.pad(gains.transpose(1, 0, 2), ((0, 0), (0, 6), (0, 128 - D // shards)))
        qkv_got, out_got, gains_got = link.run(
            "scatter_weights",
            9,
            [
                link.swap(qkv_send, ("ctx", "wsh")),
                link.owners(out_send),
                link.swap(gains, ("ctx", "wsh")),
            ],
        )

        def over_ctx(x):
            return jnp.sum(x.reshape((ctx, wsh) + x.shape[1:]).astype(F32), axis=0)

        down_half = jnp.sum(down_got.astype(F32), axis=0).astype(BF)
        out_half = jnp.sum(out_got.astype(F32), axis=0).astype(BF)
        gate_half = over_ctx(gate_got).astype(BF)
        qkv_half = over_ctx(qkv_got).astype(BF)
        gain_half = jnp.sum(gains_got, axis=0)
        down_two, out_two, gate_two, qkv_two, gain_two = link.run(
            "swap_cores",
            10,
            [
                link.gather(down_half, ("grp",)),
                link.gather(out_half, ("grp",)),
                link.gather(gate_half, ("grp",)),
                link.gather(qkv_half, ("grp",)),
                link.gather(gain_half, ("grp",)),
            ],
        )
        rows = D // shards
        down_out = down_two.reshape(FF // shards, D).astype(F32)
        out_out = out_two.transpose(1, 0, 2).reshape(rows, D).astype(F32)
        gate_out = gate_two.transpose(2, 0, 1, 3).reshape(rows, 2 * FF).astype(F32)
        qkv_out = qkv_restore(
            qkv_two.transpose(1, 2, 0, 3).reshape(wsh, rows, 640).astype(F32)
        )
        gain_out = gain_two[0] + gain_two[1]
        return (
            activations,
            input_grad,
            qkv_out,
            out_out,
            gate_out,
            down_out,
            gain_out[0, :rows],
            gain_out[1, :rows],
        )

    return local


def solution(mesh):
    whole = ("grp", "ctx", "wsh")
    in_specs = (
        P(whole, None),
        P(whole),
        P(whole),
        P(),
        P("wsh", None),
        P("wsh", None),
        P(),
        P("wsh", None),
        P("wsh", None),
        P(whole, None),
    )
    out_specs = (
        P(whole, None),
        P(whole, None),
        P(("ctx", "wsh"), None),
        P(("ctx", "wsh"), None),
        P(("ctx", "wsh"), None),
        P(("ctx", "wsh"), None),
        P(("ctx", "wsh")),
        P(("ctx", "wsh")),
    )
    return jax.shard_map(
        build(dict(mesh.shape)), mesh=mesh, in_specs=in_specs, out_specs=out_specs, check_vma=False
    )
```

```python
import itertools
import math

import jax
import jax.numpy as jnp
from jax import lax
from jax.experimental import pallas as pl
from jax.experimental.pallas import tpu as pltpu
from jax.sharding import PartitionSpec as P

HEADS = 18
KV_HEADS = 6
HEAD_DIM = 64
FF = 3072
D = 1152
QW = 1152
KW = 384
EPSILON = 1e-05
MESH = pl.DeviceIdType.MESH
F32 = jnp.float32
BF = jnp.bfloat16
VMEM_LIMIT = 56 << 20


def dot_general(a, b, ca, cb):
    return lax.dot_general(a, b, (((ca,), (cb,)), ((), ())), preferred_element_type=F32)


class Exchange:
    def __init__(self, sizes):
        self.sizes = sizes

    def place(self, axes, offset):
        where, index = {}, 0
        for axis, step in zip(axes, offset):
            size = self.sizes[axis]
            spot = lax.axis_index(axis)
            if step:
                spot = lax.rem(spot + step, size)
            where[axis] = spot
            index = index * size + spot
        return where, index

    def offsets(self, axes):
        return list(itertools.product(*[range(self.sizes[axis]) for axis in axes]))

    def gather(self, x, axes):
        count = math.prod(self.sizes[axis] for axis in axes)
        return ("peer", x, axes, lambda ref, p: ref, (count,) + x.shape, x.shape)

    def swap(self, x, axes):
        return ("peer", x, axes, lambda ref, p: ref.at[p], x.shape, x.shape[1:])

    def columns(self, x, axes, start, width):
        count = math.prod(self.sizes[axis] for axis in axes)
        source = lambda ref, p: ref.at[
            :, pl.ds(pl.multiple_of(lax.axis_index("grp") * start + p * width, 128), width)
        ]
        return ("peer", x, axes, source, (count, x.shape[0], width), (x.shape[0], width))

    def turn_over(self, x):
        return ("owner", x, None, None, x.shape, x.shape)

    def run(self, name, number, ops):
        ctx, wsh = self.sizes["ctx"], self.sizes["wsh"]
        total = 0
        for kind, x, axes, *_ in ops:
            total += 1 if kind == "owner" else math.prod(self.sizes[a] for a in axes)
        peers = {}
        for kind, x, axes, *_ in ops:
            for offset in self.offsets(axes if kind == "peer" else ("ctx", "wsh")):
                axes_of = axes if kind == "peer" else ("ctx", "wsh")
                key = tuple(sorted((a, o) for a, o in zip(axes_of, offset) if o))
                if key:
                    peers[key] = (axes_of, offset)
        count = len(ops)

        def kernel(*refs):
            ins, outs = refs[:count], refs[count : 2 * count]
            bounce = refs[2 * count : 3 * count]
            send, recv, near = refs[3 * count :]
            barrier = pltpu.get_barrier_semaphore()
            for axes, offset in peers.values():
                where, _ = self.place(axes, offset)
                pl.semaphore_signal(barrier, 1, device_id=where, device_id_type=MESH)
            pl.semaphore_wait(barrier, len(peers))
            first, second, remote, late = [], [], [], []
            slot = 0
            for op, (kind, x, axes, source, _, _) in enumerate(ops):
                if kind == "peer":
                    none = tuple(0 for _ in axes)
                    _, me = self.place(axes, none)
                    for offset in self.offsets(axes):
                        where, index = self.place(axes, offset)
                        if any(offset):
                            copy = pltpu.make_async_remote_copy(
                                source(ins[op], index),
                                outs[op].at[me],
                                send.at[slot],
                                recv.at[slot],
                                device_id=where,
                                device_id_type=MESH,
                            )
                            copy.start()
                            remote.append(copy)
                        else:
                            copy = pltpu.make_async_copy(
                                source(ins[op], me), bounce[op], near.at[op]
                            )
                            copy.start()
                            first.append(copy)
                            second.append(
                                pltpu.make_async_copy(bounce[op], outs[op].at[me], near.at[op])
                            )
                        slot += 1
                else:
                    my_c, my_w = lax.axis_index("ctx"), lax.axis_index("wsh")
                    shard = my_w * ctx + my_c
                    to_c, to_w = shard // wsh, lax.rem(shard, wsh)
                    own = jnp.logical_and(to_c == my_c, to_w == my_w)
                    copy = pltpu.make_async_remote_copy(
                        ins[op],
                        outs[op],
                        send.at[slot],
                        recv.at[slot],
                        device_id={"ctx": to_c, "wsh": to_w},
                        device_id_type=MESH,
                    )
                    inward = pltpu.make_async_copy(ins[op], bounce[op], near.at[op])
                    outward = pltpu.make_async_copy(bounce[op], outs[op], near.at[op])

                    @pl.when(jnp.logical_not(own))
                    def _():
                        copy.start()

                    late.append((own, copy, inward, outward))
                    slot += 1
            for one, two in zip(first, second):
                one.wait()
                two.start()
            for own, copy, inward, outward in late:

                @pl.when(own)
                def _():
                    inward.start()
                    inward.wait()
                    outward.start()
                    outward.wait()

            for copy in second:
                copy.wait()
            for own, copy, inward, outward in late:

                @pl.when(jnp.logical_not(own))
                def _():
                    copy.wait()

            for copy in remote:
                copy.wait()

        return pl.pallas_call(
            kernel,
            name=name,
            out_shape=[jax.ShapeDtypeStruct(op[4], op[1].dtype) for op in ops],
            in_specs=[pl.BlockSpec(memory_space=pl.ANY)] * count,
            out_specs=[pl.BlockSpec(memory_space=pl.ANY)] * count,
            scratch_shapes=[pltpu.VMEM(op[5], op[1].dtype) for op in ops]
            + [
                pltpu.SemaphoreType.DMA((total,)),
                pltpu.SemaphoreType.DMA((total,)),
                pltpu.SemaphoreType.DMA((count,)),
            ],
            compiler_params=pltpu.CompilerParams(
                collective_id=number, has_side_effects=True, vmem_limit_bytes=VMEM_LIMIT
            ),
        )(*[op[1] for op in ops])


def head_plan(w):
    pair, odd = w // 2, w % 2
    start = 9 * pair + 4 * odd
    if odd:
        f_heads, h_heads = [start + 2, start + 3, start + 4], [start, start + 1]
        f_kv, h_kv = 3 * pair + 2, 3 * pair + 1
    else:
        f_heads, h_heads = [start, start + 1, start + 2], [start + 3, start + 4]
        f_kv, h_kv = 3 * pair, 3 * pair + 1
    q_order = [f_heads[0], h_heads[0], f_heads[1], h_heads[1], f_heads[2], None]
    return q_order, [f_kv, h_kv]


def qkv_columns(weight):
    blank = jnp.zeros((weight.shape[0], HEAD_DIM), weight.dtype)
    parts = []
    for w in range(4):
        q_order, kv_order = head_plan(w)
        pieces = [
            blank if h is None else weight[:, h * HEAD_DIM : (h + 1) * HEAD_DIM] for h in q_order
        ]
        for base in (QW, QW + KW):
            pieces += [
                weight[:, base + h * HEAD_DIM : base + (h + 1) * HEAD_DIM] for h in kv_order
            ]
        parts.append(jnp.concatenate(pieces, axis=1))
    return jnp.stack(parts)


def qkv_restore(parts):
    found = {}
    for w in range(4):
        q_order, kv_order = head_plan(w)
        slots = list(q_order) + [HEADS + h for h in kv_order]
        slots += [HEADS + KV_HEADS + h for h in kv_order]
        for at, head in enumerate(slots):
            if head is not None:
                found.setdefault(head, []).append(
                    parts[w][:, at * HEAD_DIM : (at + 1) * HEAD_DIM]
                )
    pieces = []
    for head in range(HEADS + 2 * KV_HEADS):
        term = found[head][0]
        for other in found[head][1:]:
            term = term + other
        pieces.append(term)
    return jnp.concatenate(pieces, axis=1)


def spread_rows(rows, odd):
    n = rows.shape[1]
    half = jnp.zeros((32, n), rows.dtype)
    blank = jnp.zeros((64, n), rows.dtype)
    even_rows = jnp.concatenate(
        [rows[0:64], rows[192:256], rows[64:128], rows[256:288], half, rows[128:192], blank]
    )
    odd_rows = jnp.concatenate(
        [rows[96:160], half, rows[0:32], rows[160:224], rows[32:96], rows[224:288], blank]
    )
    return jnp.where(odd, odd_rows, even_rows)


def collect_rows(wide, odd):
    f0, h0, f1, h1, f2 = (wide[64 * i : 64 * i + 64] for i in range(5))
    even_rows = jnp.concatenate([f0, f1, f2, h0, h1[:32]])
    odd_rows = jnp.concatenate([h0[32:], h1, f0, f1, f2])
    return jnp.where(odd, odd_rows, even_rows)


def turn(x, cos, sin, lanes):
    swapped = jnp.where(lanes, pltpu.roll(x, 96, 1), pltpu.roll(x, 32, 1))
    return x * cos + swapped * sin


def project(normed, weight, cos, sin):
    rows = normed.shape[0]
    tile = 256

    def kernel(n_ref, w_ref, c_ref, s_ref, q_ref, kv_ref):
        full = jnp.dot(n_ref[...], w_ref[...], preferred_element_type=F32)
        cos_t, sin_t = c_ref[...], s_ref[...]
        low = lax.rem(lax.broadcasted_iota(jnp.int32, (tile, 128), 1), 64) < 32
        for b in range(3):
            block = turn(full[:, 128 * b : 128 * b + 128], cos_t, sin_t, low)
            q_ref[:, 128 * b : 128 * b + 128] = (block.astype(BF).astype(F32) * 0.125).astype(BF)
        kv_ref[:, :128] = turn(full[:, 384:512], cos_t, sin_t, low).astype(BF)
        kv_ref[:, 128:] = full[:, 512:].astype(BF)

    return pl.pallas_call(
        kernel,
        name="project",
        grid=(rows // tile,),
        in_specs=[
            pl.BlockSpec((tile, D), lambda i: (i, 0)),
            pl.BlockSpec((D, 640), lambda i: (0, 0)),
            pl.BlockSpec((tile, 128), lambda i: (i, 0)),
            pl.BlockSpec((tile, 128), lambda i: (i, 0)),
        ],
        out_specs=[
            pl.BlockSpec((tile, 384), lambda i: (i, 0)),
            pl.BlockSpec((tile, 256), lambda i: (i, 0)),
        ],
        out_shape=[
            jax.ShapeDtypeStruct((rows, 384), BF),
            jax.ShapeDtypeStruct((rows, 256), BF),
        ],
        compiler_params=pltpu.CompilerParams(vmem_limit_bytes=VMEM_LIMIT),
    )(normed, weight, cos, sin)


def unproject(q_grad, kv_grad, weight, cos, sin):
    rows = q_grad.shape[0]
    tile = 256

    def kernel(q_ref, kv_ref, w_ref, c_ref, s_ref, pg_ref, dn_ref):
        cos_t, sin_t = c_ref[...], -s_ref[...]
        low = lax.rem(lax.broadcasted_iota(jnp.int32, (tile, 128), 1), 64) < 32
        total = kv_ref[0].astype(F32)
        for c in range(1, kv_ref.shape[0]):
            total += kv_ref[c].astype(F32)
        for b in range(3):
            block = q_ref[:, 128 * b : 128 * b + 128].astype(BF).astype(F32)
            pg_ref[:, 128 * b : 128 * b + 128] = turn(block, cos_t, sin_t, low).astype(BF)
        block = total[:, :128].astype(BF).astype(F32)
        pg_ref[:, 384:512] = turn(block, cos_t, sin_t, low).astype(BF)
        pg_ref[:, 512:] = total[:, 128:].astype(BF)
        dn_ref[...] = dot_general(pg_ref[...], w_ref[...], 1, 1).astype(BF)

    return pl.pallas_call(
        kernel,
        name="unproject",
        grid=(rows // tile,),
        in_specs=[
            pl.BlockSpec((tile, 384), lambda i: (i, 0)),
            pl.BlockSpec((kv_grad.shape[0], tile, 256), lambda i: (0, i, 0)),
            pl.BlockSpec((D, 640), lambda i: (0, 0)),
            pl.BlockSpec((tile, 128), lambda i: (i, 0)),
            pl.BlockSpec((tile, 128), lambda i: (i, 0)),
        ],
        out_specs=[
            pl.BlockSpec((tile, 640), lambda i: (i, 0)),
            pl.BlockSpec((tile, D), lambda i: (i, 0)),
        ],
        out_shape=[
            jax.ShapeDtypeStruct((rows, 640), BF),
            jax.ShapeDtypeStruct((rows, D), BF),
        ],
        compiler_params=pltpu.CompilerParams(vmem_limit_bytes=VMEM_LIMIT),
    )(q_grad, kv_grad, weight, cos, sin)


TQ = 256
TK = 512


def head_block(block, head):
    low = lax.broadcasted_iota(jnp.int32, block.shape, 1) < 64
    return jnp.where(low if head == 0 else jnp.logical_not(low), block, jnp.zeros_like(block))


def visible(kp_ref, ks_ref, qp_ref, qs_ref, start):
    key_pos = kp_ref[pl.ds(start, TK), :]
    key_seg = ks_ref[pl.ds(start, TK), :]
    return (key_pos <= qp_ref[...]) & ((key_seg == 0) | (key_seg == qs_ref[...]))


HEAD_SLOTS = [(0, 0), (0, 1), (1, 0), (1, 1), (2, 0)]


def attend_forward(q, kv, q_pos, q_seg, k_pos, k_seg):
    rows, keys = q.shape[0], kv.shape[0]

    def kernel(q_ref, kv_ref, qp_ref, qs_ref, kp_ref, ks_ref, a_ref, o_ref, lse_ref, acc, top, tot):
        acc[...] = jnp.zeros_like(acc)
        top[...] = jnp.full_like(top, -1e30)
        tot[...] = jnp.zeros_like(tot)
        heads = [head_block(q_ref[:, 128 * b : 128 * b + 128], h) for b, h in HEAD_SLOTS]

        @pl.loop(0, keys // TK)
        def _(t):
            start = pl.multiple_of(t * TK, TK)
            k_tile = kv_ref[pl.ds(start, TK), :128]
            v_tile = kv_ref[pl.ds(start, TK), 128:]
            seen = visible(kp_ref, ks_ref, qp_ref, qs_ref, start)
            for j in range(5):
                scores = dot_general(k_tile, heads[j], 1, 1)
                scores = jnp.where(seen, scores, -1e30)
                old = top[j : j + 1, :]
                new = jnp.maximum(old, jnp.max(scores, axis=0, keepdims=True))
                expons = jnp.exp(scores - new)
                shrink = jnp.exp(old - new)
                tot[j : j + 1, :] = tot[j : j + 1, :] * shrink + jnp.sum(
                    expons, axis=0, keepdims=True
                )
                acc[j] = acc[j] * shrink + dot_general(v_tile, expons.astype(BF), 0, 0)
                top[j : j + 1, :] = new

        for j, (b, h) in enumerate(HEAD_SLOTS):
            out = acc[j] / tot[j : j + 1, :]
            acc[j] = out
        lse_ref[...] = top[...] + jnp.log(jnp.maximum(tot[...], 1e-37))
        low = lax.broadcasted_iota(jnp.int32, (TQ, 128), 1) < 64
        for b in range(3):
            first = acc[2 * b].T
            if b < 2:
                block = jnp.where(low, first, acc[2 * b + 1].T)
            else:
                block = jnp.where(low, first, 0.0)
            o_ref[:, 128 * b : 128 * b + 128] = block
            a_ref[:, 128 * b : 128 * b + 128] = block.astype(BF)

    return pl.pallas_call(
        kernel,
        name="attend_forward",
        grid=(rows // TQ,),
        in_specs=[
            pl.BlockSpec((TQ, 384), lambda i: (i, 0)),
            pl.BlockSpec((keys, 256), lambda i: (0, 0)),
            pl.BlockSpec((1, TQ), lambda i: (0, i)),
            pl.BlockSpec((1, TQ), lambda i: (0, i)),
            pl.BlockSpec((keys, 1), lambda i: (0, 0)),
            pl.BlockSpec((keys, 1), lambda i: (0, 0)),
        ],
        out_specs=[
            pl.BlockSpec((TQ, 384), lambda i: (i, 0)),
            pl.BlockSpec((TQ, 384), lambda i: (i, 0)),
            pl.BlockSpec((8, TQ), lambda i: (0, i)),
        ],
        out_shape=[
            jax.ShapeDtypeStruct((rows, 384), BF),
            jax.ShapeDtypeStruct((rows, 384), F32),
            jax.ShapeDtypeStruct((8, rows), F32),
        ],
        scratch_shapes=[
            pltpu.VMEM((5, 128, TQ), F32),
            pltpu.VMEM((8, TQ), F32),
            pltpu.VMEM((8, TQ), F32),
        ],
        compiler_params=pltpu.CompilerParams(vmem_limit_bytes=VMEM_LIMIT),
    )(q, kv, q_pos, q_seg, k_pos, k_seg)


def attend_backward(link, q, kv, q_pos, q_seg, k_pos, k_seg, lse, out, out_grad, send_rows):
    rows, keys = q.shape[0], kv.shape[0]
    steps = rows // TQ
    axes = ("ctx", "wsh")
    peers = link.offsets(axes)

    def kernel(
        q_ref, kv_ref, qp_ref, qs_ref, kp_ref, ks_ref, lse_ref, o_ref, do_ref, rows_ref,
        dq_ref, dkv_ref, got_ref, acc, kv_acc, bounce, send, recv, near,
    ):
        _, me = link.place(axes, peers[0])
        copies = []
        for at, offset in enumerate(peers[1:]):
            where, index = link.place(axes, offset)
            copies.append(
                pltpu.make_async_remote_copy(
                    rows_ref.at[index],
                    got_ref.at[me],
                    send.at[at],
                    recv.at[at],
                    device_id=where,
                    device_id_type=MESH,
                )
            )
        inward = pltpu.make_async_copy(rows_ref.at[me], bounce, near)
        outward = pltpu.make_async_copy(bounce, got_ref.at[me], near)

        @pl.when(pl.program_id(0) == 0)
        def _():
            barrier = pltpu.get_barrier_semaphore()
            for offset in peers[1:]:
                where, _ = link.place(axes, offset)
                pl.semaphore_signal(barrier, 1, device_id=where, device_id_type=MESH)
            pl.semaphore_wait(barrier, len(peers) - 1)
            for copy in copies:
                copy.start()
            inward.start()
            inward.wait()
            outward.start()
            kv_acc[...] = jnp.zeros_like(kv_acc)

        acc[...] = jnp.zeros_like(acc)
        heads = [head_block(q_ref[:, 128 * b : 128 * b + 128], h) for b, h in HEAD_SLOTS]
        grads = [head_block(do_ref[:, 128 * b : 128 * b + 128], h) for b, h in HEAD_SLOTS]
        delta = []
        for j, (b, h) in enumerate(HEAD_SLOTS):
            product = grads[j].astype(F32) * o_ref[:, 128 * b : 128 * b + 128]
            delta.append(jnp.sum(product.T, axis=0, keepdims=True))

        @pl.loop(0, keys // TK)
        def _(t):
            start = pl.multiple_of(t * TK, TK)
            k_tile = kv_ref[pl.ds(start, TK), :128]
            v_tile = kv_ref[pl.ds(start, TK), 128:]
            seen = visible(kp_ref, ks_ref, qp_ref, qs_ref, start)
            k_sum = jnp.zeros((TK, 128), F32)
            v_sum = jnp.zeros((TK, 128), F32)
            for j in range(5):
                scores = dot_general(k_tile, heads[j], 1, 1)
                probs = jnp.where(seen, jnp.exp(scores - lse_ref[j : j + 1, :]), 0.0)
                prob_grad = dot_general(v_tile, grads[j], 1, 1)
                score_grad = (probs * (prob_grad - delta[j])).astype(BF)
                v_sum += jnp.dot(probs.astype(BF), grads[j], preferred_element_type=F32)
                k_sum += jnp.dot(score_grad, heads[j], preferred_element_type=F32)
                acc[j] += dot_general(k_tile, score_grad, 0, 0)
            kv_acc[pl.ds(start, TK), :128] += k_sum
            kv_acc[pl.ds(start, TK), 128:] += v_sum

        low = lax.broadcasted_iota(jnp.int32, (TQ, 128), 1) < 64
        for b in range(3):
            first = acc[2 * b].T * 0.125
            if b < 2:
                block = jnp.where(low, first, acc[2 * b + 1].T * 0.125)
            else:
                block = jnp.where(low, first, 0.0)
            dq_ref[:, 128 * b : 128 * b + 128] = block.astype(BF)

        @pl.when(pl.program_id(0) == steps - 1)
        def _():
            dkv_ref[...] = kv_acc[...].astype(BF)
            outward.wait()
            for copy in copies:
                copy.wait()

    return pl.pallas_call(
        kernel,
        name="attend_backward",
        grid=(steps,),
        in_specs=[
            pl.BlockSpec((TQ, 384), lambda i: (i, 0)),
            pl.BlockSpec((keys, 256), lambda i: (0, 0)),
            pl.BlockSpec((1, TQ), lambda i: (0, i)),
            pl.BlockSpec((1, TQ), lambda i: (0, i)),
            pl.BlockSpec((keys, 1), lambda i: (0, 0)),
            pl.BlockSpec((keys, 1), lambda i: (0, 0)),
            pl.BlockSpec((8, TQ), lambda i: (0, i)),
            pl.BlockSpec((TQ, 384), lambda i: (i, 0)),
            pl.BlockSpec((TQ, 384), lambda i: (i, 0)),
            pl.BlockSpec(memory_space=pl.ANY),
        ],
        out_specs=[
            pl.BlockSpec((TQ, 384), lambda i: (i, 0)),
            pl.BlockSpec((keys, 256), lambda i: (0, 0)),
            pl.BlockSpec(memory_space=pl.ANY),
        ],
        out_shape=[
            jax.ShapeDtypeStruct((rows, 384), BF),
            jax.ShapeDtypeStruct((keys, 256), BF),
            jax.ShapeDtypeStruct(send_rows.shape, BF),
        ],
        scratch_shapes=[
            pltpu.VMEM((5, 128, TQ), F32),
            pltpu.VMEM((keys, 256), F32),
            pltpu.VMEM(send_rows.shape[1:], BF),
            pltpu.SemaphoreType.DMA((len(peers),)),
            pltpu.SemaphoreType.DMA((len(peers),)),
            pltpu.SemaphoreType.DMA,
        ],
        compiler_params=pltpu.CompilerParams(
            collective_id=11, has_side_effects=True, vmem_limit_bytes=VMEM_LIMIT
        ),
    )(q, kv, q_pos, q_seg, k_pos, k_seg, lse, out, out_grad, send_rows)


def rms_factor(values):
    return lax.rsqrt(jnp.mean(values * values, axis=-1, keepdims=True) + EPSILON)


def norm_back(grad_normed, inputs, factor, gain):
    weighted = grad_normed * gain
    inner_mean = jnp.mean(weighted * inputs, axis=-1, keepdims=True)
    input_part = factor * weighted - inputs * (factor * factor * factor) * inner_mean
    return (input_part, jnp.sum(grad_normed * inputs * factor, axis=0))


def rope_tables(positions):
    frequency = jnp.exp(jnp.arange(32, dtype=F32) * (-math.log(10000.0) / 32))
    angles = positions.astype(F32)[:, None] * jnp.tile(frequency, 4)[None, :]
    sign = jnp.where(jnp.arange(128) % 64 < 32, -1.0, 1.0).astype(F32)
    return jnp.cos(angles), jnp.sin(angles) * sign[None, :]


def build(sizes):
    ctx, wsh = sizes["ctx"], sizes["wsh"]
    shards = ctx * wsh
    link = Exchange(sizes)

    def local(
        tokens,
        segment_ids,
        positions,
        attend_gain,
        query_key_value,
        attend_out,
        feed_gain,
        gate_up,
        down_weight,
        upstream,
    ):
        own = tokens.shape[0]
        plane = own * wsh
        group = plane * ctx
        core = lax.axis_index("grp")
        odd = lax.rem(lax.axis_index("wsh"), 2) == 1
        inputs = tokens.astype(F32)
        factor_one = rms_factor(inputs)
        normed_one = (inputs * factor_one * attend_gain).astype(BF)
        marks = jnp.pad(segment_ids * 65536 + positions, (0, 1024 - own)).reshape(8, 128)

        normed_all, w_qkv, marks_plane = link.run(
            "gather_one",
            1,
            [
                link.gather(normed_one, ("wsh",)),
                link.swap(qkv_columns(query_key_value), ("wsh",)),
                link.gather(marks, ("wsh",)),
            ],
        )
        normed_all = normed_all.reshape(plane, D)
        w_qkv = w_qkv.reshape(D, 640)
        plane_marks = marks_plane.reshape(wsh, 1024)[:, :own].reshape(plane)
        q_pos, q_seg = plane_marks % 65536, plane_marks // 65536
        cos, sin = rope_tables(q_pos)
        queries, kv_own = project(normed_all, w_qkv, cos, sin)

        kv_all, marks_all, dy_all, w_half = link.run(
            "gather_keys",
            2,
            [
                link.gather(kv_own, ("ctx",)),
                link.gather(marks_plane, ("ctx",)),
                link.gather(upstream, ("wsh",)),
                link.columns(gate_up, ("wsh",), FF, FF // wsh),
            ],
        )
        kv_all = kv_all.reshape(group, 256)
        dy_all = dy_all.reshape(plane, D)
        w_half = w_half.reshape(D, FF // wsh)
        marks_all = marks_all.reshape(shards, 1024)[:, :own].reshape(group, 1)
        k_pos, k_seg = marks_all % 65536, marks_all // 65536
        q_pos, q_seg = q_pos.reshape(1, plane), q_seg.reshape(1, plane)
        attended, attended_wide, lse = attend_forward(queries, kv_all, q_pos, q_seg, k_pos, k_seg)

        w_out = spread_rows(attend_out, odd)
        out_part = jnp.dot(attended, w_out, preferred_element_type=F32).astype(BF)
        out_parts, w_both = link.run(
            "scatter_out",
            3,
            [
                link.swap(out_part.reshape(wsh, own, D), ("wsh",)),
                link.gather(w_half, ("grp",)),
            ],
        )
        w_gate, w_up = w_both[0], w_both[1]
        middle = inputs + jnp.sum(out_parts.astype(F32), axis=0)
        factor_two = rms_factor(middle)
        normed_two = (middle * factor_two * feed_gain).astype(BF)
        (normed_two_all,) = link.run("gather_two", 4, [link.gather(normed_two, ("wsh",))])
        normed_two_all = normed_two_all.reshape(plane, D)

        gate_part = jnp.dot(normed_two_all, w_gate, preferred_element_type=F32)
        up_part = jnp.dot(normed_two_all, w_up, preferred_element_type=F32)
        hidden_grad = dot_general(dy_all, down_weight, 1, 1)
        sigmoid_gate = jax.nn.sigmoid(gate_part)
        silu_gate = gate_part * sigmoid_gate
        hidden = (silu_gate * up_part).astype(BF)
        gate_grad = (
            hidden_grad * up_part * sigmoid_gate * (1.0 + gate_part * (1.0 - sigmoid_gate))
        ).astype(BF)
        up_grad = (hidden_grad * silu_gate).astype(BF)
        down_part = jnp.dot(hidden, down_weight, preferred_element_type=F32).astype(BF)
        two_part = (dot_general(gate_grad, w_gate, 1, 1) + dot_general(up_grad, w_up, 1, 1)).astype(
            BF
        )
        down_grad = dot_general(hidden, dy_all, 0, 0).astype(BF)
        gate_w_grad = dot_general(normed_two_all, gate_grad, 0, 0).astype(BF)
        up_w_grad = dot_general(normed_two_all, up_grad, 0, 0).astype(BF)
        ffn_rows = FF // shards // 2
        down_halves = down_grad.reshape(ctx, 2, ffn_rows, D).transpose(1, 0, 2, 3)
        gate_halves = jnp.stack([gate_w_grad, up_w_grad]).reshape(2, shards, D // shards, FF // wsh)
        two_parts, down_pair, gate_pair = link.run(
            "scatter_feed",
            5,
            [
                link.swap(two_part.reshape(wsh, own, D), ("wsh",)),
                link.swap(down_halves, ("grp",)),
                link.swap(gate_halves, ("grp",)),
            ],
        )
        normed_two_grad = jnp.sum(two_parts.astype(F32), axis=0)
        middle_part, feed_gain_grad = norm_back(normed_two_grad, middle, factor_two, feed_gain)
        middle_grad = upstream.astype(F32) + middle_part
        branch_grad = middle_grad.astype(BF)
        down_send = (down_pair[0].astype(F32) + down_pair[1].astype(F32)).astype(BF)
        gate_send = (gate_pair[0].astype(F32) + gate_pair[1].astype(F32)).astype(BF)

        branch_all, down_got = link.run(
            "gather_branch",
            6,
            [
                link.gather(branch_grad, ("wsh",)),
                link.swap(down_send, ("ctx",)),
            ],
        )
        branch_all = branch_all.reshape(plane, D)
        attended_grad = dot_general(branch_all, w_out, 1, 1).astype(BF)
        q_grad, kv_grad, gate_got = attend_backward(
            link, queries, kv_all, q_pos, q_seg, k_pos, k_seg, lse, attended_wide, attended_grad,
            gate_send,
        )
        out_grad = collect_rows(dot_general(attended, branch_all, 0, 0), odd).astype(BF)
        out_halves = out_grad.reshape(ctx, D // shards, 2, 576).transpose(2, 0, 1, 3)
        kv_parts, down_parts, out_pair = link.run(
            "scatter_keys",
            7,
            [
                link.swap(kv_grad.reshape(ctx, plane, 256), ("ctx",)),
                link.swap(down_part.reshape(wsh, own, D), ("wsh",)),
                link.swap(out_halves, ("grp",)),
            ],
        )
        activations = (middle + jnp.sum(down_parts.astype(F32), axis=0)).astype(BF)
        out_send = (out_pair[0].astype(F32) + out_pair[1].astype(F32)).astype(BF)
        projected_grad, one_part = unproject(q_grad, kv_parts, w_qkv, cos, sin)
        qkv_grad = dot_general(normed_all, projected_grad, 0, 0).astype(BF)
        qkv_halves = qkv_grad.reshape(shards, D // shards, 2, 320).transpose(2, 0, 1, 3)
        down_half = jnp.sum(down_got.astype(F32), axis=0).astype(BF)
        one_parts, qkv_pair, out_got, down_half = link.run(
            "scatter_one",
            8,
            [
                link.swap(one_part.reshape(wsh, own, D), ("wsh",)),
                link.swap(qkv_halves, ("grp",)),
                link.swap(out_send, ("ctx",)),
                link.turn_over(down_half),
            ],
        )
        normed_one_grad = jnp.sum(one_parts.astype(F32), axis=0)
        input_part, attend_gain_grad = norm_back(normed_one_grad, inputs, factor_one, attend_gain)
        input_grad = middle_grad + input_part
        qkv_send = (qkv_pair[0].astype(F32) + qkv_pair[1].astype(F32)).astype(BF)
        gains = jnp.stack([attend_gain_grad, feed_gain_grad]).reshape(2, shards, D // shards)
        gains = jnp.pad(gains.transpose(1, 0, 2), ((0, 0), (0, 6), (0, 128 - D // shards)))
        out_half = jnp.sum(out_got.astype(F32), axis=0).astype(BF)
        qkv_got, gains_got, out_half = link.run(
            "scatter_weights",
            9,
            [
                link.swap(qkv_send, ("ctx", "wsh")),
                link.swap(gains, ("ctx", "wsh")),
                link.turn_over(out_half),
            ],
        )

        def over_ctx(x):
            return jnp.sum(x.reshape((ctx, wsh) + x.shape[1:]).astype(F32), axis=0)

        gate_half = over_ctx(gate_got).astype(BF)
        qkv_half = over_ctx(qkv_got).astype(BF)
        gain_half = jnp.sum(gains_got, axis=0)
        down_two, out_two, gate_two, qkv_two, gain_two = link.run(
            "swap_cores",
            10,
            [
                link.gather(down_half, ("grp",)),
                link.gather(out_half, ("grp",)),
                link.gather(gate_half, ("grp",)),
                link.gather(qkv_half, ("grp",)),
                link.gather(gain_half, ("grp",)),
            ],
        )
        rows = D // shards
        down_out = down_two.reshape(FF // shards, D).astype(F32)
        out_out = out_two.transpose(1, 0, 2).reshape(rows, D).astype(F32)
        gate_out = gate_two.transpose(2, 0, 1, 3).reshape(rows, 2 * FF).astype(F32)
        qkv_out = qkv_restore(
            qkv_two.transpose(1, 2, 0, 3).reshape(wsh, rows, 640).astype(F32)
        )
        gain_out = gain_two[0] + gain_two[1]
        return (
            activations,
            input_grad,
            qkv_out,
            out_out,
            gate_out,
            down_out,
            gain_out[0, :rows],
            gain_out[1, :rows],
        )

    return local


def solution(mesh):
    whole = ("grp", "ctx", "wsh")
    in_specs = (
        P(whole, None),
        P(whole),
        P(whole),
        P(),
        P("wsh", None),
        P("wsh", None),
        P(),
        P("wsh", None),
        P("wsh", None),
        P(whole, None),
    )
    out_specs = (
        P(whole, None),
        P(whole, None),
        P(("ctx", "wsh"), None),
        P(("ctx", "wsh"), None),
        P(("ctx", "wsh"), None),
        P(("ctx", "wsh"), None),
        P(("ctx", "wsh")),
        P(("ctx", "wsh")),
    )
    return jax.shard_map(
        build(dict(mesh.shape)), mesh=mesh, in_specs=in_specs, out_specs=out_specs, check_vma=False
    )
```

```python
import itertools
import math

import jax
import jax.numpy as jnp
from jax import lax
from jax.experimental import pallas as pl
from jax.experimental.pallas import tpu as pltpu
from jax.sharding import PartitionSpec as P

HEADS = 18
KV_HEADS = 6
HEAD_DIM = 64
FF = 3072
D = 1152
QW = 1152
KW = 384
EPSILON = 1e-05
MESH = pl.DeviceIdType.MESH
F32 = jnp.float32
BF = jnp.bfloat16
VMEM_LIMIT = 56 << 20


def dot_general(a, b, ca, cb):
    return lax.dot_general(a, b, (((ca,), (cb,)), ((), ())), preferred_element_type=F32)


class Exchange:
    def __init__(self, sizes):
        self.sizes = sizes

    def place(self, axes, offset):
        where, index = {}, 0
        for axis, step in zip(axes, offset):
            size = self.sizes[axis]
            spot = lax.axis_index(axis)
            if step:
                spot = lax.rem(spot + step, size)
            where[axis] = spot
            index = index * size + spot
        return where, index

    def offsets(self, axes):
        return list(itertools.product(*[range(self.sizes[axis]) for axis in axes]))

    def gather(self, x, axes):
        count = math.prod(self.sizes[axis] for axis in axes)
        return ("peer", x, axes, lambda ref, p: ref, (count,) + x.shape, x.shape)

    def swap(self, x, axes):
        return ("peer", x, axes, lambda ref, p: ref.at[p], x.shape, x.shape[1:])

    def columns(self, x, axes, start, width):
        count = math.prod(self.sizes[axis] for axis in axes)
        source = lambda ref, p: ref.at[
            :, pl.ds(pl.multiple_of(lax.axis_index("grp") * start + p * width, 128), width)
        ]
        return ("peer", x, axes, source, (count, x.shape[0], width), (x.shape[0], width))

    def turn_over(self, x):
        return ("owner", x, None, None, x.shape, x.shape)

    def run(self, name, number, ops):
        ctx, wsh = self.sizes["ctx"], self.sizes["wsh"]
        total = 0
        for kind, x, axes, *_ in ops:
            total += 1 if kind == "owner" else math.prod(self.sizes[a] for a in axes)
        peers = {}
        for kind, x, axes, *_ in ops:
            for offset in self.offsets(axes if kind == "peer" else ("ctx", "wsh")):
                axes_of = axes if kind == "peer" else ("ctx", "wsh")
                key = tuple(sorted((a, o) for a, o in zip(axes_of, offset) if o))
                if key:
                    peers[key] = (axes_of, offset)
        count = len(ops)

        def kernel(*refs):
            ins, outs = refs[:count], refs[count : 2 * count]
            bounce = refs[2 * count : 3 * count]
            send, recv, near = refs[3 * count :]
            barrier = pltpu.get_barrier_semaphore()
            for axes, offset in peers.values():
                where, _ = self.place(axes, offset)
                pl.semaphore_signal(barrier, 1, device_id=where, device_id_type=MESH)
            pl.semaphore_wait(barrier, len(peers))
            first, second, remote, late = [], [], [], []
            slot = 0
            for op, (kind, x, axes, source, _, _) in enumerate(ops):
                if kind == "peer":
                    none = tuple(0 for _ in axes)
                    _, me = self.place(axes, none)
                    for offset in self.offsets(axes):
                        where, index = self.place(axes, offset)
                        if any(offset):
                            copy = pltpu.make_async_remote_copy(
                                source(ins[op], index),
                                outs[op].at[me],
                                send.at[slot],
                                recv.at[slot],
                                device_id=where,
                                device_id_type=MESH,
                            )
                            copy.start()
                            remote.append(copy)
                        else:
                            copy = pltpu.make_async_copy(
                                source(ins[op], me), bounce[op], near.at[op]
                            )
                            copy.start()
                            first.append(copy)
                            second.append(
                                pltpu.make_async_copy(bounce[op], outs[op].at[me], near.at[op])
                            )
                        slot += 1
                else:
                    my_c, my_w = lax.axis_index("ctx"), lax.axis_index("wsh")
                    shard = my_w * ctx + my_c
                    to_c, to_w = shard // wsh, lax.rem(shard, wsh)
                    own = jnp.logical_and(to_c == my_c, to_w == my_w)
                    copy = pltpu.make_async_remote_copy(
                        ins[op],
                        outs[op],
                        send.at[slot],
                        recv.at[slot],
                        device_id={"ctx": to_c, "wsh": to_w},
                        device_id_type=MESH,
                    )
                    inward = pltpu.make_async_copy(ins[op], bounce[op], near.at[op])
                    outward = pltpu.make_async_copy(bounce[op], outs[op], near.at[op])

                    @pl.when(jnp.logical_not(own))
                    def _():
                        copy.start()

                    late.append((own, copy, inward, outward))
                    slot += 1
            for one, two in zip(first, second):
                one.wait()
                two.start()
            for own, copy, inward, outward in late:

                @pl.when(own)
                def _():
                    inward.start()
                    inward.wait()
                    outward.start()
                    outward.wait()

            for copy in second:
                copy.wait()
            for own, copy, inward, outward in late:

                @pl.when(jnp.logical_not(own))
                def _():
                    copy.wait()

            for copy in remote:
                copy.wait()

        return pl.pallas_call(
            kernel,
            name=name,
            out_shape=[jax.ShapeDtypeStruct(op[4], op[1].dtype) for op in ops],
            in_specs=[pl.BlockSpec(memory_space=pl.ANY)] * count,
            out_specs=[pl.BlockSpec(memory_space=pl.ANY)] * count,
            scratch_shapes=[pltpu.VMEM(op[5], op[1].dtype) for op in ops]
            + [
                pltpu.SemaphoreType.DMA((total,)),
                pltpu.SemaphoreType.DMA((total,)),
                pltpu.SemaphoreType.DMA((count,)),
            ],
            compiler_params=pltpu.CompilerParams(
                collective_id=number, has_side_effects=True, vmem_limit_bytes=VMEM_LIMIT
            ),
        )(*[op[1] for op in ops])


def head_plan(w):
    pair, odd = w // 2, w % 2
    start = 9 * pair + 4 * odd
    if odd:
        f_heads, h_heads = [start + 2, start + 3, start + 4], [start, start + 1]
        f_kv, h_kv = 3 * pair + 2, 3 * pair + 1
    else:
        f_heads, h_heads = [start, start + 1, start + 2], [start + 3, start + 4]
        f_kv, h_kv = 3 * pair, 3 * pair + 1
    q_order = [f_heads[0], h_heads[0], f_heads[1], h_heads[1], f_heads[2], None]
    return q_order, [f_kv, h_kv]


def qkv_columns(weight):
    blank = jnp.zeros((weight.shape[0], HEAD_DIM), weight.dtype)
    parts = []
    for w in range(4):
        q_order, kv_order = head_plan(w)
        pieces = [
            blank if h is None else weight[:, h * HEAD_DIM : (h + 1) * HEAD_DIM] for h in q_order
        ]
        for base in (QW, QW + KW):
            pieces += [
                weight[:, base + h * HEAD_DIM : base + (h + 1) * HEAD_DIM] for h in kv_order
            ]
        parts.append(jnp.concatenate(pieces, axis=1))
    return jnp.stack(parts)


def qkv_restore(parts):
    found = {}
    for w in range(4):
        q_order, kv_order = head_plan(w)
        slots = list(q_order) + [HEADS + h for h in kv_order]
        slots += [HEADS + KV_HEADS + h for h in kv_order]
        for at, head in enumerate(slots):
            if head is not None:
                found.setdefault(head, []).append(
                    parts[w][:, at * HEAD_DIM : (at + 1) * HEAD_DIM]
                )
    pieces = []
    for head in range(HEADS + 2 * KV_HEADS):
        term = found[head][0]
        for other in found[head][1:]:
            term = term + other
        pieces.append(term)
    return jnp.concatenate(pieces, axis=1)


def spread_rows(rows, odd):
    n = rows.shape[1]
    half = jnp.zeros((32, n), rows.dtype)
    blank = jnp.zeros((64, n), rows.dtype)
    even_rows = jnp.concatenate(
        [rows[0:64], rows[192:256], rows[64:128], rows[256:288], half, rows[128:192], blank]
    )
    odd_rows = jnp.concatenate(
        [rows[96:160], half, rows[0:32], rows[160:224], rows[32:96], rows[224:288], blank]
    )
    return jnp.where(odd, odd_rows, even_rows)


def turn(x, cos, sin, lanes):
    swapped = jnp.where(lanes, pltpu.roll(x, 96, 1), pltpu.roll(x, 32, 1))
    return x * cos + swapped * sin


def project(normed, weight, cos, sin):
    rows = normed.shape[0]
    tile = 256

    def kernel(n_ref, w_ref, c_ref, s_ref, q_ref, kv_ref):
        full = jnp.dot(n_ref[...], w_ref[...], preferred_element_type=F32)
        cos_t, sin_t = c_ref[...], s_ref[...]
        low = lax.rem(lax.broadcasted_iota(jnp.int32, (tile, 128), 1), 64) < 32
        for b in range(3):
            block = turn(full[:, 128 * b : 128 * b + 128], cos_t, sin_t, low)
            q_ref[:, 128 * b : 128 * b + 128] = (block.astype(BF).astype(F32) * 0.125).astype(BF)
        kv_ref[:, :128] = turn(full[:, 384:512], cos_t, sin_t, low).astype(BF)
        kv_ref[:, 128:] = full[:, 512:].astype(BF)

    return pl.pallas_call(
        kernel,
        name="project",
        grid=(rows // tile,),
        in_specs=[
            pl.BlockSpec((tile, D), lambda i: (i, 0)),
            pl.BlockSpec((D, 640), lambda i: (0, 0)),
            pl.BlockSpec((tile, 128), lambda i: (i, 0)),
            pl.BlockSpec((tile, 128), lambda i: (i, 0)),
        ],
        out_specs=[
            pl.BlockSpec((tile, 384), lambda i: (i, 0)),
            pl.BlockSpec((tile, 256), lambda i: (i, 0)),
        ],
        out_shape=[
            jax.ShapeDtypeStruct((rows, 384), BF),
            jax.ShapeDtypeStruct((rows, 256), BF),
        ],
        compiler_params=pltpu.CompilerParams(vmem_limit_bytes=VMEM_LIMIT),
    )(normed, weight, cos, sin)


TQ = 256
TK = 512


def head_block(block, head):
    low = lax.broadcasted_iota(jnp.int32, block.shape, 1) < 64
    return jnp.where(low if head == 0 else jnp.logical_not(low), block, jnp.zeros_like(block))


def visible(kp_ref, ks_ref, qp_ref, qs_ref, start):
    key_pos = kp_ref[pl.ds(start, TK), :]
    key_seg = ks_ref[pl.ds(start, TK), :]
    return (key_pos <= qp_ref[...]) & ((key_seg == 0) | (key_seg == qs_ref[...]))


HEAD_SLOTS = [(0, 0), (0, 1), (1, 0), (1, 1), (2, 0)]


def attend_forward(q, kv, q_pos, q_seg, k_pos, k_seg):
    rows, keys = q.shape[0], kv.shape[0]

    def kernel(q_ref, kv_ref, qp_ref, qs_ref, kp_ref, ks_ref, a_ref, o_ref, lse_ref, acc, top, tot):
        acc[...] = jnp.zeros_like(acc)
        top[...] = jnp.full_like(top, -1e30)
        tot[...] = jnp.zeros_like(tot)
        heads = [head_block(q_ref[:, 128 * b : 128 * b + 128], h) for b, h in HEAD_SLOTS]

        @pl.loop(0, keys // TK)
        def _(t):
            start = pl.multiple_of(t * TK, TK)
            k_tile = kv_ref[pl.ds(start, TK), :128]
            v_tile = kv_ref[pl.ds(start, TK), 128:]
            seen = visible(kp_ref, ks_ref, qp_ref, qs_ref, start)
            for j in range(5):
                scores = dot_general(k_tile, heads[j], 1, 1)
                scores = jnp.where(seen, scores, -1e30)
                old = top[j : j + 1, :]
                new = jnp.maximum(old, jnp.max(scores, axis=0, keepdims=True))
                expons = jnp.exp(scores - new)
                shrink = jnp.exp(old - new)
                tot[j : j + 1, :] = tot[j : j + 1, :] * shrink + jnp.sum(
                    expons, axis=0, keepdims=True
                )
                acc[j] = acc[j] * shrink + dot_general(v_tile, expons.astype(BF), 0, 0)
                top[j : j + 1, :] = new

        for j, (b, h) in enumerate(HEAD_SLOTS):
            out = acc[j] / tot[j : j + 1, :]
            acc[j] = out
        lse_ref[...] = top[...] + jnp.log(jnp.maximum(tot[...], 1e-37))
        low = lax.broadcasted_iota(jnp.int32, (TQ, 128), 1) < 64
        for b in range(3):
            first = acc[2 * b].T
            if b < 2:
                block = jnp.where(low, first, acc[2 * b + 1].T)
            else:
                block = jnp.where(low, first, 0.0)
            o_ref[:, 128 * b : 128 * b + 128] = block
            a_ref[:, 128 * b : 128 * b + 128] = block.astype(BF)

    return pl.pallas_call(
        kernel,
        name="attend_forward",
        grid=(rows // TQ,),
        in_specs=[
            pl.BlockSpec((TQ, 384), lambda i: (i, 0)),
            pl.BlockSpec((keys, 256), lambda i: (0, 0)),
            pl.BlockSpec((1, TQ), lambda i: (0, i)),
            pl.BlockSpec((1, TQ), lambda i: (0, i)),
            pl.BlockSpec((keys, 1), lambda i: (0, 0)),
            pl.BlockSpec((keys, 1), lambda i: (0, 0)),
        ],
        out_specs=[
            pl.BlockSpec((TQ, 384), lambda i: (i, 0)),
            pl.BlockSpec((TQ, 384), lambda i: (i, 0)),
            pl.BlockSpec((8, TQ), lambda i: (0, i)),
        ],
        out_shape=[
            jax.ShapeDtypeStruct((rows, 384), BF),
            jax.ShapeDtypeStruct((rows, 384), F32),
            jax.ShapeDtypeStruct((8, rows), F32),
        ],
        scratch_shapes=[
            pltpu.VMEM((5, 128, TQ), F32),
            pltpu.VMEM((8, TQ), F32),
            pltpu.VMEM((8, TQ), F32),
        ],
        compiler_params=pltpu.CompilerParams(vmem_limit_bytes=VMEM_LIMIT),
    )(q, kv, q_pos, q_seg, k_pos, k_seg)


def owner_of(link):
    ctx, wsh = link.sizes["ctx"], link.sizes["wsh"]
    my_c, my_w = lax.axis_index("ctx"), lax.axis_index("wsh")
    shard = my_w * ctx + my_c
    to_c, to_w = shard // wsh, lax.rem(shard, wsh)
    return {"ctx": to_c, "wsh": to_w}, jnp.logical_and(to_c == my_c, to_w == my_w)


def attend_backward(
    link, q, kv, q_pos, q_seg, k_pos, k_seg, lse, out, out_grad, send_rows, send_down
):
    rows, keys = q.shape[0], kv.shape[0]
    steps = rows // TQ
    axes = ("ctx",)
    peers = link.offsets(axes)
    everyone = link.offsets(("ctx", "wsh"))

    def kernel(
        q_ref, kv_ref, qp_ref, qs_ref, kp_ref, ks_ref, lse_ref, o_ref, do_ref, rows_ref, down_ref,
        dq_ref, dkv_ref, got_ref, down_got, acc, kv_acc, bounce, bounce_two, send, recv, near,
    ):
        _, me = link.place(axes, peers[0])
        copies = []
        for at, offset in enumerate(peers[1:]):
            where, index = link.place(axes, offset)
            copies.append(
                pltpu.make_async_remote_copy(
                    rows_ref.at[index],
                    got_ref.at[me],
                    send.at[at],
                    recv.at[at],
                    device_id=where,
                    device_id_type=MESH,
                )
            )
        owner, stays = owner_of(link)
        move = pltpu.make_async_remote_copy(
            down_ref,
            down_got,
            send.at[len(peers)],
            recv.at[len(peers)],
            device_id=owner,
            device_id_type=MESH,
        )
        inward = pltpu.make_async_copy(rows_ref.at[me], bounce, near.at[0])
        outward = pltpu.make_async_copy(bounce, got_ref.at[me], near.at[0])
        stay_in = pltpu.make_async_copy(down_ref, bounce_two, near.at[1])
        stay_out = pltpu.make_async_copy(bounce_two, down_got, near.at[1])

        @pl.when(pl.program_id(0) == 0)
        def _():
            greet([link.place(("ctx", "wsh"), offset)[0] for offset in everyone[1:]])
            for copy in copies:
                copy.start()

            @pl.when(jnp.logical_not(stays))
            def _():
                move.start()

            @pl.when(stays)
            def _():
                stay_in.start()
                stay_in.wait()
                stay_out.start()

            inward.start()
            inward.wait()
            outward.start()
            kv_acc[...] = jnp.zeros_like(kv_acc)

        acc[...] = jnp.zeros_like(acc)
        heads = [head_block(q_ref[:, 128 * b : 128 * b + 128], h) for b, h in HEAD_SLOTS]
        grads = [head_block(do_ref[:, 128 * b : 128 * b + 128], h) for b, h in HEAD_SLOTS]
        delta = []
        for j, (b, h) in enumerate(HEAD_SLOTS):
            product = grads[j].astype(F32) * o_ref[:, 128 * b : 128 * b + 128]
            delta.append(jnp.sum(product.T, axis=0, keepdims=True))

        @pl.loop(0, keys // TK)
        def _(t):
            start = pl.multiple_of(t * TK, TK)
            k_tile = kv_ref[pl.ds(start, TK), :128]
            v_tile = kv_ref[pl.ds(start, TK), 128:]
            seen = visible(kp_ref, ks_ref, qp_ref, qs_ref, start)
            k_sum = jnp.zeros((TK, 128), F32)
            v_sum = jnp.zeros((TK, 128), F32)
            for j in range(5):
                scores = dot_general(k_tile, heads[j], 1, 1)
                probs = jnp.where(seen, jnp.exp(scores - lse_ref[j : j + 1, :]), 0.0)
                prob_grad = dot_general(v_tile, grads[j], 1, 1)
                score_grad = (probs * (prob_grad - delta[j])).astype(BF)
                v_sum += jnp.dot(probs.astype(BF), grads[j], preferred_element_type=F32)
                k_sum += jnp.dot(score_grad, heads[j], preferred_element_type=F32)
                acc[j] += dot_general(k_tile, score_grad, 0, 0)
            kv_acc[pl.ds(start, TK), :128] += k_sum
            kv_acc[pl.ds(start, TK), 128:] += v_sum

        low = lax.broadcasted_iota(jnp.int32, (TQ, 128), 1) < 64
        for b in range(3):
            first = acc[2 * b].T * 0.125
            if b < 2:
                block = jnp.where(low, first, acc[2 * b + 1].T * 0.125)
            else:
                block = jnp.where(low, first, 0.0)
            dq_ref[:, 128 * b : 128 * b + 128] = block.astype(BF)

        @pl.when(pl.program_id(0) == steps - 1)
        def _():
            dkv_ref[...] = kv_acc[...].astype(BF)
            outward.wait()
            for copy in copies:
                copy.wait()

            @pl.when(jnp.logical_not(stays))
            def _():
                move.wait()

            @pl.when(stays)
            def _():
                stay_out.wait()

    return pl.pallas_call(
        kernel,
        name="attend_backward",
        grid=(steps,),
        in_specs=[
            pl.BlockSpec((TQ, 384), lambda i: (i, 0)),
            pl.BlockSpec((keys, 256), lambda i: (0, 0)),
            pl.BlockSpec((1, TQ), lambda i: (0, i)),
            pl.BlockSpec((1, TQ), lambda i: (0, i)),
            pl.BlockSpec((keys, 1), lambda i: (0, 0)),
            pl.BlockSpec((keys, 1), lambda i: (0, 0)),
            pl.BlockSpec((8, TQ), lambda i: (0, i)),
            pl.BlockSpec((TQ, 384), lambda i: (i, 0)),
            pl.BlockSpec((TQ, 384), lambda i: (i, 0)),
            pl.BlockSpec(memory_space=pl.ANY),
            pl.BlockSpec(memory_space=pl.ANY),
        ],
        out_specs=[
            pl.BlockSpec((TQ, 384), lambda i: (i, 0)),
            pl.BlockSpec((keys, 256), lambda i: (0, 0)),
            pl.BlockSpec(memory_space=pl.ANY),
            pl.BlockSpec(memory_space=pl.ANY),
        ],
        out_shape=[
            jax.ShapeDtypeStruct((rows, 384), BF),
            jax.ShapeDtypeStruct((keys, 256), BF),
            jax.ShapeDtypeStruct(send_rows.shape, BF),
            jax.ShapeDtypeStruct(send_down.shape, BF),
        ],
        scratch_shapes=[
            pltpu.VMEM((5, 128, TQ), F32),
            pltpu.VMEM((keys, 256), F32),
            pltpu.VMEM(send_rows.shape[1:], BF),
            pltpu.VMEM(send_down.shape, BF),
            pltpu.SemaphoreType.DMA((len(peers) + 1,)),
            pltpu.SemaphoreType.DMA((len(peers) + 1,)),
            pltpu.SemaphoreType.DMA((2,)),
        ],
        compiler_params=pltpu.CompilerParams(
            collective_id=11, has_side_effects=True, vmem_limit_bytes=VMEM_LIMIT
        ),
    )(q, kv, q_pos, q_seg, k_pos, k_seg, lse, out, out_grad, send_rows, send_down)


class Wires:
    def __init__(self, send, recv):
        self.send, self.recv, self.used = send, recv, 0

    def copy(self, source, target, where):
        at = self.used
        self.used += 1
        return pltpu.make_async_remote_copy(
            source,
            target,
            self.send.at[at],
            self.recv.at[at],
            device_id=where,
            device_id_type=MESH,
        )

    def start(self, source, target, where):
        copy = self.copy(source, target, where)
        copy.start()
        return copy


def greet(places):
    barrier = pltpu.get_barrier_semaphore()
    for where in places:
        pl.semaphore_signal(barrier, 1, device_id=where, device_id_type=MESH)
    pl.semaphore_wait(barrier, len(places))


def square():
    w = lax.axis_index("wsh")
    return w, w + 1 - 2 * lax.rem(w, 2), w + 2 - 4 * (w // 2), 3 - w


class SquareScatter:
    def __init__(self, wires, parts, near, total):
        self.wires, self.parts, self.near, self.total = wires, parts, near, total
        self.half = parts.shape[1] // 2
        self.a, self.b = pl.ds(0, self.half), pl.ds(self.half, self.half)
        self.own, self.x, self.y, self.z = square()
        self.pending = []

    def send_diagonal(self):
        wires, parts = self.wires, self.parts
        self.one = wires.start(parts.at[self.z, self.a], self.near.at[0], {"wsh": self.x})
        self.two = wires.start(parts.at[self.z, self.b], self.near.at[1], {"wsh": self.y})

    def send_x(self):
        self.pending.append(
            self.wires.start(
                self.parts.at[self.x, self.a], self.total.at[0, self.a], {"wsh": self.x}
            )
        )

    def send_y(self):
        self.pending.append(
            self.wires.start(
                self.parts.at[self.y, self.b], self.total.at[1, self.b], {"wsh": self.y}
            )
        )

    def relay(self):
        near, parts = self.near, self.parts
        self.one.wait()
        near[2] = (near[0].astype(F32) + parts[self.y, self.a].astype(F32)).astype(BF)
        self.pending.append(
            self.wires.start(near.at[2], self.total.at[1, self.a], {"wsh": self.y})
        )
        self.two.wait()
        near[3] = (near[1].astype(F32) + parts[self.x, self.b].astype(F32)).astype(BF)
        self.pending.append(
            self.wires.start(near.at[3], self.total.at[0, self.b], {"wsh": self.x})
        )

    def result(self):
        for copy in self.pending:
            copy.wait()
        return (
            self.parts[self.own].astype(F32)
            + self.total[0].astype(F32)
            + self.total[1].astype(F32)
        )


def square_scratch(rows):
    return [pltpu.VMEM((4, rows // 2, D), BF), pltpu.VMEM((2, rows, D), BF)]


def finish(
    link, q_grad, kv_grad, weight, cos, sin, normed, tokens, gain, middle_grad, gate_got, down_got,
    attended, branch, feed_sum, down_part, middle,
):
    ctx, wsh = link.sizes["ctx"], link.sizes["wsh"]
    shards = ctx * wsh
    rows = D // shards
    chunk = D // ctx
    fold = ctx // wsh
    own_rows = tokens.shape[0]
    plane = normed.shape[0]
    axes = ("ctx", "wsh")
    peers = link.offsets(axes)
    gate_width = gate_got.shape[2]
    down_rows = down_got.shape[0]

    def kernel(
        q_ref, kv_send, w_ref, c_ref, s_ref, n_ref, x_ref, g_ref, mg_ref, gate_ref, down_ref,
        at_ref, br_ref, fs_ref, dp_ref, mid_ref,
        act_ref, ig_ref, qkv_ref, out_ref, gate_out, down_out, gains_out,
        kv_ref, pg, parts, near, total, near2, total2, acc, wide, q_own, q_pair, q_send, q_got,
        q_mid, q_fin, kv_own, kv_pair, kv_go, kv_got, kv_mid, kv_fin, gate_mid, gate_fin, down_fin, out_halves,
        out_pair, out_send, out_mid, out_got, out_fin, gains, gains_got, gains_fin,
        send, recv,
    ):
        wires = Wires(send, recv)
        core = lax.axis_index("grp")
        first, second = core == 0, core == 1
        sibling = {"grp": 1 - core}
        my_c, my_w = lax.axis_index("ctx"), lax.axis_index("wsh")
        odd = lax.rem(my_w, 2) == 1
        greet([link.place(axes, offset)[0] for offset in peers[1:]] + [sibling])
        _, me = link.place(axes, peers[0])

        def over_ctx(got, mid):
            for w in range(wsh):
                strip = got[0, w * rows : w * rows + rows, :].astype(F32)
                for c in range(1, ctx):
                    strip += got[c, w * rows : w * rows + rows, :].astype(F32)
                mid[w] = strip.astype(BF)

        def in_plane(mid, slot_of):
            copies = []
            for offset in link.offsets(("wsh",))[1:]:
                where, index = link.place(("wsh",), offset)
                copies.append(wires.copy(mid.at[index], slot_of(my_w), where))
            return copies

        def begin(cond, *copies):
            @pl.when(cond)
            def _():
                for copy in copies:
                    copy.start()

        kv_copies = []
        for offset in link.offsets(("ctx",))[1:]:
            where, index = link.place(("ctx",), offset)
            kv_copies.append(wires.start(kv_send.at[index], kv_ref.at[my_c], where))
        layer = SquareScatter(wires, dp_ref, near2, total2)
        layer.send_diagonal()
        layer.send_x()
        layer.send_y()
        kv_ref[my_c] = kv_send[my_c]

        wide[...] = dot_general(at_ref[...], br_ref[...], 0, 0)

        def out_strips(pieces):
            at = 0
            for start, size in pieces:
                acc_rows = wide[start : start + size, :].astype(BF)
                part = jnp.concatenate([acc_rows[:, :576], jnp.zeros((size, 64), BF)], axis=1)
                out_halves[0, at : at + size, :] = part
                part = jnp.concatenate([acc_rows[:, 576:], jnp.zeros((size, 64), BF)], axis=1)
                out_halves[1, at : at + size, :] = part
                at += size

        @pl.when(odd)
        def _():
            out_strips([(96, 32), (192, 64), (0, 64), (128, 64), (256, 64)])

        @pl.when(jnp.logical_not(odd))
        def _():
            out_strips([(0, 64), (128, 64), (256, 64), (64, 64), (192, 32)])

        out_swap = wires.start(out_halves.at[1 - core], out_pair, sibling)
        low = lax.rem(lax.broadcasted_iota(jnp.int32, (own_rows, 128), 1), 64) < 32

        @pl.loop(0, wsh)
        def _(slot):
            at = pl.ds(pl.multiple_of(slot * own_rows, 16), own_rows)
            for b in range(3):
                block = q_ref[at, 128 * b : 128 * b + 128].astype(F32)
                pg[at, 128 * b : 128 * b + 128] = turn(
                    block, c_ref[at, :], -s_ref[at, :], low
                ).astype(BF)

        layer.relay()
        for b in range(3):
            acc[384 * b : 384 * b + 384, :] = dot_general(
                n_ref[:, 384 * b : 384 * b + 384], pg[:, :384], 0, 0
            )

        for c in range(ctx):
            q_own[c] = acc[c * chunk : c * chunk + chunk, :].astype(BF)
        q_swap = wires.copy(q_own, q_pair, sibling)
        begin(second, q_swap)

        down_fin[core] = down_ref[...]
        down_copy = wires.start(down_fin.at[core], down_fin.at[core], sibling)

        over_ctx(gate_ref, gate_mid)
        gate_moves = in_plane(gate_mid, lambda w: gate_fin.at[core, w])
        for copy in gate_moves:
            copy.start()
        gate_fin[core, my_w] = gate_mid[my_w]
        act_ref[...] = (mid_ref[...] + layer.result()).astype(BF)
        out_swap.wait()
        for k in range(ctx):
            strip = slice(k * rows, k * rows + rows)
            out_send[k % wsh, k // wsh] = (
                out_halves[core, strip, :].astype(F32) + out_pair[strip, :].astype(F32)
            ).astype(BF)
        out_moves = in_plane(out_send, lambda w: out_mid.at[w])
        for copy in out_moves:
            copy.start()
        out_mid[my_w] = out_send[my_w]

        @pl.when(first)
        def _():
            q_swap.wait_recv()

            @pl.loop(0, ctx)
            def _(c):
                q_send[c] = (q_own[c].astype(F32) + q_pair[c].astype(F32)).astype(BF)

        @pl.when(second)
        def _():
            q_swap.wait_send()

        for copy in gate_moves:
            copy.wait()
        gate_copy = wires.start(gate_fin.at[core], gate_fin.at[core], sibling)
        down_copy.wait()
        down_out[:down_rows, :] = down_fin[0].astype(F32)
        down_out[down_rows:, :] = down_fin[1].astype(F32)
        gate_copy.wait()
        for half in range(2):
            for w in range(wsh):
                left = (half * wsh + w) * gate_width
                gate_out[:, left : left + gate_width] = gate_fin[half, w].astype(F32)

        for copy in out_moves:
            copy.wait()

        for copy in kv_copies:
            copy.wait()
        q_copies, kvg_copies, out_copies = [], [], []
        for offset in link.offsets(("ctx",))[1:]:
            where, index = link.place(("ctx",), offset)
            q_copies.append(wires.copy(q_send.at[index], q_got.at[my_c], where))
            kvg_copies.append(wires.copy(kv_go.at[index], kv_got.at[my_c], where))
        begin(first, *q_copies)
        for offset in link.offsets(("ctx",))[1:]:
            where, index = link.place(("ctx",), offset)
            part = out_mid.at[index // fold, lax.rem(index, fold)]
            out_copies.append(wires.start(part, out_got.at[my_c], where))
        out_got[my_c] = out_mid[my_c // fold, lax.rem(my_c, fold)]
        scatter = SquareScatter(wires, parts, near, total)
        gain_sum = jnp.zeros((1, D), F32)
        for slot in (scatter.z, scatter.x, scatter.y, scatter.own):
            at = pl.ds(pl.multiple_of(slot * own_rows, 16), own_rows)
            summed = kv_ref[0, at, :].astype(F32)
            for c in range(1, ctx):
                summed += kv_ref[c, at, :].astype(F32)
            block = summed[:, :128].astype(BF).astype(F32)
            pg[at, 384:512] = turn(block, c_ref[at, :], -s_ref[at, :], low).astype(BF)
            pg[at, 512:] = summed[:, 128:].astype(BF)
            part = dot_general(pg[at, :], w_ref[...], 1, 1)
            parts[slot] = part.astype(BF)
            gain_sum += jnp.sum(part * n_ref[at, :].astype(F32), axis=0, keepdims=True)
            if slot is scatter.z:
                scatter.send_diagonal()
            elif slot is scatter.x:
                scatter.send_x()
            elif slot is scatter.y:
                scatter.send_y()

        for b in range(3):
            acc[384 * b : 384 * b + 384, :256] = dot_general(
                n_ref[:, 384 * b : 384 * b + 384], pg[:, 384:], 0, 0
            )

        for c in range(ctx):
            kv_own[c] = acc[c * chunk : c * chunk + chunk, :256].astype(BF)
        kv_swap = wires.copy(kv_own, kv_pair, sibling)
        begin(first, kv_swap)
        both = jnp.concatenate([gain_sum / g_ref[...], fs_ref[...]], axis=0)
        gains[...] = jnp.zeros_like(gains)
        for s in range(shards):
            gains[s, :2, :rows] = both[:, rows * s : rows * s + rows]
        gain_copies = []
        for offset in peers[1:]:
            where, index = link.place(axes, offset)
            gain_copies.append(wires.start(gains.at[index], gains_got.at[me], where))
        gains_got[me] = gains[me]
        scatter.relay()

        @pl.when(second)
        def _():
            kv_swap.wait_recv()

            @pl.loop(0, ctx)
            def _(c):
                kv_go[c] = (kv_own[c].astype(F32) + kv_pair[c].astype(F32)).astype(BF)

            for copy in kvg_copies:
                copy.start()
            kv_got[my_c] = kv_go[my_c]

        @pl.when(first)
        def _():
            kv_swap.wait_send()
            q_got[my_c] = q_send[my_c]
            for copy in q_copies:
                copy.wait()
            over_ctx(q_got, q_mid)

        q_moves = in_plane(q_mid, lambda w: q_fin.at[w])
        begin(first, *q_moves)
        for copy in out_copies:
            copy.wait()
        out_fin[core] = jnp.sum(out_got[...].astype(F32), axis=0).astype(BF)

        out_copy = wires.start(out_fin.at[core], out_fin.at[core], sibling)

        grad = scatter.result()
        x = x_ref[...].astype(F32)
        factor = lax.rsqrt(jnp.mean(x * x, axis=-1, keepdims=True) + EPSILON)
        weighted = grad * g_ref[...]
        inner = jnp.mean(weighted * x, axis=-1, keepdims=True)
        ig_ref[...] = mg_ref[...] + factor * weighted - x * (factor * factor * factor) * inner
        q_final = wires.copy(q_fin, q_fin, sibling)
        kv_final = wires.copy(kv_fin, kv_fin, sibling)

        kv_moves = in_plane(kv_mid, lambda w: kv_fin.at[w])

        @pl.when(first)
        def _():
            for copy in q_moves:
                copy.wait()
            q_fin[my_w] = q_mid[my_w]
            q_final.start()

        @pl.when(second)
        def _():
            for copy in kvg_copies:
                copy.wait()
            over_ctx(kv_got, kv_mid)
            for copy in kv_moves:
                copy.start()
            for copy in kv_moves:
                copy.wait()
            kv_fin[my_w] = kv_mid[my_w]
            kv_final.start()

        for copy in gain_copies:
            copy.wait()
        gains_fin[core] = jnp.sum(gains_got[...], axis=0)
        gain_copy = wires.start(gains_fin.at[core], gains_fin.at[core], sibling)
        out_copy.wait()
        out_ref[...] = jnp.concatenate(
            [out_fin[0, :, :576].astype(F32), out_fin[1, :, :576].astype(F32)], axis=1
        )

        @pl.when(first)
        def _():
            q_final.wait_send()
            kv_final.wait_recv()

        @pl.when(second)
        def _():
            kv_final.wait_send()
            q_final.wait_recv()

        qkv_ref[...] = qkv_restore(
            [
                jnp.concatenate([q_fin[w].astype(F32), kv_fin[w].astype(F32)], axis=1)
                for w in range(wsh)
            ]
        )
        gain_copy.wait()
        gains_out[...] = gains_fin[0] + gains_fin[1]

    operands = (
        q_grad, kv_grad, weight, cos, sin, normed, tokens, gain, middle_grad, gate_got, down_got,
        attended, branch, feed_sum, down_part, middle,
    )
    vmem = pl.BlockSpec(memory_space=pltpu.VMEM)
    return pl.pallas_call(
        kernel,
        name="finish",
        in_specs=[vmem] * len(operands),
        out_specs=[vmem] * 7,
        out_shape=[
            jax.ShapeDtypeStruct((own_rows, D), BF),
            jax.ShapeDtypeStruct((own_rows, D), F32),
            jax.ShapeDtypeStruct((rows, QW + 2 * KW), F32),
            jax.ShapeDtypeStruct((rows, D), F32),
            jax.ShapeDtypeStruct((rows, 2 * FF), F32),
            jax.ShapeDtypeStruct((2 * down_rows, D), F32),
            jax.ShapeDtypeStruct((8, 128), F32),
        ],
        scratch_shapes=[
            pltpu.VMEM((ctx, plane, 256), BF),
            pltpu.VMEM((plane, 640), BF),
            pltpu.VMEM((4, own_rows, D), BF),
            *square_scratch(own_rows),
            *square_scratch(own_rows),
            pltpu.VMEM((D, 384), F32),
            pltpu.VMEM((384, D), F32),
            *[pltpu.VMEM((ctx, chunk, 384), BF)] * 4,
            *[pltpu.VMEM((wsh, rows, 384), BF)] * 2,
            *[pltpu.VMEM((ctx, chunk, 256), BF)] * 4,
            *[pltpu.VMEM((wsh, rows, 256), BF)] * 2,
            pltpu.VMEM((wsh, rows, gate_width), BF),
            pltpu.VMEM((2, wsh, rows, gate_width), BF),
            pltpu.VMEM((2, down_rows, D), BF),
            pltpu.VMEM((2, 288, 640), BF),
            pltpu.VMEM((288, 640), BF),
            pltpu.VMEM((wsh, fold, rows, 640), BF),
            pltpu.VMEM((wsh, fold, rows, 640), BF),
            pltpu.VMEM((ctx, rows, 640), BF),
            pltpu.VMEM((2, rows, 640), BF),
            pltpu.VMEM((shards, 8, 128), F32),
            pltpu.VMEM((shards, 8, 128), F32),
            pltpu.VMEM((2, 8, 128), F32),
            pltpu.SemaphoreType.DMA((3 * shards + 2 * ctx + 32,)),
            pltpu.SemaphoreType.DMA((3 * shards + 2 * ctx + 32,)),
        ],
        compiler_params=pltpu.CompilerParams(
            collective_id=8, has_side_effects=True, vmem_limit_bytes=VMEM_LIMIT
        ),
    )(*operands)


def rms_factor(values):
    return lax.rsqrt(jnp.mean(values * values, axis=-1, keepdims=True) + EPSILON)


def norm_back(grad_normed, inputs, factor, gain):
    weighted = grad_normed * gain
    inner_mean = jnp.mean(weighted * inputs, axis=-1, keepdims=True)
    input_part = factor * weighted - inputs * (factor * factor * factor) * inner_mean
    return (input_part, jnp.sum(grad_normed * inputs * factor, axis=0))


def rope_tables(positions):
    frequency = jnp.exp(jnp.arange(32, dtype=F32) * (-math.log(10000.0) / 32))
    angles = positions.astype(F32)[:, None] * jnp.tile(frequency, 4)[None, :]
    sign = jnp.where(jnp.arange(128) % 64 < 32, -1.0, 1.0).astype(F32)
    return jnp.cos(angles), jnp.sin(angles) * sign[None, :]


def build(sizes):
    ctx, wsh = sizes["ctx"], sizes["wsh"]
    shards = ctx * wsh
    link = Exchange(sizes)

    def local(
        tokens,
        segment_ids,
        positions,
        attend_gain,
        query_key_value,
        attend_out,
        feed_gain,
        gate_up,
        down_weight,
        upstream,
    ):
        own = tokens.shape[0]
        plane = own * wsh
        group = plane * ctx
        core = lax.axis_index("grp")
        odd = lax.rem(lax.axis_index("wsh"), 2) == 1
        inputs = tokens.astype(F32)
        factor_one = rms_factor(inputs)
        normed_one = (inputs * factor_one * attend_gain).astype(BF)
        marks = jnp.pad(segment_ids * 65536 + positions, (0, 1024 - own)).reshape(8, 128)

        normed_all, w_qkv, marks_plane = link.run(
            "gather_one",
            1,
            [
                link.gather(normed_one, ("wsh",)),
                link.swap(qkv_columns(query_key_value), ("wsh",)),
                link.gather(marks, ("wsh",)),
            ],
        )
        normed_all = normed_all.reshape(plane, D)
        w_qkv = w_qkv.reshape(D, 640)
        plane_marks = marks_plane.reshape(wsh, 1024)[:, :own].reshape(plane)
        q_pos, q_seg = plane_marks % 65536, plane_marks // 65536
        cos, sin = rope_tables(q_pos)
        queries, kv_own = project(normed_all, w_qkv, cos, sin)

        kv_all, marks_all, dy_all, w_half = link.run(
            "gather_keys",
            2,
            [
                link.gather(kv_own, ("ctx",)),
                link.gather(marks_plane, ("ctx",)),
                link.gather(upstream, ("wsh",)),
                link.columns(gate_up, ("wsh",), FF, FF // wsh),
            ],
        )
        kv_all = kv_all.reshape(group, 256)
        dy_all = dy_all.reshape(plane, D)
        w_half = w_half.reshape(D, FF // wsh)
        marks_all = marks_all.reshape(shards, 1024)[:, :own].reshape(group, 1)
        k_pos, k_seg = marks_all % 65536, marks_all // 65536
        q_pos, q_seg = q_pos.reshape(1, plane), q_seg.reshape(1, plane)
        attended, attended_wide, lse = attend_forward(queries, kv_all, q_pos, q_seg, k_pos, k_seg)

        w_out = spread_rows(attend_out, odd)
        out_part = jnp.dot(attended, w_out, preferred_element_type=F32).astype(BF)
        out_parts, w_both = link.run(
            "scatter_out",
            3,
            [
                link.swap(out_part.reshape(wsh, own, D), ("wsh",)),
                link.gather(w_half, ("grp",)),
            ],
        )
        w_gate, w_up = w_both[0], w_both[1]
        middle = inputs + jnp.sum(out_parts.astype(F32), axis=0)
        factor_two = rms_factor(middle)
        normed_two = (middle * factor_two * feed_gain).astype(BF)
        (normed_two_all,) = link.run("gather_two", 4, [link.gather(normed_two, ("wsh",))])
        normed_two_all = normed_two_all.reshape(plane, D)

        gate_part = jnp.dot(normed_two_all, w_gate, preferred_element_type=F32)
        up_part = jnp.dot(normed_two_all, w_up, preferred_element_type=F32)
        hidden_grad = dot_general(dy_all, down_weight, 1, 1)
        sigmoid_gate = jax.nn.sigmoid(gate_part)
        silu_gate = gate_part * sigmoid_gate
        hidden = (silu_gate * up_part).astype(BF)
        gate_grad = (
            hidden_grad * up_part * sigmoid_gate * (1.0 + gate_part * (1.0 - sigmoid_gate))
        ).astype(BF)
        up_grad = (hidden_grad * silu_gate).astype(BF)
        down_part = jnp.dot(hidden, down_weight, preferred_element_type=F32).astype(BF)
        two_part = (dot_general(gate_grad, w_gate, 1, 1) + dot_general(up_grad, w_up, 1, 1)).astype(
            BF
        )
        down_grad = dot_general(hidden, dy_all, 0, 0).astype(BF)
        gate_w_grad = dot_general(normed_two_all, gate_grad, 0, 0).astype(BF)
        up_w_grad = dot_general(normed_two_all, up_grad, 0, 0).astype(BF)
        ffn_rows = FF // shards // 2
        down_halves = down_grad.reshape(ctx, 2, ffn_rows, D).transpose(1, 0, 2, 3)
        gate_halves = jnp.stack([gate_w_grad, up_w_grad]).reshape(2, ctx, D // ctx, FF // wsh)
        two_parts, down_pair, gate_pair = link.run(
            "scatter_feed",
            5,
            [
                link.swap(two_part.reshape(wsh, own, D), ("wsh",)),
                link.swap(down_halves, ("grp",)),
                link.swap(gate_halves, ("grp",)),
            ],
        )
        normed_two_grad = jnp.sum(two_parts.astype(F32), axis=0)
        middle_part, feed_gain_grad = norm_back(normed_two_grad, middle, factor_two, feed_gain)
        middle_grad = upstream.astype(F32) + middle_part
        branch_grad = middle_grad.astype(BF)
        down_send = (down_pair[0].astype(F32) + down_pair[1].astype(F32)).astype(BF)
        gate_send = (gate_pair[0].astype(F32) + gate_pair[1].astype(F32)).astype(BF)

        branch_all, down_got = link.run(
            "gather_branch",
            6,
            [
                link.gather(branch_grad, ("wsh",)),
                link.swap(down_send, ("ctx",)),
            ],
        )
        branch_all = branch_all.reshape(plane, D)
        attended_grad = dot_general(branch_all, w_out, 1, 1).astype(BF)
        down_sum = jnp.sum(down_got.astype(F32), axis=0).astype(BF)
        q_grad, kv_grad, gate_got, down_got = attend_backward(
            link, queries, kv_all, q_pos, q_seg, k_pos, k_seg, lse, attended_wide, attended_grad,
            gate_send, down_sum,
        )
        (activations, input_grad, qkv_out, out_out, gate_out, down_out, gain_out) = finish(
            link, q_grad, kv_grad.reshape(ctx, plane, 256), w_qkv, cos, sin, normed_all, tokens,
            attend_gain[None, :], middle_grad, gate_got, down_got, attended, branch_all,
            feed_gain_grad[None, :], down_part.reshape(wsh, own, D), middle,
        )
        width = D // shards
        return (
            activations,
            input_grad,
            qkv_out,
            out_out,
            gate_out,
            down_out,
            gain_out[0, :width],
            gain_out[1, :width],
        )

    return local


def solution(mesh):
    whole = ("grp", "ctx", "wsh")
    in_specs = (
        P(whole, None),
        P(whole),
        P(whole),
        P(),
        P("wsh", None),
        P("wsh", None),
        P(),
        P("wsh", None),
        P("wsh", None),
        P(whole, None),
    )
    out_specs = (
        P(whole, None),
        P(whole, None),
        P(("ctx", "wsh"), None),
        P(("ctx", "wsh"), None),
        P(("ctx", "wsh"), None),
        P(("ctx", "wsh"), None),
        P(("ctx", "wsh")),
        P(("ctx", "wsh")),
    )
    return jax.shard_map(
        build(dict(mesh.shape)), mesh=mesh, in_specs=in_specs, out_specs=out_specs, check_vma=False
    )
```

```python
import itertools
import math

import jax
import jax.numpy as jnp
from jax import lax
from jax.experimental import pallas as pl
from jax.experimental.pallas import tpu as pltpu
from jax.sharding import PartitionSpec as P

HEADS = 18
KV_HEADS = 6
HEAD_DIM = 64
FF = 3072
D = 1152
QW = 1152
KW = 384
EPSILON = 1e-05
MESH = pl.DeviceIdType.MESH
F32 = jnp.float32
BF = jnp.bfloat16
VMEM_LIMIT = 56 << 20


def dot_general(a, b, ca, cb):
    return lax.dot_general(a, b, (((ca,), (cb,)), ((), ())), preferred_element_type=F32)


class Exchange:
    def __init__(self, sizes):
        self.sizes = sizes

    def place(self, axes, offset):
        where, index = {}, 0
        for axis, step in zip(axes, offset):
            size = self.sizes[axis]
            spot = lax.axis_index(axis)
            if step:
                spot = lax.rem(spot + step, size)
            where[axis] = spot
            index = index * size + spot
        return where, index

    def offsets(self, axes):
        return list(itertools.product(*[range(self.sizes[axis]) for axis in axes]))

    def gather(self, x, axes):
        count = math.prod(self.sizes[axis] for axis in axes)
        return ("peer", x, axes, lambda ref, p: ref, (count,) + x.shape, x.shape)

    def swap(self, x, axes):
        return ("peer", x, axes, lambda ref, p: ref.at[p], x.shape, x.shape[1:])

    def columns(self, x, axes, start, width):
        count = math.prod(self.sizes[axis] for axis in axes)
        source = lambda ref, p: ref.at[
            :, pl.ds(pl.multiple_of(lax.axis_index("grp") * start + p * width, 128), width)
        ]
        return ("peer", x, axes, source, (count, x.shape[0], width), (x.shape[0], width))

    def turn_over(self, x):
        return ("owner", x, None, None, x.shape, x.shape)

    def run(self, name, number, ops):
        ctx, wsh = self.sizes["ctx"], self.sizes["wsh"]
        total = 0
        for kind, x, axes, *_ in ops:
            total += 1 if kind == "owner" else math.prod(self.sizes[a] for a in axes)
        peers = {}
        for kind, x, axes, *_ in ops:
            for offset in self.offsets(axes if kind == "peer" else ("ctx", "wsh")):
                axes_of = axes if kind == "peer" else ("ctx", "wsh")
                key = tuple(sorted((a, o) for a, o in zip(axes_of, offset) if o))
                if key:
                    peers[key] = (axes_of, offset)
        count = len(ops)

        def kernel(*refs):
            ins, outs = refs[:count], refs[count : 2 * count]
            bounce = refs[2 * count : 3 * count]
            send, recv, near = refs[3 * count :]
            barrier = pltpu.get_barrier_semaphore()
            for axes, offset in peers.values():
                where, _ = self.place(axes, offset)
                pl.semaphore_signal(barrier, 1, device_id=where, device_id_type=MESH)
            pl.semaphore_wait(barrier, len(peers))
            first, second, remote, late = [], [], [], []
            slot = 0
            for op, (kind, x, axes, source, _, _) in enumerate(ops):
                if kind == "peer":
                    none = tuple(0 for _ in axes)
                    _, me = self.place(axes, none)
                    for offset in self.offsets(axes):
                        where, index = self.place(axes, offset)
                        if any(offset):
                            copy = pltpu.make_async_remote_copy(
                                source(ins[op], index),
                                outs[op].at[me],
                                send.at[slot],
                                recv.at[slot],
                                device_id=where,
                                device_id_type=MESH,
                            )
                            copy.start()
                            remote.append(copy)
                        else:
                            copy = pltpu.make_async_copy(
                                source(ins[op], me), bounce[op], near.at[op]
                            )
                            copy.start()
                            first.append(copy)
                            second.append(
                                pltpu.make_async_copy(bounce[op], outs[op].at[me], near.at[op])
                            )
                        slot += 1
                else:
                    my_c, my_w = lax.axis_index("ctx"), lax.axis_index("wsh")
                    shard = my_w * ctx + my_c
                    to_c, to_w = shard // wsh, lax.rem(shard, wsh)
                    own = jnp.logical_and(to_c == my_c, to_w == my_w)
                    copy = pltpu.make_async_remote_copy(
                        ins[op],
                        outs[op],
                        send.at[slot],
                        recv.at[slot],
                        device_id={"ctx": to_c, "wsh": to_w},
                        device_id_type=MESH,
                    )
                    inward = pltpu.make_async_copy(ins[op], bounce[op], near.at[op])
                    outward = pltpu.make_async_copy(bounce[op], outs[op], near.at[op])

                    @pl.when(jnp.logical_not(own))
                    def _():
                        copy.start()

                    late.append((own, copy, inward, outward))
                    slot += 1
            for one, two in zip(first, second):
                one.wait()
                two.start()
            for own, copy, inward, outward in late:

                @pl.when(own)
                def _():
                    inward.start()
                    inward.wait()
                    outward.start()
                    outward.wait()

            for copy in second:
                copy.wait()
            for own, copy, inward, outward in late:

                @pl.when(jnp.logical_not(own))
                def _():
                    copy.wait()

            for copy in remote:
                copy.wait()

        return pl.pallas_call(
            kernel,
            name=name,
            out_shape=[jax.ShapeDtypeStruct(op[4], op[1].dtype) for op in ops],
            in_specs=[pl.BlockSpec(memory_space=pl.ANY)] * count,
            out_specs=[pl.BlockSpec(memory_space=pl.ANY)] * count,
            scratch_shapes=[pltpu.VMEM(op[5], op[1].dtype) for op in ops]
            + [
                pltpu.SemaphoreType.DMA((total,)),
                pltpu.SemaphoreType.DMA((total,)),
                pltpu.SemaphoreType.DMA((count,)),
            ],
            compiler_params=pltpu.CompilerParams(
                collective_id=number, has_side_effects=True, vmem_limit_bytes=VMEM_LIMIT
            ),
        )(*[op[1] for op in ops])


def head_plan(w):
    pair, odd = w // 2, w % 2
    start = 9 * pair + 4 * odd
    if odd:
        f_heads, h_heads = [start + 2, start + 3, start + 4], [start, start + 1]
        f_kv, h_kv = 3 * pair + 2, 3 * pair + 1
    else:
        f_heads, h_heads = [start, start + 1, start + 2], [start + 3, start + 4]
        f_kv, h_kv = 3 * pair, 3 * pair + 1
    q_order = [f_heads[0], h_heads[0], f_heads[1], h_heads[1], f_heads[2], None]
    return q_order, [f_kv, h_kv]


def qkv_columns(weight):
    blank = jnp.zeros((weight.shape[0], HEAD_DIM), weight.dtype)
    parts = []
    for w in range(4):
        q_order, kv_order = head_plan(w)
        pieces = [
            blank if h is None else weight[:, h * HEAD_DIM : (h + 1) * HEAD_DIM] for h in q_order
        ]
        for base in (QW, QW + KW):
            pieces += [
                weight[:, base + h * HEAD_DIM : base + (h + 1) * HEAD_DIM] for h in kv_order
            ]
        parts.append(jnp.concatenate(pieces, axis=1))
    return jnp.stack(parts)


def qkv_restore(parts):
    found = {}
    for w in range(4):
        q_order, kv_order = head_plan(w)
        slots = list(q_order) + [HEADS + h for h in kv_order]
        slots += [HEADS + KV_HEADS + h for h in kv_order]
        for at, head in enumerate(slots):
            if head is not None:
                found.setdefault(head, []).append(
                    parts[w][:, at * HEAD_DIM : (at + 1) * HEAD_DIM]
                )
    pieces = []
    for head in range(HEADS + 2 * KV_HEADS):
        term = found[head][0]
        for other in found[head][1:]:
            term = term + other
        pieces.append(term)
    return jnp.concatenate(pieces, axis=1)


def spread_rows(rows, odd):
    n = rows.shape[1]
    half = jnp.zeros((32, n), rows.dtype)
    blank = jnp.zeros((64, n), rows.dtype)
    even_rows = jnp.concatenate(
        [rows[0:64], rows[192:256], rows[64:128], rows[256:288], half, rows[128:192], blank]
    )
    odd_rows = jnp.concatenate(
        [rows[96:160], half, rows[0:32], rows[160:224], rows[32:96], rows[224:288], blank]
    )
    return jnp.where(odd, odd_rows, even_rows)


def turn(x, cos, sin, lanes):
    swapped = jnp.where(lanes, pltpu.roll(x, 96, 1), pltpu.roll(x, 32, 1))
    return x * cos + swapped * sin


def project(normed, weight, cos, sin):
    rows = normed.shape[0]
    tile = 256

    def kernel(n_ref, w_ref, c_ref, s_ref, q_ref, kv_ref):
        full = jnp.dot(n_ref[...], w_ref[...], preferred_element_type=F32)
        cos_t, sin_t = c_ref[...], s_ref[...]
        low = lax.rem(lax.broadcasted_iota(jnp.int32, (tile, 128), 1), 64) < 32
        for b in range(3):
            block = turn(full[:, 128 * b : 128 * b + 128], cos_t, sin_t, low)
            q_ref[:, 128 * b : 128 * b + 128] = (block.astype(BF).astype(F32) * 0.125).astype(BF)
        kv_ref[:, :128] = turn(full[:, 384:512], cos_t, sin_t, low).astype(BF)
        kv_ref[:, 128:] = full[:, 512:].astype(BF)

    return pl.pallas_call(
        kernel,
        name="project",
        grid=(rows // tile,),
        in_specs=[
            pl.BlockSpec((tile, D), lambda i: (i, 0)),
            pl.BlockSpec((D, 640), lambda i: (0, 0)),
            pl.BlockSpec((tile, 128), lambda i: (i, 0)),
            pl.BlockSpec((tile, 128), lambda i: (i, 0)),
        ],
        out_specs=[
            pl.BlockSpec((tile, 384), lambda i: (i, 0)),
            pl.BlockSpec((tile, 256), lambda i: (i, 0)),
        ],
        out_shape=[
            jax.ShapeDtypeStruct((rows, 384), BF),
            jax.ShapeDtypeStruct((rows, 256), BF),
        ],
        compiler_params=pltpu.CompilerParams(vmem_limit_bytes=VMEM_LIMIT),
    )(normed, weight, cos, sin)


TQ = 256
TK = 512


def head_block(block, head):
    low = lax.broadcasted_iota(jnp.int32, block.shape, 1) < 64
    return jnp.where(low if head == 0 else jnp.logical_not(low), block, jnp.zeros_like(block))


def visible(kp_ref, ks_ref, qp_ref, qs_ref, start):
    key_pos = kp_ref[pl.ds(start, TK), :]
    key_seg = ks_ref[pl.ds(start, TK), :]
    return (key_pos <= qp_ref[...]) & ((key_seg == 0) | (key_seg == qs_ref[...]))


HEAD_SLOTS = [(0, 0), (0, 1), (1, 0), (1, 1), (2, 0)]


def attend_forward(q, kv, q_pos, q_seg, k_pos, k_seg):
    rows, keys = q.shape[0], kv.shape[0]

    def kernel(q_ref, kv_ref, qp_ref, qs_ref, kp_ref, ks_ref, a_ref, o_ref, lse_ref, acc, top, tot):
        acc[...] = jnp.zeros_like(acc)
        top[...] = jnp.full_like(top, -1e30)
        tot[...] = jnp.zeros_like(tot)
        heads = [head_block(q_ref[:, 128 * b : 128 * b + 128], h) for b, h in HEAD_SLOTS]

        @pl.loop(0, keys // TK)
        def _(t):
            start = pl.multiple_of(t * TK, TK)
            k_tile = kv_ref[pl.ds(start, TK), :128]
            v_tile = kv_ref[pl.ds(start, TK), 128:]
            seen = visible(kp_ref, ks_ref, qp_ref, qs_ref, start)
            for j in range(5):
                scores = dot_general(k_tile, heads[j], 1, 1)
                scores = jnp.where(seen, scores, -1e30)
                old = top[j : j + 1, :]
                new = jnp.maximum(old, jnp.max(scores, axis=0, keepdims=True))
                expons = jnp.exp(scores - new)
                shrink = jnp.exp(old - new)
                tot[j : j + 1, :] = tot[j : j + 1, :] * shrink + jnp.sum(
                    expons, axis=0, keepdims=True
                )
                acc[j] = acc[j] * shrink + dot_general(v_tile, expons.astype(BF), 0, 0)
                top[j : j + 1, :] = new

        for j, (b, h) in enumerate(HEAD_SLOTS):
            out = acc[j] / tot[j : j + 1, :]
            acc[j] = out
        lse_ref[...] = top[...] + jnp.log(jnp.maximum(tot[...], 1e-37))
        low = lax.broadcasted_iota(jnp.int32, (TQ, 128), 1) < 64
        for b in range(3):
            first = acc[2 * b].T
            if b < 2:
                block = jnp.where(low, first, acc[2 * b + 1].T)
            else:
                block = jnp.where(low, first, 0.0)
            o_ref[:, 128 * b : 128 * b + 128] = block
            a_ref[:, 128 * b : 128 * b + 128] = block.astype(BF)

    return pl.pallas_call(
        kernel,
        name="attend_forward",
        grid=(rows // TQ,),
        in_specs=[
            pl.BlockSpec((TQ, 384), lambda i: (i, 0)),
            pl.BlockSpec((keys, 256), lambda i: (0, 0)),
            pl.BlockSpec((1, TQ), lambda i: (0, i)),
            pl.BlockSpec((1, TQ), lambda i: (0, i)),
            pl.BlockSpec((keys, 1), lambda i: (0, 0)),
            pl.BlockSpec((keys, 1), lambda i: (0, 0)),
        ],
        out_specs=[
            pl.BlockSpec((TQ, 384), lambda i: (i, 0)),
            pl.BlockSpec((TQ, 384), lambda i: (i, 0)),
            pl.BlockSpec((8, TQ), lambda i: (0, i)),
        ],
        out_shape=[
            jax.ShapeDtypeStruct((rows, 384), BF),
            jax.ShapeDtypeStruct((rows, 384), F32),
            jax.ShapeDtypeStruct((8, rows), F32),
        ],
        scratch_shapes=[
            pltpu.VMEM((5, 128, TQ), F32),
            pltpu.VMEM((8, TQ), F32),
            pltpu.VMEM((8, TQ), F32),
        ],
        compiler_params=pltpu.CompilerParams(vmem_limit_bytes=VMEM_LIMIT),
    )(q, kv, q_pos, q_seg, k_pos, k_seg)


def owner_of(link):
    ctx, wsh = link.sizes["ctx"], link.sizes["wsh"]
    my_c, my_w = lax.axis_index("ctx"), lax.axis_index("wsh")
    shard = my_w * ctx + my_c
    to_c, to_w = shard // wsh, lax.rem(shard, wsh)
    return {"ctx": to_c, "wsh": to_w}, jnp.logical_and(to_c == my_c, to_w == my_w)


def attend_backward(
    link, q, kv, q_pos, q_seg, k_pos, k_seg, lse, out, out_grad, send_rows, send_down
):
    rows, keys = q.shape[0], kv.shape[0]
    steps = rows // TQ
    axes = ("ctx",)
    peers = link.offsets(axes)
    everyone = link.offsets(("ctx", "wsh"))

    def kernel(
        q_ref, kv_ref, qp_ref, qs_ref, kp_ref, ks_ref, lse_ref, o_ref, do_ref, rows_ref, down_ref,
        dq_ref, dkv_ref, got_ref, down_got, acc, kv_acc, bounce, bounce_two, send, recv, near,
    ):
        _, me = link.place(axes, peers[0])
        copies = []
        for at, offset in enumerate(peers[1:]):
            where, index = link.place(axes, offset)
            copies.append(
                pltpu.make_async_remote_copy(
                    rows_ref.at[index],
                    got_ref.at[me],
                    send.at[at],
                    recv.at[at],
                    device_id=where,
                    device_id_type=MESH,
                )
            )
        owner, stays = owner_of(link)
        move = pltpu.make_async_remote_copy(
            down_ref,
            down_got,
            send.at[len(peers)],
            recv.at[len(peers)],
            device_id=owner,
            device_id_type=MESH,
        )
        inward = pltpu.make_async_copy(rows_ref.at[me], bounce, near.at[0])
        outward = pltpu.make_async_copy(bounce, got_ref.at[me], near.at[0])
        stay_in = pltpu.make_async_copy(down_ref, bounce_two, near.at[1])
        stay_out = pltpu.make_async_copy(bounce_two, down_got, near.at[1])

        @pl.when(pl.program_id(0) == 0)
        def _():
            greet([link.place(("ctx", "wsh"), offset)[0] for offset in everyone[1:]])
            for copy in copies:
                copy.start()

            @pl.when(jnp.logical_not(stays))
            def _():
                move.start()

            @pl.when(stays)
            def _():
                stay_in.start()
                stay_in.wait()
                stay_out.start()

            inward.start()
            inward.wait()
            outward.start()
            kv_acc[...] = jnp.zeros_like(kv_acc)

        acc[...] = jnp.zeros_like(acc)
        heads = [head_block(q_ref[:, 128 * b : 128 * b + 128], h) for b, h in HEAD_SLOTS]
        grads = [head_block(do_ref[:, 128 * b : 128 * b + 128], h) for b, h in HEAD_SLOTS]
        delta = []
        for j, (b, h) in enumerate(HEAD_SLOTS):
            product = grads[j].astype(F32) * o_ref[:, 128 * b : 128 * b + 128]
            delta.append(jnp.sum(product.T, axis=0, keepdims=True))

        @pl.loop(0, keys // TK)
        def _(t):
            start = pl.multiple_of(t * TK, TK)
            k_tile = kv_ref[pl.ds(start, TK), :128]
            v_tile = kv_ref[pl.ds(start, TK), 128:]
            seen = visible(kp_ref, ks_ref, qp_ref, qs_ref, start)
            k_sum = jnp.zeros((TK, 128), F32)
            v_sum = jnp.zeros((TK, 128), F32)
            for j in range(5):
                scores = dot_general(k_tile, heads[j], 1, 1)
                probs = jnp.where(seen, jnp.exp(scores - lse_ref[j : j + 1, :]), 0.0)
                prob_grad = dot_general(v_tile, grads[j], 1, 1)
                score_grad = (probs * (prob_grad - delta[j])).astype(BF)
                v_sum += jnp.dot(probs.astype(BF), grads[j], preferred_element_type=F32)
                k_sum += jnp.dot(score_grad, heads[j], preferred_element_type=F32)
                acc[j] += dot_general(k_tile, score_grad, 0, 0)
            kv_acc[pl.ds(start, TK), :128] += k_sum
            kv_acc[pl.ds(start, TK), 128:] += v_sum

        low = lax.broadcasted_iota(jnp.int32, (TQ, 128), 1) < 64
        for b in range(3):
            first = acc[2 * b].T * 0.125
            if b < 2:
                block = jnp.where(low, first, acc[2 * b + 1].T * 0.125)
            else:
                block = jnp.where(low, first, 0.0)
            dq_ref[:, 128 * b : 128 * b + 128] = block.astype(BF)

        @pl.when(pl.program_id(0) == steps - 1)
        def _():
            dkv_ref[...] = kv_acc[...].astype(BF)
            outward.wait()
            for copy in copies:
                copy.wait()

            @pl.when(jnp.logical_not(stays))
            def _():
                move.wait()

            @pl.when(stays)
            def _():
                stay_out.wait()

    return pl.pallas_call(
        kernel,
        name="attend_backward",
        grid=(steps,),
        in_specs=[
            pl.BlockSpec((TQ, 384), lambda i: (i, 0)),
            pl.BlockSpec((keys, 256), lambda i: (0, 0)),
            pl.BlockSpec((1, TQ), lambda i: (0, i)),
            pl.BlockSpec((1, TQ), lambda i: (0, i)),
            pl.BlockSpec((keys, 1), lambda i: (0, 0)),
            pl.BlockSpec((keys, 1), lambda i: (0, 0)),
            pl.BlockSpec((8, TQ), lambda i: (0, i)),
            pl.BlockSpec((TQ, 384), lambda i: (i, 0)),
            pl.BlockSpec((TQ, 384), lambda i: (i, 0)),
            pl.BlockSpec(memory_space=pl.ANY),
            pl.BlockSpec(memory_space=pl.ANY),
        ],
        out_specs=[
            pl.BlockSpec((TQ, 384), lambda i: (i, 0)),
            pl.BlockSpec((keys, 256), lambda i: (0, 0)),
            pl.BlockSpec(memory_space=pl.ANY),
            pl.BlockSpec(memory_space=pl.ANY),
        ],
        out_shape=[
            jax.ShapeDtypeStruct((rows, 384), BF),
            jax.ShapeDtypeStruct((keys, 256), BF),
            jax.ShapeDtypeStruct(send_rows.shape, BF),
            jax.ShapeDtypeStruct(send_down.shape, BF),
        ],
        scratch_shapes=[
            pltpu.VMEM((5, 128, TQ), F32),
            pltpu.VMEM((keys, 256), F32),
            pltpu.VMEM(send_rows.shape[1:], BF),
            pltpu.VMEM(send_down.shape, BF),
            pltpu.SemaphoreType.DMA((len(peers) + 1,)),
            pltpu.SemaphoreType.DMA((len(peers) + 1,)),
            pltpu.SemaphoreType.DMA((2,)),
        ],
        compiler_params=pltpu.CompilerParams(
            collective_id=11, has_side_effects=True, vmem_limit_bytes=VMEM_LIMIT
        ),
    )(q, kv, q_pos, q_seg, k_pos, k_seg, lse, out, out_grad, send_rows, send_down)


class Wires:
    def __init__(self, send, recv):
        self.send, self.recv, self.used = send, recv, 0

    def copy(self, source, target, where):
        at = self.used
        self.used += 1
        return pltpu.make_async_remote_copy(
            source,
            target,
            self.send.at[at],
            self.recv.at[at],
            device_id=where,
            device_id_type=MESH,
        )

    def start(self, source, target, where):
        copy = self.copy(source, target, where)
        copy.start()
        return copy


def greet(places):
    barrier = pltpu.get_barrier_semaphore()
    for where in places:
        pl.semaphore_signal(barrier, 1, device_id=where, device_id_type=MESH)
    pl.semaphore_wait(barrier, len(places))


def square():
    w = lax.axis_index("wsh")
    return w, w + 1 - 2 * lax.rem(w, 2), w + 2 - 4 * (w // 2), 3 - w


class SquareScatter:
    def __init__(self, wires, parts, near, total):
        self.wires, self.parts, self.near, self.total = wires, parts, near, total
        self.half = parts.shape[1] // 2
        self.a, self.b = pl.ds(0, self.half), pl.ds(self.half, self.half)
        self.own, self.x, self.y, self.z = square()
        self.pending = []

    def send_diagonal(self):
        wires, parts = self.wires, self.parts
        self.one = wires.start(parts.at[self.z, self.a], self.near.at[0], {"wsh": self.x})
        self.two = wires.start(parts.at[self.z, self.b], self.near.at[1], {"wsh": self.y})

    def send_x(self):
        self.pending.append(
            self.wires.start(
                self.parts.at[self.x, self.a], self.total.at[0, self.a], {"wsh": self.x}
            )
        )

    def send_y(self):
        self.pending.append(
            self.wires.start(
                self.parts.at[self.y, self.b], self.total.at[1, self.b], {"wsh": self.y}
            )
        )

    def relay(self):
        near, parts = self.near, self.parts
        self.one.wait()
        near[2] = (near[0].astype(F32) + parts[self.y, self.a].astype(F32)).astype(BF)
        self.pending.append(
            self.wires.start(near.at[2], self.total.at[1, self.a], {"wsh": self.y})
        )
        self.two.wait()
        near[3] = (near[1].astype(F32) + parts[self.x, self.b].astype(F32)).astype(BF)
        self.pending.append(
            self.wires.start(near.at[3], self.total.at[0, self.b], {"wsh": self.x})
        )

    def result(self):
        for copy in self.pending:
            copy.wait()
        return (
            self.parts[self.own].astype(F32)
            + self.total[0].astype(F32)
            + self.total[1].astype(F32)
        )


def square_scratch(rows):
    return [pltpu.VMEM((4, rows // 2, D), BF), pltpu.VMEM((2, rows, D), BF)]


class SquareGather:
    def __init__(self, wires, out):
        self.wires, self.out = wires, out
        half = out.shape[1] // 2
        self.a, self.b = pl.ds(0, half), pl.ds(half, half)
        self.own, self.x, self.y, self.z = square()

    def move(self, slot, part, to):
        return self.wires.start(self.out.at[slot, part], self.out.at[slot, part], {"wsh": to})

    def begin(self):
        self.xa = self.move(self.own, self.a, self.x)
        self.yb = self.move(self.own, self.b, self.y)
        self.xb = self.move(self.own, self.b, self.x)
        self.ya = self.move(self.own, self.a, self.y)

    def relay(self):
        self.xa.wait()
        self.one = self.move(self.x, self.a, self.y)
        self.yb.wait()
        self.two = self.move(self.y, self.b, self.x)

    def wait_x(self):
        self.xb.wait()

    def wait_y(self):
        self.ya.wait()

    def wait_z(self):
        self.one.wait()
        self.two.wait()


def feed(link, attended, w_out, tokens, gain, w_half, down, dy):
    ctx, wsh = link.sizes["ctx"], link.sizes["wsh"]
    own_rows = tokens.shape[0]
    plane = dy.shape[0]
    units = down.shape[0]
    chunk = D // ctx
    pick = units // ctx // 2

    def kernel(
        at_ref, wo_ref, x_ref, g_ref, wh_ref, dw_ref, dy_ref,
        mid_ref, mg_ref, br_ref, ag_ref, fs_ref, dp_ref, gs_ref, ds_ref,
        w_both, parts, near, total, near2, total2, n2, hgrad, hidden, gate_g, up_g,
        down_h, down_pair, down_send, down_got, gate_h, gate_pair, send, recv, local,
    ):
        wires = Wires(send, recv)
        core = lax.axis_index("grp")
        sibling = {"grp": 1 - core}
        my_c = lax.axis_index("ctx")
        own, x, y, z = square()
        levels = [link.place(("ctx",), offset) for offset in link.offsets(("ctx",))[1:]]
        greet([{"wsh": x}, {"wsh": y}, sibling] + [where for where, _ in levels])

        def rows_of(slot):
            return pl.ds(pl.multiple_of(slot * own_rows, 16), own_rows)

        w_copy = pltpu.make_async_copy(wh_ref, w_both.at[core], local)
        w_copy.start()

        first = SquareScatter(wires, parts, near, total)
        for slot in (z, x, y, own):
            parts[slot] = jnp.dot(
                at_ref[rows_of(slot), :], wo_ref[...], preferred_element_type=F32
            ).astype(BF)
            if slot is z:
                first.send_diagonal()
            elif slot is x:
                first.send_x()
            elif slot is y:
                first.send_y()
        w_swap = wires.start(wh_ref, w_both.at[core], sibling)
        hgrad[...] = dot_general(dy_ref[...], dw_ref[...], 1, 1)
        first.relay()
        middle = x_ref[...].astype(F32) + first.result()
        mid_ref[...] = middle
        factor = lax.rsqrt(jnp.mean(middle * middle, axis=-1, keepdims=True) + EPSILON)
        n2[own] = (middle * factor * g_ref[...]).astype(BF)
        gather = SquareGather(wires, n2)
        gather.begin()
        w_copy.wait()
        w_swap.wait()

        def block(slot):
            at = rows_of(slot)
            gate = jnp.dot(n2[slot], w_both[0], preferred_element_type=F32)
            up = jnp.dot(n2[slot], w_both[1], preferred_element_type=F32)
            sigmoid = 1.0 / (1.0 + jnp.exp(-gate))
            silu = gate * sigmoid
            hidden[at, :] = (silu * up).astype(BF)
            back = hgrad[at, :]
            gate_g[at, :] = (back * up * sigmoid * (1.0 + gate * (1.0 - sigmoid))).astype(BF)
            up_g[at, :] = (back * silu).astype(BF)
            parts[slot] = (
                dot_general(gate_g[at, :], w_both[0], 1, 1)
                + dot_general(up_g[at, :], w_both[1], 1, 1)
            ).astype(BF)

        second = SquareScatter(wires, parts, near2, total2)
        block(own)
        gather.relay()
        gather.wait_x()
        block(x)
        second.send_x()
        gather.wait_y()
        block(y)
        second.send_y()
        gather.wait_z()
        block(z)
        second.send_diagonal()

        strip = dot_general(hidden[...], dy_ref[...], 0, 0).astype(BF)
        for k in range(ctx):
            for g in range(2):
                top = (2 * k + g) * pick
                down_h[g, k] = strip[top : top + pick, :]
        down_swap = wires.start(down_h.at[1 - core], down_pair, sibling)
        second.relay()
        tokens_all = n2[...].reshape(plane, D)
        for g, source in enumerate((gate_g, up_g)):
            strip = dot_general(tokens_all, source[...], 0, 0).astype(BF)
            for c in range(ctx):
                gate_h[g, c] = strip[c * chunk : c * chunk + chunk, :]
        gate_swap = wires.start(gate_h.at[1 - core], gate_pair, sibling)
        down_swap.wait()
        down_send[...] = (down_h[core].astype(F32) + down_pair[...].astype(F32)).astype(BF)
        down_copies = []
        for where, index in levels:
            down_copies.append(wires.start(down_send.at[index], down_got.at[my_c], where))
        down_got[my_c] = down_send[my_c]

        grad = second.result()
        middle = mid_ref[...]
        factor = lax.rsqrt(jnp.mean(middle * middle, axis=-1, keepdims=True) + EPSILON)
        weighted = grad * g_ref[...]
        inner = jnp.mean(weighted * middle, axis=-1, keepdims=True)
        middle_grad = (
            dy_ref[rows_of(own), :].astype(F32)
            + factor * weighted
            - middle * (factor * factor * factor) * inner
        )
        mg_ref[...] = middle_grad
        br_ref[own] = middle_grad.astype(BF)
        branch = SquareGather(wires, br_ref)
        branch.begin()
        fs_ref[...] = jnp.sum(grad * middle * factor, axis=0, keepdims=True)

        def outward(slot):
            ag_ref[rows_of(slot), :] = dot_general(br_ref[slot], wo_ref[...], 1, 1).astype(BF)

        outward(own)
        gate_swap.wait()
        for c in range(ctx):
            gs_ref[c] = (gate_h[core, c].astype(F32) + gate_pair[c].astype(F32)).astype(BF)
        branch.relay()
        for slot in range(wsh):
            at = slice(slot * own_rows, slot * own_rows + own_rows)
            dp_ref[slot] = jnp.dot(
                hidden[at, :], dw_ref[...], preferred_element_type=F32
            ).astype(BF)
        branch.wait_x()
        outward(x)
        branch.wait_y()
        outward(y)
        branch.wait_z()
        outward(z)
        for copy in down_copies:
            copy.wait()
        ds_ref[...] = jnp.sum(down_got[...].astype(F32), axis=0).astype(BF)

    operands = (attended, w_out, tokens, gain, w_half, down, dy)
    vmem = pl.BlockSpec(memory_space=pltpu.VMEM)
    return pl.pallas_call(
        kernel,
        name="feed",
        in_specs=[vmem] * len(operands),
        out_specs=[vmem] * 8,
        out_shape=[
            jax.ShapeDtypeStruct((own_rows, D), F32),
            jax.ShapeDtypeStruct((own_rows, D), F32),
            jax.ShapeDtypeStruct((wsh, own_rows, D), BF),
            jax.ShapeDtypeStruct((plane, 384), BF),
            jax.ShapeDtypeStruct((1, D), F32),
            jax.ShapeDtypeStruct((wsh, own_rows, D), BF),
            jax.ShapeDtypeStruct((ctx, chunk, units), BF),
            jax.ShapeDtypeStruct((pick, D), BF),
        ],
        scratch_shapes=[
            pltpu.VMEM((2, D, units), BF),
            pltpu.VMEM((4, own_rows, D), BF),
            *square_scratch(own_rows),
            *square_scratch(own_rows),
            pltpu.VMEM((4, own_rows, D), BF),
            pltpu.VMEM((plane, units), F32),
            *[pltpu.VMEM((plane, units), BF)] * 3,
            pltpu.VMEM((2, ctx, pick, D), BF),
            *[pltpu.VMEM((ctx, pick, D), BF)] * 3,
            pltpu.VMEM((2, ctx, chunk, units), BF),
            pltpu.VMEM((ctx, chunk, units), BF),
            pltpu.SemaphoreType.DMA((ctx + 28,)),
            pltpu.SemaphoreType.DMA((ctx + 28,)),
            pltpu.SemaphoreType.DMA,
        ],
        compiler_params=pltpu.CompilerParams(
            collective_id=3, has_side_effects=True, vmem_limit_bytes=VMEM_LIMIT
        ),
    )(*operands)


def finish(
    link, q_grad, kv_grad, weight, cos, sin, normed, tokens, gain, middle_grad, gate_got, down_got,
    attended, branch, feed_sum, down_part, middle,
):
    ctx, wsh = link.sizes["ctx"], link.sizes["wsh"]
    shards = ctx * wsh
    rows = D // shards
    chunk = D // ctx
    fold = ctx // wsh
    own_rows = tokens.shape[0]
    plane = normed.shape[0]
    axes = ("ctx", "wsh")
    peers = link.offsets(axes)
    gate_width = gate_got.shape[2]
    down_rows = down_got.shape[0]

    def kernel(
        q_ref, kv_send, w_ref, c_ref, s_ref, n_ref, x_ref, g_ref, mg_ref, gate_ref, down_ref,
        at_ref, br_ref, fs_ref, dp_ref, mid_ref,
        act_ref, ig_ref, qkv_ref, out_ref, gate_out, down_out, gains_out,
        kv_ref, pg, parts, near, total, near2, total2, acc, wide, q_own, q_pair, q_send, q_got,
        q_mid, q_fin, kv_own, kv_pair, kv_go, kv_got, kv_mid, kv_fin, gate_mid, gate_fin, down_fin, out_halves,
        out_pair, out_send, out_mid, out_got, out_fin, gains, gains_got, gains_fin,
        send, recv,
    ):
        wires = Wires(send, recv)
        core = lax.axis_index("grp")
        first, second = core == 0, core == 1
        sibling = {"grp": 1 - core}
        my_c, my_w = lax.axis_index("ctx"), lax.axis_index("wsh")
        odd = lax.rem(my_w, 2) == 1
        greet([link.place(axes, offset)[0] for offset in peers[1:]] + [sibling])
        _, me = link.place(axes, peers[0])

        def over_ctx(got, mid):
            for w in range(wsh):
                strip = got[0, w * rows : w * rows + rows, :].astype(F32)
                for c in range(1, ctx):
                    strip += got[c, w * rows : w * rows + rows, :].astype(F32)
                mid[w] = strip.astype(BF)

        def in_plane(mid, slot_of):
            copies = []
            for offset in link.offsets(("wsh",))[1:]:
                where, index = link.place(("wsh",), offset)
                copies.append(wires.copy(mid.at[index], slot_of(my_w), where))
            return copies

        def begin(cond, *copies):
            @pl.when(cond)
            def _():
                for copy in copies:
                    copy.start()

        kv_copies = []
        for offset in link.offsets(("ctx",))[1:]:
            where, index = link.place(("ctx",), offset)
            kv_copies.append(wires.start(kv_send.at[index], kv_ref.at[my_c], where))
        layer = SquareScatter(wires, dp_ref, near2, total2)
        layer.send_diagonal()
        layer.send_x()
        layer.send_y()
        kv_ref[my_c] = kv_send[my_c]

        wide[...] = dot_general(at_ref[...], br_ref[...], 0, 0)

        def out_strips(pieces):
            at = 0
            for start, size in pieces:
                acc_rows = wide[start : start + size, :].astype(BF)
                part = jnp.concatenate([acc_rows[:, :576], jnp.zeros((size, 64), BF)], axis=1)
                out_halves[0, at : at + size, :] = part
                part = jnp.concatenate([acc_rows[:, 576:], jnp.zeros((size, 64), BF)], axis=1)
                out_halves[1, at : at + size, :] = part
                at += size

        @pl.when(odd)
        def _():
            out_strips([(96, 32), (192, 64), (0, 64), (128, 64), (256, 64)])

        @pl.when(jnp.logical_not(odd))
        def _():
            out_strips([(0, 64), (128, 64), (256, 64), (64, 64), (192, 32)])

        out_swap = wires.start(out_halves.at[1 - core], out_pair, sibling)
        low = lax.rem(lax.broadcasted_iota(jnp.int32, (own_rows, 128), 1), 64) < 32

        @pl.loop(0, wsh)
        def _(slot):
            at = pl.ds(pl.multiple_of(slot * own_rows, 16), own_rows)
            for b in range(3):
                block = q_ref[at, 128 * b : 128 * b + 128].astype(F32)
                pg[at, 128 * b : 128 * b + 128] = turn(
                    block, c_ref[at, :], -s_ref[at, :], low
                ).astype(BF)

        layer.relay()
        for b in range(3):
            acc[384 * b : 384 * b + 384, :] = dot_general(
                n_ref[:, 384 * b : 384 * b + 384], pg[:, :384], 0, 0
            )

        for c in range(ctx):
            q_own[c] = acc[c * chunk : c * chunk + chunk, :].astype(BF)
        q_swap = wires.copy(q_own, q_pair, sibling)
        begin(second, q_swap)

        down_fin[core] = down_ref[...]
        down_copy = wires.start(down_fin.at[core], down_fin.at[core], sibling)

        over_ctx(gate_ref, gate_mid)
        gate_moves = in_plane(gate_mid, lambda w: gate_fin.at[core, w])
        for copy in gate_moves:
            copy.start()
        gate_fin[core, my_w] = gate_mid[my_w]
        act_ref[...] = (mid_ref[...] + layer.result()).astype(BF)
        out_swap.wait()
        for k in range(ctx):
            strip = slice(k * rows, k * rows + rows)
            out_send[k % wsh, k // wsh] = (
                out_halves[core, strip, :].astype(F32) + out_pair[strip, :].astype(F32)
            ).astype(BF)
        out_moves = in_plane(out_send, lambda w: out_mid.at[w])
        for copy in out_moves:
            copy.start()
        out_mid[my_w] = out_send[my_w]

        @pl.when(first)
        def _():
            q_swap.wait_recv()

            @pl.loop(0, ctx)
            def _(c):
                q_send[c] = (q_own[c].astype(F32) + q_pair[c].astype(F32)).astype(BF)

        @pl.when(second)
        def _():
            q_swap.wait_send()

        for copy in gate_moves:
            copy.wait()
        gate_copy = wires.start(gate_fin.at[core], gate_fin.at[core], sibling)
        down_copy.wait()
        down_out[:down_rows, :] = down_fin[0].astype(F32)
        down_out[down_rows:, :] = down_fin[1].astype(F32)
        gate_copy.wait()
        for half in range(2):
            for w in range(wsh):
                left = (half * wsh + w) * gate_width
                gate_out[:, left : left + gate_width] = gate_fin[half, w].astype(F32)

        for copy in out_moves:
            copy.wait()

        for copy in kv_copies:
            copy.wait()
        q_copies, kvg_copies, out_copies = [], [], []
        for offset in link.offsets(("ctx",))[1:]:
            where, index = link.place(("ctx",), offset)
            q_copies.append(wires.copy(q_send.at[index], q_got.at[my_c], where))
            kvg_copies.append(wires.copy(kv_go.at[index], kv_got.at[my_c], where))
        begin(first, *q_copies)
        for offset in link.offsets(("ctx",))[1:]:
            where, index = link.place(("ctx",), offset)
            part = out_mid.at[index // fold, lax.rem(index, fold)]
            out_copies.append(wires.start(part, out_got.at[my_c], where))
        out_got[my_c] = out_mid[my_c // fold, lax.rem(my_c, fold)]
        scatter = SquareScatter(wires, parts, near, total)
        gain_sum = jnp.zeros((1, D), F32)
        for slot in (scatter.z, scatter.x, scatter.y, scatter.own):
            at = pl.ds(pl.multiple_of(slot * own_rows, 16), own_rows)
            summed = kv_ref[0, at, :].astype(F32)
            for c in range(1, ctx):
                summed += kv_ref[c, at, :].astype(F32)
            block = summed[:, :128].astype(BF).astype(F32)
            pg[at, 384:512] = turn(block, c_ref[at, :], -s_ref[at, :], low).astype(BF)
            pg[at, 512:] = summed[:, 128:].astype(BF)
            part = dot_general(pg[at, :], w_ref[...], 1, 1)
            parts[slot] = part.astype(BF)
            gain_sum += jnp.sum(part * n_ref[at, :].astype(F32), axis=0, keepdims=True)
            if slot is scatter.z:
                scatter.send_diagonal()
            elif slot is scatter.x:
                scatter.send_x()
            elif slot is scatter.y:
                scatter.send_y()

        for b in range(3):
            acc[384 * b : 384 * b + 384, :256] = dot_general(
                n_ref[:, 384 * b : 384 * b + 384], pg[:, 384:], 0, 0
            )

        for c in range(ctx):
            kv_own[c] = acc[c * chunk : c * chunk + chunk, :256].astype(BF)
        kv_swap = wires.copy(kv_own, kv_pair, sibling)
        begin(first, kv_swap)
        both = jnp.concatenate([gain_sum / g_ref[...], fs_ref[...]], axis=0)
        gains[...] = jnp.zeros_like(gains)
        for s in range(shards):
            gains[s, :2, :rows] = both[:, rows * s : rows * s + rows]
        gain_copies = []
        for offset in peers[1:]:
            where, index = link.place(axes, offset)
            gain_copies.append(wires.start(gains.at[index], gains_got.at[me], where))
        gains_got[me] = gains[me]
        scatter.relay()

        @pl.when(second)
        def _():
            kv_swap.wait_recv()

            @pl.loop(0, ctx)
            def _(c):
                kv_go[c] = (kv_own[c].astype(F32) + kv_pair[c].astype(F32)).astype(BF)

            for copy in kvg_copies:
                copy.start()
            kv_got[my_c] = kv_go[my_c]

        @pl.when(first)
        def _():
            kv_swap.wait_send()
            q_got[my_c] = q_send[my_c]
            for copy in q_copies:
                copy.wait()
            over_ctx(q_got, q_mid)

        q_moves = in_plane(q_mid, lambda w: q_fin.at[w])
        begin(first, *q_moves)
        for copy in out_copies:
            copy.wait()
        out_fin[core] = jnp.sum(out_got[...].astype(F32), axis=0).astype(BF)

        out_copy = wires.start(out_fin.at[core], out_fin.at[core], sibling)

        grad = scatter.result()
        x = x_ref[...].astype(F32)
        factor = lax.rsqrt(jnp.mean(x * x, axis=-1, keepdims=True) + EPSILON)
        weighted = grad * g_ref[...]
        inner = jnp.mean(weighted * x, axis=-1, keepdims=True)
        ig_ref[...] = mg_ref[...] + factor * weighted - x * (factor * factor * factor) * inner
        q_final = wires.copy(q_fin, q_fin, sibling)
        kv_final = wires.copy(kv_fin, kv_fin, sibling)

        kv_moves = in_plane(kv_mid, lambda w: kv_fin.at[w])

        @pl.when(first)
        def _():
            for copy in q_moves:
                copy.wait()
            q_fin[my_w] = q_mid[my_w]
            q_final.start()

        @pl.when(second)
        def _():
            for copy in kvg_copies:
                copy.wait()
            over_ctx(kv_got, kv_mid)
            for copy in kv_moves:
                copy.start()
            for copy in kv_moves:
                copy.wait()
            kv_fin[my_w] = kv_mid[my_w]
            kv_final.start()

        for copy in gain_copies:
            copy.wait()
        gains_fin[core] = jnp.sum(gains_got[...], axis=0)
        gain_copy = wires.start(gains_fin.at[core], gains_fin.at[core], sibling)
        out_copy.wait()
        out_ref[...] = jnp.concatenate(
            [out_fin[0, :, :576].astype(F32), out_fin[1, :, :576].astype(F32)], axis=1
        )

        @pl.when(first)
        def _():
            q_final.wait_send()
            kv_final.wait_recv()

        @pl.when(second)
        def _():
            kv_final.wait_send()
            q_final.wait_recv()

        qkv_ref[...] = qkv_restore(
            [
                jnp.concatenate([q_fin[w].astype(F32), kv_fin[w].astype(F32)], axis=1)
                for w in range(wsh)
            ]
        )
        gain_copy.wait()
        gains_out[...] = gains_fin[0] + gains_fin[1]

    operands = (
        q_grad, kv_grad, weight, cos, sin, normed, tokens, gain, middle_grad, gate_got, down_got,
        attended, branch, feed_sum, down_part, middle,
    )
    vmem = pl.BlockSpec(memory_space=pltpu.VMEM)
    return pl.pallas_call(
        kernel,
        name="finish",
        in_specs=[vmem] * len(operands),
        out_specs=[vmem] * 7,
        out_shape=[
            jax.ShapeDtypeStruct((own_rows, D), BF),
            jax.ShapeDtypeStruct((own_rows, D), F32),
            jax.ShapeDtypeStruct((rows, QW + 2 * KW), F32),
            jax.ShapeDtypeStruct((rows, D), F32),
            jax.ShapeDtypeStruct((rows, 2 * FF), F32),
            jax.ShapeDtypeStruct((2 * down_rows, D), F32),
            jax.ShapeDtypeStruct((8, 128), F32),
        ],
        scratch_shapes=[
            pltpu.VMEM((ctx, plane, 256), BF),
            pltpu.VMEM((plane, 640), BF),
            pltpu.VMEM((4, own_rows, D), BF),
            *square_scratch(own_rows),
            *square_scratch(own_rows),
            pltpu.VMEM((D, 384), F32),
            pltpu.VMEM((384, D), F32),
            *[pltpu.VMEM((ctx, chunk, 384), BF)] * 4,
            *[pltpu.VMEM((wsh, rows, 384), BF)] * 2,
            *[pltpu.VMEM((ctx, chunk, 256), BF)] * 4,
            *[pltpu.VMEM((wsh, rows, 256), BF)] * 2,
            pltpu.VMEM((wsh, rows, gate_width), BF),
            pltpu.VMEM((2, wsh, rows, gate_width), BF),
            pltpu.VMEM((2, down_rows, D), BF),
            pltpu.VMEM((2, 288, 640), BF),
            pltpu.VMEM((288, 640), BF),
            pltpu.VMEM((wsh, fold, rows, 640), BF),
            pltpu.VMEM((wsh, fold, rows, 640), BF),
            pltpu.VMEM((ctx, rows, 640), BF),
            pltpu.VMEM((2, rows, 640), BF),
            pltpu.VMEM((shards, 8, 128), F32),
            pltpu.VMEM((shards, 8, 128), F32),
            pltpu.VMEM((2, 8, 128), F32),
            pltpu.SemaphoreType.DMA((3 * shards + 2 * ctx + 32,)),
            pltpu.SemaphoreType.DMA((3 * shards + 2 * ctx + 32,)),
        ],
        compiler_params=pltpu.CompilerParams(
            collective_id=8, has_side_effects=True, vmem_limit_bytes=VMEM_LIMIT
        ),
    )(*operands)


def rms_factor(values):
    return lax.rsqrt(jnp.mean(values * values, axis=-1, keepdims=True) + EPSILON)


def rope_tables(positions):
    frequency = jnp.exp(jnp.arange(32, dtype=F32) * (-math.log(10000.0) / 32))
    angles = positions.astype(F32)[:, None] * jnp.tile(frequency, 4)[None, :]
    sign = jnp.where(jnp.arange(128) % 64 < 32, -1.0, 1.0).astype(F32)
    return jnp.cos(angles), jnp.sin(angles) * sign[None, :]


def build(sizes):
    ctx, wsh = sizes["ctx"], sizes["wsh"]
    shards = ctx * wsh
    link = Exchange(sizes)

    def local(
        tokens,
        segment_ids,
        positions,
        attend_gain,
        query_key_value,
        attend_out,
        feed_gain,
        gate_up,
        down_weight,
        upstream,
    ):
        own = tokens.shape[0]
        plane = own * wsh
        group = plane * ctx
        core = lax.axis_index("grp")
        odd = lax.rem(lax.axis_index("wsh"), 2) == 1
        inputs = tokens.astype(F32)
        factor_one = rms_factor(inputs)
        normed_one = (inputs * factor_one * attend_gain).astype(BF)
        marks = jnp.pad(segment_ids * 65536 + positions, (0, 1024 - own)).reshape(8, 128)

        normed_all, w_qkv, marks_plane = link.run(
            "gather_one",
            1,
            [
                link.gather(normed_one, ("wsh",)),
                link.swap(qkv_columns(query_key_value), ("wsh",)),
                link.gather(marks, ("wsh",)),
            ],
        )
        normed_all = normed_all.reshape(plane, D)
        w_qkv = w_qkv.reshape(D, 640)
        plane_marks = marks_plane.reshape(wsh, 1024)[:, :own].reshape(plane)
        q_pos, q_seg = plane_marks % 65536, plane_marks // 65536
        cos, sin = rope_tables(q_pos)
        queries, kv_own = project(normed_all, w_qkv, cos, sin)

        kv_all, marks_all, dy_all, w_half = link.run(
            "gather_keys",
            2,
            [
                link.gather(kv_own, ("ctx",)),
                link.gather(marks_plane, ("ctx",)),
                link.gather(upstream, ("wsh",)),
                link.columns(gate_up, ("wsh",), FF, FF // wsh),
            ],
        )
        kv_all = kv_all.reshape(group, 256)
        dy_all = dy_all.reshape(plane, D)
        w_half = w_half.reshape(D, FF // wsh)
        marks_all = marks_all.reshape(shards, 1024)[:, :own].reshape(group, 1)
        k_pos, k_seg = marks_all % 65536, marks_all // 65536
        q_pos, q_seg = q_pos.reshape(1, plane), q_seg.reshape(1, plane)
        attended, attended_wide, lse = attend_forward(queries, kv_all, q_pos, q_seg, k_pos, k_seg)

        w_out = spread_rows(attend_out, odd)
        (
            middle,
            middle_grad,
            branch_all,
            attended_grad,
            feed_sum,
            down_part,
            gate_send,
            down_sum,
        ) = feed(link, attended, w_out, tokens, feed_gain[None, :], w_half, down_weight, dy_all)
        q_grad, kv_grad, gate_got, down_got = attend_backward(
            link, queries, kv_all, q_pos, q_seg, k_pos, k_seg, lse, attended_wide, attended_grad,
            gate_send, down_sum,
        )
        (activations, input_grad, qkv_out, out_out, gate_out, down_out, gain_out) = finish(
            link, q_grad, kv_grad.reshape(ctx, plane, 256), w_qkv, cos, sin, normed_all, tokens,
            attend_gain[None, :], middle_grad, gate_got, down_got, attended,
            branch_all.reshape(plane, D), feed_sum, down_part, middle,
        )
        width = D // shards
        return (
            activations,
            input_grad,
            qkv_out,
            out_out,
            gate_out,
            down_out,
            gain_out[0, :width],
            gain_out[1, :width],
        )

    return local


def solution(mesh):
    whole = ("grp", "ctx", "wsh")
    in_specs = (
        P(whole, None),
        P(whole),
        P(whole),
        P(),
        P("wsh", None),
        P("wsh", None),
        P(),
        P("wsh", None),
        P("wsh", None),
        P(whole, None),
    )
    out_specs = (
        P(whole, None),
        P(whole, None),
        P(("ctx", "wsh"), None),
        P(("ctx", "wsh"), None),
        P(("ctx", "wsh"), None),
        P(("ctx", "wsh"), None),
        P(("ctx", "wsh")),
        P(("ctx", "wsh")),
    )
    return jax.shard_map(
        build(dict(mesh.shape)), mesh=mesh, in_specs=in_specs, out_specs=out_specs, check_vma=False
    )
```

```python
import itertools
import math

import jax
import jax.numpy as jnp
from jax import lax
from jax.experimental import pallas as pl
from jax.experimental.pallas import tpu as pltpu
from jax.sharding import PartitionSpec as P

HEADS = 18
KV_HEADS = 6
HEAD_DIM = 64
FF = 3072
D = 1152
QW = 1152
KW = 384
EPSILON = 1e-05
MESH = pl.DeviceIdType.MESH
F32 = jnp.float32
BF = jnp.bfloat16
VMEM_LIMIT = 56 << 20


def dot_general(a, b, ca, cb):
    return lax.dot_general(a, b, (((ca,), (cb,)), ((), ())), preferred_element_type=F32)


class Exchange:
    def __init__(self, sizes):
        self.sizes = sizes

    def place(self, axes, offset):
        where, index = {}, 0
        for axis, step in zip(axes, offset):
            size = self.sizes[axis]
            spot = lax.axis_index(axis)
            if step:
                spot = lax.rem(spot + step, size)
            where[axis] = spot
            index = index * size + spot
        return where, index

    def offsets(self, axes):
        return list(itertools.product(*[range(self.sizes[axis]) for axis in axes]))


def head_plan(w):
    pair, odd = w // 2, w % 2
    start = 9 * pair + 4 * odd
    if odd:
        f_heads, h_heads = [start + 2, start + 3, start + 4], [start, start + 1]
        f_kv, h_kv = 3 * pair + 2, 3 * pair + 1
    else:
        f_heads, h_heads = [start, start + 1, start + 2], [start + 3, start + 4]
        f_kv, h_kv = 3 * pair, 3 * pair + 1
    q_order = [f_heads[0], h_heads[0], f_heads[1], h_heads[1], f_heads[2], None]
    return q_order, [f_kv, h_kv]


def qkv_restore(parts):
    found = {}
    for w in range(4):
        q_order, kv_order = head_plan(w)
        slots = list(q_order) + [HEADS + h for h in kv_order]
        slots += [HEADS + KV_HEADS + h for h in kv_order]
        for at, head in enumerate(slots):
            if head is not None:
                found.setdefault(head, []).append(
                    parts[w][:, at * HEAD_DIM : (at + 1) * HEAD_DIM]
                )
    pieces = []
    for head in range(HEADS + 2 * KV_HEADS):
        term = found[head][0]
        for other in found[head][1:]:
            term = term + other
        pieces.append(term)
    return jnp.concatenate(pieces, axis=1)


def spread_rows(rows, odd):
    n = rows.shape[1]
    half = jnp.zeros((32, n), rows.dtype)
    blank = jnp.zeros((64, n), rows.dtype)
    even_rows = jnp.concatenate(
        [rows[0:64], rows[192:256], rows[64:128], rows[256:288], half, rows[128:192], blank]
    )
    odd_rows = jnp.concatenate(
        [rows[96:160], half, rows[0:32], rows[160:224], rows[32:96], rows[224:288], blank]
    )
    return jnp.where(odd, odd_rows, even_rows)


def turn(x, cos, sin, lanes):
    swapped = jnp.where(lanes, pltpu.roll(x, 96, 1), pltpu.roll(x, 32, 1))
    return x * cos + swapped * sin


TQ = 256
TK = 512


def head_block(block, head):
    low = lax.broadcasted_iota(jnp.int32, block.shape, 1) < 64
    return jnp.where(low if head == 0 else jnp.logical_not(low), block, jnp.zeros_like(block))


def visible(kp_ref, ks_ref, qp_ref, qs_ref, start):
    key_pos = jnp.tile(kp_ref[pl.ds(start, TK), :], (1, TQ // 128))
    key_seg = jnp.tile(ks_ref[pl.ds(start, TK), :], (1, TQ // 128))
    return (key_pos <= qp_ref[...]) & ((key_seg == 0) | (key_seg == qs_ref[...]))


HEAD_SLOTS = [(0, 0), (0, 1), (1, 0), (1, 1), (2, 0)]


def attend_forward(link, q, kv, q_pos, q_seg, k_pos, k_seg, gate_up):
    rows, keys = q.shape[0], kv.shape[0]
    steps = rows // TQ
    wsh = link.sizes["wsh"]
    units = FF // wsh
    peers = link.offsets(("wsh",))

    def kernel(
        q_ref, kv_ref, qp_ref, qs_ref, kp_ref, ks_ref, gu_ref,
        a_ref, o_ref, lse_ref, wh_ref,
        acc, top, tot, bounce, send, recv, near,
    ):
        def columns(p):
            left = lax.axis_index("grp") * FF + p * units
            return gu_ref.at[:, pl.ds(pl.multiple_of(left, 128), units)]

        wires = Wires(send, recv)
        _, me = link.place(("wsh",), peers[0])
        copies = []
        for offset in peers[1:]:
            where, index = link.place(("wsh",), offset)
            copies.append(wires.copy(columns(index), wh_ref.at[me], where))
        inward = pltpu.make_async_copy(columns(me), bounce, near)
        outward = pltpu.make_async_copy(bounce, wh_ref.at[me], near)

        @pl.when(pl.program_id(0) == 0)
        def _():
            greet([link.place(("wsh",), offset)[0] for offset in peers[1:]])
            for copy in copies:
                copy.start()
            inward.start()
            inward.wait()
            outward.start()

        acc[...] = jnp.zeros_like(acc)
        top[...] = jnp.full_like(top, -1e30)
        tot[...] = jnp.zeros_like(tot)
        heads = [head_block(q_ref[:, 128 * b : 128 * b + 128], h) for b, h in HEAD_SLOTS]

        @pl.loop(0, keys // TK)
        def _(t):
            start = pl.multiple_of(t * TK, TK)
            k_tile = kv_ref[pl.ds(start, TK), :128]
            v_tile = kv_ref[pl.ds(start, TK), 128:]
            seen = visible(kp_ref, ks_ref, qp_ref, qs_ref, start)
            for j in range(5):
                scores = dot_general(k_tile, heads[j], 1, 1)
                scores = jnp.where(seen, scores, -1e30)
                old = top[j : j + 1, :]
                new = jnp.maximum(old, jnp.max(scores, axis=0, keepdims=True))
                expons = jnp.exp(scores - new)
                shrink = jnp.exp(old - new)
                tot[j : j + 1, :] = tot[j : j + 1, :] * shrink + jnp.sum(
                    expons, axis=0, keepdims=True
                )
                acc[j] = acc[j] * shrink + dot_general(v_tile, expons.astype(BF), 0, 0)
                top[j : j + 1, :] = new

        for j, (b, h) in enumerate(HEAD_SLOTS):
            out = acc[j] / tot[j : j + 1, :]
            acc[j] = out
        lse_ref[...] = top[...] + jnp.log(jnp.maximum(tot[...], 1e-37))
        low = lax.broadcasted_iota(jnp.int32, (TQ, 128), 1) < 64
        for b in range(3):
            first = acc[2 * b].T
            if b < 2:
                block = jnp.where(low, first, acc[2 * b + 1].T)
            else:
                block = jnp.where(low, first, 0.0)
            o_ref[:, 128 * b : 128 * b + 128] = block
            a_ref[:, 128 * b : 128 * b + 128] = block.astype(BF)

        @pl.when(pl.program_id(0) == steps - 1)
        def _():
            outward.wait()
            for copy in copies:
                copy.wait()

    return pl.pallas_call(
        kernel,
        name="attend_forward",
        grid=(steps,),
        in_specs=[
            pl.BlockSpec((TQ, 384), lambda i: (i, 0)),
            pl.BlockSpec((keys, 256), lambda i: (0, 0)),
            pl.BlockSpec((1, TQ), lambda i: (0, i)),
            pl.BlockSpec((1, TQ), lambda i: (0, i)),
            pl.BlockSpec((keys, 128), lambda i: (0, 0)),
            pl.BlockSpec((keys, 128), lambda i: (0, 0)),
            pl.BlockSpec(memory_space=pl.ANY),
        ],
        out_specs=[
            pl.BlockSpec((TQ, 384), lambda i: (i, 0)),
            pl.BlockSpec((TQ, 384), lambda i: (i, 0)),
            pl.BlockSpec((8, TQ), lambda i: (0, i)),
            pl.BlockSpec(memory_space=pl.ANY),
        ],
        out_shape=[
            jax.ShapeDtypeStruct((rows, 384), BF),
            jax.ShapeDtypeStruct((rows, 384), F32),
            jax.ShapeDtypeStruct((8, rows), F32),
            jax.ShapeDtypeStruct((wsh, gate_up.shape[0], units), BF),
        ],
        scratch_shapes=[
            pltpu.VMEM((5, 128, TQ), F32),
            pltpu.VMEM((8, TQ), F32),
            pltpu.VMEM((8, TQ), F32),
            pltpu.VMEM((gate_up.shape[0], units), BF),
            pltpu.SemaphoreType.DMA((wsh,)),
            pltpu.SemaphoreType.DMA((wsh,)),
            pltpu.SemaphoreType.DMA,
        ],
        compiler_params=pltpu.CompilerParams(
            collective_id=2, has_side_effects=True, vmem_limit_bytes=VMEM_LIMIT
        ),
    )(q, kv, q_pos, q_seg, k_pos, k_seg, gate_up)


def owner_of(link):
    ctx, wsh = link.sizes["ctx"], link.sizes["wsh"]
    my_c, my_w = lax.axis_index("ctx"), lax.axis_index("wsh")
    shard = my_w * ctx + my_c
    to_c, to_w = shard // wsh, lax.rem(shard, wsh)
    return {"ctx": to_c, "wsh": to_w}, jnp.logical_and(to_c == my_c, to_w == my_w)


def attend_backward(
    link, q, kv, q_pos, q_seg, k_pos, k_seg, lse, out, out_grad, send_rows, send_down
):
    rows, keys = q.shape[0], kv.shape[0]
    steps = rows // TQ
    axes = ("ctx",)
    peers = link.offsets(axes)
    everyone = link.offsets(("ctx", "wsh"))

    def kernel(
        q_ref, kv_ref, qp_ref, qs_ref, kp_ref, ks_ref, lse_ref, o_ref, do_ref, rows_ref, down_ref,
        dq_ref, dkv_ref, got_ref, down_got, acc, kv_acc, bounce, bounce_two, send, recv, near,
    ):
        _, me = link.place(axes, peers[0])
        copies = []
        for at, offset in enumerate(peers[1:]):
            where, index = link.place(axes, offset)
            copies.append(
                pltpu.make_async_remote_copy(
                    rows_ref.at[index],
                    got_ref.at[me],
                    send.at[at],
                    recv.at[at],
                    device_id=where,
                    device_id_type=MESH,
                )
            )
        owner, stays = owner_of(link)
        move = pltpu.make_async_remote_copy(
            down_ref,
            down_got,
            send.at[len(peers)],
            recv.at[len(peers)],
            device_id=owner,
            device_id_type=MESH,
        )
        inward = pltpu.make_async_copy(rows_ref.at[me], bounce, near.at[0])
        outward = pltpu.make_async_copy(bounce, got_ref.at[me], near.at[0])
        stay_in = pltpu.make_async_copy(down_ref, bounce_two, near.at[1])
        stay_out = pltpu.make_async_copy(bounce_two, down_got, near.at[1])

        @pl.when(pl.program_id(0) == 0)
        def _():
            greet([link.place(("ctx", "wsh"), offset)[0] for offset in everyone[1:]])
            for copy in copies:
                copy.start()

            @pl.when(jnp.logical_not(stays))
            def _():
                move.start()

            @pl.when(stays)
            def _():
                stay_in.start()
                stay_in.wait()
                stay_out.start()

            inward.start()
            inward.wait()
            outward.start()
            kv_acc[...] = jnp.zeros_like(kv_acc)

        acc[...] = jnp.zeros_like(acc)
        heads = [head_block(q_ref[:, 128 * b : 128 * b + 128], h) for b, h in HEAD_SLOTS]
        grads = [head_block(do_ref[:, 128 * b : 128 * b + 128], h) for b, h in HEAD_SLOTS]
        delta = []
        for j, (b, h) in enumerate(HEAD_SLOTS):
            product = grads[j].astype(F32) * o_ref[:, 128 * b : 128 * b + 128]
            delta.append(jnp.sum(product.T, axis=0, keepdims=True))

        @pl.loop(0, keys // TK)
        def _(t):
            start = pl.multiple_of(t * TK, TK)
            k_tile = kv_ref[pl.ds(start, TK), :128]
            v_tile = kv_ref[pl.ds(start, TK), 128:]
            seen = visible(kp_ref, ks_ref, qp_ref, qs_ref, start)
            k_sum = jnp.zeros((TK, 128), F32)
            v_sum = jnp.zeros((TK, 128), F32)
            for j in range(5):
                scores = dot_general(k_tile, heads[j], 1, 1)
                probs = jnp.where(seen, jnp.exp(scores - lse_ref[j : j + 1, :]), 0.0)
                prob_grad = dot_general(v_tile, grads[j], 1, 1)
                score_grad = (probs * (prob_grad - delta[j])).astype(BF)
                v_sum += jnp.dot(probs.astype(BF), grads[j], preferred_element_type=F32)
                k_sum += jnp.dot(score_grad, heads[j], preferred_element_type=F32)
                acc[j] += dot_general(k_tile, score_grad, 0, 0)
            kv_acc[pl.ds(start, TK), :128] += k_sum
            kv_acc[pl.ds(start, TK), 128:] += v_sum

        low = lax.broadcasted_iota(jnp.int32, (TQ, 128), 1) < 64
        for b in range(3):
            first = acc[2 * b].T * 0.125
            if b < 2:
                block = jnp.where(low, first, acc[2 * b + 1].T * 0.125)
            else:
                block = jnp.where(low, first, 0.0)
            dq_ref[:, 128 * b : 128 * b + 128] = block.astype(BF)

        @pl.when(pl.program_id(0) == steps - 1)
        def _():
            dkv_ref[...] = kv_acc[...].astype(BF)
            outward.wait()
            for copy in copies:
                copy.wait()

            @pl.when(jnp.logical_not(stays))
            def _():
                move.wait()

            @pl.when(stays)
            def _():
                stay_out.wait()

    return pl.pallas_call(
        kernel,
        name="attend_backward",
        grid=(steps,),
        in_specs=[
            pl.BlockSpec((TQ, 384), lambda i: (i, 0)),
            pl.BlockSpec((keys, 256), lambda i: (0, 0)),
            pl.BlockSpec((1, TQ), lambda i: (0, i)),
            pl.BlockSpec((1, TQ), lambda i: (0, i)),
            pl.BlockSpec((keys, 128), lambda i: (0, 0)),
            pl.BlockSpec((keys, 128), lambda i: (0, 0)),
            pl.BlockSpec((8, TQ), lambda i: (0, i)),
            pl.BlockSpec((TQ, 384), lambda i: (i, 0)),
            pl.BlockSpec((TQ, 384), lambda i: (i, 0)),
            pl.BlockSpec(memory_space=pl.ANY),
            pl.BlockSpec(memory_space=pl.ANY),
        ],
        out_specs=[
            pl.BlockSpec((TQ, 384), lambda i: (i, 0)),
            pl.BlockSpec((keys, 256), lambda i: (0, 0)),
            pl.BlockSpec(memory_space=pl.ANY),
            pl.BlockSpec(memory_space=pl.ANY),
        ],
        out_shape=[
            jax.ShapeDtypeStruct((rows, 384), BF),
            jax.ShapeDtypeStruct((keys, 256), BF),
            jax.ShapeDtypeStruct(send_rows.shape, BF),
            jax.ShapeDtypeStruct(send_down.shape, BF),
        ],
        scratch_shapes=[
            pltpu.VMEM((5, 128, TQ), F32),
            pltpu.VMEM((keys, 256), F32),
            pltpu.VMEM(send_rows.shape[1:], BF),
            pltpu.VMEM(send_down.shape, BF),
            pltpu.SemaphoreType.DMA((len(peers) + 1,)),
            pltpu.SemaphoreType.DMA((len(peers) + 1,)),
            pltpu.SemaphoreType.DMA((2,)),
        ],
        compiler_params=pltpu.CompilerParams(
            collective_id=11, has_side_effects=True, vmem_limit_bytes=VMEM_LIMIT
        ),
    )(q, kv, q_pos, q_seg, k_pos, k_seg, lse, out, out_grad, send_rows, send_down)


class Wires:
    def __init__(self, send, recv):
        self.send, self.recv, self.used = send, recv, 0

    def copy(self, source, target, where):
        at = self.used
        self.used += 1
        return pltpu.make_async_remote_copy(
            source,
            target,
            self.send.at[at],
            self.recv.at[at],
            device_id=where,
            device_id_type=MESH,
        )

    def start(self, source, target, where):
        copy = self.copy(source, target, where)
        copy.start()
        return copy


def greet(places):
    barrier = pltpu.get_barrier_semaphore()
    for where in places:
        pl.semaphore_signal(barrier, 1, device_id=where, device_id_type=MESH)
    pl.semaphore_wait(barrier, len(places))


def square():
    w = lax.axis_index("wsh")
    return w, w + 1 - 2 * lax.rem(w, 2), w + 2 - 4 * (w // 2), 3 - w


class SquareScatter:
    def __init__(self, wires, parts, near, total):
        self.wires, self.parts, self.near, self.total = wires, parts, near, total
        self.half = parts.shape[1] // 2
        self.a, self.b = pl.ds(0, self.half), pl.ds(self.half, self.half)
        self.own, self.x, self.y, self.z = square()
        self.pending = []

    def send_diagonal(self):
        wires, parts = self.wires, self.parts
        self.one = wires.start(parts.at[self.z, self.a], self.near.at[0], {"wsh": self.x})
        self.two = wires.start(parts.at[self.z, self.b], self.near.at[1], {"wsh": self.y})

    def send_x(self):
        self.pending.append(
            self.wires.start(
                self.parts.at[self.x, self.a], self.total.at[0, self.a], {"wsh": self.x}
            )
        )

    def send_y(self):
        self.pending.append(
            self.wires.start(
                self.parts.at[self.y, self.b], self.total.at[1, self.b], {"wsh": self.y}
            )
        )

    def relay(self):
        near, parts = self.near, self.parts
        self.one.wait()
        near[2] = (near[0].astype(F32) + parts[self.y, self.a].astype(F32)).astype(BF)
        self.pending.append(
            self.wires.start(near.at[2], self.total.at[1, self.a], {"wsh": self.y})
        )
        self.two.wait()
        near[3] = (near[1].astype(F32) + parts[self.x, self.b].astype(F32)).astype(BF)
        self.pending.append(
            self.wires.start(near.at[3], self.total.at[0, self.b], {"wsh": self.x})
        )

    def result(self):
        for copy in self.pending:
            copy.wait()
        return (
            self.parts[self.own].astype(F32)
            + self.total[0].astype(F32)
            + self.total[1].astype(F32)
        )


def square_scratch(rows):
    return [pltpu.VMEM((4, rows // 2, D), BF), pltpu.VMEM((2, rows, D), BF)]


class SquareGather:
    def __init__(self, wires, out):
        self.wires, self.out = wires, out
        half = out.shape[1] // 2
        self.a, self.b = pl.ds(0, half), pl.ds(half, half)
        self.own, self.x, self.y, self.z = square()

    def move(self, slot, part, to):
        return self.wires.start(self.out.at[slot, part], self.out.at[slot, part], {"wsh": to})

    def begin(self):
        self.xa = self.move(self.own, self.a, self.x)
        self.yb = self.move(self.own, self.b, self.y)
        self.xb = self.move(self.own, self.b, self.x)
        self.ya = self.move(self.own, self.a, self.y)

    def relay(self):
        self.xa.wait()
        self.one = self.move(self.x, self.a, self.y)
        self.yb.wait()
        self.two = self.move(self.y, self.b, self.x)

    def wait_x(self):
        self.xb.wait()

    def wait_y(self):
        self.ya.wait()

    def wait_z(self):
        self.one.wait()
        self.two.wait()


def feed(link, attended, w_out, tokens, gain, w_half, down, dy):
    ctx, wsh = link.sizes["ctx"], link.sizes["wsh"]
    own_rows = tokens.shape[0]
    plane = dy.shape[0]
    units = down.shape[0]
    chunk = D // ctx
    pick = units // ctx // 2

    def kernel(
        at_ref, wo_ref, x_ref, g_ref, wh_ref, dw_ref, dy_ref,
        mid_ref, mg_ref, br_ref, ag_ref, fs_ref, dp_ref, gs_ref, ds_ref,
        w_both, parts, near, total, near2, total2, n2, hgrad, hidden, gate_g, up_g,
        down_h, down_pair, down_send, down_got, gate_h, gate_pair, send, recv, local,
    ):
        wires = Wires(send, recv)
        core = lax.axis_index("grp")
        sibling = {"grp": 1 - core}
        my_c = lax.axis_index("ctx")
        own, x, y, z = square()
        levels = [link.place(("ctx",), offset) for offset in link.offsets(("ctx",))[1:]]
        greet([{"wsh": x}, {"wsh": y}, sibling] + [where for where, _ in levels])

        def rows_of(slot):
            return pl.ds(pl.multiple_of(slot * own_rows, 16), own_rows)

        w_copy = pltpu.make_async_copy(wh_ref, w_both.at[core], local)
        w_copy.start()

        first = SquareScatter(wires, parts, near, total)
        for slot in (z, x, y, own):
            parts[slot] = jnp.dot(
                at_ref[rows_of(slot), :], wo_ref[...], preferred_element_type=F32
            ).astype(BF)
            if slot is z:
                first.send_diagonal()
            elif slot is x:
                first.send_x()
            elif slot is y:
                first.send_y()
        w_swap = wires.start(wh_ref, w_both.at[core], sibling)
        hgrad[...] = dot_general(dy_ref[...], dw_ref[...], 1, 1)
        first.relay()
        middle = x_ref[...].astype(F32) + first.result()
        mid_ref[...] = middle
        factor = lax.rsqrt(jnp.mean(middle * middle, axis=-1, keepdims=True) + EPSILON)
        n2[own] = (middle * factor * g_ref[...]).astype(BF)
        gather = SquareGather(wires, n2)
        gather.begin()
        w_copy.wait()
        w_swap.wait()

        def block(slot):
            at = rows_of(slot)
            gate = jnp.dot(n2[slot], w_both[0], preferred_element_type=F32)
            up = jnp.dot(n2[slot], w_both[1], preferred_element_type=F32)
            sigmoid = 1.0 / (1.0 + jnp.exp(-gate))
            silu = gate * sigmoid
            hidden[at, :] = (silu * up).astype(BF)
            back = hgrad[at, :]
            gate_g[at, :] = (back * up * sigmoid * (1.0 + gate * (1.0 - sigmoid))).astype(BF)
            up_g[at, :] = (back * silu).astype(BF)
            parts[slot] = (
                dot_general(gate_g[at, :], w_both[0], 1, 1)
                + dot_general(up_g[at, :], w_both[1], 1, 1)
            ).astype(BF)

        second = SquareScatter(wires, parts, near2, total2)
        block(own)
        gather.relay()
        gather.wait_x()
        block(x)
        second.send_x()
        gather.wait_y()
        block(y)
        second.send_y()
        gather.wait_z()
        block(z)
        second.send_diagonal()

        strip = dot_general(hidden[...], dy_ref[...], 0, 0).astype(BF)
        for k in range(ctx):
            for g in range(2):
                top = (2 * k + g) * pick
                down_h[g, k] = strip[top : top + pick, :]
        down_swap = wires.start(down_h.at[1 - core], down_pair, sibling)
        second.relay()
        tokens_all = n2[...].reshape(plane, D)
        for g, source in enumerate((gate_g, up_g)):
            strip = dot_general(tokens_all, source[...], 0, 0).astype(BF)
            for c in range(ctx):
                gate_h[g, c] = strip[c * chunk : c * chunk + chunk, :]
        gate_swap = wires.start(gate_h.at[1 - core], gate_pair, sibling)
        down_swap.wait()
        down_send[...] = (down_h[core].astype(F32) + down_pair[...].astype(F32)).astype(BF)
        down_copies = []
        for where, index in levels:
            down_copies.append(wires.start(down_send.at[index], down_got.at[my_c], where))
        down_got[my_c] = down_send[my_c]

        grad = second.result()
        middle = mid_ref[...]
        factor = lax.rsqrt(jnp.mean(middle * middle, axis=-1, keepdims=True) + EPSILON)
        weighted = grad * g_ref[...]
        inner = jnp.mean(weighted * middle, axis=-1, keepdims=True)
        middle_grad = (
            dy_ref[rows_of(own), :].astype(F32)
            + factor * weighted
            - middle * (factor * factor * factor) * inner
        )
        mg_ref[...] = middle_grad
        br_ref[own] = middle_grad.astype(BF)
        branch = SquareGather(wires, br_ref)
        branch.begin()
        fs_ref[...] = jnp.sum(grad * middle * factor, axis=0, keepdims=True)

        def outward(slot):
            ag_ref[rows_of(slot), :] = dot_general(br_ref[slot], wo_ref[...], 1, 1).astype(BF)

        outward(own)
        gate_swap.wait()
        for c in range(ctx):
            gs_ref[c] = (gate_h[core, c].astype(F32) + gate_pair[c].astype(F32)).astype(BF)
        branch.relay()
        for slot in range(wsh):
            at = slice(slot * own_rows, slot * own_rows + own_rows)
            dp_ref[slot] = jnp.dot(
                hidden[at, :], dw_ref[...], preferred_element_type=F32
            ).astype(BF)
        branch.wait_x()
        outward(x)
        branch.wait_y()
        outward(y)
        branch.wait_z()
        outward(z)
        for copy in down_copies:
            copy.wait()
        ds_ref[...] = jnp.sum(down_got[...].astype(F32), axis=0).astype(BF)

    operands = (attended, w_out, tokens, gain, w_half, down, dy)
    vmem = pl.BlockSpec(memory_space=pltpu.VMEM)
    return pl.pallas_call(
        kernel,
        name="feed",
        in_specs=[vmem] * len(operands),
        out_specs=[vmem] * 8,
        out_shape=[
            jax.ShapeDtypeStruct((own_rows, D), F32),
            jax.ShapeDtypeStruct((own_rows, D), F32),
            jax.ShapeDtypeStruct((wsh, own_rows, D), BF),
            jax.ShapeDtypeStruct((plane, 384), BF),
            jax.ShapeDtypeStruct((1, D), F32),
            jax.ShapeDtypeStruct((wsh, own_rows, D), BF),
            jax.ShapeDtypeStruct((ctx, chunk, units), BF),
            jax.ShapeDtypeStruct((pick, D), BF),
        ],
        scratch_shapes=[
            pltpu.VMEM((2, D, units), BF),
            pltpu.VMEM((4, own_rows, D), BF),
            *square_scratch(own_rows),
            *square_scratch(own_rows),
            pltpu.VMEM((4, own_rows, D), BF),
            pltpu.VMEM((plane, units), F32),
            *[pltpu.VMEM((plane, units), BF)] * 3,
            pltpu.VMEM((2, ctx, pick, D), BF),
            *[pltpu.VMEM((ctx, pick, D), BF)] * 3,
            pltpu.VMEM((2, ctx, chunk, units), BF),
            pltpu.VMEM((ctx, chunk, units), BF),
            pltpu.SemaphoreType.DMA((ctx + 28,)),
            pltpu.SemaphoreType.DMA((ctx + 28,)),
            pltpu.SemaphoreType.DMA,
        ],
        compiler_params=pltpu.CompilerParams(
            collective_id=3, has_side_effects=True, vmem_limit_bytes=VMEM_LIMIT
        ),
    )(*operands)


def head(link, tokens, gain, weight, marks, upstream):
    ctx, wsh = link.sizes["ctx"], link.sizes["wsh"]
    own_rows = tokens.shape[0]
    plane, group = own_rows * wsh, own_rows * wsh * ctx
    half = weight.shape[0] // 2

    def kernel(
        x_ref, g_ref, w_ref, m_ref, up_ref,
        q_ref, kv_ref, n_ref, wq_ref, kpos_ref, kseg_ref, q_marks, dy_ref, c_ref, s_ref,
        cols, marks_all, send, recv,
    ):
        wires = Wires(send, recv)
        core = lax.axis_index("grp")
        sibling = {"grp": 1 - core}
        my_c = lax.axis_index("ctx")
        own, x, y, z = square()
        levels = [link.place(("ctx",), offset) for offset in link.offsets(("ctx",))[1:]]
        greet(
            [{"wsh": x}, {"wsh": y}, {"wsh": z}, sibling] + [where for where, _ in levels]
        )
        mark_copies = []
        for p in (x, y, z):
            mark_copies.append(
                wires.start(m_ref, marks_all.at[my_c, own], {"wsh": p})
            )
        marks_all[my_c, own] = m_ref[...]
        side = pl.ds(pl.multiple_of(core * half, 16), half)

        for w in range(wsh):
            q_order, kv_order = head_plan(w)
            slots = [h for h in q_order] + [HEADS + h for h in kv_order]
            slots += [HEADS + KV_HEADS + h for h in kv_order]
            blank = jnp.zeros((w_ref.shape[0], HEAD_DIM), BF)
            for pair in range(5):
                two = [
                    blank if h is None else w_ref[:, h * HEAD_DIM : h * HEAD_DIM + HEAD_DIM]
                    for h in slots[2 * pair : 2 * pair + 2]
                ]
                cols[w, :, 128 * pair : 128 * pair + 128] = jnp.concatenate(two, axis=1)
        w_copies = []
        for p in (x, y, z):
            w_copies.append(
                wires.start(cols.at[p, side], wq_ref.at[own, side], {"wsh": p})
            )
        tokens_in = x_ref[...].astype(F32)
        factor = lax.rsqrt(jnp.mean(tokens_in * tokens_in, axis=-1, keepdims=True) + EPSILON)
        n_ref[own] = (tokens_in * factor * g_ref[...]).astype(BF)
        gather = SquareGather(wires, n_ref)
        gather.begin()
        wq_ref[own] = cols[own]
        dy_ref[own] = up_ref[...]

        for copy in mark_copies:
            copy.wait()
        level_copies = []
        for where, _ in levels:
            level_copies.append(wires.start(marks_all.at[my_c], marks_all.at[my_c], where))
        lane = lax.broadcasted_iota(jnp.int32, (1, 128), 1)
        power = lax.rem(lane, 32).astype(F32) * (-math.log(10000.0) / 32)
        frequency = jnp.exp(power)
        sign = jnp.where(lax.rem(lane, 64) < 32, -1.0, 1.0)

        def upright(row):
            return jnp.broadcast_to(row, (128, row.shape[1])).T

        for w in range(wsh):
            at = slice(w * own_rows, w * own_rows + own_rows)
            angles = upright(marks_all[my_c, w, 0:1, :])[:own_rows] * frequency
            c_ref[at, :] = jnp.cos(angles)
            s_ref[at, :] = jnp.sin(angles) * sign
        gather.relay()
        forward = []
        for p, copy in zip((x, y, z), w_copies):
            copy.wait()
            forward.append(wires.start(wq_ref.at[p, side], wq_ref.at[p, side], sibling))
        dy_gather = SquareGather(wires, dy_ref)
        dy_gather.begin()
        for copy in forward:
            copy.wait()

        low = lax.rem(lax.broadcasted_iota(jnp.int32, (own_rows, 128), 1), 64) < 32
        kv_copies = []

        def block(slot):
            at = pl.ds(pl.multiple_of(slot * own_rows, 16), own_rows)
            full = jnp.dot(
                n_ref[slot], wq_ref[...].reshape(D, 640), preferred_element_type=F32
            )
            cos_t, sin_t = c_ref[at, :], s_ref[at, :]
            for b in range(3):
                turned = turn(full[:, 128 * b : 128 * b + 128], cos_t, sin_t, low)
                q_ref[at, 128 * b : 128 * b + 128] = (
                    turned.astype(BF).astype(F32) * 0.125
                ).astype(BF)
            kv_ref[my_c, at, :128] = turn(full[:, 384:512], cos_t, sin_t, low).astype(BF)
            kv_ref[my_c, at, 128:] = full[:, 512:].astype(BF)
            for where, _ in levels:
                kv_copies.append(
                    wires.start(kv_ref.at[my_c, at], kv_ref.at[my_c, at], where)
                )

        block(own)
        gather.wait_x()
        block(x)
        gather.wait_y()
        block(y)
        gather.wait_z()
        block(z)
        dy_gather.relay()

        for copy in level_copies:
            copy.wait()
        for w in range(wsh):
            q_marks[:, w * own_rows : w * own_rows + own_rows] = marks_all[my_c, w, :, :own_rows]

        @pl.loop(0, ctx)
        def _(c):
            for w in range(wsh):
                at = pl.ds(pl.multiple_of(c * plane + w * own_rows, 16), own_rows)
                kpos_ref[at, :] = upright(marks_all[c, w, 0:1, :])[:own_rows]
                kseg_ref[at, :] = upright(marks_all[c, w, 1:2, :])[:own_rows]

        dy_gather.wait_x()
        dy_gather.wait_y()
        dy_gather.wait_z()
        for copy in kv_copies:
            copy.wait()

    operands = (tokens, gain, weight, marks, upstream)
    vmem = pl.BlockSpec(memory_space=pltpu.VMEM)
    return pl.pallas_call(
        kernel,
        name="head",
        in_specs=[vmem] * len(operands),
        out_specs=[vmem] * 10,
        out_shape=[
            jax.ShapeDtypeStruct((plane, 384), BF),
            jax.ShapeDtypeStruct((ctx, plane, 256), BF),
            jax.ShapeDtypeStruct((wsh, own_rows, D), BF),
            jax.ShapeDtypeStruct((wsh, 2 * half, 640), BF),
            jax.ShapeDtypeStruct((group, 128), F32),
            jax.ShapeDtypeStruct((group, 128), F32),
            jax.ShapeDtypeStruct((8, plane), F32),
            jax.ShapeDtypeStruct((wsh, own_rows, D), BF),
            jax.ShapeDtypeStruct((plane, 128), F32),
            jax.ShapeDtypeStruct((plane, 128), F32),
        ],
        scratch_shapes=[
            pltpu.VMEM((wsh, 2 * half, 640), BF),
            pltpu.VMEM((ctx, wsh, 8, 256), F32),
            pltpu.SemaphoreType.DMA((5 * ctx + 24,)),
            pltpu.SemaphoreType.DMA((5 * ctx + 24,)),
        ],
        compiler_params=pltpu.CompilerParams(
            collective_id=1, has_side_effects=True, vmem_limit_bytes=VMEM_LIMIT
        ),
    )(*operands)


def finish(
    link, q_grad, kv_grad, weight, cos, sin, normed, tokens, gain, middle_grad, gate_got, down_got,
    attended, branch, feed_sum, down_part, middle,
):
    ctx, wsh = link.sizes["ctx"], link.sizes["wsh"]
    shards = ctx * wsh
    rows = D // shards
    chunk = D // ctx
    fold = ctx // wsh
    own_rows = tokens.shape[0]
    plane = normed.shape[0]
    axes = ("ctx", "wsh")
    peers = link.offsets(axes)
    gate_width = gate_got.shape[2]
    down_rows = down_got.shape[0]

    def kernel(
        q_ref, kv_send, w_ref, c_ref, s_ref, n_ref, x_ref, g_ref, mg_ref, gate_ref, down_ref,
        at_ref, br_ref, fs_ref, dp_ref, mid_ref,
        act_ref, ig_ref, qkv_ref, out_ref, gate_out, down_out, gains_out,
        kv_ref, pg, parts, near, total, near2, total2, acc, wide, q_own, q_pair, q_send, q_got,
        q_mid, q_fin, kv_own, kv_pair, kv_go, kv_got, kv_mid, kv_fin, gate_mid, gate_fin, down_fin, out_halves,
        out_pair, out_send, out_mid, out_got, out_fin, gains, gains_got, gains_fin,
        send, recv,
    ):
        wires = Wires(send, recv)
        core = lax.axis_index("grp")
        first, second = core == 0, core == 1
        sibling = {"grp": 1 - core}
        my_c, my_w = lax.axis_index("ctx"), lax.axis_index("wsh")
        odd = lax.rem(my_w, 2) == 1
        greet([link.place(axes, offset)[0] for offset in peers[1:]] + [sibling])
        _, me = link.place(axes, peers[0])

        def over_ctx(got, mid):
            for w in range(wsh):
                strip = got[0, w * rows : w * rows + rows, :].astype(F32)
                for c in range(1, ctx):
                    strip += got[c, w * rows : w * rows + rows, :].astype(F32)
                mid[w] = strip.astype(BF)

        def in_plane(mid, slot_of):
            copies = []
            for offset in link.offsets(("wsh",))[1:]:
                where, index = link.place(("wsh",), offset)
                copies.append(wires.copy(mid.at[index], slot_of(my_w), where))
            return copies

        def begin(cond, *copies):
            @pl.when(cond)
            def _():
                for copy in copies:
                    copy.start()

        kv_copies = []
        for offset in link.offsets(("ctx",))[1:]:
            where, index = link.place(("ctx",), offset)
            kv_copies.append(wires.start(kv_send.at[index], kv_ref.at[my_c], where))
        layer = SquareScatter(wires, dp_ref, near2, total2)
        layer.send_diagonal()
        layer.send_x()
        layer.send_y()
        kv_ref[my_c] = kv_send[my_c]

        wide[...] = dot_general(at_ref[...], br_ref[...], 0, 0)

        def out_strips(pieces):
            at = 0
            for start, size in pieces:
                acc_rows = wide[start : start + size, :].astype(BF)
                part = jnp.concatenate([acc_rows[:, :576], jnp.zeros((size, 64), BF)], axis=1)
                out_halves[0, at : at + size, :] = part
                part = jnp.concatenate([acc_rows[:, 576:], jnp.zeros((size, 64), BF)], axis=1)
                out_halves[1, at : at + size, :] = part
                at += size

        @pl.when(odd)
        def _():
            out_strips([(96, 32), (192, 64), (0, 64), (128, 64), (256, 64)])

        @pl.when(jnp.logical_not(odd))
        def _():
            out_strips([(0, 64), (128, 64), (256, 64), (64, 64), (192, 32)])

        out_swap = wires.start(out_halves.at[1 - core], out_pair, sibling)
        low = lax.rem(lax.broadcasted_iota(jnp.int32, (own_rows, 128), 1), 64) < 32

        @pl.loop(0, wsh)
        def _(slot):
            at = pl.ds(pl.multiple_of(slot * own_rows, 16), own_rows)
            for b in range(3):
                block = q_ref[at, 128 * b : 128 * b + 128].astype(F32)
                pg[at, 128 * b : 128 * b + 128] = turn(
                    block, c_ref[at, :], -s_ref[at, :], low
                ).astype(BF)

        layer.relay()
        for b in range(3):
            acc[384 * b : 384 * b + 384, :] = dot_general(
                n_ref[:, 384 * b : 384 * b + 384], pg[:, :384], 0, 0
            )

        for c in range(ctx):
            q_own[c] = acc[c * chunk : c * chunk + chunk, :].astype(BF)
        q_swap = wires.copy(q_own, q_pair, sibling)
        begin(second, q_swap)

        down_fin[core] = down_ref[...]
        down_copy = wires.start(down_fin.at[core], down_fin.at[core], sibling)

        over_ctx(gate_ref, gate_mid)
        gate_moves = in_plane(gate_mid, lambda w: gate_fin.at[core, w])
        for copy in gate_moves:
            copy.start()
        gate_fin[core, my_w] = gate_mid[my_w]
        act_ref[...] = (mid_ref[...] + layer.result()).astype(BF)
        out_swap.wait()
        for k in range(ctx):
            strip = slice(k * rows, k * rows + rows)
            out_send[k % wsh, k // wsh] = (
                out_halves[core, strip, :].astype(F32) + out_pair[strip, :].astype(F32)
            ).astype(BF)
        out_moves = in_plane(out_send, lambda w: out_mid.at[w])
        for copy in out_moves:
            copy.start()
        out_mid[my_w] = out_send[my_w]

        @pl.when(first)
        def _():
            q_swap.wait_recv()

            @pl.loop(0, ctx)
            def _(c):
                q_send[c] = (q_own[c].astype(F32) + q_pair[c].astype(F32)).astype(BF)

        @pl.when(second)
        def _():
            q_swap.wait_send()

        for copy in gate_moves:
            copy.wait()
        gate_copy = wires.start(gate_fin.at[core], gate_fin.at[core], sibling)
        down_copy.wait()
        down_out[:down_rows, :] = down_fin[0].astype(F32)
        down_out[down_rows:, :] = down_fin[1].astype(F32)
        gate_copy.wait()
        for half in range(2):
            for w in range(wsh):
                left = (half * wsh + w) * gate_width
                gate_out[:, left : left + gate_width] = gate_fin[half, w].astype(F32)

        for copy in out_moves:
            copy.wait()

        for copy in kv_copies:
            copy.wait()
        q_copies, kvg_copies, out_copies = [], [], []
        for offset in link.offsets(("ctx",))[1:]:
            where, index = link.place(("ctx",), offset)
            q_copies.append(wires.copy(q_send.at[index], q_got.at[my_c], where))
            kvg_copies.append(wires.copy(kv_go.at[index], kv_got.at[my_c], where))
        begin(first, *q_copies)
        for offset in link.offsets(("ctx",))[1:]:
            where, index = link.place(("ctx",), offset)
            part = out_mid.at[index // fold, lax.rem(index, fold)]
            out_copies.append(wires.start(part, out_got.at[my_c], where))
        out_got[my_c] = out_mid[my_c // fold, lax.rem(my_c, fold)]
        scatter = SquareScatter(wires, parts, near, total)
        gain_sum = jnp.zeros((1, D), F32)
        for slot in (scatter.z, scatter.x, scatter.y, scatter.own):
            at = pl.ds(pl.multiple_of(slot * own_rows, 16), own_rows)
            summed = kv_ref[0, at, :].astype(F32)
            for c in range(1, ctx):
                summed += kv_ref[c, at, :].astype(F32)
            block = summed[:, :128].astype(BF).astype(F32)
            pg[at, 384:512] = turn(block, c_ref[at, :], -s_ref[at, :], low).astype(BF)
            pg[at, 512:] = summed[:, 128:].astype(BF)
            part = dot_general(pg[at, :], w_ref[...], 1, 1)
            parts[slot] = part.astype(BF)
            gain_sum += jnp.sum(part * n_ref[at, :].astype(F32), axis=0, keepdims=True)
            if slot is scatter.z:
                scatter.send_diagonal()
            elif slot is scatter.x:
                scatter.send_x()
            elif slot is scatter.y:
                scatter.send_y()

        for b in range(3):
            acc[384 * b : 384 * b + 384, :256] = dot_general(
                n_ref[:, 384 * b : 384 * b + 384], pg[:, 384:], 0, 0
            )

        for c in range(ctx):
            kv_own[c] = acc[c * chunk : c * chunk + chunk, :256].astype(BF)
        kv_swap = wires.copy(kv_own, kv_pair, sibling)
        begin(first, kv_swap)
        both = jnp.concatenate([gain_sum / g_ref[...], fs_ref[...]], axis=0)
        gains[...] = jnp.zeros_like(gains)
        for s in range(shards):
            gains[s, :2, :rows] = both[:, rows * s : rows * s + rows]
        gain_copies = []
        for offset in peers[1:]:
            where, index = link.place(axes, offset)
            gain_copies.append(wires.start(gains.at[index], gains_got.at[me], where))
        gains_got[me] = gains[me]
        scatter.relay()

        @pl.when(second)
        def _():
            kv_swap.wait_recv()

            @pl.loop(0, ctx)
            def _(c):
                kv_go[c] = (kv_own[c].astype(F32) + kv_pair[c].astype(F32)).astype(BF)

            for copy in kvg_copies:
                copy.start()
            kv_got[my_c] = kv_go[my_c]

        @pl.when(first)
        def _():
            kv_swap.wait_send()
            q_got[my_c] = q_send[my_c]
            for copy in q_copies:
                copy.wait()
            over_ctx(q_got, q_mid)

        q_moves = in_plane(q_mid, lambda w: q_fin.at[w])
        begin(first, *q_moves)
        for copy in out_copies:
            copy.wait()
        out_fin[core] = jnp.sum(out_got[...].astype(F32), axis=0).astype(BF)

        out_copy = wires.start(out_fin.at[core], out_fin.at[core], sibling)

        grad = scatter.result()
        x = x_ref[...].astype(F32)
        factor = lax.rsqrt(jnp.mean(x * x, axis=-1, keepdims=True) + EPSILON)
        weighted = grad * g_ref[...]
        inner = jnp.mean(weighted * x, axis=-1, keepdims=True)
        ig_ref[...] = mg_ref[...] + factor * weighted - x * (factor * factor * factor) * inner
        q_final = wires.copy(q_fin, q_fin, sibling)
        kv_final = wires.copy(kv_fin, kv_fin, sibling)

        kv_moves = in_plane(kv_mid, lambda w: kv_fin.at[w])

        @pl.when(first)
        def _():
            for copy in q_moves:
                copy.wait()
            q_fin[my_w] = q_mid[my_w]
            q_final.start()

        @pl.when(second)
        def _():
            for copy in kvg_copies:
                copy.wait()
            over_ctx(kv_got, kv_mid)
            for copy in kv_moves:
                copy.start()
            for copy in kv_moves:
                copy.wait()
            kv_fin[my_w] = kv_mid[my_w]
            kv_final.start()

        for copy in gain_copies:
            copy.wait()
        gains_fin[core] = jnp.sum(gains_got[...], axis=0)
        gain_copy = wires.start(gains_fin.at[core], gains_fin.at[core], sibling)
        out_copy.wait()
        out_ref[...] = jnp.concatenate(
            [out_fin[0, :, :576].astype(F32), out_fin[1, :, :576].astype(F32)], axis=1
        )

        @pl.when(first)
        def _():
            q_final.wait_send()
            kv_final.wait_recv()

        @pl.when(second)
        def _():
            kv_final.wait_send()
            q_final.wait_recv()

        qkv_ref[...] = qkv_restore(
            [
                jnp.concatenate([q_fin[w].astype(F32), kv_fin[w].astype(F32)], axis=1)
                for w in range(wsh)
            ]
        )
        gain_copy.wait()
        gains_out[...] = gains_fin[0] + gains_fin[1]

    operands = (
        q_grad, kv_grad, weight, cos, sin, normed, tokens, gain, middle_grad, gate_got, down_got,
        attended, branch, feed_sum, down_part, middle,
    )
    vmem = pl.BlockSpec(memory_space=pltpu.VMEM)
    return pl.pallas_call(
        kernel,
        name="finish",
        in_specs=[vmem] * len(operands),
        out_specs=[vmem] * 7,
        out_shape=[
            jax.ShapeDtypeStruct((own_rows, D), BF),
            jax.ShapeDtypeStruct((own_rows, D), F32),
            jax.ShapeDtypeStruct((rows, QW + 2 * KW), F32),
            jax.ShapeDtypeStruct((rows, D), F32),
            jax.ShapeDtypeStruct((rows, 2 * FF), F32),
            jax.ShapeDtypeStruct((2 * down_rows, D), F32),
            jax.ShapeDtypeStruct((8, 128), F32),
        ],
        scratch_shapes=[
            pltpu.VMEM((ctx, plane, 256), BF),
            pltpu.VMEM((plane, 640), BF),
            pltpu.VMEM((4, own_rows, D), BF),
            *square_scratch(own_rows),
            *square_scratch(own_rows),
            pltpu.VMEM((D, 384), F32),
            pltpu.VMEM((384, D), F32),
            *[pltpu.VMEM((ctx, chunk, 384), BF)] * 4,
            *[pltpu.VMEM((wsh, rows, 384), BF)] * 2,
            *[pltpu.VMEM((ctx, chunk, 256), BF)] * 4,
            *[pltpu.VMEM((wsh, rows, 256), BF)] * 2,
            pltpu.VMEM((wsh, rows, gate_width), BF),
            pltpu.VMEM((2, wsh, rows, gate_width), BF),
            pltpu.VMEM((2, down_rows, D), BF),
            pltpu.VMEM((2, 288, 640), BF),
            pltpu.VMEM((288, 640), BF),
            pltpu.VMEM((wsh, fold, rows, 640), BF),
            pltpu.VMEM((wsh, fold, rows, 640), BF),
            pltpu.VMEM((ctx, rows, 640), BF),
            pltpu.VMEM((2, rows, 640), BF),
            pltpu.VMEM((shards, 8, 128), F32),
            pltpu.VMEM((shards, 8, 128), F32),
            pltpu.VMEM((2, 8, 128), F32),
            pltpu.SemaphoreType.DMA((3 * shards + 2 * ctx + 32,)),
            pltpu.SemaphoreType.DMA((3 * shards + 2 * ctx + 32,)),
        ],
        compiler_params=pltpu.CompilerParams(
            collective_id=8, has_side_effects=True, vmem_limit_bytes=VMEM_LIMIT
        ),
    )(*operands)


def build(sizes):
    ctx, wsh = sizes["ctx"], sizes["wsh"]
    shards = ctx * wsh
    link = Exchange(sizes)

    def local(
        tokens,
        segment_ids,
        positions,
        attend_gain,
        query_key_value,
        attend_out,
        feed_gain,
        gate_up,
        down_weight,
        upstream,
    ):
        own = tokens.shape[0]
        plane = own * wsh
        group = plane * ctx
        odd = lax.rem(lax.axis_index("wsh"), 2) == 1
        marks = jnp.pad(
            jnp.stack([positions, segment_ids]).astype(F32), ((0, 6), (0, 256 - own))
        )
        (
            queries,
            kv_all,
            normed_all,
            w_qkv,
            k_pos,
            k_seg,
            q_marks,
            dy_all,
            cos,
            sin,
        ) = head(link, tokens, attend_gain[None, :], query_key_value, marks, upstream)
        kv_all = kv_all.reshape(group, 256)
        normed_all, dy_all = normed_all.reshape(plane, D), dy_all.reshape(plane, D)
        w_qkv = w_qkv.reshape(D, 640)
        q_pos, q_seg = q_marks[0:1], q_marks[1:2]
        attended, attended_wide, lse, w_half = attend_forward(
            link, queries, kv_all, q_pos, q_seg, k_pos, k_seg, gate_up
        )
        w_half = w_half.reshape(D, FF // wsh)
        w_out = spread_rows(attend_out, odd)
        (
            middle,
            middle_grad,
            branch_all,
            attended_grad,
            feed_sum,
            down_part,
            gate_send,
            down_sum,
        ) = feed(link, attended, w_out, tokens, feed_gain[None, :], w_half, down_weight, dy_all)
        q_grad, kv_grad, gate_got, down_got = attend_backward(
            link, queries, kv_all, q_pos, q_seg, k_pos, k_seg, lse, attended_wide, attended_grad,
            gate_send, down_sum,
        )
        (activations, input_grad, qkv_out, out_out, gate_out, down_out, gain_out) = finish(
            link, q_grad, kv_grad.reshape(ctx, plane, 256), w_qkv, cos, sin, normed_all, tokens,
            attend_gain[None, :], middle_grad, gate_got, down_got, attended,
            branch_all.reshape(plane, D), feed_sum, down_part, middle,
        )
        width = D // shards
        return (
            activations,
            input_grad,
            qkv_out,
            out_out,
            gate_out,
            down_out,
            gain_out[0, :width],
            gain_out[1, :width],
        )

    return local


def solution(mesh):
    whole = ("grp", "ctx", "wsh")
    in_specs = (
        P(whole, None),
        P(whole),
        P(whole),
        P(),
        P("wsh", None),
        P("wsh", None),
        P(),
        P("wsh", None),
        P("wsh", None),
        P(whole, None),
    )
    out_specs = (
        P(whole, None),
        P(whole, None),
        P(("ctx", "wsh"), None),
        P(("ctx", "wsh"), None),
        P(("ctx", "wsh"), None),
        P(("ctx", "wsh"), None),
        P(("ctx", "wsh")),
        P(("ctx", "wsh")),
    )
    return jax.shard_map(
        build(dict(mesh.shape)), mesh=mesh, in_specs=in_specs, out_specs=out_specs, check_vma=False
    )
```

```python
import itertools
import math

import jax
import jax.numpy as jnp
from jax import lax
from jax.experimental import pallas as pl
from jax.experimental.pallas import tpu as pltpu
from jax.sharding import PartitionSpec as P

HEADS = 18
KV_HEADS = 6
HEAD_DIM = 64
FF = 3072
D = 1152
QW = 1152
KW = 384
EPSILON = 1e-05
MESH = pl.DeviceIdType.MESH
F32 = jnp.float32
BF = jnp.bfloat16
VMEM_LIMIT = 56 << 20


def dot_general(a, b, ca, cb):
    return lax.dot_general(a, b, (((ca,), (cb,)), ((), ())), preferred_element_type=F32)


class Exchange:
    def __init__(self, sizes):
        self.sizes = sizes

    def place(self, axes, offset):
        where, index = {}, 0
        for axis, step in zip(axes, offset):
            size = self.sizes[axis]
            spot = lax.axis_index(axis)
            if step:
                spot = lax.rem(spot + step, size)
            where[axis] = spot
            index = index * size + spot
        return where, index

    def offsets(self, axes):
        return list(itertools.product(*[range(self.sizes[axis]) for axis in axes]))


def head_plan(w):
    pair, odd = w // 2, w % 2
    start = 9 * pair + 4 * odd
    if odd:
        f_heads, h_heads = [start + 2, start + 3, start + 4], [start, start + 1]
        f_kv, h_kv = 3 * pair + 2, 3 * pair + 1
    else:
        f_heads, h_heads = [start, start + 1, start + 2], [start + 3, start + 4]
        f_kv, h_kv = 3 * pair, 3 * pair + 1
    q_order = [f_heads[0], h_heads[0], f_heads[1], h_heads[1], f_heads[2], None]
    return q_order, [f_kv, h_kv]


def qkv_restore(parts):
    found = {}
    for w in range(4):
        q_order, kv_order = head_plan(w)
        slots = list(q_order) + [HEADS + h for h in kv_order]
        slots += [HEADS + KV_HEADS + h for h in kv_order]
        for at, head in enumerate(slots):
            if head is not None:
                found.setdefault(head, []).append(
                    parts[w][:, at * HEAD_DIM : (at + 1) * HEAD_DIM]
                )
    pieces = []
    for head in range(HEADS + 2 * KV_HEADS):
        term = found[head][0]
        for other in found[head][1:]:
            term = term + other
        pieces.append(term)
    return jnp.concatenate(pieces, axis=1)


def turn(x, cos, sin, lanes):
    swapped = jnp.where(lanes, pltpu.roll(x, 96, 1), pltpu.roll(x, 32, 1))
    return x * cos + swapped * sin


TQ = 256
TK = 512


def head_block(block, head):
    low = lax.broadcasted_iota(jnp.int32, block.shape, 1) < 64
    return jnp.where(low if head == 0 else jnp.logical_not(low), block, jnp.zeros_like(block))


def visible(kp_ref, ks_ref, qm_ref, start):
    key_pos = jnp.tile(kp_ref[pl.ds(start, TK), :], (1, TQ // 128))
    key_seg = jnp.tile(ks_ref[pl.ds(start, TK), :], (1, TQ // 128))
    return (key_pos <= qm_ref[0:1, :]) & ((key_seg == 0) | (key_seg == qm_ref[1:2, :]))


ODD_ROWS = [(96, 32), (192, 64), (0, 64), (128, 64), (256, 64)]
EVEN_ROWS = [(0, 64), (128, 64), (256, 64), (64, 64), (192, 32)]
HEAD_SLOTS = [(0, 0), (0, 1), (1, 0), (1, 1), (2, 0)]


def attend_forward(link, q, kv, q_marks, k_pos, k_seg, gate_up):
    rows, keys = q.shape[0], kv.shape[0]
    steps = rows // TQ
    wsh = link.sizes["wsh"]
    units = FF // wsh
    peers = link.offsets(("wsh",))

    def kernel(
        q_ref, kv_ref, qm_ref, kp_ref, ks_ref, gu_ref,
        a_ref, o_ref, lse_ref, wh_ref,
        acc, top, tot, bounce, send, recv, near,
    ):
        def columns(p):
            left = lax.axis_index("grp") * FF + p * units
            return gu_ref.at[:, pl.ds(pl.multiple_of(left, 128), units)]

        wires = Wires(send, recv)
        _, me = link.place(("wsh",), peers[0])
        copies = []
        for offset in peers[1:]:
            where, index = link.place(("wsh",), offset)
            copies.append(wires.copy(columns(index), wh_ref.at[me], where))
        inward = pltpu.make_async_copy(columns(me), bounce, near)
        outward = pltpu.make_async_copy(bounce, wh_ref.at[me], near)

        @pl.when(pl.program_id(0) == 0)
        def _():
            greet([link.place(("wsh",), offset)[0] for offset in peers[1:]])
            for copy in copies:
                copy.start()
            inward.start()
            inward.wait()
            outward.start()

        acc[...] = jnp.zeros_like(acc)
        top[...] = jnp.full_like(top, -1e30)
        tot[...] = jnp.zeros_like(tot)
        heads = [head_block(q_ref[:, 128 * b : 128 * b + 128], h) for b, h in HEAD_SLOTS]

        @pl.loop(0, keys // TK)
        def _(t):
            start = pl.multiple_of(t * TK, TK)
            k_tile = kv_ref[pl.ds(start, TK), :128]
            v_tile = kv_ref[pl.ds(start, TK), 128:]
            seen = visible(kp_ref, ks_ref, qm_ref, start)
            for j in range(5):
                scores = dot_general(k_tile, heads[j], 1, 1)
                scores = jnp.where(seen, scores, -1e30)
                old = top[j : j + 1, :]
                new = jnp.maximum(old, jnp.max(scores, axis=0, keepdims=True))
                expons = jnp.exp(scores - new)
                shrink = jnp.exp(old - new)
                tot[j : j + 1, :] = tot[j : j + 1, :] * shrink + jnp.sum(
                    expons, axis=0, keepdims=True
                )
                acc[j] = acc[j] * shrink + dot_general(v_tile, expons.astype(BF), 0, 0)
                top[j : j + 1, :] = new

        for j, (b, h) in enumerate(HEAD_SLOTS):
            out = acc[j] / tot[j : j + 1, :]
            acc[j] = out
        lse_ref[...] = top[...] + jnp.log(jnp.maximum(tot[...], 1e-37))
        low = lax.broadcasted_iota(jnp.int32, (TQ, 128), 1) < 64
        for b in range(3):
            first = acc[2 * b].T
            if b < 2:
                block = jnp.where(low, first, acc[2 * b + 1].T)
            else:
                block = jnp.where(low, first, 0.0)
            o_ref[:, 128 * b : 128 * b + 128] = block
            a_ref[:, 128 * b : 128 * b + 128] = block.astype(BF)

        @pl.when(pl.program_id(0) == steps - 1)
        def _():
            outward.wait()
            for copy in copies:
                copy.wait()

    return pl.pallas_call(
        kernel,
        name="attend_forward",
        grid=(steps,),
        in_specs=[
            pl.BlockSpec((TQ, 384), lambda i: (i, 0)),
            pl.BlockSpec((keys, 256), lambda i: (0, 0)),
            pl.BlockSpec((8, TQ), lambda i: (0, i)),
            pl.BlockSpec((keys, 128), lambda i: (0, 0)),
            pl.BlockSpec((keys, 128), lambda i: (0, 0)),
            pl.BlockSpec(memory_space=pl.ANY),
        ],
        out_specs=[
            pl.BlockSpec((TQ, 384), lambda i: (i, 0)),
            pl.BlockSpec((TQ, 384), lambda i: (i, 0)),
            pl.BlockSpec((8, TQ), lambda i: (0, i)),
            pl.BlockSpec(memory_space=pl.ANY),
        ],
        out_shape=[
            jax.ShapeDtypeStruct((rows, 384), BF),
            jax.ShapeDtypeStruct((rows, 384), F32),
            jax.ShapeDtypeStruct((8, rows), F32),
            jax.ShapeDtypeStruct((wsh, gate_up.shape[0], units), BF),
        ],
        scratch_shapes=[
            pltpu.VMEM((5, 128, TQ), F32),
            pltpu.VMEM((8, TQ), F32),
            pltpu.VMEM((8, TQ), F32),
            pltpu.VMEM((gate_up.shape[0], units), BF),
            pltpu.SemaphoreType.DMA((wsh,)),
            pltpu.SemaphoreType.DMA((wsh,)),
            pltpu.SemaphoreType.DMA,
        ],
        compiler_params=pltpu.CompilerParams(
            collective_id=2, has_side_effects=True, vmem_limit_bytes=VMEM_LIMIT
        ),
    )(q, kv, q_marks, k_pos, k_seg, gate_up)


def owner_of(link):
    ctx, wsh = link.sizes["ctx"], link.sizes["wsh"]
    my_c, my_w = lax.axis_index("ctx"), lax.axis_index("wsh")
    shard = my_w * ctx + my_c
    to_c, to_w = shard // wsh, lax.rem(shard, wsh)
    return {"ctx": to_c, "wsh": to_w}, jnp.logical_and(to_c == my_c, to_w == my_w)


BK = 384


def attend_backward(
    link, q, kv, q_marks, k_pos, k_seg, lse, out, out_grad, send_rows
):
    ctx = link.sizes["ctx"]
    rows, keys = q.shape[0], kv.shape[0]
    steps = rows // TQ
    span = keys // ctx
    levels = link.offsets(("ctx",))[1:]

    def kernel(
        q_ref, kv_ref, qm_ref, kp_ref, ks_ref, lse_ref, o_ref, do_ref, rows_ref,
        dq_ref, got_kv, got_rows,
        acc, heads, grads, delta, kv_send, bounce, send, recv, kv_out, kv_in, near,
    ):
        wires = Wires(send, recv)
        my_c = lax.axis_index("ctx")
        greet([link.place(("ctx",), offset)[0] for offset in levels])
        copies = []
        for offset in levels:
            where, index = link.place(("ctx",), offset)
            copies.append(wires.start(rows_ref.at[index], got_rows.at[my_c], where))
        inward = pltpu.make_async_copy(rows_ref.at[my_c], bounce, near.at[0])
        outward = pltpu.make_async_copy(bounce, got_rows.at[my_c], near.at[0])
        inward.start()
        acc[...] = jnp.zeros_like(acc)
        delta[...] = jnp.zeros_like(delta)
        for i in range(steps):
            at = slice(i * TQ, i * TQ + TQ)
            for j, (b, h) in enumerate(HEAD_SLOTS):
                lanes = slice(128 * b, 128 * b + 128)
                heads[i, j] = head_block(q_ref[at, lanes], h)
                grad = head_block(do_ref[at, lanes], h)
                grads[i, j] = grad
                product = grad.astype(F32) * o_ref[at, lanes]
                delta[i, j : j + 1, :] = jnp.sum(product.T, axis=0, keepdims=True)
        inward.wait()
        outward.start()

        @pl.loop(0, ctx)
        def _(d):
            chunk = lax.rem(my_c + 1 + d, ctx)

            @pl.loop(0, span // BK)
            def _(t):
                inner = pl.multiple_of(t * BK, 128)
                at = pl.ds(pl.multiple_of(chunk * span + t * BK, 128), BK)
                k_tile = kv_ref[at, :128]
                v_tile = kv_ref[at, 128:]
                key_pos = jnp.tile(kp_ref[at, :], (1, TQ // 128))
                key_seg = jnp.tile(ks_ref[at, :], (1, TQ // 128))
                k_sum = jnp.zeros((BK, 128), F32)
                v_sum = jnp.zeros((BK, 128), F32)
                for i in range(steps):
                    cols = slice(i * TQ, i * TQ + TQ)
                    seen = (key_pos <= qm_ref[0:1, cols]) & (
                        (key_seg == 0) | (key_seg == qm_ref[1:2, cols])
                    )
                    for j in range(5):
                        scores = dot_general(k_tile, heads[i, j], 1, 1)
                        probs = jnp.where(seen, jnp.exp(scores - lse_ref[j : j + 1, cols]), 0.0)
                        prob_grad = dot_general(v_tile, grads[i, j], 1, 1)
                        score_grad = (probs * (prob_grad - delta[i, j : j + 1, :])).astype(BF)
                        v_sum += jnp.dot(
                            probs.astype(BF), grads[i, j], preferred_element_type=F32
                        )
                        k_sum += jnp.dot(score_grad, heads[i, j], preferred_element_type=F32)
                        acc[i, j] += dot_general(k_tile, score_grad, 0, 0)
                kv_send[chunk, pl.ds(inner, BK), :128] = k_sum.astype(BF)
                kv_send[chunk, pl.ds(inner, BK), 128:] = v_sum.astype(BF)

            @pl.when(d < ctx - 1)
            def _():
                pltpu.make_async_remote_copy(
                    kv_send.at[chunk],
                    got_kv.at[my_c],
                    kv_out.at[d],
                    kv_in.at[d],
                    device_id={"ctx": chunk},
                    device_id_type=MESH,
                ).start()

        near_kv = pltpu.make_async_copy(kv_send.at[my_c], got_kv.at[my_c], near.at[1])
        near_kv.start()
        low = lax.broadcasted_iota(jnp.int32, (TQ, 128), 1) < 64
        for i in range(steps):
            for b in range(3):
                first = acc[i, 2 * b].T * 0.125
                if b < 2:
                    block = jnp.where(low, first, acc[i, 2 * b + 1].T * 0.125)
                else:
                    block = jnp.where(low, first, 0.0)
                dq_ref[i * TQ : i * TQ + TQ, 128 * b : 128 * b + 128] = block.astype(BF)

        near_kv.wait()
        outward.wait()
        for copy in copies:
            copy.wait()

        for d in range(ctx - 1):
            pltpu.make_async_remote_copy(
                kv_send.at[0],
                got_kv.at[0],
                kv_out.at[d],
                kv_in.at[d],
                device_id={"ctx": my_c},
                device_id_type=MESH,
            ).wait()

    vmem = pl.BlockSpec(memory_space=pltpu.VMEM)
    anywhere = pl.BlockSpec(memory_space=pl.ANY)
    return pl.pallas_call(
        kernel,
        name="attend_backward",
        in_specs=[vmem] * 8 + [anywhere],
        out_specs=[vmem] + [anywhere] * 2,
        out_shape=[
            jax.ShapeDtypeStruct((rows, 384), BF),
            jax.ShapeDtypeStruct((ctx, span, 256), BF),
            jax.ShapeDtypeStruct(send_rows.shape, BF),
        ],
        scratch_shapes=[
            pltpu.VMEM((steps, 5, 128, TQ), F32),
            pltpu.VMEM((steps, 5, TQ, 128), BF),
            pltpu.VMEM((steps, 5, TQ, 128), BF),
            pltpu.VMEM((steps, 8, TQ), F32),
            pltpu.VMEM((ctx, span, 256), BF),
            pltpu.VMEM(send_rows.shape[1:], BF),
            pltpu.SemaphoreType.DMA((ctx,)),
            pltpu.SemaphoreType.DMA((ctx,)),
            pltpu.SemaphoreType.DMA((ctx,)),
            pltpu.SemaphoreType.DMA((ctx,)),
            pltpu.SemaphoreType.DMA((2,)),
        ],
        compiler_params=pltpu.CompilerParams(
            collective_id=11, has_side_effects=True, vmem_limit_bytes=VMEM_LIMIT
        ),
    )(q, kv, q_marks, k_pos, k_seg, lse, out, out_grad, send_rows)


class Wires:
    def __init__(self, send, recv):
        self.send, self.recv, self.used = send, recv, 0

    def copy(self, source, target, where):
        at = self.used
        self.used += 1
        return pltpu.make_async_remote_copy(
            source,
            target,
            self.send.at[at],
            self.recv.at[at],
            device_id=where,
            device_id_type=MESH,
        )

    def start(self, source, target, where):
        copy = self.copy(source, target, where)
        copy.start()
        return copy


def greet(places):
    barrier = pltpu.get_barrier_semaphore()
    for where in places:
        pl.semaphore_signal(barrier, 1, device_id=where, device_id_type=MESH)
    pl.semaphore_wait(barrier, len(places))


def square():
    w = lax.axis_index("wsh")
    return w, w + 1 - 2 * lax.rem(w, 2), w + 2 - 4 * (w // 2), 3 - w


class SquareScatter:
    def __init__(self, wires, parts, near, total):
        self.wires, self.parts, self.near, self.total = wires, parts, near, total
        self.half = parts.shape[1] // 2
        self.a, self.b = pl.ds(0, self.half), pl.ds(self.half, self.half)
        self.own, self.x, self.y, self.z = square()
        self.pending = []

    def send_diagonal(self):
        wires, parts = self.wires, self.parts
        self.one = wires.start(parts.at[self.z, self.a], self.near.at[0], {"wsh": self.x})
        self.two = wires.start(parts.at[self.z, self.b], self.near.at[1], {"wsh": self.y})

    def send_x(self):
        self.pending.append(
            self.wires.start(
                self.parts.at[self.x, self.a], self.total.at[0, self.a], {"wsh": self.x}
            )
        )

    def send_y(self):
        self.pending.append(
            self.wires.start(
                self.parts.at[self.y, self.b], self.total.at[1, self.b], {"wsh": self.y}
            )
        )

    def relay(self):
        near, parts = self.near, self.parts
        self.one.wait()
        near[2] = (near[0].astype(F32) + parts[self.y, self.a].astype(F32)).astype(BF)
        self.pending.append(
            self.wires.start(near.at[2], self.total.at[1, self.a], {"wsh": self.y})
        )
        self.two.wait()
        near[3] = (near[1].astype(F32) + parts[self.x, self.b].astype(F32)).astype(BF)
        self.pending.append(
            self.wires.start(near.at[3], self.total.at[0, self.b], {"wsh": self.x})
        )

    def result(self):
        for copy in self.pending:
            copy.wait()
        return (
            self.parts[self.own].astype(F32)
            + self.total[0].astype(F32)
            + self.total[1].astype(F32)
        )


def square_scratch(rows):
    return [pltpu.VMEM((4, rows // 2, D), BF), pltpu.VMEM((2, rows, D), BF)]


class SquareGather:
    def __init__(self, wires, out):
        self.wires, self.out = wires, out
        half = out.shape[1] // 2
        self.a, self.b = pl.ds(0, half), pl.ds(half, half)
        self.own, self.x, self.y, self.z = square()

    def move(self, slot, part, to):
        return self.wires.start(self.out.at[slot, part], self.out.at[slot, part], {"wsh": to})

    def begin(self):
        self.xa = self.move(self.own, self.a, self.x)
        self.yb = self.move(self.own, self.b, self.y)
        self.xb = self.move(self.own, self.b, self.x)
        self.ya = self.move(self.own, self.a, self.y)

    def relay(self):
        self.xa.wait()
        self.one = self.move(self.x, self.a, self.y)
        self.yb.wait()
        self.two = self.move(self.y, self.b, self.x)

    def wait_x(self):
        self.xb.wait()

    def wait_y(self):
        self.ya.wait()

    def wait_z(self):
        self.one.wait()
        self.two.wait()


def feed(link, attended, w_out, tokens, gain, w_half, down, dy):
    ctx, wsh = link.sizes["ctx"], link.sizes["wsh"]
    own_rows = tokens.shape[0]
    plane = dy.shape[0]
    units = down.shape[0]
    chunk = D // ctx
    pick = units // ctx // 2

    def kernel(
        at_ref, ao_ref, x_ref, g_ref, wh_ref, dw_ref, dy_ref,
        mid_ref, mg_ref, br_ref, ag_ref, fs_ref, dp_ref, gs_ref, gl_ref, ds_ref,
        wo_ref, w_both, parts, near, total, near2, total2, n2, hgrad, hidden, gate_g, up_g,
        down_h, down_pair, down_send, down_got, gate_h, gate_pair, send, recv, local,
    ):
        wires = Wires(send, recv)
        core = lax.axis_index("grp")
        sibling = {"grp": 1 - core}
        my_c = lax.axis_index("ctx")
        own, x, y, z = square()
        levels = [link.place(("ctx",), offset) for offset in link.offsets(("ctx",))[1:]]
        greet([{"wsh": x}, {"wsh": y}, sibling] + [where for where, _ in levels])

        def rows_of(slot):
            return pl.ds(pl.multiple_of(slot * own_rows, 16), own_rows)

        w_copy = pltpu.make_async_copy(wh_ref, w_both.at[core], local)
        w_copy.start()

        odd = lax.rem(own, 2) == 1
        wo_ref[...] = jnp.zeros_like(wo_ref)

        def spread(pieces):
            at = 0
            for start, size in pieces:
                wo_ref[start : start + size, :] = ao_ref[at : at + size, :]
                at += size

        @pl.when(odd)
        def _():
            spread(ODD_ROWS)

        @pl.when(jnp.logical_not(odd))
        def _():
            spread(EVEN_ROWS)

        first = SquareScatter(wires, parts, near, total)
        for slot in (z, x, y, own):
            parts[slot] = jnp.dot(
                at_ref[rows_of(slot), :], wo_ref[...], preferred_element_type=F32
            ).astype(BF)
            if slot is z:
                first.send_diagonal()
            elif slot is x:
                first.send_x()
            elif slot is y:
                first.send_y()
        w_swap = wires.start(wh_ref, w_both.at[core], sibling)
        hgrad[...] = dot_general(dy_ref[...], dw_ref[...], 1, 1)
        first.relay()
        middle = x_ref[...].astype(F32) + first.result()
        mid_ref[...] = middle
        factor = lax.rsqrt(jnp.mean(middle * middle, axis=-1, keepdims=True) + EPSILON)
        n2[own] = (middle * factor * g_ref[1:2, :]).astype(BF)
        gather = SquareGather(wires, n2)
        gather.begin()
        w_copy.wait()
        w_swap.wait()

        def block(slot):
            at = rows_of(slot)
            gate = jnp.dot(n2[slot], w_both[0], preferred_element_type=F32)
            up = jnp.dot(n2[slot], w_both[1], preferred_element_type=F32)
            sigmoid = 1.0 / (1.0 + jnp.exp(-gate))
            silu = gate * sigmoid
            hidden[at, :] = (silu * up).astype(BF)
            back = hgrad[at, :]
            gate_g[at, :] = (back * up * sigmoid * (1.0 + gate * (1.0 - sigmoid))).astype(BF)
            up_g[at, :] = (back * silu).astype(BF)
            parts[slot] = (
                dot_general(gate_g[at, :], w_both[0], 1, 1)
                + dot_general(up_g[at, :], w_both[1], 1, 1)
            ).astype(BF)

        second = SquareScatter(wires, parts, near2, total2)
        block(own)
        gather.relay()
        gather.wait_x()
        block(x)
        second.send_x()
        gather.wait_y()
        block(y)
        second.send_y()
        gather.wait_z()
        block(z)
        second.send_diagonal()

        strip = dot_general(hidden[...], dy_ref[...], 0, 0).astype(BF)
        for k in range(ctx):
            for g in range(2):
                top = (2 * k + g) * pick
                down_h[g, k] = strip[top : top + pick, :]
        down_swap = wires.start(down_h.at[1 - core], down_pair, sibling)
        second.relay()
        tokens_all = n2[...].reshape(plane, D)
        for g, source in enumerate((gate_g, up_g)):
            strip = dot_general(tokens_all, source[...], 0, 0).astype(BF)
            for c in range(ctx):
                gate_h[g, c] = strip[c * chunk : c * chunk + chunk, :]
        gate_swap = wires.start(gate_h.at[1 - core], gate_pair, sibling)
        down_swap.wait()
        down_send[...] = (down_h[core].astype(F32) + down_pair[...].astype(F32)).astype(BF)
        down_copies = []
        for where, index in levels:
            down_copies.append(wires.start(down_send.at[index], down_got.at[my_c], where))
        down_got[my_c] = down_send[my_c]

        grad = second.result()
        middle = mid_ref[...]
        factor = lax.rsqrt(jnp.mean(middle * middle, axis=-1, keepdims=True) + EPSILON)
        weighted = grad * g_ref[1:2, :]
        inner = jnp.mean(weighted * middle, axis=-1, keepdims=True)
        middle_grad = (
            dy_ref[rows_of(own), :].astype(F32)
            + factor * weighted
            - middle * (factor * factor * factor) * inner
        )
        mg_ref[...] = middle_grad
        br_ref[own] = middle_grad.astype(BF)
        branch = SquareGather(wires, br_ref)
        branch.begin()
        fs_ref[...] = jnp.sum(grad * middle * factor, axis=0, keepdims=True)

        def outward(slot):
            ag_ref[rows_of(slot), :] = dot_general(br_ref[slot], wo_ref[...], 1, 1).astype(BF)

        outward(own)
        gate_swap.wait()
        for c in range(ctx):
            both = (gate_h[core, c].astype(F32) + gate_pair[c].astype(F32)).astype(BF)
            gs_ref[c] = both[:, : units // 2]
            gl_ref[c] = both[:, units // 2 :]
        branch.relay()
        for slot in range(wsh):
            at = slice(slot * own_rows, slot * own_rows + own_rows)
            dp_ref[slot] = jnp.dot(
                hidden[at, :], dw_ref[...], preferred_element_type=F32
            ).astype(BF)
        branch.wait_x()
        outward(x)
        branch.wait_y()
        outward(y)
        branch.wait_z()
        outward(z)
        for copy in down_copies:
            copy.wait()
        ds_ref[...] = jnp.sum(down_got[...].astype(F32), axis=0).astype(BF)

    operands = (attended, w_out, tokens, gain, w_half, down, dy)
    vmem = pl.BlockSpec(memory_space=pltpu.VMEM)
    return pl.pallas_call(
        kernel,
        name="feed",
        in_specs=[vmem] * len(operands),
        out_specs=[vmem] * 9,
        out_shape=[
            jax.ShapeDtypeStruct((own_rows, D), F32),
            jax.ShapeDtypeStruct((own_rows, D), F32),
            jax.ShapeDtypeStruct((wsh, own_rows, D), BF),
            jax.ShapeDtypeStruct((plane, 384), BF),
            jax.ShapeDtypeStruct((1, D), F32),
            jax.ShapeDtypeStruct((wsh, own_rows, D), BF),
            jax.ShapeDtypeStruct((ctx, chunk, units // 2), BF),
            jax.ShapeDtypeStruct((ctx, chunk, units // 2), BF),
            jax.ShapeDtypeStruct((pick, D), BF),
        ],
        scratch_shapes=[
            pltpu.VMEM((384, D), BF),
            pltpu.VMEM((2, D, units), BF),
            pltpu.VMEM((4, own_rows, D), BF),
            *square_scratch(own_rows),
            *square_scratch(own_rows),
            pltpu.VMEM((4, own_rows, D), BF),
            pltpu.VMEM((plane, units), F32),
            *[pltpu.VMEM((plane, units), BF)] * 3,
            pltpu.VMEM((2, ctx, pick, D), BF),
            *[pltpu.VMEM((ctx, pick, D), BF)] * 3,
            pltpu.VMEM((2, ctx, chunk, units), BF),
            pltpu.VMEM((ctx, chunk, units), BF),
            pltpu.SemaphoreType.DMA((ctx + 28,)),
            pltpu.SemaphoreType.DMA((ctx + 28,)),
            pltpu.SemaphoreType.DMA,
        ],
        compiler_params=pltpu.CompilerParams(
            collective_id=3, has_side_effects=True, vmem_limit_bytes=VMEM_LIMIT
        ),
    )(*operands)


def head(link, tokens, gain, weight, marks, upstream):
    ctx, wsh = link.sizes["ctx"], link.sizes["wsh"]
    own_rows = tokens.shape[0]
    plane, group = own_rows * wsh, own_rows * wsh * ctx
    half = weight.shape[0] // 2

    def kernel(
        x_ref, g_ref, w_ref, m_ref, up_ref,
        q_ref, kv_ref, n_ref, wq_ref, kpos_ref, kseg_ref, q_marks, dy_ref, c_ref, s_ref,
        cols, mine, marks_all, send, recv,
    ):
        wires = Wires(send, recv)
        core = lax.axis_index("grp")
        sibling = {"grp": 1 - core}
        my_c = lax.axis_index("ctx")
        own, x, y, z = square()
        levels = [link.place(("ctx",), offset) for offset in link.offsets(("ctx",))[1:]]
        greet(
            [{"wsh": x}, {"wsh": y}, {"wsh": z}, sibling] + [where for where, _ in levels]
        )
        mine[...] = jnp.zeros_like(mine)
        mine[:2, :own_rows] = m_ref[...]
        mark_copies = []
        for p in (x, y, z):
            mark_copies.append(wires.start(mine, marks_all.at[my_c, own], {"wsh": p}))
        marks_all[my_c, own] = mine[...]
        side = pl.ds(pl.multiple_of(core * half, 16), half)

        for w in range(wsh):
            q_order, kv_order = head_plan(w)
            slots = [h for h in q_order] + [HEADS + h for h in kv_order]
            slots += [HEADS + KV_HEADS + h for h in kv_order]
            blank = jnp.zeros((w_ref.shape[0], HEAD_DIM), BF)
            for pair in range(5):
                two = [
                    blank if h is None else w_ref[:, h * HEAD_DIM : h * HEAD_DIM + HEAD_DIM]
                    for h in slots[2 * pair : 2 * pair + 2]
                ]
                cols[w, :, 128 * pair : 128 * pair + 128] = jnp.concatenate(two, axis=1)
        w_copies = []
        for p in (x, y, z):
            w_copies.append(
                wires.start(cols.at[p, side], wq_ref.at[own, side], {"wsh": p})
            )
        tokens_in = x_ref[...].astype(F32)
        factor = lax.rsqrt(jnp.mean(tokens_in * tokens_in, axis=-1, keepdims=True) + EPSILON)
        n_ref[own] = (tokens_in * factor * g_ref[0:1, :]).astype(BF)
        gather = SquareGather(wires, n_ref)
        gather.begin()
        wq_ref[own] = cols[own]
        dy_ref[own] = up_ref[...]

        for copy in mark_copies:
            copy.wait()
        level_copies = []
        for where, _ in levels:
            level_copies.append(wires.start(marks_all.at[my_c], marks_all.at[my_c], where))
        lane = lax.broadcasted_iota(jnp.int32, (1, 128), 1)
        power = lax.rem(lane, 32).astype(F32) * (-math.log(10000.0) / 32)
        frequency = jnp.exp(power)
        sign = jnp.where(lax.rem(lane, 64) < 32, -1.0, 1.0)

        def upright(row):
            return jnp.broadcast_to(row, (128, row.shape[1])).T

        for w in range(wsh):
            at = slice(w * own_rows, w * own_rows + own_rows)
            angles = upright(marks_all[my_c, w, 0:1, :])[:own_rows] * frequency
            c_ref[at, :] = jnp.cos(angles)
            s_ref[at, :] = jnp.sin(angles) * sign
        gather.relay()
        forward = []
        for p, copy in zip((x, y, z), w_copies):
            copy.wait()
            forward.append(wires.start(wq_ref.at[p, side], wq_ref.at[p, side], sibling))
        dy_gather = SquareGather(wires, dy_ref)
        dy_gather.begin()
        for copy in forward:
            copy.wait()

        low = lax.rem(lax.broadcasted_iota(jnp.int32, (own_rows, 128), 1), 64) < 32
        kv_copies = []

        def block(slot):
            at = pl.ds(pl.multiple_of(slot * own_rows, 16), own_rows)
            full = jnp.dot(
                n_ref[slot], wq_ref[...].reshape(D, 640), preferred_element_type=F32
            )
            cos_t, sin_t = c_ref[at, :], s_ref[at, :]
            for b in range(3):
                turned = turn(full[:, 128 * b : 128 * b + 128], cos_t, sin_t, low)
                q_ref[at, 128 * b : 128 * b + 128] = (
                    turned.astype(BF).astype(F32) * 0.125
                ).astype(BF)
            kv_ref[my_c, at, :128] = turn(full[:, 384:512], cos_t, sin_t, low).astype(BF)
            kv_ref[my_c, at, 128:] = full[:, 512:].astype(BF)
            for where, _ in levels:
                kv_copies.append(
                    wires.start(kv_ref.at[my_c, at], kv_ref.at[my_c, at], where)
                )

        block(own)
        gather.wait_x()
        block(x)
        gather.wait_y()
        block(y)
        gather.wait_z()
        block(z)
        dy_gather.relay()

        for copy in level_copies:
            copy.wait()
        for w in range(wsh):
            q_marks[:, w * own_rows : w * own_rows + own_rows] = marks_all[my_c, w, :, :own_rows]

        @pl.loop(0, ctx)
        def _(c):
            for w in range(wsh):
                at = pl.ds(pl.multiple_of(c * plane + w * own_rows, 16), own_rows)
                kpos_ref[at, :] = upright(marks_all[c, w, 0:1, :])[:own_rows]
                kseg_ref[at, :] = upright(marks_all[c, w, 1:2, :])[:own_rows]

        dy_gather.wait_x()
        dy_gather.wait_y()
        dy_gather.wait_z()
        for copy in kv_copies:
            copy.wait()

    operands = (tokens, gain, weight, marks, upstream)
    vmem = pl.BlockSpec(memory_space=pltpu.VMEM)
    return pl.pallas_call(
        kernel,
        name="head",
        in_specs=[vmem] * len(operands),
        out_specs=[vmem] * 10,
        out_shape=[
            jax.ShapeDtypeStruct((plane, 384), BF),
            jax.ShapeDtypeStruct((ctx, plane, 256), BF),
            jax.ShapeDtypeStruct((wsh, own_rows, D), BF),
            jax.ShapeDtypeStruct((wsh, 2 * half, 640), BF),
            jax.ShapeDtypeStruct((group, 128), F32),
            jax.ShapeDtypeStruct((group, 128), F32),
            jax.ShapeDtypeStruct((8, plane), F32),
            jax.ShapeDtypeStruct((wsh, own_rows, D), BF),
            jax.ShapeDtypeStruct((plane, 128), F32),
            jax.ShapeDtypeStruct((plane, 128), F32),
        ],
        scratch_shapes=[
            pltpu.VMEM((wsh, 2 * half, 640), BF),
            pltpu.VMEM((8, 256), F32),
            pltpu.VMEM((ctx, wsh, 8, 256), F32),
            pltpu.SemaphoreType.DMA((5 * ctx + 24,)),
            pltpu.SemaphoreType.DMA((5 * ctx + 24,)),
        ],
        compiler_params=pltpu.CompilerParams(
            collective_id=1, has_side_effects=True, vmem_limit_bytes=VMEM_LIMIT
        ),
    )(*operands)


def finish(
    link, q_grad, kv_grad, weight, cos, sin, normed, tokens, gain, middle_grad, gate_got, down_got,
    attended, branch, feed_sum, down_part, middle, gate_late,
):
    ctx, wsh = link.sizes["ctx"], link.sizes["wsh"]
    shards = ctx * wsh
    rows = D // shards
    chunk = D // ctx
    fold = ctx // wsh
    own_rows = tokens.shape[0]
    plane = normed.shape[0]
    axes = ("ctx", "wsh")
    peers = link.offsets(axes)
    gate_width = gate_got.shape[2]
    down_rows = down_got.shape[0]

    def kernel(
        q_ref, kv_ref, w_ref, c_ref, s_ref, n_ref, x_ref, g_ref, mg_ref, gate_ref, down_ref,
        at_ref, br_ref, fs_ref, dp_ref, mid_ref, late_ref,
        act_ref, ig_ref, q_fin, kv_fin, out_fin, gate_fin, late_fin, down_fin, gains_out,
        pg, parts, near, total, near2, total2, wide, q_own, q_pair, q_send, q_got,
        q_mid, kv_own, kv_pair, kv_go, kv_got, kv_mid, gate_mid, late_got,
        late_mid, out_halves,
        out_pair, out_send, out_mid, out_got, gains, gains_got, gains_fin,
        send, recv,
    ):
        wires = Wires(send, recv)
        core = lax.axis_index("grp")
        first, second = core == 0, core == 1
        sibling = {"grp": 1 - core}
        my_c, my_w = lax.axis_index("ctx"), lax.axis_index("wsh")
        odd = lax.rem(my_w, 2) == 1
        greet([link.place(axes, offset)[0] for offset in peers[1:]] + [sibling])
        _, me = link.place(axes, peers[0])

        def over_ctx(got, mid):
            for w in range(wsh):
                strip = got[0, w * rows : w * rows + rows, :].astype(F32)
                for c in range(1, ctx):
                    strip += got[c, w * rows : w * rows + rows, :].astype(F32)
                mid[w] = strip.astype(BF)

        def in_plane(mid, slot_of):
            copies = []
            for offset in link.offsets(("wsh",))[1:]:
                where, index = link.place(("wsh",), offset)
                copies.append(wires.copy(mid.at[index], slot_of(my_w), where))
            return copies

        def begin(cond, *copies):
            @pl.when(cond)
            def _():
                for copy in copies:
                    copy.start()

        levels = [link.place(("ctx",), offset) for offset in link.offsets(("ctx",))[1:]]
        late_copies = []
        for where, index in levels:
            late_copies.append(wires.start(late_ref.at[index], late_got.at[my_c], where))

        owner, stays = owner_of(link)
        moves = jnp.logical_not(stays)
        down_move = wires.copy(down_ref, down_fin.at[core], owner)
        begin(moves, down_move)

        @pl.when(stays)
        def _():
            down_fin[core] = down_ref[...]

        low = lax.rem(lax.broadcasted_iota(jnp.int32, (own_rows, 128), 1), 64) < 32
        scatter = SquareScatter(wires, parts, near, total)
        gain_sum = jnp.zeros((1, D), F32)
        for slot in (scatter.z, scatter.x, scatter.y, scatter.own):
            at = pl.ds(pl.multiple_of(slot * own_rows, 16), own_rows)
            cos_t, sin_t = c_ref[at, :], -s_ref[at, :]
            for b in range(3):
                block = q_ref[at, 128 * b : 128 * b + 128].astype(F32)
                pg[at, 128 * b : 128 * b + 128] = turn(block, cos_t, sin_t, low).astype(BF)
            summed = kv_ref[0, at, :].astype(F32)
            for c in range(1, ctx):
                summed += kv_ref[c, at, :].astype(F32)
            block = summed[:, :128].astype(BF).astype(F32)
            pg[at, 384:512] = turn(block, cos_t, sin_t, low).astype(BF)
            pg[at, 512:] = summed[:, 128:].astype(BF)
            part = dot_general(pg[at, :], w_ref[...], 1, 1)
            parts[slot] = part.astype(BF)
            gain_sum += jnp.sum(part * n_ref[at, :].astype(F32), axis=0, keepdims=True)
            if slot is scatter.z:
                scatter.send_diagonal()
            elif slot is scatter.x:
                scatter.send_x()
            elif slot is scatter.y:
                scatter.send_y()

        strip = dot_general(n_ref[...], pg[:, 384:], 0, 0).astype(BF)
        for c in range(ctx):
            kv_own[c] = strip[c * chunk : c * chunk + chunk, :]
        kv_swap = wires.copy(kv_own, kv_pair, sibling)
        begin(first, kv_swap)
        scatter.relay()
        strip = dot_general(n_ref[...], pg[:, :384], 0, 0).astype(BF)
        for c in range(ctx):
            q_own[c] = strip[c * chunk : c * chunk + chunk, :]
        q_swap = wires.copy(q_own, q_pair, sibling)
        begin(second, q_swap)
        layer = SquareScatter(wires, dp_ref, near2, total2)
        layer.send_diagonal()
        layer.send_x()
        layer.send_y()
        wide[...] = dot_general(at_ref[...], br_ref[...], 0, 0)

        def out_strips(pieces):
            at = 0
            for start, size in pieces:
                acc_rows = wide[start : start + size, :].astype(BF)
                part = jnp.concatenate([acc_rows[:, :576], jnp.zeros((size, 64), BF)], axis=1)
                out_halves[0, at : at + size, :] = part
                part = jnp.concatenate([acc_rows[:, 576:], jnp.zeros((size, 64), BF)], axis=1)
                out_halves[1, at : at + size, :] = part
                at += size

        @pl.when(odd)
        def _():
            out_strips(ODD_ROWS)

        @pl.when(jnp.logical_not(odd))
        def _():
            out_strips(EVEN_ROWS)

        out_swap = wires.start(out_halves.at[1 - core], out_pair, sibling)
        q_copies, kvg_copies, out_copies = [], [], []
        for where, index in levels:
            q_copies.append(wires.copy(q_send.at[index], q_got.at[my_c], where))
            kvg_copies.append(wires.copy(kv_go.at[index], kv_got.at[my_c], where))

        @pl.when(first)
        def _():
            q_swap.wait_recv()

            @pl.loop(0, ctx)
            def _(c):
                q_send[c] = (q_own[c].astype(F32) + q_pair[c].astype(F32)).astype(BF)

            for copy in q_copies:
                copy.start()
            q_got[my_c] = q_send[my_c]
            kv_swap.wait_send()

        @pl.when(second)
        def _():
            kv_swap.wait_recv()

            @pl.loop(0, ctx)
            def _(c):
                kv_go[c] = (kv_own[c].astype(F32) + kv_pair[c].astype(F32)).astype(BF)

            for copy in kvg_copies:
                copy.start()
            kv_got[my_c] = kv_go[my_c]
            q_swap.wait_send()

        both = jnp.concatenate([gain_sum / g_ref[0:1, :], fs_ref[...]], axis=0)
        gains[...] = jnp.zeros_like(gains)
        for s in range(shards):
            gains[s, :2, :rows] = both[:, rows * s : rows * s + rows]
        gain_copies = []
        for offset in peers[1:]:
            where, index = link.place(axes, offset)
            gain_copies.append(wires.start(gains.at[index], gains_got.at[me], where))
        gains_got[me] = gains[me]
        layer.relay()

        out_swap.wait()
        for k in range(ctx):
            strip = slice(k * rows, k * rows + rows)
            out_send[k % wsh, k // wsh] = (
                out_halves[core, strip, :].astype(F32) + out_pair[strip, :].astype(F32)
            ).astype(BF)
        out_moves = in_plane(out_send, lambda w: out_mid.at[w])
        for copy in out_moves:
            copy.start()
        out_mid[my_w] = out_send[my_w]

        grad = scatter.result()
        x = x_ref[...].astype(F32)
        factor = lax.rsqrt(jnp.mean(x * x, axis=-1, keepdims=True) + EPSILON)
        weighted = grad * g_ref[0:1, :]
        inner = jnp.mean(weighted * x, axis=-1, keepdims=True)
        ig_ref[...] = mg_ref[...] + factor * weighted - x * (factor * factor * factor) * inner
        for copy in out_moves:
            copy.wait()
        for where, index in levels:
            part = out_mid.at[index // fold, lax.rem(index, fold)]
            out_copies.append(wires.start(part, out_got.at[my_c], where))
        out_got[my_c] = out_mid[my_c // fold, lax.rem(my_c, fold)]


        @pl.when(moves)
        def _():
            down_move.wait()

        down_copy = wires.start(down_fin.at[core], down_fin.at[core], sibling)
        over_ctx(gate_ref, gate_mid)
        gate_moves = in_plane(gate_mid, lambda w: gate_fin.at[core, w])
        for copy in gate_moves:
            copy.start()
        gate_fin[core, my_w] = gate_mid[my_w]
        for copy in late_copies:
            copy.wait()
        late_got[my_c] = late_ref[my_c]
        over_ctx(late_got, late_mid)
        late_moves = in_plane(late_mid, lambda w: late_fin.at[core, w])
        for copy in late_moves:
            copy.start()
        late_fin[core, my_w] = late_mid[my_w]
        act_ref[...] = (mid_ref[...] + layer.result()).astype(BF)

        q_moves = in_plane(q_mid, lambda w: q_fin.at[w])
        kv_moves = in_plane(kv_mid, lambda w: kv_fin.at[w])

        @pl.when(first)
        def _():
            for copy in q_copies:
                copy.wait()
            over_ctx(q_got, q_mid)
            for copy in q_moves:
                copy.start()
            q_fin[my_w] = q_mid[my_w]

        @pl.when(second)
        def _():
            for copy in kvg_copies:
                copy.wait()
            over_ctx(kv_got, kv_mid)
            for copy in kv_moves:
                copy.start()
            kv_fin[my_w] = kv_mid[my_w]

        for copy in gate_moves + late_moves:
            copy.wait()
        gate_copy = wires.start(gate_fin.at[core], gate_fin.at[core], sibling)
        late_copy = wires.start(late_fin.at[core], late_fin.at[core], sibling)
        for copy in out_copies:
            copy.wait()
        out_fin[core] = jnp.sum(out_got[...].astype(F32), axis=0).astype(BF)
        out_copy = wires.start(out_fin.at[core], out_fin.at[core], sibling)
        for copy in gain_copies:
            copy.wait()
        gains_fin[core] = jnp.sum(gains_got[...], axis=0)
        gain_copy = wires.start(gains_fin.at[core], gains_fin.at[core], sibling)
        q_final = wires.copy(q_fin, q_fin, sibling)
        kv_final = wires.copy(kv_fin, kv_fin, sibling)

        @pl.when(first)
        def _():
            for copy in q_moves:
                copy.wait()
            q_final.start()

        @pl.when(second)
        def _():
            for copy in kv_moves:
                copy.wait()
            kv_final.start()

        down_copy.wait()
        gate_copy.wait()
        late_copy.wait()
        out_copy.wait()

        @pl.when(first)
        def _():
            q_final.wait_send()
            kv_final.wait_recv()

        @pl.when(second)
        def _():
            kv_final.wait_send()
            q_final.wait_recv()

        gain_copy.wait()
        gains_out[...] = gains_fin[0] + gains_fin[1]

    operands = (
        q_grad, kv_grad, weight, cos, sin, normed, tokens, gain, middle_grad, gate_got, down_got,
        attended, branch, feed_sum, down_part, middle, gate_late,
    )
    vmem = pl.BlockSpec(memory_space=pltpu.VMEM)
    return pl.pallas_call(
        kernel,
        name="finish",
        in_specs=[vmem] * len(operands),
        out_specs=[vmem] * 9,
        out_shape=[
            jax.ShapeDtypeStruct((own_rows, D), BF),
            jax.ShapeDtypeStruct((own_rows, D), F32),
            jax.ShapeDtypeStruct((wsh, rows, 384), BF),
            jax.ShapeDtypeStruct((wsh, rows, 256), BF),
            jax.ShapeDtypeStruct((2, rows, 640), BF),
            jax.ShapeDtypeStruct((2, wsh, rows, gate_width), BF),
            jax.ShapeDtypeStruct((2, wsh, rows, gate_width), BF),
            jax.ShapeDtypeStruct((2, down_rows, D), BF),
            jax.ShapeDtypeStruct((8, 128), F32),
        ],
        scratch_shapes=[
            pltpu.VMEM((plane, 640), BF),
            pltpu.VMEM((4, own_rows, D), BF),
            *square_scratch(own_rows),
            *square_scratch(own_rows),
            pltpu.VMEM((384, D), F32),
            *[pltpu.VMEM((ctx, chunk, 384), BF)] * 4,
            pltpu.VMEM((wsh, rows, 384), BF),
            *[pltpu.VMEM((ctx, chunk, 256), BF)] * 4,
            pltpu.VMEM((wsh, rows, 256), BF),
            pltpu.VMEM((wsh, rows, gate_width), BF),
            pltpu.VMEM((ctx, chunk, gate_width), BF),
            pltpu.VMEM((wsh, rows, gate_width), BF),
            pltpu.VMEM((2, 288, 640), BF),
            pltpu.VMEM((288, 640), BF),
            pltpu.VMEM((wsh, fold, rows, 640), BF),
            pltpu.VMEM((wsh, fold, rows, 640), BF),
            pltpu.VMEM((ctx, rows, 640), BF),
            pltpu.VMEM((shards, 8, 128), F32),
            pltpu.VMEM((shards, 8, 128), F32),
            pltpu.VMEM((2, 8, 128), F32),
            pltpu.SemaphoreType.DMA((shards + 5 * ctx + 48,)),
            pltpu.SemaphoreType.DMA((shards + 5 * ctx + 48,)),
        ],
        compiler_params=pltpu.CompilerParams(
            collective_id=8, has_side_effects=True, vmem_limit_bytes=VMEM_LIMIT
        ),
    )(*operands)


def wrap(act, input_grad, q_sum, kv_sum, out_sum, gate_sum, late_sum, down_sum):
    wsh, rows, _ = q_sum.shape
    down_rows = down_sum.shape[1]
    width = gate_sum.shape[3]

    def kernel(
        act_in, ig_in, q_in, kv_in, out_in, gate_in, late_in, down_in,
        act_ref, ig_ref, qkv_ref, out_ref, gate_ref, down_ref,
    ):
        act_ref[...] = act_in[...]
        ig_ref[...] = ig_in[...]
        qkv_ref[...] = qkv_restore(
            [
                jnp.concatenate([q_in[w].astype(F32), kv_in[w].astype(F32)], axis=1)
                for w in range(wsh)
            ]
        )
        out_ref[...] = jnp.concatenate(
            [out_in[0, :, :576].astype(F32), out_in[1, :, :576].astype(F32)], axis=1
        )
        for half in range(2):
            for w in range(wsh):
                left = (half * wsh + w) * 2 * width
                gate_ref[:, left : left + width] = gate_in[half, w].astype(F32)
                left += width
                gate_ref[:, left : left + width] = late_in[half, w].astype(F32)
            down_ref[half * down_rows : half * down_rows + down_rows, :] = down_in[half].astype(
                F32
            )

    vmem = pl.BlockSpec(memory_space=pltpu.VMEM)
    return pl.pallas_call(
        kernel,
        name="wrap",
        in_specs=[vmem] * 8,
        out_specs=[vmem] * 6,
        out_shape=[
            jax.ShapeDtypeStruct(act.shape, BF),
            jax.ShapeDtypeStruct(act.shape, F32),
            jax.ShapeDtypeStruct((rows, QW + 2 * KW), F32),
            jax.ShapeDtypeStruct((rows, D), F32),
            jax.ShapeDtypeStruct((rows, 2 * FF), F32),
            jax.ShapeDtypeStruct((2 * down_rows, D), F32),
        ],
        compiler_params=pltpu.CompilerParams(vmem_limit_bytes=VMEM_LIMIT),
    )(act, input_grad, q_sum, kv_sum, out_sum, gate_sum, late_sum, down_sum)


def build(sizes):
    ctx, wsh = sizes["ctx"], sizes["wsh"]
    shards = ctx * wsh
    link = Exchange(sizes)

    def local(
        tokens,
        segment_ids,
        positions,
        attend_gain,
        query_key_value,
        attend_out,
        feed_gain,
        gate_up,
        down_weight,
        upstream,
    ):
        own = tokens.shape[0]
        plane = own * wsh
        group = plane * ctx
        marks = jnp.stack([positions, segment_ids]).astype(F32)
        both_gains = jnp.stack([attend_gain, feed_gain])
        (
            queries,
            kv_all,
            normed_all,
            w_qkv,
            k_pos,
            k_seg,
            q_marks,
            dy_all,
            cos,
            sin,
        ) = head(link, tokens, both_gains, query_key_value, marks, upstream)
        kv_all = kv_all.reshape(group, 256)
        normed_all, dy_all = normed_all.reshape(plane, D), dy_all.reshape(plane, D)
        w_qkv = w_qkv.reshape(D, 640)
        attended, attended_wide, lse, w_half = attend_forward(
            link, queries, kv_all, q_marks, k_pos, k_seg, gate_up
        )
        w_half = w_half.reshape(D, FF // wsh)
        (
            middle,
            middle_grad,
            branch_all,
            attended_grad,
            feed_sum,
            down_part,
            gate_send,
            gate_late,
            down_sum,
        ) = feed(link, attended, attend_out, tokens, both_gains, w_half, down_weight, dy_all)
        q_grad, kv_grad, gate_got = attend_backward(
            link, queries, kv_all, q_marks, k_pos, k_seg, lse, attended_wide, attended_grad,
            gate_send,
        )
        *sums, gain_out = finish(
            link, q_grad, kv_grad, w_qkv, cos, sin, normed_all, tokens,
            both_gains, middle_grad, gate_got, down_sum, attended,
            branch_all.reshape(plane, D), feed_sum, down_part, middle, gate_late,
        )
        activations, input_grad, qkv_out, out_out, gate_out, down_out = wrap(*sums)
        width = D // shards
        return (
            activations,
            input_grad,
            qkv_out,
            out_out,
            gate_out,
            down_out,
            gain_out[0, :width],
            gain_out[1, :width],
        )

    return local


def solution(mesh):
    whole = ("grp", "ctx", "wsh")
    in_specs = (
        P(whole, None),
        P(whole),
        P(whole),
        P(),
        P("wsh", None),
        P("wsh", None),
        P(),
        P("wsh", None),
        P("wsh", None),
        P(whole, None),
    )
    out_specs = (
        P(whole, None),
        P(whole, None),
        P(("ctx", "wsh"), None),
        P(("ctx", "wsh"), None),
        P(("ctx", "wsh"), None),
        P(("ctx", "wsh"), None),
        P(("ctx", "wsh")),
        P(("ctx", "wsh")),
    )
    return jax.shard_map(
        build(dict(mesh.shape)), mesh=mesh, in_specs=in_specs, out_specs=out_specs, check_vma=False
    )
```

```python
import itertools
import math

import jax
import jax.numpy as jnp
from jax import lax
from jax.experimental import pallas as pl
from jax.experimental.pallas import tpu as pltpu
from jax.sharding import PartitionSpec as P

HEADS = 18
KV_HEADS = 6
HEAD_DIM = 64
FF = 3072
D = 1152
QW = 1152
KW = 384
EPSILON = 1e-05
MESH = pl.DeviceIdType.MESH
F32 = jnp.float32
BF = jnp.bfloat16
VMEM_LIMIT = 56 << 20


def dot_general(a, b, ca, cb):
    return lax.dot_general(a, b, (((ca,), (cb,)), ((), ())), preferred_element_type=F32)


class Exchange:
    def __init__(self, sizes):
        self.sizes = sizes

    def place(self, axes, offset):
        where, index = {}, 0
        for axis, step in zip(axes, offset):
            size = self.sizes[axis]
            spot = lax.axis_index(axis)
            if step:
                spot = lax.rem(spot + step, size)
            where[axis] = spot
            index = index * size + spot
        return where, index

    def offsets(self, axes):
        return list(itertools.product(*[range(self.sizes[axis]) for axis in axes]))


def head_plan(w):
    pair, odd = w // 2, w % 2
    start = 9 * pair + 4 * odd
    if odd:
        f_heads, h_heads = [start + 2, start + 3, start + 4], [start, start + 1]
        f_kv, h_kv = 3 * pair + 2, 3 * pair + 1
    else:
        f_heads, h_heads = [start, start + 1, start + 2], [start + 3, start + 4]
        f_kv, h_kv = 3 * pair, 3 * pair + 1
    q_order = [f_heads[0], h_heads[0], f_heads[1], h_heads[1], f_heads[2], None]
    return q_order, [f_kv, h_kv]


def qkv_restore(parts):
    found = {}
    for w in range(4):
        q_order, kv_order = head_plan(w)
        slots = list(q_order) + [HEADS + h for h in kv_order]
        slots += [HEADS + KV_HEADS + h for h in kv_order]
        for at, head in enumerate(slots):
            if head is not None:
                found.setdefault(head, []).append(
                    parts[w][:, at * HEAD_DIM : (at + 1) * HEAD_DIM]
                )
    pieces = []
    for head in range(HEADS + 2 * KV_HEADS):
        term = found[head][0]
        for other in found[head][1:]:
            term = term + other
        pieces.append(term)
    return jnp.concatenate(pieces, axis=1)


def turn(x, cos, sin, lanes):
    swapped = jnp.where(lanes, pltpu.roll(x, 96, 1), pltpu.roll(x, 32, 1))
    return x * cos + swapped * sin


TQ = 256
TK = 512


def head_block(block, head):
    low = lax.broadcasted_iota(jnp.int32, block.shape, 1) < 64
    return jnp.where(low if head == 0 else jnp.logical_not(low), block, jnp.zeros_like(block))


def visible(kp_ref, ks_ref, qm_ref, start):
    key_pos = jnp.tile(kp_ref[pl.ds(start, TK), :], (1, TQ // 128))
    key_seg = jnp.tile(ks_ref[pl.ds(start, TK), :], (1, TQ // 128))
    return (key_pos <= qm_ref[0:1, :]) & ((key_seg == 0) | (key_seg == qm_ref[1:2, :]))


ODD_ROWS = [(96, 32), (192, 64), (0, 64), (128, 64), (256, 64)]
EVEN_ROWS = [(0, 64), (128, 64), (256, 64), (64, 64), (192, 32)]
HEAD_SLOTS = [(0, 0), (0, 1), (1, 0), (1, 1), (2, 0)]


def attend_forward(link, q, kv, q_marks, k_pos, k_seg, gate_up):
    rows, keys = q.shape[0], kv.shape[0]
    steps = rows // TQ
    wsh = link.sizes["wsh"]
    units = FF // wsh
    peers = link.offsets(("wsh",))

    def kernel(
        q_ref, kv_ref, qm_ref, kp_ref, ks_ref, gu_ref,
        a_ref, o_ref, lse_ref, wh_ref,
        acc, top, tot, bounce, send, recv, near,
    ):
        def columns(p):
            left = lax.axis_index("grp") * FF + p * units
            return gu_ref.at[:, pl.ds(pl.multiple_of(left, 128), units)]

        wires = Wires(send, recv)
        _, me = link.place(("wsh",), peers[0])
        copies = []
        for offset in peers[1:]:
            where, index = link.place(("wsh",), offset)
            copies.append(wires.copy(columns(index), wh_ref.at[me], where))
        inward = pltpu.make_async_copy(columns(me), bounce, near)
        outward = pltpu.make_async_copy(bounce, wh_ref.at[me], near)

        @pl.when(pl.program_id(0) == 0)
        def _():
            greet([link.place(("wsh",), offset)[0] for offset in peers[1:]])
            for copy in copies:
                copy.start()
            inward.start()
            inward.wait()
            outward.start()

        acc[...] = jnp.zeros_like(acc)
        top[...] = jnp.full_like(top, -1e30)
        tot[...] = jnp.zeros_like(tot)
        heads = [head_block(q_ref[:, 128 * b : 128 * b + 128], h) for b, h in HEAD_SLOTS]

        @pl.loop(0, keys // TK)
        def _(t):
            start = pl.multiple_of(t * TK, TK)
            k_tile = kv_ref[pl.ds(start, TK), :128]
            v_tile = kv_ref[pl.ds(start, TK), 128:]
            seen = visible(kp_ref, ks_ref, qm_ref, start)
            scores = [
                jnp.where(seen, dot_general(k_tile, heads[j], 1, 1), -1e30) for j in range(5)
            ]
            old = [top[j : j + 1, :] for j in range(5)]
            new = [
                jnp.maximum(old[j], jnp.max(scores[j], axis=0, keepdims=True)) for j in range(5)
            ]
            expons = [jnp.exp(scores[j] - new[j]) for j in range(5)]
            shrink = [jnp.exp(old[j] - new[j]) for j in range(5)]
            mixed = [dot_general(v_tile, expons[j].astype(BF), 0, 0) for j in range(5)]
            for j in range(5):
                tot[j : j + 1, :] = tot[j : j + 1, :] * shrink[j] + jnp.sum(
                    expons[j], axis=0, keepdims=True
                )
                acc[j] = acc[j] * shrink[j] + mixed[j]
                top[j : j + 1, :] = new[j]

        for j, (b, h) in enumerate(HEAD_SLOTS):
            out = acc[j] / tot[j : j + 1, :]
            acc[j] = out
        lse_ref[...] = top[...] + jnp.log(jnp.maximum(tot[...], 1e-37))
        low = lax.broadcasted_iota(jnp.int32, (TQ, 128), 1) < 64
        for b in range(3):
            first = acc[2 * b].T
            if b < 2:
                block = jnp.where(low, first, acc[2 * b + 1].T)
            else:
                block = jnp.where(low, first, 0.0)
            o_ref[:, 128 * b : 128 * b + 128] = block
            a_ref[:, 128 * b : 128 * b + 128] = block.astype(BF)

        @pl.when(pl.program_id(0) == steps - 1)
        def _():
            outward.wait()
            for copy in copies:
                copy.wait()

    return pl.pallas_call(
        kernel,
        name="attend_forward",
        grid=(steps,),
        in_specs=[
            pl.BlockSpec((TQ, 384), lambda i: (i, 0)),
            pl.BlockSpec((keys, 256), lambda i: (0, 0)),
            pl.BlockSpec((8, TQ), lambda i: (0, i)),
            pl.BlockSpec((keys, 128), lambda i: (0, 0)),
            pl.BlockSpec((keys, 128), lambda i: (0, 0)),
            pl.BlockSpec(memory_space=pl.ANY),
        ],
        out_specs=[
            pl.BlockSpec((TQ, 384), lambda i: (i, 0)),
            pl.BlockSpec((TQ, 384), lambda i: (i, 0)),
            pl.BlockSpec((8, TQ), lambda i: (0, i)),
            pl.BlockSpec(memory_space=pl.ANY),
        ],
        out_shape=[
            jax.ShapeDtypeStruct((rows, 384), BF),
            jax.ShapeDtypeStruct((rows, 384), F32),
            jax.ShapeDtypeStruct((8, rows), F32),
            jax.ShapeDtypeStruct((wsh, gate_up.shape[0], units), BF),
        ],
        scratch_shapes=[
            pltpu.VMEM((5, 128, TQ), F32),
            pltpu.VMEM((8, TQ), F32),
            pltpu.VMEM((8, TQ), F32),
            pltpu.VMEM((gate_up.shape[0], units), BF),
            pltpu.SemaphoreType.DMA((wsh,)),
            pltpu.SemaphoreType.DMA((wsh,)),
            pltpu.SemaphoreType.DMA,
        ],
        compiler_params=pltpu.CompilerParams(
            collective_id=2, has_side_effects=True, vmem_limit_bytes=VMEM_LIMIT
        ),
    )(q, kv, q_marks, k_pos, k_seg, gate_up)


def owner_of(link):
    ctx, wsh = link.sizes["ctx"], link.sizes["wsh"]
    my_c, my_w = lax.axis_index("ctx"), lax.axis_index("wsh")
    shard = my_w * ctx + my_c
    to_c, to_w = shard // wsh, lax.rem(shard, wsh)
    return {"ctx": to_c, "wsh": to_w}, jnp.logical_and(to_c == my_c, to_w == my_w)


BK = 384


def attend_backward(
    link, q, kv, q_marks, k_pos, k_seg, lse, out, out_grad, send_rows
):
    ctx = link.sizes["ctx"]
    rows, keys = q.shape[0], kv.shape[0]
    steps = rows // TQ
    span = keys // ctx
    levels = link.offsets(("ctx",))[1:]

    def kernel(
        q_ref, kv_ref, qm_ref, kp_ref, ks_ref, lse_ref, o_ref, do_ref, rows_ref,
        dq_ref, got_kv, got_rows,
        acc, heads, grads, delta, marks, lses, k_sum, v_sum, kv_send, bounce, send, recv, kv_out, kv_in, near,
    ):
        wires = Wires(send, recv)
        my_c = lax.axis_index("ctx")
        greet([link.place(("ctx",), offset)[0] for offset in levels])
        copies = []
        for offset in levels:
            where, index = link.place(("ctx",), offset)
            copies.append(wires.start(rows_ref.at[index], got_rows.at[my_c], where))
        inward = pltpu.make_async_copy(rows_ref.at[my_c], bounce, near.at[0])
        outward = pltpu.make_async_copy(bounce, got_rows.at[my_c], near.at[0])
        inward.start()
        acc[...] = jnp.zeros_like(acc)
        delta[...] = jnp.zeros_like(delta)
        for i in range(steps):
            at = slice(i * TQ, i * TQ + TQ)
            marks[i] = qm_ref[:, at]
            lses[i] = lse_ref[:, at]
            for j, (b, h) in enumerate(HEAD_SLOTS):
                lanes = slice(128 * b, 128 * b + 128)
                heads[i, j] = head_block(q_ref[at, lanes], h)
                grad = head_block(do_ref[at, lanes], h)
                grads[i, j] = grad
                product = grad.astype(F32) * o_ref[at, lanes]
                delta[i, j : j + 1, :] = jnp.sum(product.T, axis=0, keepdims=True)
        inward.wait()
        outward.start()

        @pl.loop(0, ctx)
        def _(d):
            chunk = lax.rem(my_c + 1 + d, ctx)

            @pl.loop(0, span // BK)
            def _(t):
                inner = pl.multiple_of(t * BK, 128)
                at = pl.ds(pl.multiple_of(chunk * span + t * BK, 128), BK)
                k_tile = kv_ref[at, :128]
                v_tile = kv_ref[at, 128:]
                key_pos = jnp.tile(kp_ref[at, :], (1, TQ // 128))
                key_seg = jnp.tile(ks_ref[at, :], (1, TQ // 128))
                k_sum[...] = jnp.zeros_like(k_sum)
                v_sum[...] = jnp.zeros_like(v_sum)

                @pl.loop(0, steps)
                def _(i):
                    seen = (key_pos <= marks[i, 0:1, :]) & (
                        (key_seg == 0) | (key_seg == marks[i, 1:2, :])
                    )
                    k_part = jnp.zeros((BK, 128), F32)
                    v_part = jnp.zeros((BK, 128), F32)
                    for j in range(5):
                        scores = dot_general(k_tile, heads[i, j], 1, 1)
                        probs = jnp.where(seen, jnp.exp(scores - lses[i, j : j + 1, :]), 0.0)
                        prob_grad = dot_general(v_tile, grads[i, j], 1, 1)
                        score_grad = (probs * (prob_grad - delta[i, j : j + 1, :])).astype(BF)
                        v_part += jnp.dot(
                            probs.astype(BF), grads[i, j], preferred_element_type=F32
                        )
                        k_part += jnp.dot(score_grad, heads[i, j], preferred_element_type=F32)
                        acc[i, j] += dot_general(k_tile, score_grad, 0, 0)
                    k_sum[...] += k_part
                    v_sum[...] += v_part

                kv_send[chunk, pl.ds(inner, BK), :128] = k_sum[...].astype(BF)
                kv_send[chunk, pl.ds(inner, BK), 128:] = v_sum[...].astype(BF)

            @pl.when(d < ctx - 1)
            def _():
                pltpu.make_async_remote_copy(
                    kv_send.at[chunk],
                    got_kv.at[my_c],
                    kv_out.at[d],
                    kv_in.at[d],
                    device_id={"ctx": chunk},
                    device_id_type=MESH,
                ).start()

        near_kv = pltpu.make_async_copy(kv_send.at[my_c], got_kv.at[my_c], near.at[1])
        near_kv.start()
        low = lax.broadcasted_iota(jnp.int32, (TQ, 128), 1) < 64
        for i in range(steps):
            for b in range(3):
                first = acc[i, 2 * b].T * 0.125
                if b < 2:
                    block = jnp.where(low, first, acc[i, 2 * b + 1].T * 0.125)
                else:
                    block = jnp.where(low, first, 0.0)
                dq_ref[i * TQ : i * TQ + TQ, 128 * b : 128 * b + 128] = block.astype(BF)

        near_kv.wait()
        outward.wait()
        for copy in copies:
            copy.wait()

        for d in range(ctx - 1):
            pltpu.make_async_remote_copy(
                kv_send.at[0],
                got_kv.at[0],
                kv_out.at[d],
                kv_in.at[d],
                device_id={"ctx": my_c},
                device_id_type=MESH,
            ).wait()

    vmem = pl.BlockSpec(memory_space=pltpu.VMEM)
    anywhere = pl.BlockSpec(memory_space=pl.ANY)
    return pl.pallas_call(
        kernel,
        name="attend_backward",
        in_specs=[vmem] * 8 + [anywhere],
        out_specs=[vmem] + [anywhere] * 2,
        out_shape=[
            jax.ShapeDtypeStruct((rows, 384), BF),
            jax.ShapeDtypeStruct((ctx, span, 256), BF),
            jax.ShapeDtypeStruct(send_rows.shape, BF),
        ],
        scratch_shapes=[
            pltpu.VMEM((steps, 5, 128, TQ), F32),
            pltpu.VMEM((steps, 5, TQ, 128), BF),
            pltpu.VMEM((steps, 5, TQ, 128), BF),
            pltpu.VMEM((steps, 8, TQ), F32),
            pltpu.VMEM((steps, 8, TQ), F32),
            pltpu.VMEM((steps, 8, TQ), F32),
            pltpu.VMEM((BK, 128), F32),
            pltpu.VMEM((BK, 128), F32),
            pltpu.VMEM((ctx, span, 256), BF),
            pltpu.VMEM(send_rows.shape[1:], BF),
            pltpu.SemaphoreType.DMA((ctx,)),
            pltpu.SemaphoreType.DMA((ctx,)),
            pltpu.SemaphoreType.DMA((ctx,)),
            pltpu.SemaphoreType.DMA((ctx,)),
            pltpu.SemaphoreType.DMA((2,)),
        ],
        compiler_params=pltpu.CompilerParams(
            collective_id=11, has_side_effects=True, vmem_limit_bytes=VMEM_LIMIT
        ),
    )(q, kv, q_marks, k_pos, k_seg, lse, out, out_grad, send_rows)


class Wires:
    def __init__(self, send, recv):
        self.send, self.recv, self.used = send, recv, 0

    def copy(self, source, target, where):
        at = self.used
        self.used += 1
        return pltpu.make_async_remote_copy(
            source,
            target,
            self.send.at[at],
            self.recv.at[at],
            device_id=where,
            device_id_type=MESH,
        )

    def start(self, source, target, where):
        copy = self.copy(source, target, where)
        copy.start()
        return copy


def greet(places):
    barrier = pltpu.get_barrier_semaphore()
    for where in places:
        pl.semaphore_signal(barrier, 1, device_id=where, device_id_type=MESH)
    pl.semaphore_wait(barrier, len(places))


def square():
    w = lax.axis_index("wsh")
    return w, w + 1 - 2 * lax.rem(w, 2), w + 2 - 4 * (w // 2), 3 - w


class SquareScatter:
    def __init__(self, wires, parts, near, total):
        self.wires, self.parts, self.near, self.total = wires, parts, near, total
        self.half = parts.shape[1] // 2
        self.a, self.b = pl.ds(0, self.half), pl.ds(self.half, self.half)
        self.own, self.x, self.y, self.z = square()
        self.pending = []

    def send_diagonal(self):
        wires, parts = self.wires, self.parts
        self.one = wires.start(parts.at[self.z, self.a], self.near.at[0], {"wsh": self.x})
        self.two = wires.start(parts.at[self.z, self.b], self.near.at[1], {"wsh": self.y})

    def send_x(self):
        self.pending.append(
            self.wires.start(
                self.parts.at[self.x, self.a], self.total.at[0, self.a], {"wsh": self.x}
            )
        )

    def send_y(self):
        self.pending.append(
            self.wires.start(
                self.parts.at[self.y, self.b], self.total.at[1, self.b], {"wsh": self.y}
            )
        )

    def relay(self):
        near, parts = self.near, self.parts
        self.one.wait()
        near[2] = (near[0].astype(F32) + parts[self.y, self.a].astype(F32)).astype(BF)
        self.pending.append(
            self.wires.start(near.at[2], self.total.at[1, self.a], {"wsh": self.y})
        )
        self.two.wait()
        near[3] = (near[1].astype(F32) + parts[self.x, self.b].astype(F32)).astype(BF)
        self.pending.append(
            self.wires.start(near.at[3], self.total.at[0, self.b], {"wsh": self.x})
        )

    def result(self):
        for copy in self.pending:
            copy.wait()
        return (
            self.parts[self.own].astype(F32)
            + self.total[0].astype(F32)
            + self.total[1].astype(F32)
        )


def square_scratch(rows):
    return [pltpu.VMEM((4, rows // 2, D), BF), pltpu.VMEM((2, rows, D), BF)]


class SquareGather:
    def __init__(self, wires, out):
        self.wires, self.out = wires, out
        half = out.shape[1] // 2
        self.a, self.b = pl.ds(0, half), pl.ds(half, half)
        self.own, self.x, self.y, self.z = square()

    def move(self, slot, part, to):
        return self.wires.start(self.out.at[slot, part], self.out.at[slot, part], {"wsh": to})

    def begin(self):
        self.xa = self.move(self.own, self.a, self.x)
        self.yb = self.move(self.own, self.b, self.y)
        self.xb = self.move(self.own, self.b, self.x)
        self.ya = self.move(self.own, self.a, self.y)

    def relay(self):
        self.xa.wait()
        self.one = self.move(self.x, self.a, self.y)
        self.yb.wait()
        self.two = self.move(self.y, self.b, self.x)

    def wait_x(self):
        self.xb.wait()

    def wait_y(self):
        self.ya.wait()

    def wait_z(self):
        self.one.wait()
        self.two.wait()


def feed(link, attended, w_out, tokens, gain, w_half, down, dy):
    ctx, wsh = link.sizes["ctx"], link.sizes["wsh"]
    own_rows = tokens.shape[0]
    plane = dy.shape[0]
    units = down.shape[0]
    chunk = D // ctx
    pick = units // ctx // 2

    def kernel(
        at_ref, ao_ref, x_ref, g_ref, wh_ref, dw_ref, dy_ref,
        mid_ref, mg_ref, br_ref, ag_ref, fs_ref, dp_ref, gs_ref, gl_ref, ds_ref,
        wo_ref, w_both, parts, near, total, near2, total2, n2, hgrad, hidden, gate_g, up_g,
        down_h, down_pair, down_send, down_got, gate_h, gate_pair, send, recv, local,
    ):
        wires = Wires(send, recv)
        core = lax.axis_index("grp")
        sibling = {"grp": 1 - core}
        my_c = lax.axis_index("ctx")
        own, x, y, z = square()
        levels = [link.place(("ctx",), offset) for offset in link.offsets(("ctx",))[1:]]
        greet([{"wsh": x}, {"wsh": y}, sibling] + [where for where, _ in levels])

        def rows_of(slot):
            return pl.ds(pl.multiple_of(slot * own_rows, 16), own_rows)

        w_copy = pltpu.make_async_copy(wh_ref, w_both.at[core], local)
        w_copy.start()

        odd = lax.rem(own, 2) == 1
        wo_ref[...] = jnp.zeros_like(wo_ref)

        def spread(pieces):
            at = 0
            for start, size in pieces:
                wo_ref[start : start + size, :] = ao_ref[at : at + size, :]
                at += size

        @pl.when(odd)
        def _():
            spread(ODD_ROWS)

        @pl.when(jnp.logical_not(odd))
        def _():
            spread(EVEN_ROWS)

        first = SquareScatter(wires, parts, near, total)
        for slot in (z, x, y, own):
            parts[slot] = jnp.dot(
                at_ref[rows_of(slot), :], wo_ref[...], preferred_element_type=F32
            ).astype(BF)
            if slot is z:
                first.send_diagonal()
            elif slot is x:
                first.send_x()
            elif slot is y:
                first.send_y()
        w_swap = wires.start(wh_ref, w_both.at[core], sibling)
        hgrad[...] = dot_general(dy_ref[...], dw_ref[...], 1, 1)
        first.relay()
        middle = x_ref[...].astype(F32) + first.result()
        mid_ref[...] = middle
        factor = lax.rsqrt(jnp.mean(middle * middle, axis=-1, keepdims=True) + EPSILON)
        n2[own] = (middle * factor * g_ref[1:2, :]).astype(BF)
        gather = SquareGather(wires, n2)
        gather.begin()
        w_copy.wait()
        w_swap.wait()

        def block(slot):
            at = rows_of(slot)
            gate = jnp.dot(n2[slot], w_both[0], preferred_element_type=F32)
            up = jnp.dot(n2[slot], w_both[1], preferred_element_type=F32)
            sigmoid = 1.0 / (1.0 + jnp.exp(-gate))
            silu = gate * sigmoid
            hidden[at, :] = (silu * up).astype(BF)
            back = hgrad[at, :]
            gate_g[at, :] = (back * up * sigmoid * (1.0 + gate * (1.0 - sigmoid))).astype(BF)
            up_g[at, :] = (back * silu).astype(BF)
            parts[slot] = (
                dot_general(gate_g[at, :], w_both[0], 1, 1)
                + dot_general(up_g[at, :], w_both[1], 1, 1)
            ).astype(BF)

        second = SquareScatter(wires, parts, near2, total2)
        block(own)
        gather.relay()
        gather.wait_x()
        block(x)
        second.send_x()
        gather.wait_y()
        block(y)
        second.send_y()
        gather.wait_z()
        block(z)
        second.send_diagonal()

        strip = dot_general(hidden[...], dy_ref[...], 0, 0).astype(BF)
        for k in range(ctx):
            for g in range(2):
                top = (2 * k + g) * pick
                down_h[g, k] = strip[top : top + pick, :]
        down_swap = wires.start(down_h.at[1 - core], down_pair, sibling)
        second.relay()
        tokens_all = n2[...].reshape(plane, D)
        for g, source in enumerate((gate_g, up_g)):
            strip = dot_general(tokens_all, source[...], 0, 0).astype(BF)
            for c in range(ctx):
                gate_h[g, c] = strip[c * chunk : c * chunk + chunk, :]
        gate_swap = wires.start(gate_h.at[1 - core], gate_pair, sibling)
        down_swap.wait()
        down_send[...] = (down_h[core].astype(F32) + down_pair[...].astype(F32)).astype(BF)
        down_copies = []
        for where, index in levels:
            down_copies.append(wires.start(down_send.at[index], down_got.at[my_c], where))
        down_got[my_c] = down_send[my_c]

        grad = second.result()
        middle = mid_ref[...]
        factor = lax.rsqrt(jnp.mean(middle * middle, axis=-1, keepdims=True) + EPSILON)
        weighted = grad * g_ref[1:2, :]
        inner = jnp.mean(weighted * middle, axis=-1, keepdims=True)
        middle_grad = (
            dy_ref[rows_of(own), :].astype(F32)
            + factor * weighted
            - middle * (factor * factor * factor) * inner
        )
        mg_ref[...] = middle_grad
        br_ref[own] = middle_grad.astype(BF)
        branch = SquareGather(wires, br_ref)
        branch.begin()
        fs_ref[...] = jnp.sum(grad * middle * factor, axis=0, keepdims=True)

        def outward(slot):
            ag_ref[rows_of(slot), :] = dot_general(br_ref[slot], wo_ref[...], 1, 1).astype(BF)

        outward(own)
        gate_swap.wait()
        for c in range(ctx):
            both = (gate_h[core, c].astype(F32) + gate_pair[c].astype(F32)).astype(BF)
            gs_ref[c] = both[:, : units // 2]
            gl_ref[c] = both[:, units // 2 :]
        branch.relay()
        for slot in range(wsh):
            at = slice(slot * own_rows, slot * own_rows + own_rows)
            dp_ref[slot] = jnp.dot(
                hidden[at, :], dw_ref[...], preferred_element_type=F32
            ).astype(BF)
        branch.wait_x()
        outward(x)
        branch.wait_y()
        outward(y)
        branch.wait_z()
        outward(z)
        for copy in down_copies:
            copy.wait()
        ds_ref[...] = jnp.sum(down_got[...].astype(F32), axis=0).astype(BF)

    operands = (attended, w_out, tokens, gain, w_half, down, dy)
    vmem = pl.BlockSpec(memory_space=pltpu.VMEM)
    return pl.pallas_call(
        kernel,
        name="feed",
        in_specs=[vmem] * len(operands),
        out_specs=[vmem] * 9,
        out_shape=[
            jax.ShapeDtypeStruct((own_rows, D), F32),
            jax.ShapeDtypeStruct((own_rows, D), F32),
            jax.ShapeDtypeStruct((wsh, own_rows, D), BF),
            jax.ShapeDtypeStruct((plane, 384), BF),
            jax.ShapeDtypeStruct((1, D), F32),
            jax.ShapeDtypeStruct((wsh, own_rows, D), BF),
            jax.ShapeDtypeStruct((ctx, chunk, units // 2), BF),
            jax.ShapeDtypeStruct((ctx, chunk, units // 2), BF),
            jax.ShapeDtypeStruct((pick, D), BF),
        ],
        scratch_shapes=[
            pltpu.VMEM((384, D), BF),
            pltpu.VMEM((2, D, units), BF),
            pltpu.VMEM((4, own_rows, D), BF),
            *square_scratch(own_rows),
            *square_scratch(own_rows),
            pltpu.VMEM((4, own_rows, D), BF),
            pltpu.VMEM((plane, units), F32),
            *[pltpu.VMEM((plane, units), BF)] * 3,
            pltpu.VMEM((2, ctx, pick, D), BF),
            *[pltpu.VMEM((ctx, pick, D), BF)] * 3,
            pltpu.VMEM((2, ctx, chunk, units), BF),
            pltpu.VMEM((ctx, chunk, units), BF),
            pltpu.SemaphoreType.DMA((ctx + 28,)),
            pltpu.SemaphoreType.DMA((ctx + 28,)),
            pltpu.SemaphoreType.DMA,
        ],
        compiler_params=pltpu.CompilerParams(
            collective_id=3, has_side_effects=True, vmem_limit_bytes=VMEM_LIMIT
        ),
    )(*operands)


def head(link, tokens, gain, weight, marks, upstream):
    ctx, wsh = link.sizes["ctx"], link.sizes["wsh"]
    own_rows = tokens.shape[0]
    plane, group = own_rows * wsh, own_rows * wsh * ctx
    half = weight.shape[0] // 2

    def kernel(
        x_ref, g_ref, w_ref, m_ref, up_ref,
        q_ref, kv_ref, n_ref, wq_ref, kpos_ref, kseg_ref, q_marks, dy_ref, c_ref, s_ref,
        cols, mine, marks_all, send, recv,
    ):
        wires = Wires(send, recv)
        core = lax.axis_index("grp")
        sibling = {"grp": 1 - core}
        my_c = lax.axis_index("ctx")
        own, x, y, z = square()
        levels = [link.place(("ctx",), offset) for offset in link.offsets(("ctx",))[1:]]
        greet(
            [{"wsh": x}, {"wsh": y}, {"wsh": z}, sibling] + [where for where, _ in levels]
        )
        mine[...] = jnp.zeros_like(mine)
        mine[:2, :own_rows] = m_ref[...]
        mark_copies = []
        for p in (x, y, z):
            mark_copies.append(wires.start(mine, marks_all.at[my_c, own], {"wsh": p}))
        marks_all[my_c, own] = mine[...]
        side = pl.ds(pl.multiple_of(core * half, 16), half)

        for w in range(wsh):
            q_order, kv_order = head_plan(w)
            slots = [h for h in q_order] + [HEADS + h for h in kv_order]
            slots += [HEADS + KV_HEADS + h for h in kv_order]
            blank = jnp.zeros((w_ref.shape[0], HEAD_DIM), BF)
            for pair in range(5):
                two = [
                    blank if h is None else w_ref[:, h * HEAD_DIM : h * HEAD_DIM + HEAD_DIM]
                    for h in slots[2 * pair : 2 * pair + 2]
                ]
                cols[w, :, 128 * pair : 128 * pair + 128] = jnp.concatenate(two, axis=1)
        w_copies = []
        for p in (x, y, z):
            w_copies.append(
                wires.start(cols.at[p, side], wq_ref.at[own, side], {"wsh": p})
            )
        tokens_in = x_ref[...].astype(F32)
        factor = lax.rsqrt(jnp.mean(tokens_in * tokens_in, axis=-1, keepdims=True) + EPSILON)
        n_ref[own] = (tokens_in * factor * g_ref[0:1, :]).astype(BF)
        wq_ref[own] = cols[own]
        dy_ref[own] = up_ref[...]

        for copy in mark_copies:
            copy.wait()
        level_copies = []
        for where, _ in levels:
            level_copies.append(wires.start(marks_all.at[my_c], marks_all.at[my_c], where))
        lane = lax.broadcasted_iota(jnp.int32, (1, 128), 1)
        power = lax.rem(lane, 32).astype(F32) * (-math.log(10000.0) / 32)
        frequency = jnp.exp(power)
        sign = jnp.where(lax.rem(lane, 64) < 32, -1.0, 1.0)

        def upright(row):
            return jnp.broadcast_to(row, (128, row.shape[1])).T

        for w in range(wsh):
            at = slice(w * own_rows, w * own_rows + own_rows)
            angles = upright(marks_all[my_c, w, 0:1, :])[:own_rows] * frequency
            c_ref[at, :] = jnp.cos(angles)
            s_ref[at, :] = jnp.sin(angles) * sign
        forward = []
        for p, copy in zip((x, y, z), w_copies):
            copy.wait()
            forward.append(wires.start(wq_ref.at[p, side], wq_ref.at[p, side], sibling))
        gather = SquareGather(wires, n_ref)
        gather.begin()
        for copy in forward:
            copy.wait()

        low = lax.rem(lax.broadcasted_iota(jnp.int32, (own_rows, 128), 1), 64) < 32
        kv_copies = []

        def block(slot):
            at = pl.ds(pl.multiple_of(slot * own_rows, 16), own_rows)
            full = jnp.dot(
                n_ref[slot], wq_ref[...].reshape(D, 640), preferred_element_type=F32
            )
            cos_t, sin_t = c_ref[at, :], s_ref[at, :]
            for b in range(3):
                turned = turn(full[:, 128 * b : 128 * b + 128], cos_t, sin_t, low)
                q_ref[at, 128 * b : 128 * b + 128] = (
                    turned.astype(BF).astype(F32) * 0.125
                ).astype(BF)
            kv_ref[my_c, at, :128] = turn(full[:, 384:512], cos_t, sin_t, low).astype(BF)
            kv_ref[my_c, at, 128:] = full[:, 512:].astype(BF)
            for where, _ in levels:
                kv_copies.append(
                    wires.start(kv_ref.at[my_c, at], kv_ref.at[my_c, at], where)
                )

        block(own)
        gather.relay()
        dy_gather = SquareGather(wires, dy_ref)
        dy_gather.begin()
        gather.wait_x()
        block(x)
        gather.wait_y()
        block(y)
        gather.wait_z()
        block(z)
        dy_gather.relay()

        for copy in level_copies:
            copy.wait()
        for w in range(wsh):
            q_marks[:, w * own_rows : w * own_rows + own_rows] = marks_all[my_c, w, :, :own_rows]

        @pl.loop(0, ctx)
        def _(c):
            for w in range(wsh):
                at = pl.ds(pl.multiple_of(c * plane + w * own_rows, 16), own_rows)
                kpos_ref[at, :] = upright(marks_all[c, w, 0:1, :])[:own_rows]
                kseg_ref[at, :] = upright(marks_all[c, w, 1:2, :])[:own_rows]

        dy_gather.wait_x()
        dy_gather.wait_y()
        dy_gather.wait_z()
        for copy in kv_copies:
            copy.wait()

    operands = (tokens, gain, weight, marks, upstream)
    vmem = pl.BlockSpec(memory_space=pltpu.VMEM)
    return pl.pallas_call(
        kernel,
        name="head",
        in_specs=[vmem] * len(operands),
        out_specs=[vmem] * 10,
        out_shape=[
            jax.ShapeDtypeStruct((plane, 384), BF),
            jax.ShapeDtypeStruct((ctx, plane, 256), BF),
            jax.ShapeDtypeStruct((wsh, own_rows, D), BF),
            jax.ShapeDtypeStruct((wsh, 2 * half, 640), BF),
            jax.ShapeDtypeStruct((group, 128), F32),
            jax.ShapeDtypeStruct((group, 128), F32),
            jax.ShapeDtypeStruct((8, plane), F32),
            jax.ShapeDtypeStruct((wsh, own_rows, D), BF),
            jax.ShapeDtypeStruct((plane, 128), F32),
            jax.ShapeDtypeStruct((plane, 128), F32),
        ],
        scratch_shapes=[
            pltpu.VMEM((wsh, 2 * half, 640), BF),
            pltpu.VMEM((8, 256), F32),
            pltpu.VMEM((ctx, wsh, 8, 256), F32),
            pltpu.SemaphoreType.DMA((5 * ctx + 24,)),
            pltpu.SemaphoreType.DMA((5 * ctx + 24,)),
        ],
        compiler_params=pltpu.CompilerParams(
            collective_id=1, has_side_effects=True, vmem_limit_bytes=VMEM_LIMIT
        ),
    )(*operands)


def finish(
    link, q_grad, kv_grad, weight, cos, sin, normed, tokens, gain, middle_grad, gate_got, down_got,
    attended, branch, feed_sum, down_part, middle, gate_late,
):
    ctx, wsh = link.sizes["ctx"], link.sizes["wsh"]
    shards = ctx * wsh
    rows = D // shards
    chunk = D // ctx
    fold = ctx // wsh
    own_rows = tokens.shape[0]
    plane = normed.shape[0]
    axes = ("ctx", "wsh")
    peers = link.offsets(axes)
    gate_width = gate_got.shape[2]
    down_rows = down_got.shape[0]

    def kernel(
        q_ref, kv_ref, w_ref, c_ref, s_ref, n_ref, x_ref, g_ref, mg_ref, gate_ref, down_ref,
        at_ref, br_ref, fs_ref, dp_ref, mid_ref, late_ref,
        act_ref, ig_ref, q_fin, kv_fin, out_fin, gate_fin, late_fin, down_fin, gains_out,
        pg, parts, near, total, near2, total2, wide, q_own, q_pair, q_send, q_got,
        q_mid, kv_own, kv_pair, kv_go, kv_got, kv_mid, gate_mid, late_got,
        late_mid, out_halves,
        out_pair, out_send, out_mid, out_got, gains, gains_got, gains_fin,
        send, recv,
    ):
        wires = Wires(send, recv)
        core = lax.axis_index("grp")
        first, second = core == 0, core == 1
        sibling = {"grp": 1 - core}
        my_c, my_w = lax.axis_index("ctx"), lax.axis_index("wsh")
        odd = lax.rem(my_w, 2) == 1
        greet([link.place(axes, offset)[0] for offset in peers[1:]] + [sibling])
        _, me = link.place(axes, peers[0])

        def over_ctx(got, mid):
            for w in range(wsh):
                strip = got[0, w * rows : w * rows + rows, :].astype(F32)
                for c in range(1, ctx):
                    strip += got[c, w * rows : w * rows + rows, :].astype(F32)
                mid[w] = strip.astype(BF)

        def in_plane(mid, slot_of):
            copies = []
            for offset in link.offsets(("wsh",))[1:]:
                where, index = link.place(("wsh",), offset)
                copies.append(wires.copy(mid.at[index], slot_of(my_w), where))
            return copies

        def begin(cond, *copies):
            @pl.when(cond)
            def _():
                for copy in copies:
                    copy.start()

        levels = [link.place(("ctx",), offset) for offset in link.offsets(("ctx",))[1:]]
        late_copies = []
        for where, index in levels:
            late_copies.append(wires.start(late_ref.at[index], late_got.at[my_c], where))

        owner, stays = owner_of(link)
        moves = jnp.logical_not(stays)
        down_move = wires.copy(down_ref, down_fin.at[core], owner)
        begin(moves, down_move)

        @pl.when(stays)
        def _():
            down_fin[core] = down_ref[...]

        low = lax.rem(lax.broadcasted_iota(jnp.int32, (own_rows, 128), 1), 64) < 32
        scatter = SquareScatter(wires, parts, near, total)
        gain_sum = jnp.zeros((1, D), F32)
        for slot in (scatter.z, scatter.x, scatter.y, scatter.own):
            at = pl.ds(pl.multiple_of(slot * own_rows, 16), own_rows)
            cos_t, sin_t = c_ref[at, :], -s_ref[at, :]
            for b in range(3):
                block = q_ref[at, 128 * b : 128 * b + 128].astype(F32)
                pg[at, 128 * b : 128 * b + 128] = turn(block, cos_t, sin_t, low).astype(BF)
            summed = kv_ref[0, at, :].astype(F32)
            for c in range(1, ctx):
                summed += kv_ref[c, at, :].astype(F32)
            block = summed[:, :128].astype(BF).astype(F32)
            pg[at, 384:512] = turn(block, cos_t, sin_t, low).astype(BF)
            pg[at, 512:] = summed[:, 128:].astype(BF)
            part = dot_general(pg[at, :], w_ref[...], 1, 1)
            parts[slot] = part.astype(BF)
            gain_sum += jnp.sum(part * n_ref[at, :].astype(F32), axis=0, keepdims=True)
            if slot is scatter.z:
                scatter.send_diagonal()
            elif slot is scatter.x:
                scatter.send_x()
            elif slot is scatter.y:
                scatter.send_y()

        strip = dot_general(n_ref[...], pg[:, 384:], 0, 0).astype(BF)
        for c in range(ctx):
            kv_own[c] = strip[c * chunk : c * chunk + chunk, :]
        kv_swap = wires.copy(kv_own, kv_pair, sibling)
        begin(first, kv_swap)
        scatter.relay()
        strip = dot_general(n_ref[...], pg[:, :384], 0, 0).astype(BF)
        for c in range(ctx):
            q_own[c] = strip[c * chunk : c * chunk + chunk, :]
        q_swap = wires.copy(q_own, q_pair, sibling)
        begin(second, q_swap)
        layer = SquareScatter(wires, dp_ref, near2, total2)
        layer.send_diagonal()
        layer.send_x()
        layer.send_y()
        wide[...] = dot_general(at_ref[...], br_ref[...], 0, 0)

        def out_strips(pieces):
            at = 0
            for start, size in pieces:
                acc_rows = wide[start : start + size, :].astype(BF)
                part = jnp.concatenate([acc_rows[:, :576], jnp.zeros((size, 64), BF)], axis=1)
                out_halves[0, at : at + size, :] = part
                part = jnp.concatenate([acc_rows[:, 576:], jnp.zeros((size, 64), BF)], axis=1)
                out_halves[1, at : at + size, :] = part
                at += size

        @pl.when(odd)
        def _():
            out_strips(ODD_ROWS)

        @pl.when(jnp.logical_not(odd))
        def _():
            out_strips(EVEN_ROWS)

        out_swap = wires.start(out_halves.at[1 - core], out_pair, sibling)
        q_copies, kvg_copies, out_copies = [], [], []
        for where, index in levels:
            q_copies.append(wires.copy(q_send.at[index], q_got.at[my_c], where))
            kvg_copies.append(wires.copy(kv_go.at[index], kv_got.at[my_c], where))

        @pl.when(first)
        def _():
            q_swap.wait_recv()

            @pl.loop(0, ctx)
            def _(c):
                q_send[c] = (q_own[c].astype(F32) + q_pair[c].astype(F32)).astype(BF)

            for copy in q_copies:
                copy.start()
            q_got[my_c] = q_send[my_c]
            kv_swap.wait_send()

        @pl.when(second)
        def _():
            kv_swap.wait_recv()

            @pl.loop(0, ctx)
            def _(c):
                kv_go[c] = (kv_own[c].astype(F32) + kv_pair[c].astype(F32)).astype(BF)

            for copy in kvg_copies:
                copy.start()
            kv_got[my_c] = kv_go[my_c]
            q_swap.wait_send()

        both = jnp.concatenate([gain_sum / g_ref[0:1, :], fs_ref[...]], axis=0)
        gains[...] = jnp.zeros_like(gains)
        for s in range(shards):
            gains[s, :2, :rows] = both[:, rows * s : rows * s + rows]
        gain_copies = []
        for offset in peers[1:]:
            where, index = link.place(axes, offset)
            gain_copies.append(wires.start(gains.at[index], gains_got.at[me], where))
        gains_got[me] = gains[me]
        layer.relay()

        out_swap.wait()
        for k in range(ctx):
            strip = slice(k * rows, k * rows + rows)
            out_send[k % wsh, k // wsh] = (
                out_halves[core, strip, :].astype(F32) + out_pair[strip, :].astype(F32)
            ).astype(BF)
        out_moves = in_plane(out_send, lambda w: out_mid.at[w])
        for copy in out_moves:
            copy.start()
        out_mid[my_w] = out_send[my_w]

        grad = scatter.result()
        x = x_ref[...].astype(F32)
        factor = lax.rsqrt(jnp.mean(x * x, axis=-1, keepdims=True) + EPSILON)
        weighted = grad * g_ref[0:1, :]
        inner = jnp.mean(weighted * x, axis=-1, keepdims=True)
        ig_ref[...] = mg_ref[...] + factor * weighted - x * (factor * factor * factor) * inner
        for copy in out_moves:
            copy.wait()
        for where, index in levels:
            part = out_mid.at[index // fold, lax.rem(index, fold)]
            out_copies.append(wires.start(part, out_got.at[my_c], where))
        out_got[my_c] = out_mid[my_c // fold, lax.rem(my_c, fold)]


        @pl.when(moves)
        def _():
            down_move.wait()

        down_copy = wires.start(down_fin.at[core], down_fin.at[core], sibling)
        over_ctx(gate_ref, gate_mid)
        gate_moves = in_plane(gate_mid, lambda w: gate_fin.at[core, w])
        for copy in gate_moves:
            copy.start()
        gate_fin[core, my_w] = gate_mid[my_w]
        for copy in late_copies:
            copy.wait()
        late_got[my_c] = late_ref[my_c]
        over_ctx(late_got, late_mid)
        late_moves = in_plane(late_mid, lambda w: late_fin.at[core, w])
        for copy in late_moves:
            copy.start()
        late_fin[core, my_w] = late_mid[my_w]
        act_ref[...] = (mid_ref[...] + layer.result()).astype(BF)

        q_moves = in_plane(q_mid, lambda w: q_fin.at[w])
        kv_moves = in_plane(kv_mid, lambda w: kv_fin.at[w])

        @pl.when(first)
        def _():
            for copy in q_copies:
                copy.wait()
            over_ctx(q_got, q_mid)
            for copy in q_moves:
                copy.start()
            q_fin[my_w] = q_mid[my_w]

        @pl.when(second)
        def _():
            for copy in kvg_copies:
                copy.wait()
            over_ctx(kv_got, kv_mid)
            for copy in kv_moves:
                copy.start()
            kv_fin[my_w] = kv_mid[my_w]

        for copy in gate_moves + late_moves:
            copy.wait()
        gate_copy = wires.start(gate_fin.at[core], gate_fin.at[core], sibling)
        late_copy = wires.start(late_fin.at[core], late_fin.at[core], sibling)
        for copy in out_copies:
            copy.wait()
        out_fin[core] = jnp.sum(out_got[...].astype(F32), axis=0).astype(BF)
        out_copy = wires.start(out_fin.at[core], out_fin.at[core], sibling)
        for copy in gain_copies:
            copy.wait()
        gains_fin[core] = jnp.sum(gains_got[...], axis=0)
        gain_copy = wires.start(gains_fin.at[core], gains_fin.at[core], sibling)
        q_final = wires.copy(q_fin, q_fin, sibling)
        kv_final = wires.copy(kv_fin, kv_fin, sibling)

        @pl.when(first)
        def _():
            for copy in q_moves:
                copy.wait()
            q_final.start()

        @pl.when(second)
        def _():
            for copy in kv_moves:
                copy.wait()
            kv_final.start()

        down_copy.wait()
        gate_copy.wait()
        late_copy.wait()
        out_copy.wait()

        @pl.when(first)
        def _():
            q_final.wait_send()
            kv_final.wait_recv()

        @pl.when(second)
        def _():
            kv_final.wait_send()
            q_final.wait_recv()

        gain_copy.wait()
        gains_out[...] = gains_fin[0] + gains_fin[1]

    operands = (
        q_grad, kv_grad, weight, cos, sin, normed, tokens, gain, middle_grad, gate_got, down_got,
        attended, branch, feed_sum, down_part, middle, gate_late,
    )
    vmem = pl.BlockSpec(memory_space=pltpu.VMEM)
    return pl.pallas_call(
        kernel,
        name="finish",
        in_specs=[vmem] * len(operands),
        out_specs=[vmem] * 9,
        out_shape=[
            jax.ShapeDtypeStruct((own_rows, D), BF),
            jax.ShapeDtypeStruct((own_rows, D), F32),
            jax.ShapeDtypeStruct((wsh, rows, 384), BF),
            jax.ShapeDtypeStruct((wsh, rows, 256), BF),
            jax.ShapeDtypeStruct((2, rows, 640), BF),
            jax.ShapeDtypeStruct((2, wsh, rows, gate_width), BF),
            jax.ShapeDtypeStruct((2, wsh, rows, gate_width), BF),
            jax.ShapeDtypeStruct((2, down_rows, D), BF),
            jax.ShapeDtypeStruct((8, 128), F32),
        ],
        scratch_shapes=[
            pltpu.VMEM((plane, 640), BF),
            pltpu.VMEM((4, own_rows, D), BF),
            *square_scratch(own_rows),
            *square_scratch(own_rows),
            pltpu.VMEM((384, D), F32),
            *[pltpu.VMEM((ctx, chunk, 384), BF)] * 4,
            pltpu.VMEM((wsh, rows, 384), BF),
            *[pltpu.VMEM((ctx, chunk, 256), BF)] * 4,
            pltpu.VMEM((wsh, rows, 256), BF),
            pltpu.VMEM((wsh, rows, gate_width), BF),
            pltpu.VMEM((ctx, chunk, gate_width), BF),
            pltpu.VMEM((wsh, rows, gate_width), BF),
            pltpu.VMEM((2, 288, 640), BF),
            pltpu.VMEM((288, 640), BF),
            pltpu.VMEM((wsh, fold, rows, 640), BF),
            pltpu.VMEM((wsh, fold, rows, 640), BF),
            pltpu.VMEM((ctx, rows, 640), BF),
            pltpu.VMEM((shards, 8, 128), F32),
            pltpu.VMEM((shards, 8, 128), F32),
            pltpu.VMEM((2, 8, 128), F32),
            pltpu.SemaphoreType.DMA((shards + 5 * ctx + 48,)),
            pltpu.SemaphoreType.DMA((shards + 5 * ctx + 48,)),
        ],
        compiler_params=pltpu.CompilerParams(
            collective_id=8, has_side_effects=True, vmem_limit_bytes=VMEM_LIMIT
        ),
    )(*operands)


def wrap(act, input_grad, q_sum, kv_sum, out_sum, gate_sum, late_sum, down_sum):
    wsh, rows, _ = q_sum.shape
    down_rows = down_sum.shape[1]
    width = gate_sum.shape[3]

    def kernel(
        act_in, ig_in, q_in, kv_in, out_in, gate_in, late_in, down_in,
        act_ref, ig_ref, qkv_ref, out_ref, gate_ref, down_ref,
    ):
        act_ref[...] = act_in[...]
        ig_ref[...] = ig_in[...]
        qkv_ref[...] = qkv_restore(
            [
                jnp.concatenate([q_in[w].astype(F32), kv_in[w].astype(F32)], axis=1)
                for w in range(wsh)
            ]
        )
        out_ref[...] = jnp.concatenate(
            [out_in[0, :, :576].astype(F32), out_in[1, :, :576].astype(F32)], axis=1
        )
        for half in range(2):
            for w in range(wsh):
                left = (half * wsh + w) * 2 * width
                gate_ref[:, left : left + width] = gate_in[half, w].astype(F32)
                left += width
                gate_ref[:, left : left + width] = late_in[half, w].astype(F32)
            down_ref[half * down_rows : half * down_rows + down_rows, :] = down_in[half].astype(
                F32
            )

    vmem = pl.BlockSpec(memory_space=pltpu.VMEM)
    return pl.pallas_call(
        kernel,
        name="wrap",
        in_specs=[vmem] * 8,
        out_specs=[vmem] * 6,
        out_shape=[
            jax.ShapeDtypeStruct(act.shape, BF),
            jax.ShapeDtypeStruct(act.shape, F32),
            jax.ShapeDtypeStruct((rows, QW + 2 * KW), F32),
            jax.ShapeDtypeStruct((rows, D), F32),
            jax.ShapeDtypeStruct((rows, 2 * FF), F32),
            jax.ShapeDtypeStruct((2 * down_rows, D), F32),
        ],
        compiler_params=pltpu.CompilerParams(vmem_limit_bytes=VMEM_LIMIT),
    )(act, input_grad, q_sum, kv_sum, out_sum, gate_sum, late_sum, down_sum)


def build(sizes):
    ctx, wsh = sizes["ctx"], sizes["wsh"]
    shards = ctx * wsh
    link = Exchange(sizes)

    def local(
        tokens,
        segment_ids,
        positions,
        attend_gain,
        query_key_value,
        attend_out,
        feed_gain,
        gate_up,
        down_weight,
        upstream,
    ):
        own = tokens.shape[0]
        plane = own * wsh
        group = plane * ctx
        marks = jnp.stack([positions, segment_ids]).astype(F32)
        both_gains = jnp.stack([attend_gain, feed_gain])
        (
            queries,
            kv_all,
            normed_all,
            w_qkv,
            k_pos,
            k_seg,
            q_marks,
            dy_all,
            cos,
            sin,
        ) = head(link, tokens, both_gains, query_key_value, marks, upstream)
        kv_all = kv_all.reshape(group, 256)
        normed_all, dy_all = normed_all.reshape(plane, D), dy_all.reshape(plane, D)
        w_qkv = w_qkv.reshape(D, 640)
        attended, attended_wide, lse, w_half = attend_forward(
            link, queries, kv_all, q_marks, k_pos, k_seg, gate_up
        )
        w_half = w_half.reshape(D, FF // wsh)
        (
            middle,
            middle_grad,
            branch_all,
            attended_grad,
            feed_sum,
            down_part,
            gate_send,
            gate_late,
            down_sum,
        ) = feed(link, attended, attend_out, tokens, both_gains, w_half, down_weight, dy_all)
        q_grad, kv_grad, gate_got = attend_backward(
            link, queries, kv_all, q_marks, k_pos, k_seg, lse, attended_wide, attended_grad,
            gate_send,
        )
        *sums, gain_out = finish(
            link, q_grad, kv_grad, w_qkv, cos, sin, normed_all, tokens,
            both_gains, middle_grad, gate_got, down_sum, attended,
            branch_all.reshape(plane, D), feed_sum, down_part, middle, gate_late,
        )
        activations, input_grad, qkv_out, out_out, gate_out, down_out = wrap(*sums)
        width = D // shards
        return (
            activations,
            input_grad,
            qkv_out,
            out_out,
            gate_out,
            down_out,
            gain_out[0, :width],
            gain_out[1, :width],
        )

    return local


def solution(mesh):
    whole = ("grp", "ctx", "wsh")
    in_specs = (
        P(whole, None),
        P(whole),
        P(whole),
        P(),
        P("wsh", None),
        P("wsh", None),
        P(),
        P("wsh", None),
        P("wsh", None),
        P(whole, None),
    )
    out_specs = (
        P(whole, None),
        P(whole, None),
        P(("ctx", "wsh"), None),
        P(("ctx", "wsh"), None),
        P(("ctx", "wsh"), None),
        P(("ctx", "wsh"), None),
        P(("ctx", "wsh")),
        P(("ctx", "wsh")),
    )
    return jax.shard_map(
        build(dict(mesh.shape)), mesh=mesh, in_specs=in_specs, out_specs=out_specs, check_vma=False
    )
```

```python
import itertools
import math

import jax
import jax.numpy as jnp
from jax import lax
from jax.experimental import pallas as pl
from jax.experimental.pallas import tpu as pltpu
from jax.sharding import PartitionSpec as P

HEADS = 18
KV_HEADS = 6
HEAD_DIM = 64
FF = 3072
D = 1152
QW = 1152
KW = 384
EPSILON = 1e-05
MESH = pl.DeviceIdType.MESH
F32 = jnp.float32
BF = jnp.bfloat16
VMEM_LIMIT = 56 << 20


def dot_general(a, b, ca, cb):
    return lax.dot_general(a, b, (((ca,), (cb,)), ((), ())), preferred_element_type=F32)


class Exchange:
    def __init__(self, sizes):
        self.sizes = sizes

    def place(self, axes, offset):
        where, index = {}, 0
        for axis, step in zip(axes, offset):
            size = self.sizes[axis]
            spot = lax.axis_index(axis)
            if step:
                spot = lax.rem(spot + step, size)
            where[axis] = spot
            index = index * size + spot
        return where, index

    def offsets(self, axes):
        return list(itertools.product(*[range(self.sizes[axis]) for axis in axes]))


def head_plan(w):
    pair, odd = w // 2, w % 2
    start = 9 * pair + 4 * odd
    if odd:
        f_heads, h_heads = [start + 2, start + 3, start + 4], [start, start + 1]
        f_kv, h_kv = 3 * pair + 2, 3 * pair + 1
    else:
        f_heads, h_heads = [start, start + 1, start + 2], [start + 3, start + 4]
        f_kv, h_kv = 3 * pair, 3 * pair + 1
    q_order = [f_heads[0], h_heads[0], f_heads[1], h_heads[1], f_heads[2], None]
    return q_order, [f_kv, h_kv]


def qkv_restore(parts):
    found = {}
    for w in range(4):
        q_order, kv_order = head_plan(w)
        slots = list(q_order) + [HEADS + h for h in kv_order]
        slots += [HEADS + KV_HEADS + h for h in kv_order]
        for at, head in enumerate(slots):
            if head is not None:
                found.setdefault(head, []).append(
                    parts[w][:, at * HEAD_DIM : (at + 1) * HEAD_DIM]
                )
    pieces = []
    for head in range(HEADS + 2 * KV_HEADS):
        term = found[head][0]
        for other in found[head][1:]:
            term = term + other
        pieces.append(term)
    return jnp.concatenate(pieces, axis=1)


def turn(x, cos, sin, lanes):
    swapped = jnp.where(lanes, pltpu.roll(x, 96, 1), pltpu.roll(x, 32, 1))
    return x * cos + swapped * sin


TQ = 256


def head_block(block, head):
    low = lax.broadcasted_iota(jnp.int32, block.shape, 1) < 64
    return jnp.where(low if head == 0 else jnp.logical_not(low), block, jnp.zeros_like(block))


ODD_ROWS = [(96, 32), (192, 64), (0, 64), (128, 64), (256, 64)]
EVEN_ROWS = [(0, 64), (128, 64), (256, 64), (64, 64), (192, 32)]
HEAD_SLOTS = [(0, 0), (0, 1), (1, 0), (1, 1), (2, 0)]


BK = 384


def attend_backward(
    link, q, kv, q_marks, k_pos, k_seg, lse, out, out_grad, send_rows
):
    ctx = link.sizes["ctx"]
    rows, keys = q.shape[0], kv.shape[0]
    steps = rows // TQ
    span = keys // ctx
    levels = link.offsets(("ctx",))[1:]

    def kernel(
        q_ref, kv_ref, qm_ref, kp_ref, ks_ref, lse_ref, o_ref, do_ref, rows_ref,
        dq_ref, got_kv, got_rows,
        acc, heads, grads, delta, marks, lses, k_sum, v_sum, kv_send, bounce, send, recv, kv_out, kv_in, near,
    ):
        wires = Wires(send, recv)
        my_c = lax.axis_index("ctx")
        greet([link.place(("ctx",), offset)[0] for offset in levels])
        copies = []
        for offset in levels:
            where, index = link.place(("ctx",), offset)
            copies.append(wires.start(rows_ref.at[index], got_rows.at[my_c], where))
        inward = pltpu.make_async_copy(rows_ref.at[my_c], bounce, near.at[0])
        outward = pltpu.make_async_copy(bounce, got_rows.at[my_c], near.at[0])
        inward.start()
        acc[...] = jnp.zeros_like(acc)
        delta[...] = jnp.zeros_like(delta)
        for i in range(steps):
            at = slice(i * TQ, i * TQ + TQ)
            marks[i] = qm_ref[:, at]
            lses[i] = lse_ref[:, at]
            for j, (b, h) in enumerate(HEAD_SLOTS):
                lanes = slice(128 * b, 128 * b + 128)
                heads[i, j] = head_block(q_ref[at, lanes], h)
                grad = head_block(do_ref[at, lanes], h)
                grads[i, j] = grad
                product = grad.astype(F32) * o_ref[at, lanes]
                delta[i, j : j + 1, :] = jnp.sum(product.T, axis=0, keepdims=True)
        inward.wait()
        outward.start()

        @pl.loop(0, ctx)
        def _(d):
            chunk = lax.rem(my_c + 1 + d, ctx)

            @pl.loop(0, span // BK)
            def _(t):
                inner = pl.multiple_of(t * BK, 128)
                at = pl.ds(pl.multiple_of(chunk * span + t * BK, 128), BK)
                k_tile = kv_ref[at, :128]
                v_tile = kv_ref[at, 128:]
                key_pos = jnp.tile(kp_ref[at, :], (1, TQ // 128))
                key_seg = jnp.tile(ks_ref[at, :], (1, TQ // 128))
                k_sum[...] = jnp.zeros_like(k_sum)
                v_sum[...] = jnp.zeros_like(v_sum)

                @pl.loop(0, steps)
                def _(i):
                    seen = (key_pos <= marks[i, 0:1, :]) & (
                        (key_seg == 0) | (key_seg == marks[i, 1:2, :])
                    )
                    k_part = jnp.zeros((BK, 128), F32)
                    v_part = jnp.zeros((BK, 128), F32)
                    for j in range(5):
                        scores = dot_general(k_tile, heads[i, j], 1, 1)
                        probs = jnp.where(seen, jnp.exp(scores - lses[i, j : j + 1, :]), 0.0)
                        prob_grad = dot_general(v_tile, grads[i, j], 1, 1)
                        score_grad = (probs * (prob_grad - delta[i, j : j + 1, :])).astype(BF)
                        v_part += jnp.dot(
                            probs.astype(BF), grads[i, j], preferred_element_type=F32
                        )
                        k_part += jnp.dot(score_grad, heads[i, j], preferred_element_type=F32)
                        acc[i, j] += dot_general(k_tile, score_grad, 0, 0)
                    k_sum[...] += k_part
                    v_sum[...] += v_part

                kv_send[chunk, pl.ds(inner, BK), :128] = k_sum[...].astype(BF)
                kv_send[chunk, pl.ds(inner, BK), 128:] = v_sum[...].astype(BF)

            @pl.when(d < ctx - 1)
            def _():
                pltpu.make_async_remote_copy(
                    kv_send.at[chunk],
                    got_kv.at[my_c],
                    kv_out.at[d],
                    kv_in.at[d],
                    device_id={"ctx": chunk},
                    device_id_type=MESH,
                ).start()

        near_kv = pltpu.make_async_copy(kv_send.at[my_c], got_kv.at[my_c], near.at[1])
        near_kv.start()
        low = lax.broadcasted_iota(jnp.int32, (TQ, 128), 1) < 64
        for i in range(steps):
            for b in range(3):
                first = acc[i, 2 * b].T * 0.125
                if b < 2:
                    block = jnp.where(low, first, acc[i, 2 * b + 1].T * 0.125)
                else:
                    block = jnp.where(low, first, 0.0)
                dq_ref[i * TQ : i * TQ + TQ, 128 * b : 128 * b + 128] = block.astype(BF)

        near_kv.wait()
        outward.wait()
        for copy in copies:
            copy.wait()

        for d in range(ctx - 1):
            pltpu.make_async_remote_copy(
                kv_send.at[0],
                got_kv.at[0],
                kv_out.at[d],
                kv_in.at[d],
                device_id={"ctx": my_c},
                device_id_type=MESH,
            ).wait()

    vmem = pl.BlockSpec(memory_space=pltpu.VMEM)
    anywhere = pl.BlockSpec(memory_space=pl.ANY)
    return pl.pallas_call(
        kernel,
        name="attend_backward",
        in_specs=[vmem] * 8 + [anywhere],
        out_specs=[vmem] + [anywhere] * 2,
        out_shape=[
            jax.ShapeDtypeStruct((rows, 384), BF),
            jax.ShapeDtypeStruct((ctx, span, 256), BF),
            jax.ShapeDtypeStruct(send_rows.shape, BF),
        ],
        scratch_shapes=[
            pltpu.VMEM((steps, 5, 128, TQ), F32),
            pltpu.VMEM((steps, 5, TQ, 128), BF),
            pltpu.VMEM((steps, 5, TQ, 128), BF),
            pltpu.VMEM((steps, 8, TQ), F32),
            pltpu.VMEM((steps, 8, TQ), F32),
            pltpu.VMEM((steps, 8, TQ), F32),
            pltpu.VMEM((BK, 128), F32),
            pltpu.VMEM((BK, 128), F32),
            pltpu.VMEM((ctx, span, 256), BF),
            pltpu.VMEM(send_rows.shape[1:], BF),
            pltpu.SemaphoreType.DMA((ctx,)),
            pltpu.SemaphoreType.DMA((ctx,)),
            pltpu.SemaphoreType.DMA((ctx,)),
            pltpu.SemaphoreType.DMA((ctx,)),
            pltpu.SemaphoreType.DMA((2,)),
        ],
        compiler_params=pltpu.CompilerParams(
            collective_id=11, has_side_effects=True, vmem_limit_bytes=VMEM_LIMIT
        ),
    )(q, kv, q_marks, k_pos, k_seg, lse, out, out_grad, send_rows)


class Wires:
    def __init__(self, send, recv):
        self.send, self.recv, self.used = send, recv, 0

    def copy(self, source, target, where):
        at = self.used
        self.used += 1
        return pltpu.make_async_remote_copy(
            source,
            target,
            self.send.at[at],
            self.recv.at[at],
            device_id=where,
            device_id_type=MESH,
        )

    def start(self, source, target, where):
        copy = self.copy(source, target, where)
        copy.start()
        return copy


def greet(places):
    barrier = pltpu.get_barrier_semaphore()
    for where in places:
        pl.semaphore_signal(barrier, 1, device_id=where, device_id_type=MESH)
    pl.semaphore_wait(barrier, len(places))


def square():
    w = lax.axis_index("wsh")
    return w, w + 1 - 2 * lax.rem(w, 2), w + 2 - 4 * (w // 2), 3 - w


class SquareScatter:
    def __init__(self, wires, parts, near, total):
        self.wires, self.parts, self.near, self.total = wires, parts, near, total
        self.half = parts.shape[1] // 2
        self.a, self.b = pl.ds(0, self.half), pl.ds(self.half, self.half)
        self.own, self.x, self.y, self.z = square()
        self.pending = []

    def send_diagonal(self):
        wires, parts = self.wires, self.parts
        self.one = wires.start(parts.at[self.z, self.a], self.near.at[0], {"wsh": self.x})
        self.two = wires.start(parts.at[self.z, self.b], self.near.at[1], {"wsh": self.y})

    def send_x(self):
        self.pending.append(
            self.wires.start(
                self.parts.at[self.x, self.a], self.total.at[0, self.a], {"wsh": self.x}
            )
        )

    def send_y(self):
        self.pending.append(
            self.wires.start(
                self.parts.at[self.y, self.b], self.total.at[1, self.b], {"wsh": self.y}
            )
        )

    def relay(self):
        near, parts = self.near, self.parts
        self.one.wait()
        near[2] = (near[0].astype(F32) + parts[self.y, self.a].astype(F32)).astype(BF)
        self.pending.append(
            self.wires.start(near.at[2], self.total.at[1, self.a], {"wsh": self.y})
        )
        self.two.wait()
        near[3] = (near[1].astype(F32) + parts[self.x, self.b].astype(F32)).astype(BF)
        self.pending.append(
            self.wires.start(near.at[3], self.total.at[0, self.b], {"wsh": self.x})
        )

    def result(self):
        for copy in self.pending:
            copy.wait()
        return (
            self.parts[self.own].astype(F32)
            + self.total[0].astype(F32)
            + self.total[1].astype(F32)
        )


def square_scratch(rows):
    return [pltpu.VMEM((4, rows // 2, D), BF), pltpu.VMEM((2, rows, D), BF)]


class SquareGather:
    def __init__(self, wires, out):
        self.wires, self.out = wires, out
        half = out.shape[1] // 2
        self.a, self.b = pl.ds(0, half), pl.ds(half, half)
        self.own, self.x, self.y, self.z = square()

    def move(self, slot, part, to):
        return self.wires.start(self.out.at[slot, part], self.out.at[slot, part], {"wsh": to})

    def begin(self):
        self.xa = self.move(self.own, self.a, self.x)
        self.yb = self.move(self.own, self.b, self.y)
        self.xb = self.move(self.own, self.b, self.x)
        self.ya = self.move(self.own, self.a, self.y)

    def relay(self):
        self.xa.wait()
        self.one = self.move(self.x, self.a, self.y)
        self.yb.wait()
        self.two = self.move(self.y, self.b, self.x)

    def wait_x(self):
        self.xb.wait()

    def wait_y(self):
        self.ya.wait()

    def wait_z(self):
        self.one.wait()
        self.two.wait()


def feed(link, attended, w_out, tokens, gain, w_half, down, dy):
    ctx, wsh = link.sizes["ctx"], link.sizes["wsh"]
    own_rows = tokens.shape[0]
    plane = dy.shape[0]
    units = down.shape[0]
    chunk = D // ctx
    pick = units // ctx // 2

    def kernel(
        at_ref, ao_ref, x_ref, g_ref, wh_ref, dw_ref, dy_ref,
        mid_ref, mg_ref, br_ref, ag_ref, fs_ref, dp_ref, gs_ref, gl_ref, ds_ref,
        wo_ref, w_both, parts, near, total, near2, total2, n2, hgrad, hidden, gate_g, up_g,
        down_h, down_pair, down_send, down_got, gate_h, gate_pair, send, recv, local,
    ):
        wires = Wires(send, recv)
        core = lax.axis_index("grp")
        sibling = {"grp": 1 - core}
        my_c = lax.axis_index("ctx")
        own, x, y, z = square()
        levels = [link.place(("ctx",), offset) for offset in link.offsets(("ctx",))[1:]]
        greet([{"wsh": x}, {"wsh": y}, sibling] + [where for where, _ in levels])

        def rows_of(slot):
            return pl.ds(pl.multiple_of(slot * own_rows, 16), own_rows)

        w_copy = pltpu.make_async_copy(wh_ref, w_both.at[core], local)
        w_copy.start()

        odd = lax.rem(own, 2) == 1
        wo_ref[...] = jnp.zeros_like(wo_ref)

        def spread(pieces):
            at = 0
            for start, size in pieces:
                wo_ref[start : start + size, :] = ao_ref[at : at + size, :]
                at += size

        @pl.when(odd)
        def _():
            spread(ODD_ROWS)

        @pl.when(jnp.logical_not(odd))
        def _():
            spread(EVEN_ROWS)

        first = SquareScatter(wires, parts, near, total)
        for slot in (z, x, y, own):
            parts[slot] = jnp.dot(
                at_ref[rows_of(slot), :], wo_ref[...], preferred_element_type=F32
            ).astype(BF)
            if slot is z:
                first.send_diagonal()
            elif slot is x:
                first.send_x()
            elif slot is y:
                first.send_y()
        w_swap = wires.start(wh_ref, w_both.at[core], sibling)
        hgrad[...] = dot_general(dy_ref[...], dw_ref[...], 1, 1)
        first.relay()
        middle = x_ref[...].astype(F32) + first.result()
        mid_ref[...] = middle
        factor = lax.rsqrt(jnp.mean(middle * middle, axis=-1, keepdims=True) + EPSILON)
        n2[own] = (middle * factor * g_ref[1:2, :]).astype(BF)
        gather = SquareGather(wires, n2)
        gather.begin()
        w_copy.wait()
        w_swap.wait()

        def block(slot):
            at = rows_of(slot)
            gate = jnp.dot(n2[slot], w_both[0], preferred_element_type=F32)
            up = jnp.dot(n2[slot], w_both[1], preferred_element_type=F32)
            sigmoid = 1.0 / (1.0 + jnp.exp(-gate))
            silu = gate * sigmoid
            hidden[at, :] = (silu * up).astype(BF)
            back = hgrad[at, :]
            gate_g[at, :] = (back * up * sigmoid * (1.0 + gate * (1.0 - sigmoid))).astype(BF)
            up_g[at, :] = (back * silu).astype(BF)
            parts[slot] = (
                dot_general(gate_g[at, :], w_both[0], 1, 1)
                + dot_general(up_g[at, :], w_both[1], 1, 1)
            ).astype(BF)

        second = SquareScatter(wires, parts, near2, total2)
        block(own)
        gather.relay()
        gather.wait_x()
        block(x)
        second.send_x()
        gather.wait_y()
        block(y)
        second.send_y()
        gather.wait_z()
        block(z)
        second.send_diagonal()

        strip = dot_general(hidden[...], dy_ref[...], 0, 0).astype(BF)
        for k in range(ctx):
            for g in range(2):
                top = (2 * k + g) * pick
                down_h[g, k] = strip[top : top + pick, :]
        down_swap = wires.start(down_h.at[1 - core], down_pair, sibling)
        second.relay()
        tokens_all = n2[...].reshape(plane, D)
        for g, source in enumerate((gate_g, up_g)):
            strip = dot_general(tokens_all, source[...], 0, 0).astype(BF)
            for c in range(ctx):
                gate_h[g, c] = strip[c * chunk : c * chunk + chunk, :]
        gate_swap = wires.start(gate_h.at[1 - core], gate_pair, sibling)
        down_swap.wait()
        down_send[...] = (down_h[core].astype(F32) + down_pair[...].astype(F32)).astype(BF)
        down_copies = []
        for where, index in levels:
            down_copies.append(wires.start(down_send.at[index], down_got.at[my_c], where))
        down_got[my_c] = down_send[my_c]

        grad = second.result()
        middle = mid_ref[...]
        factor = lax.rsqrt(jnp.mean(middle * middle, axis=-1, keepdims=True) + EPSILON)
        weighted = grad * g_ref[1:2, :]
        inner = jnp.mean(weighted * middle, axis=-1, keepdims=True)
        middle_grad = (
            dy_ref[rows_of(own), :].astype(F32)
            + factor * weighted
            - middle * (factor * factor * factor) * inner
        )
        mg_ref[...] = middle_grad
        br_ref[own] = middle_grad.astype(BF)
        branch = SquareGather(wires, br_ref)
        branch.begin()
        fs_ref[...] = jnp.sum(grad * middle * factor, axis=0, keepdims=True)

        def outward(slot):
            ag_ref[rows_of(slot), :] = dot_general(br_ref[slot], wo_ref[...], 1, 1).astype(BF)

        outward(own)
        gate_swap.wait()
        for c in range(ctx):
            both = (gate_h[core, c].astype(F32) + gate_pair[c].astype(F32)).astype(BF)
            gs_ref[c] = both[:, : units // 2]
            gl_ref[c] = both[:, units // 2 :]
        branch.relay()

        @pl.loop(0, wsh)
        def _(slot):
            dp_ref[slot] = jnp.dot(
                hidden[rows_of(slot), :], dw_ref[...], preferred_element_type=F32
            ).astype(BF)

        branch.wait_x()
        outward(x)
        branch.wait_y()
        outward(y)
        branch.wait_z()
        outward(z)
        for copy in down_copies:
            copy.wait()
        ds_ref[...] = jnp.sum(down_got[...].astype(F32), axis=0).astype(BF)

    operands = (attended, w_out, tokens, gain, w_half, down, dy)
    vmem = pl.BlockSpec(memory_space=pltpu.VMEM)
    return pl.pallas_call(
        kernel,
        name="feed",
        in_specs=[vmem] * len(operands),
        out_specs=[vmem] * 9,
        out_shape=[
            jax.ShapeDtypeStruct((own_rows, D), F32),
            jax.ShapeDtypeStruct((own_rows, D), F32),
            jax.ShapeDtypeStruct((wsh, own_rows, D), BF),
            jax.ShapeDtypeStruct((plane, 384), BF),
            jax.ShapeDtypeStruct((1, D), F32),
            jax.ShapeDtypeStruct((wsh, own_rows, D), BF),
            jax.ShapeDtypeStruct((ctx, chunk, units // 2), BF),
            jax.ShapeDtypeStruct((ctx, chunk, units // 2), BF),
            jax.ShapeDtypeStruct((pick, D), BF),
        ],
        scratch_shapes=[
            pltpu.VMEM((384, D), BF),
            pltpu.VMEM((2, D, units), BF),
            pltpu.VMEM((4, own_rows, D), BF),
            *square_scratch(own_rows),
            *square_scratch(own_rows),
            pltpu.VMEM((4, own_rows, D), BF),
            pltpu.VMEM((plane, units), F32),
            *[pltpu.VMEM((plane, units), BF)] * 3,
            pltpu.VMEM((2, ctx, pick, D), BF),
            *[pltpu.VMEM((ctx, pick, D), BF)] * 3,
            pltpu.VMEM((2, ctx, chunk, units), BF),
            pltpu.VMEM((ctx, chunk, units), BF),
            pltpu.SemaphoreType.DMA((ctx + 28,)),
            pltpu.SemaphoreType.DMA((ctx + 28,)),
            pltpu.SemaphoreType.DMA,
        ],
        compiler_params=pltpu.CompilerParams(
            collective_id=3, has_side_effects=True, vmem_limit_bytes=VMEM_LIMIT
        ),
    )(*operands)


def head(link, tokens, gain, weight, marks, upstream, gate_up):
    ctx, wsh = link.sizes["ctx"], link.sizes["wsh"]
    own_rows = tokens.shape[0]
    plane, group = own_rows * wsh, own_rows * wsh * ctx
    half = weight.shape[0] // 2
    units = FF // wsh
    steps = plane // TQ

    def kernel(
        x_ref, g_ref, w_ref, m_ref, up_ref, gu_ref,
        q_ref, kv_ref, n_ref, wq_ref, kpos_ref, kseg_ref, q_marks, dy_ref, c_ref, s_ref,
        a_ref, o_ref, lse_ref, wh_ref,
        cols, mine, marks_all, heads, tile_marks, acc, top, tot, bounce, send, recv, kv_out, kv_in,
        near,
    ):
        wires = Wires(send, recv)
        core = lax.axis_index("grp")
        sibling = {"grp": 1 - core}
        my_c = lax.axis_index("ctx")
        own, x, y, z = square()
        levels = [link.place(("ctx",), offset) for offset in link.offsets(("ctx",))[1:]]
        greet(
            [{"wsh": x}, {"wsh": y}, {"wsh": z}, sibling] + [where for where, _ in levels]
        )
        mine[...] = jnp.zeros_like(mine)
        mine[:2, :own_rows] = m_ref[...]
        mark_copies = []
        for p in (x, y, z):
            mark_copies.append(wires.start(mine, marks_all.at[my_c, own], {"wsh": p}))
        marks_all[my_c, own] = mine[...]
        side = pl.ds(pl.multiple_of(core * half, 16), half)

        for w in range(wsh):
            q_order, kv_order = head_plan(w)
            slots = [h for h in q_order] + [HEADS + h for h in kv_order]
            slots += [HEADS + KV_HEADS + h for h in kv_order]
            blank = jnp.zeros((w_ref.shape[0], HEAD_DIM), BF)
            for pair in range(5):
                two = [
                    blank if h is None else w_ref[:, h * HEAD_DIM : h * HEAD_DIM + HEAD_DIM]
                    for h in slots[2 * pair : 2 * pair + 2]
                ]
                cols[w, :, 128 * pair : 128 * pair + 128] = jnp.concatenate(two, axis=1)
        w_copies = []
        for p in (x, y, z):
            w_copies.append(
                wires.start(cols.at[p, side], wq_ref.at[own, side], {"wsh": p})
            )
        tokens_in = x_ref[...].astype(F32)
        factor = lax.rsqrt(jnp.mean(tokens_in * tokens_in, axis=-1, keepdims=True) + EPSILON)
        n_ref[own] = (tokens_in * factor * g_ref[0:1, :]).astype(BF)
        wq_ref[own] = cols[own]
        dy_ref[own] = up_ref[...]

        for copy in mark_copies:
            copy.wait()
        level_copies = []
        for where, _ in levels:
            level_copies.append(wires.start(marks_all.at[my_c], marks_all.at[my_c], where))
        lane = lax.broadcasted_iota(jnp.int32, (1, 128), 1)
        power = lax.rem(lane, 32).astype(F32) * (-math.log(10000.0) / 32)
        frequency = jnp.exp(power)
        sign = jnp.where(lax.rem(lane, 64) < 32, -1.0, 1.0)

        def upright(row):
            return jnp.broadcast_to(row, (128, row.shape[1])).T

        for w in range(wsh):
            at = slice(w * own_rows, w * own_rows + own_rows)
            angles = upright(marks_all[my_c, w, 0:1, :])[:own_rows] * frequency
            c_ref[at, :] = jnp.cos(angles)
            s_ref[at, :] = jnp.sin(angles) * sign
        forward = []
        for p, copy in zip((x, y, z), w_copies):
            copy.wait()
            forward.append(wires.start(wq_ref.at[p, side], wq_ref.at[p, side], sibling))
        gather = SquareGather(wires, n_ref)
        gather.begin()
        for copy in forward:
            copy.wait()

        low = lax.rem(lax.broadcasted_iota(jnp.int32, (own_rows, 128), 1), 64) < 32

        def kv_copy(slot, order, d, to):
            at = pl.ds(pl.multiple_of(slot * own_rows, 16), own_rows)
            return pltpu.make_async_remote_copy(
                kv_ref.at[my_c, at],
                kv_ref.at[my_c, at],
                kv_out.at[order, d],
                kv_in.at[order, d],
                device_id={"ctx": to},
                device_id_type=MESH,
            )

        def block(slot, order):
            at = pl.ds(pl.multiple_of(slot * own_rows, 16), own_rows)
            full = jnp.dot(
                n_ref[slot], wq_ref[...].reshape(D, 640), preferred_element_type=F32
            )
            cos_t, sin_t = c_ref[at, :], s_ref[at, :]
            for b in range(3):
                turned = turn(full[:, 128 * b : 128 * b + 128], cos_t, sin_t, low)
                q_ref[at, 128 * b : 128 * b + 128] = (
                    turned.astype(BF).astype(F32) * 0.125
                ).astype(BF)
            kv_ref[my_c, at, :128] = turn(full[:, 384:512], cos_t, sin_t, low).astype(BF)
            kv_ref[my_c, at, 128:] = full[:, 512:].astype(BF)
            for d, (_, index) in enumerate(levels):
                kv_copy(slot, order, d, index).start()

        block(own, 0)
        gather.relay()
        dy_gather = SquareGather(wires, dy_ref)
        dy_gather.begin()
        gather.wait_x()
        block(x, 1)
        gather.wait_y()
        block(y, 2)
        gather.wait_z()
        block(z, 3)
        dy_gather.relay()

        def columns(p):
            left = core * FF + p * units
            return gu_ref.at[:, pl.ds(pl.multiple_of(left, 128), units)]

        gate_copies = []
        for p in (x, y, z):
            gate_copies.append(wires.start(columns(p), wh_ref.at[own], {"wsh": p}))
        inward = pltpu.make_async_copy(columns(own), bounce, near)
        outward = pltpu.make_async_copy(bounce, wh_ref.at[own], near)
        inward.start()

        for w in range(wsh):
            q_marks[:, w * own_rows : w * own_rows + own_rows] = marks_all[my_c, w, :, :own_rows]

        for copy in level_copies:
            copy.wait()

        @pl.loop(0, ctx)
        def _(c):
            for w in range(wsh):
                at = pl.ds(pl.multiple_of(c * plane + w * own_rows, 16), own_rows)
                kpos_ref[at, :] = upright(marks_all[c, w, 0:1, :])[:own_rows]
                kseg_ref[at, :] = upright(marks_all[c, w, 1:2, :])[:own_rows]

        inward.wait()
        outward.start()

        acc[...] = jnp.zeros_like(acc)
        top[...] = jnp.full_like(top, -1e30)
        tot[...] = jnp.zeros_like(tot)
        for i in range(steps):
            at = slice(i * TQ, i * TQ + TQ)
            tile_marks[i] = q_marks[:, at]
            for j, (b, side_of) in enumerate(HEAD_SLOTS):
                heads[i, j] = head_block(q_ref[at, 128 * b : 128 * b + 128], side_of)

        @pl.loop(0, ctx)
        def _(d):
            chunk = lax.rem(my_c + ctx - d, ctx)

            @pl.when(d > 0)
            def _():
                for order in range(wsh):
                    kv_copy(0, order, d - 1, my_c).wait()

            at = pl.ds(pl.multiple_of(chunk * plane, 128), plane)
            k_tile = kv_ref[chunk, :, :128]
            v_tile = kv_ref[chunk, :, 128:]
            key_pos = jnp.tile(kpos_ref[at, :], (1, TQ // 128))
            key_seg = jnp.tile(kseg_ref[at, :], (1, TQ // 128))

            @pl.loop(0, steps)
            def _(i):
                seen = (key_pos <= tile_marks[i, 0:1, :]) & (
                    (key_seg == 0) | (key_seg == tile_marks[i, 1:2, :])
                )
                scores = [
                    jnp.where(seen, dot_general(k_tile, heads[i, j], 1, 1), -1e30)
                    for j in range(5)
                ]
                old = [top[i, j : j + 1, :] for j in range(5)]
                new = [
                    jnp.maximum(old[j], jnp.max(scores[j], axis=0, keepdims=True))
                    for j in range(5)
                ]
                expons = [jnp.exp(scores[j] - new[j]) for j in range(5)]
                shrink = [jnp.exp(old[j] - new[j]) for j in range(5)]
                mixed = [dot_general(v_tile, expons[j].astype(BF), 0, 0) for j in range(5)]
                for j in range(5):
                    tot[i, j : j + 1, :] = tot[i, j : j + 1, :] * shrink[j] + jnp.sum(
                        expons[j], axis=0, keepdims=True
                    )
                    acc[i, j] = acc[i, j] * shrink[j] + mixed[j]
                    top[i, j : j + 1, :] = new[j]

        half_lanes = lax.broadcasted_iota(jnp.int32, (TQ, 128), 1) < 64
        for i in range(steps):
            at = slice(i * TQ, i * TQ + TQ)
            lse_ref[:, at] = top[i] + jnp.log(jnp.maximum(tot[i], 1e-37))
            outs = [(acc[i, j] / tot[i, j : j + 1, :]).T for j in range(5)] + [0.0]
            for b in range(3):
                block_out = jnp.where(half_lanes, outs[2 * b], outs[2 * b + 1])
                o_ref[at, 128 * b : 128 * b + 128] = block_out
                a_ref[at, 128 * b : 128 * b + 128] = block_out.astype(BF)

        dy_gather.wait_x()
        dy_gather.wait_y()
        dy_gather.wait_z()
        for copy in gate_copies:
            copy.wait()
        outward.wait()

    operands = (tokens, gain, weight, marks, upstream, gate_up)
    vmem = pl.BlockSpec(memory_space=pltpu.VMEM)
    return pl.pallas_call(
        kernel,
        name="head",
        in_specs=[vmem] * 5 + [pl.BlockSpec(memory_space=pl.ANY)],
        out_specs=[vmem] * 13 + [pl.BlockSpec(memory_space=pl.ANY)],
        out_shape=[
            jax.ShapeDtypeStruct((plane, 384), BF),
            jax.ShapeDtypeStruct((ctx, plane, 256), BF),
            jax.ShapeDtypeStruct((wsh, own_rows, D), BF),
            jax.ShapeDtypeStruct((wsh, 2 * half, 640), BF),
            jax.ShapeDtypeStruct((group, 128), F32),
            jax.ShapeDtypeStruct((group, 128), F32),
            jax.ShapeDtypeStruct((8, plane), F32),
            jax.ShapeDtypeStruct((wsh, own_rows, D), BF),
            jax.ShapeDtypeStruct((plane, 128), F32),
            jax.ShapeDtypeStruct((plane, 128), F32),
            jax.ShapeDtypeStruct((plane, 384), BF),
            jax.ShapeDtypeStruct((plane, 384), F32),
            jax.ShapeDtypeStruct((8, plane), F32),
            jax.ShapeDtypeStruct((wsh, 2 * half, units), BF),
        ],
        scratch_shapes=[
            pltpu.VMEM((wsh, 2 * half, 640), BF),
            pltpu.VMEM((8, 256), F32),
            pltpu.VMEM((ctx, wsh, 8, 256), F32),
            pltpu.VMEM((steps, 5, TQ, 128), BF),
            pltpu.VMEM((steps, 8, TQ), F32),
            pltpu.VMEM((steps, 5, 128, TQ), F32),
            pltpu.VMEM((steps, 8, TQ), F32),
            pltpu.VMEM((steps, 8, TQ), F32),
            pltpu.VMEM((2 * half, units), BF),
            pltpu.SemaphoreType.DMA((ctx + 28,)),
            pltpu.SemaphoreType.DMA((ctx + 28,)),
            pltpu.SemaphoreType.DMA((wsh, ctx)),
            pltpu.SemaphoreType.DMA((wsh, ctx)),
            pltpu.SemaphoreType.DMA,
        ],
        compiler_params=pltpu.CompilerParams(
            collective_id=1, has_side_effects=True, vmem_limit_bytes=VMEM_LIMIT
        ),
    )(*operands)


def finish(
    link, q_grad, kv_grad, weight, cos, sin, normed, tokens, gain, middle_grad, gate_got, down_got,
    attended, branch, feed_sum, down_part, middle, gate_late,
):
    ctx, wsh = link.sizes["ctx"], link.sizes["wsh"]
    shards = ctx * wsh
    rows = D // shards
    chunk = D // ctx
    fold = ctx // wsh
    own_rows = tokens.shape[0]
    plane = normed.shape[0]
    axes = ("ctx", "wsh")
    peers = link.offsets(axes)
    gate_width = gate_got.shape[2]
    down_rows = down_got.shape[0]
    piece = down_rows // wsh

    def kernel(
        q_ref, kv_ref, w_ref, c_ref, s_ref, n_ref, x_ref, g_ref, mg_ref, gate_ref, down_ref,
        at_ref, br_ref, fs_ref, dp_ref, mid_ref, late_ref,
        act_ref, ig_ref, q_fin, kv_fin, out_fin, gate_fin, late_fin, down_fin, gains_out,
        pg, parts, near, total, near2, total2, wide, q_own, q_pair, q_send, q_got,
        q_mid, kv_own, kv_pair, kv_go, kv_got, kv_mid, gate_mid, late_got,
        late_mid, spread, spread_got, risen, landed, out_halves,
        out_pair, out_send, out_mid, out_got, gains, gains_got, gains_fin,
        send, recv,
    ):
        wires = Wires(send, recv)
        core = lax.axis_index("grp")
        first, second = core == 0, core == 1
        sibling = {"grp": 1 - core}
        my_c, my_w = lax.axis_index("ctx"), lax.axis_index("wsh")
        odd = lax.rem(my_w, 2) == 1
        greet([link.place(axes, offset)[0] for offset in peers[1:]] + [sibling])
        _, me = link.place(axes, peers[0])

        def over_ctx(got, mid):
            for w in range(wsh):
                strip = got[0, w * rows : w * rows + rows, :].astype(F32)
                for c in range(1, ctx):
                    strip += got[c, w * rows : w * rows + rows, :].astype(F32)
                mid[w] = strip.astype(BF)

        def in_plane(mid, slot_of):
            copies = []
            for offset in link.offsets(("wsh",))[1:]:
                where, index = link.place(("wsh",), offset)
                copies.append(wires.copy(mid.at[index], slot_of(my_w), where))
            return copies

        def begin(cond, *copies):
            @pl.when(cond)
            def _():
                for copy in copies:
                    copy.start()

        levels = [link.place(("ctx",), offset) for offset in link.offsets(("ctx",))[1:]]
        late_copies = []
        for where, index in levels:
            late_copies.append(wires.start(late_ref.at[index], late_got.at[my_c], where))

        for p in range(wsh):
            spread[p] = down_ref[p * piece : p * piece + piece, :]
        spread_moves = in_plane(spread, lambda w: spread_got.at[w])
        for copy in spread_moves:
            copy.start()
        spread_got[my_w] = spread[my_w]

        low = lax.rem(lax.broadcasted_iota(jnp.int32, (own_rows, 128), 1), 64) < 32
        scatter = SquareScatter(wires, parts, near, total)
        gain_sum = jnp.zeros((1, D), F32)
        for slot in (scatter.z, scatter.x, scatter.y, scatter.own):
            at = pl.ds(pl.multiple_of(slot * own_rows, 16), own_rows)
            cos_t, sin_t = c_ref[at, :], -s_ref[at, :]
            for b in range(3):
                block = q_ref[at, 128 * b : 128 * b + 128].astype(F32)
                pg[at, 128 * b : 128 * b + 128] = turn(block, cos_t, sin_t, low).astype(BF)
            summed = kv_ref[0, at, :].astype(F32)
            for c in range(1, ctx):
                summed += kv_ref[c, at, :].astype(F32)
            block = summed[:, :128].astype(BF).astype(F32)
            pg[at, 384:512] = turn(block, cos_t, sin_t, low).astype(BF)
            pg[at, 512:] = summed[:, 128:].astype(BF)
            part = dot_general(pg[at, :], w_ref[...], 1, 1)
            parts[slot] = part.astype(BF)
            gain_sum += jnp.sum(part * n_ref[at, :].astype(F32), axis=0, keepdims=True)
            if slot is scatter.z:
                scatter.send_diagonal()
            elif slot is scatter.x:
                scatter.send_x()
            elif slot is scatter.y:
                scatter.send_y()

        for copy in spread_moves:
            copy.wait()
        lane = lax.rem(my_c, wsh)
        rise, arrive = wires.used, []
        wires.used += wsh
        for p in range(wsh):
            to = (p * ctx + my_c) // wsh
            out_copy_p = pltpu.make_async_remote_copy(
                spread_got.at[p],
                risen.at[lane],
                send.at[rise + p],
                recv.at[rise + lane],
                device_id={"ctx": to},
                device_id_type=MESH,
            )

            @pl.when(to != my_c)
            def _():
                out_copy_p.start()

            @pl.when(to == my_c)
            def _():
                risen[lane] = spread_got[p]

            from_c = lax.rem(my_c, fold) * wsh + p
            in_copy_p = pltpu.make_async_remote_copy(
                spread_got.at[p],
                risen.at[p],
                send.at[rise + p],
                recv.at[rise + p],
                device_id={"ctx": to},
                device_id_type=MESH,
            )
            arrive.append((out_copy_p, to != my_c, in_copy_p, from_c != my_c))

        strip = dot_general(n_ref[...], pg[:, 384:], 0, 0).astype(BF)
        for c in range(ctx):
            kv_own[c] = strip[c * chunk : c * chunk + chunk, :]
        kv_swap = wires.copy(kv_own, kv_pair, sibling)
        begin(first, kv_swap)
        scatter.relay()
        strip = dot_general(n_ref[...], pg[:, :384], 0, 0).astype(BF)
        for c in range(ctx):
            q_own[c] = strip[c * chunk : c * chunk + chunk, :]
        q_swap = wires.copy(q_own, q_pair, sibling)
        begin(second, q_swap)
        layer = SquareScatter(wires, dp_ref, near2, total2)
        layer.send_diagonal()
        layer.send_x()
        layer.send_y()
        wide[...] = dot_general(at_ref[...], br_ref[...], 0, 0)

        def out_strips(pieces):
            at = 0
            for start, size in pieces:
                acc_rows = wide[start : start + size, :].astype(BF)
                part = jnp.concatenate([acc_rows[:, :576], jnp.zeros((size, 64), BF)], axis=1)
                out_halves[0, at : at + size, :] = part
                part = jnp.concatenate([acc_rows[:, 576:], jnp.zeros((size, 64), BF)], axis=1)
                out_halves[1, at : at + size, :] = part
                at += size

        @pl.when(odd)
        def _():
            out_strips(ODD_ROWS)

        @pl.when(jnp.logical_not(odd))
        def _():
            out_strips(EVEN_ROWS)

        out_swap = wires.start(out_halves.at[1 - core], out_pair, sibling)
        q_copies, kvg_copies, out_copies = [], [], []
        for where, index in levels:
            q_copies.append(wires.copy(q_send.at[index], q_got.at[my_c], where))
            kvg_copies.append(wires.copy(kv_go.at[index], kv_got.at[my_c], where))

        @pl.when(first)
        def _():
            q_swap.wait_recv()

            @pl.loop(0, ctx)
            def _(c):
                q_send[c] = (q_own[c].astype(F32) + q_pair[c].astype(F32)).astype(BF)

            for copy in q_copies:
                copy.start()
            q_got[my_c] = q_send[my_c]
            kv_swap.wait_send()

        @pl.when(second)
        def _():
            kv_swap.wait_recv()

            @pl.loop(0, ctx)
            def _(c):
                kv_go[c] = (kv_own[c].astype(F32) + kv_pair[c].astype(F32)).astype(BF)

            for copy in kvg_copies:
                copy.start()
            kv_got[my_c] = kv_go[my_c]
            q_swap.wait_send()

        both = jnp.concatenate([gain_sum / g_ref[0:1, :], fs_ref[...]], axis=0)
        gains[...] = jnp.zeros_like(gains)
        for s in range(shards):
            gains[s, :2, :rows] = both[:, rows * s : rows * s + rows]
        gain_copies = []
        for offset in peers[1:]:
            where, index = link.place(axes, offset)
            gain_copies.append(wires.start(gains.at[index], gains_got.at[me], where))
        gains_got[me] = gains[me]
        layer.relay()

        out_swap.wait()
        for k in range(ctx):
            strip = slice(k * rows, k * rows + rows)
            out_send[k % wsh, k // wsh] = (
                out_halves[core, strip, :].astype(F32) + out_pair[strip, :].astype(F32)
            ).astype(BF)
        out_moves = in_plane(out_send, lambda w: out_mid.at[w])
        for copy in out_moves:
            copy.start()
        out_mid[my_w] = out_send[my_w]

        grad = scatter.result()
        x = x_ref[...].astype(F32)
        factor = lax.rsqrt(jnp.mean(x * x, axis=-1, keepdims=True) + EPSILON)
        weighted = grad * g_ref[0:1, :]
        inner = jnp.mean(weighted * x, axis=-1, keepdims=True)
        ig_ref[...] = mg_ref[...] + factor * weighted - x * (factor * factor * factor) * inner
        for copy in out_moves:
            copy.wait()
        for where, index in levels:
            part = out_mid.at[index // fold, lax.rem(index, fold)]
            out_copies.append(wires.start(part, out_got.at[my_c], where))
        out_got[my_c] = out_mid[my_c // fold, lax.rem(my_c, fold)]


        for out_copy_p, goes, in_copy_p, comes in arrive:

            @pl.when(goes)
            def _():
                out_copy_p.wait_send()

            @pl.when(comes)
            def _():
                in_copy_p.wait_recv()

        land_moves = in_plane(risen, lambda w: landed.at[w])
        for copy in land_moves:
            copy.start()
        landed[my_w] = risen[my_w]
        over_ctx(gate_ref, gate_mid)
        gate_moves = in_plane(gate_mid, lambda w: gate_fin.at[core, w])
        for copy in gate_moves:
            copy.start()
        gate_fin[core, my_w] = gate_mid[my_w]
        for copy in late_copies:
            copy.wait()
        late_got[my_c] = late_ref[my_c]
        over_ctx(late_got, late_mid)
        late_moves = in_plane(late_mid, lambda w: late_fin.at[core, w])
        for copy in late_moves:
            copy.start()
        late_fin[core, my_w] = late_mid[my_w]
        act_ref[...] = (mid_ref[...] + layer.result()).astype(BF)

        q_moves = in_plane(q_mid, lambda w: q_fin.at[w])
        kv_moves = in_plane(kv_mid, lambda w: kv_fin.at[w])

        @pl.when(first)
        def _():
            for copy in q_copies:
                copy.wait()
            over_ctx(q_got, q_mid)
            for copy in q_moves:
                copy.start()
            q_fin[my_w] = q_mid[my_w]

        @pl.when(second)
        def _():
            for copy in kvg_copies:
                copy.wait()
            over_ctx(kv_got, kv_mid)
            for copy in kv_moves:
                copy.start()
            kv_fin[my_w] = kv_mid[my_w]

        for copy in land_moves:
            copy.wait()
        for p in range(wsh):
            down_fin[core, p * piece : p * piece + piece, :] = landed[p]
        down_copy = wires.start(down_fin.at[core], down_fin.at[core], sibling)
        for copy in gate_moves + late_moves:
            copy.wait()
        gate_copy = wires.start(gate_fin.at[core], gate_fin.at[core], sibling)
        late_copy = wires.start(late_fin.at[core], late_fin.at[core], sibling)
        for copy in out_copies:
            copy.wait()
        out_fin[core] = jnp.sum(out_got[...].astype(F32), axis=0).astype(BF)
        out_copy = wires.start(out_fin.at[core], out_fin.at[core], sibling)
        for copy in gain_copies:
            copy.wait()
        gains_fin[core] = jnp.sum(gains_got[...], axis=0)
        gain_copy = wires.start(gains_fin.at[core], gains_fin.at[core], sibling)
        q_final = wires.copy(q_fin, q_fin, sibling)
        kv_final = wires.copy(kv_fin, kv_fin, sibling)

        @pl.when(first)
        def _():
            for copy in q_moves:
                copy.wait()
            q_final.start()

        @pl.when(second)
        def _():
            for copy in kv_moves:
                copy.wait()
            kv_final.start()

        down_copy.wait()
        gate_copy.wait()
        late_copy.wait()
        out_copy.wait()

        @pl.when(first)
        def _():
            q_final.wait_send()
            kv_final.wait_recv()

        @pl.when(second)
        def _():
            kv_final.wait_send()
            q_final.wait_recv()

        gain_copy.wait()
        gains_out[...] = gains_fin[0] + gains_fin[1]

    operands = (
        q_grad, kv_grad, weight, cos, sin, normed, tokens, gain, middle_grad, gate_got, down_got,
        attended, branch, feed_sum, down_part, middle, gate_late,
    )
    vmem = pl.BlockSpec(memory_space=pltpu.VMEM)
    return pl.pallas_call(
        kernel,
        name="finish",
        in_specs=[vmem] * len(operands),
        out_specs=[vmem] * 9,
        out_shape=[
            jax.ShapeDtypeStruct((own_rows, D), BF),
            jax.ShapeDtypeStruct((own_rows, D), F32),
            jax.ShapeDtypeStruct((wsh, rows, 384), BF),
            jax.ShapeDtypeStruct((wsh, rows, 256), BF),
            jax.ShapeDtypeStruct((2, rows, 640), BF),
            jax.ShapeDtypeStruct((2, wsh, rows, gate_width), BF),
            jax.ShapeDtypeStruct((2, wsh, rows, gate_width), BF),
            jax.ShapeDtypeStruct((2, down_rows, D), BF),
            jax.ShapeDtypeStruct((8, 128), F32),
        ],
        scratch_shapes=[
            pltpu.VMEM((plane, 640), BF),
            pltpu.VMEM((4, own_rows, D), BF),
            *square_scratch(own_rows),
            *square_scratch(own_rows),
            pltpu.VMEM((384, D), F32),
            *[pltpu.VMEM((ctx, chunk, 384), BF)] * 4,
            pltpu.VMEM((wsh, rows, 384), BF),
            *[pltpu.VMEM((ctx, chunk, 256), BF)] * 4,
            pltpu.VMEM((wsh, rows, 256), BF),
            pltpu.VMEM((wsh, rows, gate_width), BF),
            pltpu.VMEM((ctx, chunk, gate_width), BF),
            pltpu.VMEM((wsh, rows, gate_width), BF),
            *[pltpu.VMEM((wsh, piece, D), BF)] * 4,
            pltpu.VMEM((2, 288, 640), BF),
            pltpu.VMEM((288, 640), BF),
            pltpu.VMEM((wsh, fold, rows, 640), BF),
            pltpu.VMEM((wsh, fold, rows, 640), BF),
            pltpu.VMEM((ctx, rows, 640), BF),
            pltpu.VMEM((shards, 8, 128), F32),
            pltpu.VMEM((shards, 8, 128), F32),
            pltpu.VMEM((2, 8, 128), F32),
            pltpu.SemaphoreType.DMA((shards + 5 * ctx + 48,)),
            pltpu.SemaphoreType.DMA((shards + 5 * ctx + 48,)),
        ],
        compiler_params=pltpu.CompilerParams(
            collective_id=8, has_side_effects=True, vmem_limit_bytes=VMEM_LIMIT
        ),
    )(*operands)


def wrap(act, input_grad, q_sum, kv_sum, out_sum, gate_sum, late_sum, down_sum):
    wsh, rows, _ = q_sum.shape
    down_rows = down_sum.shape[1]
    width = gate_sum.shape[3]

    def kernel(
        act_in, ig_in, q_in, kv_in, out_in, gate_in, late_in, down_in,
        act_ref, ig_ref, qkv_ref, out_ref, gate_ref, down_ref,
    ):
        act_ref[...] = act_in[...]
        ig_ref[...] = ig_in[...]
        qkv_ref[...] = qkv_restore(
            [
                jnp.concatenate([q_in[w].astype(F32), kv_in[w].astype(F32)], axis=1)
                for w in range(wsh)
            ]
        )
        out_ref[...] = jnp.concatenate(
            [out_in[0, :, :576].astype(F32), out_in[1, :, :576].astype(F32)], axis=1
        )
        for half in range(2):
            for w in range(wsh):
                left = (half * wsh + w) * 2 * width
                gate_ref[:, left : left + width] = gate_in[half, w].astype(F32)
                left += width
                gate_ref[:, left : left + width] = late_in[half, w].astype(F32)
            down_ref[half * down_rows : half * down_rows + down_rows, :] = down_in[half].astype(
                F32
            )

    vmem = pl.BlockSpec(memory_space=pltpu.VMEM)
    return pl.pallas_call(
        kernel,
        name="wrap",
        in_specs=[vmem] * 8,
        out_specs=[vmem] * 6,
        out_shape=[
            jax.ShapeDtypeStruct(act.shape, BF),
            jax.ShapeDtypeStruct(act.shape, F32),
            jax.ShapeDtypeStruct((rows, QW + 2 * KW), F32),
            jax.ShapeDtypeStruct((rows, D), F32),
            jax.ShapeDtypeStruct((rows, 2 * FF), F32),
            jax.ShapeDtypeStruct((2 * down_rows, D), F32),
        ],
        compiler_params=pltpu.CompilerParams(vmem_limit_bytes=VMEM_LIMIT),
    )(act, input_grad, q_sum, kv_sum, out_sum, gate_sum, late_sum, down_sum)


def build(sizes):
    ctx, wsh = sizes["ctx"], sizes["wsh"]
    shards = ctx * wsh
    link = Exchange(sizes)

    def local(
        tokens,
        segment_ids,
        positions,
        attend_gain,
        query_key_value,
        attend_out,
        feed_gain,
        gate_up,
        down_weight,
        upstream,
    ):
        own = tokens.shape[0]
        plane = own * wsh
        group = plane * ctx
        marks = jnp.stack([positions, segment_ids]).astype(F32)
        both_gains = jnp.stack([attend_gain, feed_gain])
        (
            queries,
            kv_all,
            normed_all,
            w_qkv,
            k_pos,
            k_seg,
            q_marks,
            dy_all,
            cos,
            sin,
            attended,
            attended_wide,
            lse,
            w_half,
        ) = head(link, tokens, both_gains, query_key_value, marks, upstream, gate_up)
        kv_all = kv_all.reshape(group, 256)
        normed_all, dy_all = normed_all.reshape(plane, D), dy_all.reshape(plane, D)
        w_qkv = w_qkv.reshape(D, 640)
        w_half = w_half.reshape(D, FF // wsh)
        (
            middle,
            middle_grad,
            branch_all,
            attended_grad,
            feed_sum,
            down_part,
            gate_send,
            gate_late,
            down_sum,
        ) = feed(link, attended, attend_out, tokens, both_gains, w_half, down_weight, dy_all)
        q_grad, kv_grad, gate_got = attend_backward(
            link, queries, kv_all, q_marks, k_pos, k_seg, lse, attended_wide, attended_grad,
            gate_send,
        )
        *sums, gain_out = finish(
            link, q_grad, kv_grad, w_qkv, cos, sin, normed_all, tokens,
            both_gains, middle_grad, gate_got, down_sum, attended,
            branch_all.reshape(plane, D), feed_sum, down_part, middle, gate_late,
        )
        activations, input_grad, qkv_out, out_out, gate_out, down_out = wrap(*sums)
        width = D // shards
        return (
            activations,
            input_grad,
            qkv_out,
            out_out,
            gate_out,
            down_out,
            gain_out[0, :width],
            gain_out[1, :width],
        )

    return local


def solution(mesh):
    whole = ("grp", "ctx", "wsh")
    in_specs = (
        P(whole, None),
        P(whole),
        P(whole),
        P(),
        P("wsh", None),
        P("wsh", None),
        P(),
        P("wsh", None),
        P("wsh", None),
        P(whole, None),
    )
    out_specs = (
        P(whole, None),
        P(whole, None),
        P(("ctx", "wsh"), None),
        P(("ctx", "wsh"), None),
        P(("ctx", "wsh"), None),
        P(("ctx", "wsh"), None),
        P(("ctx", "wsh")),
        P(("ctx", "wsh")),
    )
    return jax.shard_map(
        build(dict(mesh.shape)), mesh=mesh, in_specs=in_specs, out_specs=out_specs, check_vma=False
    )
```

```python
import itertools
import math

import jax
import jax.numpy as jnp
from jax import lax
from jax.experimental import pallas as pl
from jax.experimental.pallas import tpu as pltpu
from jax.sharding import PartitionSpec as P

HEADS = 18
KV_HEADS = 6
HEAD_DIM = 64
FF = 3072
D = 1152
QW = 1152
KW = 384
EPSILON = 1e-05
MESH = pl.DeviceIdType.MESH
F32 = jnp.float32
BF = jnp.bfloat16
VMEM_LIMIT = 56 << 20


def dot_general(a, b, ca, cb):
    return lax.dot_general(a, b, (((ca,), (cb,)), ((), ())), preferred_element_type=F32)


class Exchange:
    def __init__(self, sizes):
        self.sizes = sizes

    def place(self, axes, offset):
        where, index = {}, 0
        for axis, step in zip(axes, offset):
            size = self.sizes[axis]
            spot = lax.axis_index(axis)
            if step:
                spot = lax.rem(spot + step, size)
            where[axis] = spot
            index = index * size + spot
        return where, index

    def offsets(self, axes):
        return list(itertools.product(*[range(self.sizes[axis]) for axis in axes]))


def head_plan(w):
    pair, odd = w // 2, w % 2
    start = 9 * pair + 4 * odd
    if odd:
        f_heads, h_heads = [start + 2, start + 3, start + 4], [start, start + 1]
        f_kv, h_kv = 3 * pair + 2, 3 * pair + 1
    else:
        f_heads, h_heads = [start, start + 1, start + 2], [start + 3, start + 4]
        f_kv, h_kv = 3 * pair, 3 * pair + 1
    q_order = [f_heads[0], h_heads[0], f_heads[1], h_heads[1], f_heads[2], None]
    return q_order, [f_kv, h_kv]


def qkv_restore(parts):
    found = {}
    for w in range(4):
        q_order, kv_order = head_plan(w)
        slots = list(q_order) + [HEADS + h for h in kv_order]
        slots += [HEADS + KV_HEADS + h for h in kv_order]
        for at, head in enumerate(slots):
            if head is not None:
                found.setdefault(head, []).append(
                    parts[w][:, at * HEAD_DIM : (at + 1) * HEAD_DIM]
                )
    pieces = []
    for head in range(HEADS + 2 * KV_HEADS):
        term = found[head][0]
        for other in found[head][1:]:
            term = term + other
        pieces.append(term)
    return jnp.concatenate(pieces, axis=1)


def turn(x, cos, sin, lanes):
    swapped = jnp.where(lanes, pltpu.roll(x, 96, 1), pltpu.roll(x, 32, 1))
    return x * cos + swapped * sin


TQ = 256


def head_block(block, head):
    low = lax.broadcasted_iota(jnp.int32, block.shape, 1) < 64
    return jnp.where(low if head == 0 else jnp.logical_not(low), block, jnp.zeros_like(block))


ODD_ROWS = [(96, 32), (192, 64), (0, 64), (128, 64), (256, 64)]
EVEN_ROWS = [(0, 64), (128, 64), (256, 64), (64, 64), (192, 32)]
HEAD_SLOTS = [(0, 0), (0, 1), (1, 0), (1, 1), (2, 0)]


BK = 384
EARLY = 384


def attend_backward(
    link, q, kv, q_marks, k_pos, k_seg, lse, out, out_grad, send_rows
):
    ctx = link.sizes["ctx"]
    rows, keys = q.shape[0], kv.shape[0]
    steps = rows // TQ
    span = keys // ctx
    levels = link.offsets(("ctx",))[1:]

    def kernel(
        q_ref, kv_ref, qm_ref, kp_ref, ks_ref, lse_ref, o_ref, do_ref, rows_ref,
        dq_ref, got_kv, got_rows,
        acc, heads, grads, delta, marks, lses, k_sum, v_sum, kv_send, bounce, send, recv, kv_out, kv_in, near,
    ):
        wires = Wires(send, recv)
        my_c = lax.axis_index("ctx")
        greet([link.place(("ctx",), offset)[0] for offset in levels])
        copies = []
        for offset in levels:
            where, index = link.place(("ctx",), offset)
            copies.append(wires.start(rows_ref.at[index], got_rows.at[my_c], where))
        inward = pltpu.make_async_copy(rows_ref.at[my_c], bounce, near.at[0])
        outward = pltpu.make_async_copy(bounce, got_rows.at[my_c], near.at[0])
        inward.start()
        acc[...] = jnp.zeros_like(acc)
        delta[...] = jnp.zeros_like(delta)
        for i in range(steps):
            at = slice(i * TQ, i * TQ + TQ)
            marks[i] = qm_ref[:, at]
            lses[i] = lse_ref[:, at]
            for j, (b, h) in enumerate(HEAD_SLOTS):
                lanes = slice(128 * b, 128 * b + 128)
                heads[i, j] = head_block(q_ref[at, lanes], h)
                grad = head_block(do_ref[at, lanes], h)
                grads[i, j] = grad
                product = grad.astype(F32) * o_ref[at, lanes]
                delta[i, j : j + 1, :] = jnp.sum(product.T, axis=0, keepdims=True)
        inward.wait()
        outward.start()

        @pl.loop(0, ctx)
        def _(d):
            chunk = lax.rem(my_c + 1 + d, ctx)

            @pl.loop(0, span // BK)
            def _(t):
                inner = pl.multiple_of(t * BK, 128)
                at = pl.ds(pl.multiple_of(chunk * span + t * BK, 128), BK)
                k_tile = kv_ref[at, :128]
                v_tile = kv_ref[at, 128:]
                key_pos = jnp.tile(kp_ref[at, :], (1, TQ // 128))
                key_seg = jnp.tile(ks_ref[at, :], (1, TQ // 128))
                k_sum[...] = jnp.zeros_like(k_sum)
                v_sum[...] = jnp.zeros_like(v_sum)

                @pl.loop(0, steps)
                def _(i):
                    seen = (key_pos <= marks[i, 0:1, :]) & (
                        (key_seg == 0) | (key_seg == marks[i, 1:2, :])
                    )
                    k_part = jnp.zeros((BK, 128), F32)
                    v_part = jnp.zeros((BK, 128), F32)
                    scores = [dot_general(k_tile, heads[i, j], 1, 1) for j in range(5)]
                    back = [dot_general(v_tile, grads[i, j], 1, 1) for j in range(5)]
                    probs = [
                        jnp.where(seen, jnp.exp(scores[j] - lses[i, j : j + 1, :]), 0.0)
                        for j in range(5)
                    ]
                    score_grad = [
                        (probs[j] * (back[j] - delta[i, j : j + 1, :])).astype(BF)
                        for j in range(5)
                    ]
                    for j in range(5):
                        v_part += jnp.dot(
                            probs[j].astype(BF), grads[i, j], preferred_element_type=F32
                        )
                        k_part += jnp.dot(
                            score_grad[j], heads[i, j], preferred_element_type=F32
                        )
                        acc[i, j] += dot_general(k_tile, score_grad[j], 0, 0)
                    k_sum[...] += k_part
                    v_sum[...] += v_part

                kv_send[chunk, pl.ds(inner, BK), :128] = k_sum[...].astype(BF)
                kv_send[chunk, pl.ds(inner, BK), 128:] = v_sum[...].astype(BF)

            @pl.when(d < ctx - 1)
            def _():
                pltpu.make_async_remote_copy(
                    kv_send.at[chunk],
                    got_kv.at[my_c],
                    kv_out.at[d],
                    kv_in.at[d],
                    device_id={"ctx": chunk},
                    device_id_type=MESH,
                ).start()

        near_kv = pltpu.make_async_copy(kv_send.at[my_c], got_kv.at[my_c], near.at[1])
        near_kv.start()
        low = lax.broadcasted_iota(jnp.int32, (TQ, 128), 1) < 64
        for i in range(steps):
            for b in range(3):
                first = acc[i, 2 * b].T * 0.125
                if b < 2:
                    block = jnp.where(low, first, acc[i, 2 * b + 1].T * 0.125)
                else:
                    block = jnp.where(low, first, 0.0)
                dq_ref[i * TQ : i * TQ + TQ, 128 * b : 128 * b + 128] = block.astype(BF)

        near_kv.wait()
        outward.wait()
        for copy in copies:
            copy.wait()

        for d in range(ctx - 1):
            pltpu.make_async_remote_copy(
                kv_send.at[0],
                got_kv.at[0],
                kv_out.at[d],
                kv_in.at[d],
                device_id={"ctx": my_c},
                device_id_type=MESH,
            ).wait()

    vmem = pl.BlockSpec(memory_space=pltpu.VMEM)
    anywhere = pl.BlockSpec(memory_space=pl.ANY)
    return pl.pallas_call(
        kernel,
        name="attend_backward",
        in_specs=[vmem] * 8 + [anywhere],
        out_specs=[vmem] + [anywhere] * 2,
        out_shape=[
            jax.ShapeDtypeStruct((rows, 384), BF),
            jax.ShapeDtypeStruct((ctx, span, 256), BF),
            jax.ShapeDtypeStruct(send_rows.shape, BF),
        ],
        scratch_shapes=[
            pltpu.VMEM((steps, 5, 128, TQ), F32),
            pltpu.VMEM((steps, 5, TQ, 128), BF),
            pltpu.VMEM((steps, 5, TQ, 128), BF),
            pltpu.VMEM((steps, 8, TQ), F32),
            pltpu.VMEM((steps, 8, TQ), F32),
            pltpu.VMEM((steps, 8, TQ), F32),
            pltpu.VMEM((BK, 128), F32),
            pltpu.VMEM((BK, 128), F32),
            pltpu.VMEM((ctx, span, 256), BF),
            pltpu.VMEM(send_rows.shape[1:], BF),
            pltpu.SemaphoreType.DMA((ctx,)),
            pltpu.SemaphoreType.DMA((ctx,)),
            pltpu.SemaphoreType.DMA((ctx,)),
            pltpu.SemaphoreType.DMA((ctx,)),
            pltpu.SemaphoreType.DMA((2,)),
        ],
        compiler_params=pltpu.CompilerParams(
            collective_id=11, has_side_effects=True, vmem_limit_bytes=VMEM_LIMIT
        ),
    )(q, kv, q_marks, k_pos, k_seg, lse, out, out_grad, send_rows)


class Wires:
    def __init__(self, send, recv):
        self.send, self.recv, self.used = send, recv, 0

    def copy(self, source, target, where):
        at = self.used
        self.used += 1
        return pltpu.make_async_remote_copy(
            source,
            target,
            self.send.at[at],
            self.recv.at[at],
            device_id=where,
            device_id_type=MESH,
        )

    def start(self, source, target, where):
        copy = self.copy(source, target, where)
        copy.start()
        return copy


def greet(places):
    barrier = pltpu.get_barrier_semaphore()
    for where in places:
        pl.semaphore_signal(barrier, 1, device_id=where, device_id_type=MESH)
    pl.semaphore_wait(barrier, len(places))


def square():
    w = lax.axis_index("wsh")
    return w, w + 1 - 2 * lax.rem(w, 2), w + 2 - 4 * (w // 2), 3 - w


class SquareScatter:
    def __init__(self, wires, parts, near, total):
        self.wires, self.parts, self.near, self.total = wires, parts, near, total
        self.half = parts.shape[1] // 2
        self.a, self.b = pl.ds(0, self.half), pl.ds(self.half, self.half)
        self.own, self.x, self.y, self.z = square()
        self.pending = []

    def send_diagonal(self):
        wires, parts = self.wires, self.parts
        self.one = wires.start(parts.at[self.z, self.a], self.near.at[0], {"wsh": self.x})
        self.two = wires.start(parts.at[self.z, self.b], self.near.at[1], {"wsh": self.y})

    def send_x(self):
        self.pending.append(
            self.wires.start(
                self.parts.at[self.x, self.a], self.total.at[0, self.a], {"wsh": self.x}
            )
        )

    def send_y(self):
        self.pending.append(
            self.wires.start(
                self.parts.at[self.y, self.b], self.total.at[1, self.b], {"wsh": self.y}
            )
        )

    def relay(self):
        near, parts = self.near, self.parts
        self.one.wait()
        near[2] = (near[0].astype(F32) + parts[self.y, self.a].astype(F32)).astype(BF)
        self.pending.append(
            self.wires.start(near.at[2], self.total.at[1, self.a], {"wsh": self.y})
        )
        self.two.wait()
        near[3] = (near[1].astype(F32) + parts[self.x, self.b].astype(F32)).astype(BF)
        self.pending.append(
            self.wires.start(near.at[3], self.total.at[0, self.b], {"wsh": self.x})
        )

    def result(self):
        for copy in self.pending:
            copy.wait()
        return (
            self.parts[self.own].astype(F32)
            + self.total[0].astype(F32)
            + self.total[1].astype(F32)
        )


def square_scratch(rows):
    return [pltpu.VMEM((4, rows // 2, D), BF), pltpu.VMEM((2, rows, D), BF)]


class SquareGather:
    def __init__(self, wires, out):
        self.wires, self.out = wires, out
        half = out.shape[1] // 2
        self.a, self.b = pl.ds(0, half), pl.ds(half, half)
        self.own, self.x, self.y, self.z = square()

    def move(self, slot, part, to):
        return self.wires.start(self.out.at[slot, part], self.out.at[slot, part], {"wsh": to})

    def begin(self):
        self.xa = self.move(self.own, self.a, self.x)
        self.yb = self.move(self.own, self.b, self.y)
        self.xb = self.move(self.own, self.b, self.x)
        self.ya = self.move(self.own, self.a, self.y)

    def relay(self):
        self.xa.wait()
        self.one = self.move(self.x, self.a, self.y)
        self.yb.wait()
        self.two = self.move(self.y, self.b, self.x)

    def wait_x(self):
        self.xb.wait()

    def wait_y(self):
        self.ya.wait()

    def wait_z(self):
        self.one.wait()
        self.two.wait()


def feed(link, attended, w_out, tokens, gain, w_half, down, dy):
    ctx, wsh = link.sizes["ctx"], link.sizes["wsh"]
    own_rows = tokens.shape[0]
    plane = dy.shape[0]
    units = down.shape[0]
    chunk = D // ctx
    pick = units // ctx // 2
    early = EARLY

    def kernel(
        at_ref, ao_ref, x_ref, g_ref, wh_ref, dw_ref, dy_ref,
        mid_ref, mg_ref, br_ref, ag_ref, fs_ref, dp_ref, gs_ref, gl_ref, ds_ref,
        wo_ref, w_both, parts, near, total, near2, total2, n2, hgrad, hidden, gate_g, up_g,
        down_h, down_pair, down_send, down_got, gate_h, gate_pair, send, recv, local,
    ):
        wires = Wires(send, recv)
        core = lax.axis_index("grp")
        sibling = {"grp": 1 - core}
        my_c = lax.axis_index("ctx")
        own, x, y, z = square()
        levels = [link.place(("ctx",), offset) for offset in link.offsets(("ctx",))[1:]]
        greet([{"wsh": x}, {"wsh": y}, sibling] + [where for where, _ in levels])

        def rows_of(slot):
            return pl.ds(pl.multiple_of(slot * own_rows, 16), own_rows)

        w_copy = pltpu.make_async_copy(wh_ref, w_both.at[core], local)
        w_copy.start()

        odd = lax.rem(own, 2) == 1
        wo_ref[...] = jnp.zeros_like(wo_ref)

        def spread(pieces):
            at = 0
            for start, size in pieces:
                wo_ref[start : start + size, :] = ao_ref[at : at + size, :]
                at += size

        @pl.when(odd)
        def _():
            spread(ODD_ROWS)

        @pl.when(jnp.logical_not(odd))
        def _():
            spread(EVEN_ROWS)

        first = SquareScatter(wires, parts, near, total)
        for slot in (z, x, y, own):
            parts[slot] = jnp.dot(
                at_ref[rows_of(slot), :], wo_ref[...], preferred_element_type=F32
            ).astype(BF)
            if slot is z:
                first.send_diagonal()
            elif slot is x:
                first.send_x()
            elif slot is y:
                first.send_y()
        w_swap = wires.start(wh_ref, w_both.at[core], sibling)
        hgrad[...] = dot_general(dy_ref[...], dw_ref[...], 1, 1)
        first.relay()
        middle = x_ref[...].astype(F32) + first.result()
        mid_ref[...] = middle
        factor = lax.rsqrt(jnp.mean(middle * middle, axis=-1, keepdims=True) + EPSILON)
        n2[own] = (middle * factor * g_ref[...].reshape(1, D)).astype(BF)
        gather = SquareGather(wires, n2)
        gather.begin()
        w_copy.wait()
        w_swap.wait()

        def block(slot):
            at = rows_of(slot)
            gate = jnp.dot(n2[slot], w_both[0], preferred_element_type=F32)
            up = jnp.dot(n2[slot], w_both[1], preferred_element_type=F32)
            sigmoid = 1.0 / (1.0 + jnp.exp(-gate))
            silu = gate * sigmoid
            hidden[at, :] = (silu * up).astype(BF)
            back = hgrad[at, :]
            gate_g[at, :] = (back * up * sigmoid * (1.0 + gate * (1.0 - sigmoid))).astype(BF)
            up_g[at, :] = (back * silu).astype(BF)
            parts[slot] = (
                dot_general(gate_g[at, :], w_both[0], 1, 1)
                + dot_general(up_g[at, :], w_both[1], 1, 1)
            ).astype(BF)

        second = SquareScatter(wires, parts, near2, total2)
        block(own)
        gather.relay()
        gather.wait_x()
        block(x)
        second.send_x()
        gather.wait_y()
        block(y)
        second.send_y()
        gather.wait_z()
        block(z)
        second.send_diagonal()

        strip = dot_general(hidden[...], dy_ref[...], 0, 0).astype(BF)
        for k in range(ctx):
            for g in range(2):
                top = (2 * k + g) * pick
                down_h[g, k] = strip[top : top + pick, :]
        down_swap = wires.start(down_h.at[1 - core], down_pair, sibling)
        second.relay()
        tokens_all = n2[...].reshape(plane, D)
        for g, source in enumerate((gate_g, up_g)):
            strip = dot_general(tokens_all, source[...], 0, 0).astype(BF)
            for c in range(ctx):
                gate_h[g, c] = strip[c * chunk : c * chunk + chunk, :]
        gate_swap = wires.start(gate_h.at[1 - core], gate_pair, sibling)
        down_swap.wait()
        down_send[...] = (down_h[core].astype(F32) + down_pair[...].astype(F32)).astype(BF)
        down_copies = []
        for where, index in levels:
            down_copies.append(wires.start(down_send.at[index], down_got.at[my_c], where))
        down_got[my_c] = down_send[my_c]

        grad = second.result()
        middle = mid_ref[...]
        factor = lax.rsqrt(jnp.mean(middle * middle, axis=-1, keepdims=True) + EPSILON)
        weighted = grad * g_ref[...].reshape(1, D)
        inner = jnp.mean(weighted * middle, axis=-1, keepdims=True)
        middle_grad = (
            dy_ref[rows_of(own), :].astype(F32)
            + factor * weighted
            - middle * (factor * factor * factor) * inner
        )
        mg_ref[...] = middle_grad
        br_ref[own] = middle_grad.astype(BF)
        branch = SquareGather(wires, br_ref)
        branch.begin()
        fs_ref[...] = jnp.sum(grad * middle * factor, axis=0, keepdims=True)

        def outward(slot):
            ag_ref[rows_of(slot), :] = dot_general(br_ref[slot], wo_ref[...], 1, 1).astype(BF)

        outward(own)
        gate_swap.wait()
        for c in range(ctx):
            both = (gate_h[core, c].astype(F32) + gate_pair[c].astype(F32)).astype(BF)
            gs_ref[c] = both[:, :early]
            gl_ref[c] = both[:, early:]
        branch.relay()

        @pl.loop(0, wsh)
        def _(slot):
            dp_ref[slot] = jnp.dot(
                hidden[rows_of(slot), :], dw_ref[...], preferred_element_type=F32
            ).astype(BF)

        branch.wait_x()
        outward(x)
        branch.wait_y()
        outward(y)
        branch.wait_z()
        outward(z)
        for copy in down_copies:
            copy.wait()
        ds_ref[...] = jnp.sum(down_got[...].astype(F32), axis=0).astype(BF)

    operands = (attended, w_out, tokens, gain, w_half, down, dy)
    vmem = pl.BlockSpec(memory_space=pltpu.VMEM)
    return pl.pallas_call(
        kernel,
        name="feed",
        in_specs=[vmem] * len(operands),
        out_specs=[vmem] * 9,
        out_shape=[
            jax.ShapeDtypeStruct((own_rows, D), F32),
            jax.ShapeDtypeStruct((own_rows, D), F32),
            jax.ShapeDtypeStruct((wsh, own_rows, D), BF),
            jax.ShapeDtypeStruct((plane, 384), BF),
            jax.ShapeDtypeStruct((1, D), F32),
            jax.ShapeDtypeStruct((wsh, own_rows, D), BF),
            jax.ShapeDtypeStruct((ctx, chunk, early), BF),
            jax.ShapeDtypeStruct((ctx, chunk, units - early), BF),
            jax.ShapeDtypeStruct((pick, D), BF),
        ],
        scratch_shapes=[
            pltpu.VMEM((384, D), BF),
            pltpu.VMEM((2, D, units), BF),
            pltpu.VMEM((4, own_rows, D), BF),
            *square_scratch(own_rows),
            *square_scratch(own_rows),
            pltpu.VMEM((4, own_rows, D), BF),
            pltpu.VMEM((plane, units), F32),
            *[pltpu.VMEM((plane, units), BF)] * 3,
            pltpu.VMEM((2, ctx, pick, D), BF),
            *[pltpu.VMEM((ctx, pick, D), BF)] * 3,
            pltpu.VMEM((2, ctx, chunk, units), BF),
            pltpu.VMEM((ctx, chunk, units), BF),
            pltpu.SemaphoreType.DMA((ctx + 28,)),
            pltpu.SemaphoreType.DMA((ctx + 28,)),
            pltpu.SemaphoreType.DMA,
        ],
        compiler_params=pltpu.CompilerParams(
            collective_id=3, has_side_effects=True, vmem_limit_bytes=VMEM_LIMIT
        ),
    )(*operands)


def head(link, tokens, gain, weight, positions, segments, upstream, gate_up):
    ctx, wsh = link.sizes["ctx"], link.sizes["wsh"]
    own_rows = tokens.shape[0]
    plane, group = own_rows * wsh, own_rows * wsh * ctx
    half = weight.shape[0] // 2
    units = FF // wsh
    steps = plane // TQ

    def kernel(
        x_ref, g_ref, w_ref, pos_ref, seg_ref, up_ref, gu_ref,
        q_ref, kv_ref, n_ref, wq_ref, kpos_ref, kseg_ref, q_marks, dy_ref, c_ref, s_ref,
        a_ref, o_ref, lse_ref, wh_ref,
        cols, mine, marks_all, heads, tile_marks, acc, top, tot, bounce, send, recv, kv_out, kv_in,
        near,
    ):
        wires = Wires(send, recv)
        core = lax.axis_index("grp")
        sibling = {"grp": 1 - core}
        my_c = lax.axis_index("ctx")
        own, x, y, z = square()
        levels = [link.place(("ctx",), offset) for offset in link.offsets(("ctx",))[1:]]
        greet(
            [{"wsh": x}, {"wsh": y}, {"wsh": z}, sibling] + [where for where, _ in levels]
        )
        mine[...] = jnp.zeros_like(mine)
        mine[0:1, :own_rows] = pos_ref[...].reshape(1, own_rows).astype(F32)
        mine[1:2, :own_rows] = seg_ref[...].reshape(1, own_rows).astype(F32)
        mark_copies = []
        for p in (x, y, z):
            mark_copies.append(wires.start(mine, marks_all.at[my_c, own], {"wsh": p}))
        marks_all[my_c, own] = mine[...]
        side = pl.ds(pl.multiple_of(core * half, 16), half)

        for w in range(wsh):
            q_order, kv_order = head_plan(w)
            slots = [h for h in q_order] + [HEADS + h for h in kv_order]
            slots += [HEADS + KV_HEADS + h for h in kv_order]
            blank = jnp.zeros((w_ref.shape[0], HEAD_DIM), BF)
            for pair in range(5):
                two = [
                    blank if h is None else w_ref[:, h * HEAD_DIM : h * HEAD_DIM + HEAD_DIM]
                    for h in slots[2 * pair : 2 * pair + 2]
                ]
                cols[w, :, 128 * pair : 128 * pair + 128] = jnp.concatenate(two, axis=1)
        w_copies = []
        for p in (x, y, z):
            w_copies.append(
                wires.start(cols.at[p, side], wq_ref.at[own, side], {"wsh": p})
            )
        tokens_in = x_ref[...].astype(F32)
        factor = lax.rsqrt(jnp.mean(tokens_in * tokens_in, axis=-1, keepdims=True) + EPSILON)
        n_ref[own] = (tokens_in * factor * g_ref[...].reshape(1, D)).astype(BF)
        wq_ref[own] = cols[own]
        dy_ref[own] = up_ref[...]

        for copy in mark_copies:
            copy.wait()
        level_copies = []
        for where, _ in levels:
            level_copies.append(wires.start(marks_all.at[my_c], marks_all.at[my_c], where))
        lane = lax.broadcasted_iota(jnp.int32, (1, 128), 1)
        power = lax.rem(lane, 32).astype(F32) * (-math.log(10000.0) / 32)
        frequency = jnp.exp(power)
        sign = jnp.where(lax.rem(lane, 64) < 32, -1.0, 1.0)

        def upright(row):
            return jnp.broadcast_to(row, (128, row.shape[1])).T

        for w in range(wsh):
            at = slice(w * own_rows, w * own_rows + own_rows)
            angles = upright(marks_all[my_c, w, 0:1, :])[:own_rows] * frequency
            c_ref[at, :] = jnp.cos(angles)
            s_ref[at, :] = jnp.sin(angles) * sign
        forward = []
        for p, copy in zip((x, y, z), w_copies):
            copy.wait()
            forward.append(wires.start(wq_ref.at[p, side], wq_ref.at[p, side], sibling))
        gather = SquareGather(wires, n_ref)
        gather.begin()
        for copy in forward:
            copy.wait()

        low = lax.rem(lax.broadcasted_iota(jnp.int32, (own_rows, 128), 1), 64) < 32

        def kv_copy(slot, order, d, to):
            at = pl.ds(pl.multiple_of(slot * own_rows, 16), own_rows)
            return pltpu.make_async_remote_copy(
                kv_ref.at[my_c, at],
                kv_ref.at[my_c, at],
                kv_out.at[order, d],
                kv_in.at[order, d],
                device_id={"ctx": to},
                device_id_type=MESH,
            )

        def block(slot, order):
            at = pl.ds(pl.multiple_of(slot * own_rows, 16), own_rows)
            full = jnp.dot(
                n_ref[slot], wq_ref[...].reshape(D, 640), preferred_element_type=F32
            )
            cos_t, sin_t = c_ref[at, :], s_ref[at, :]
            for b in range(3):
                turned = turn(full[:, 128 * b : 128 * b + 128], cos_t, sin_t, low)
                q_ref[at, 128 * b : 128 * b + 128] = (
                    turned.astype(BF).astype(F32) * 0.125
                ).astype(BF)
            kv_ref[my_c, at, :128] = turn(full[:, 384:512], cos_t, sin_t, low).astype(BF)
            kv_ref[my_c, at, 128:] = full[:, 512:].astype(BF)
            for d, (_, index) in enumerate(levels):
                kv_copy(slot, order, d, index).start()

        block(own, 0)
        gather.relay()
        dy_gather = SquareGather(wires, dy_ref)
        dy_gather.begin()
        gather.wait_x()
        block(x, 1)
        gather.wait_y()
        block(y, 2)
        gather.wait_z()
        block(z, 3)
        dy_gather.relay()

        def columns(p):
            left = core * FF + p * units
            return gu_ref.at[:, pl.ds(pl.multiple_of(left, 128), units)]

        gate_copies = []
        for p in (x, y, z):
            gate_copies.append(wires.start(columns(p), wh_ref.at[own], {"wsh": p}))
        inward = pltpu.make_async_copy(columns(own), bounce, near)
        outward = pltpu.make_async_copy(bounce, wh_ref.at[own], near)
        inward.start()

        for w in range(wsh):
            q_marks[:, w * own_rows : w * own_rows + own_rows] = marks_all[my_c, w, :, :own_rows]

        for copy in level_copies:
            copy.wait()

        @pl.loop(0, ctx)
        def _(c):
            for w in range(wsh):
                at = pl.ds(pl.multiple_of(c * plane + w * own_rows, 16), own_rows)
                kpos_ref[at, :] = upright(marks_all[c, w, 0:1, :])[:own_rows]
                kseg_ref[at, :] = upright(marks_all[c, w, 1:2, :])[:own_rows]

        inward.wait()
        outward.start()

        acc[...] = jnp.zeros_like(acc)
        top[...] = jnp.full_like(top, -1e30)
        tot[...] = jnp.zeros_like(tot)
        for i in range(steps):
            at = slice(i * TQ, i * TQ + TQ)
            tile_marks[i] = q_marks[:, at]
            for j, (b, side_of) in enumerate(HEAD_SLOTS):
                heads[i, j] = head_block(q_ref[at, 128 * b : 128 * b + 128], side_of)

        @pl.loop(0, ctx)
        def _(d):
            chunk = lax.rem(my_c + ctx - d, ctx)

            @pl.when(d > 0)
            def _():
                for order in range(wsh):
                    kv_copy(0, order, d - 1, my_c).wait()

            at = pl.ds(pl.multiple_of(chunk * plane, 128), plane)
            k_tile = kv_ref[chunk, :, :128]
            v_tile = kv_ref[chunk, :, 128:]
            key_pos = jnp.tile(kpos_ref[at, :], (1, TQ // 128))
            key_seg = jnp.tile(kseg_ref[at, :], (1, TQ // 128))

            @pl.loop(0, steps)
            def _(i):
                seen = (key_pos <= tile_marks[i, 0:1, :]) & (
                    (key_seg == 0) | (key_seg == tile_marks[i, 1:2, :])
                )
                scores = [
                    jnp.where(seen, dot_general(k_tile, heads[i, j], 1, 1), -1e30)
                    for j in range(5)
                ]
                old = [top[i, j : j + 1, :] for j in range(5)]
                new = [
                    jnp.maximum(old[j], jnp.max(scores[j], axis=0, keepdims=True))
                    for j in range(5)
                ]
                expons = [jnp.exp(scores[j] - new[j]) for j in range(5)]
                shrink = [jnp.exp(old[j] - new[j]) for j in range(5)]
                mixed = [dot_general(v_tile, expons[j].astype(BF), 0, 0) for j in range(5)]
                for j in range(5):
                    tot[i, j : j + 1, :] = tot[i, j : j + 1, :] * shrink[j] + jnp.sum(
                        expons[j], axis=0, keepdims=True
                    )
                    acc[i, j] = acc[i, j] * shrink[j] + mixed[j]
                    top[i, j : j + 1, :] = new[j]

        half_lanes = lax.broadcasted_iota(jnp.int32, (TQ, 128), 1) < 64
        for i in range(steps):
            at = slice(i * TQ, i * TQ + TQ)
            lse_ref[:, at] = top[i] + jnp.log(jnp.maximum(tot[i], 1e-37))
            outs = [(acc[i, j] / tot[i, j : j + 1, :]).T for j in range(5)] + [0.0]
            for b in range(3):
                block_out = jnp.where(half_lanes, outs[2 * b], outs[2 * b + 1])
                o_ref[at, 128 * b : 128 * b + 128] = block_out
                a_ref[at, 128 * b : 128 * b + 128] = block_out.astype(BF)

        dy_gather.wait_x()
        dy_gather.wait_y()
        dy_gather.wait_z()
        for copy in gate_copies:
            copy.wait()
        outward.wait()

    operands = (tokens, gain, weight, positions, segments, upstream, gate_up)
    vmem = pl.BlockSpec(memory_space=pltpu.VMEM)
    return pl.pallas_call(
        kernel,
        name="head",
        in_specs=[vmem] * 6 + [pl.BlockSpec(memory_space=pl.ANY)],
        out_specs=[vmem] * 13 + [pl.BlockSpec(memory_space=pl.ANY)],
        out_shape=[
            jax.ShapeDtypeStruct((plane, 384), BF),
            jax.ShapeDtypeStruct((ctx, plane, 256), BF),
            jax.ShapeDtypeStruct((wsh, own_rows, D), BF),
            jax.ShapeDtypeStruct((wsh, 2 * half, 640), BF),
            jax.ShapeDtypeStruct((group, 128), F32),
            jax.ShapeDtypeStruct((group, 128), F32),
            jax.ShapeDtypeStruct((8, plane), F32),
            jax.ShapeDtypeStruct((wsh, own_rows, D), BF),
            jax.ShapeDtypeStruct((plane, 128), F32),
            jax.ShapeDtypeStruct((plane, 128), F32),
            jax.ShapeDtypeStruct((plane, 384), BF),
            jax.ShapeDtypeStruct((plane, 384), F32),
            jax.ShapeDtypeStruct((8, plane), F32),
            jax.ShapeDtypeStruct((wsh, 2 * half, units), BF),
        ],
        scratch_shapes=[
            pltpu.VMEM((wsh, 2 * half, 640), BF),
            pltpu.VMEM((8, 256), F32),
            pltpu.VMEM((ctx, wsh, 8, 256), F32),
            pltpu.VMEM((steps, 5, TQ, 128), BF),
            pltpu.VMEM((steps, 8, TQ), F32),
            pltpu.VMEM((steps, 5, 128, TQ), F32),
            pltpu.VMEM((steps, 8, TQ), F32),
            pltpu.VMEM((steps, 8, TQ), F32),
            pltpu.VMEM((2 * half, units), BF),
            pltpu.SemaphoreType.DMA((ctx + 28,)),
            pltpu.SemaphoreType.DMA((ctx + 28,)),
            pltpu.SemaphoreType.DMA((wsh, ctx)),
            pltpu.SemaphoreType.DMA((wsh, ctx)),
            pltpu.SemaphoreType.DMA,
        ],
        compiler_params=pltpu.CompilerParams(
            collective_id=1, has_side_effects=True, vmem_limit_bytes=VMEM_LIMIT
        ),
    )(*operands)


def finish(
    link, q_grad, kv_grad, weight, cos, sin, normed, tokens, gain, middle_grad, gate_got, down_got,
    attended, branch, feed_sum, down_part, middle, gate_late,
):
    ctx, wsh = link.sizes["ctx"], link.sizes["wsh"]
    shards = ctx * wsh
    rows = D // shards
    chunk = D // ctx
    fold = ctx // wsh
    own_rows = tokens.shape[0]
    plane = normed.shape[0]
    axes = ("ctx", "wsh")
    peers = link.offsets(axes)
    gate_width, late_width = gate_got.shape[2], gate_late.shape[2]
    down_rows = down_got.shape[0]
    piece = down_rows // wsh

    def kernel(
        q_ref, kv_ref, w_ref, c_ref, s_ref, n_ref, x_ref, g_ref, mg_ref, gate_ref, down_ref,
        at_ref, br_ref, fs_ref, dp_ref, mid_ref, late_ref,
        act_ref, ig_ref, q_fin, kv_fin, out_fin, gate_fin, late_fin, down_fin, gains_out,
        pg, parts, near, total, near2, total2, wide, q_own, q_pair, q_send, q_got,
        q_mid, kv_own, kv_pair, kv_go, kv_got, kv_mid, gate_mid, late_got,
        late_mid, spread, spread_got, risen, landed, out_halves,
        out_pair, out_send, out_mid, out_got, gains, gains_got, gains_fin,
        send, recv,
    ):
        wires = Wires(send, recv)
        core = lax.axis_index("grp")
        first, second = core == 0, core == 1
        sibling = {"grp": 1 - core}
        my_c, my_w = lax.axis_index("ctx"), lax.axis_index("wsh")
        odd = lax.rem(my_w, 2) == 1
        greet([link.place(axes, offset)[0] for offset in peers[1:]] + [sibling])
        _, me = link.place(axes, peers[0])

        def over_ctx(got, mid):
            for w in range(wsh):
                strip = got[0, w * rows : w * rows + rows, :].astype(F32)
                for c in range(1, ctx):
                    strip += got[c, w * rows : w * rows + rows, :].astype(F32)
                mid[w] = strip.astype(BF)

        def in_plane(mid, slot_of):
            copies = []
            for offset in link.offsets(("wsh",))[1:]:
                where, index = link.place(("wsh",), offset)
                copies.append(wires.copy(mid.at[index], slot_of(my_w), where))
            return copies

        def begin(cond, *copies):
            @pl.when(cond)
            def _():
                for copy in copies:
                    copy.start()

        levels = [link.place(("ctx",), offset) for offset in link.offsets(("ctx",))[1:]]
        late_copies = []
        for where, index in levels:
            late_copies.append(wires.start(late_ref.at[index], late_got.at[my_c], where))

        for p in range(wsh):
            spread[p] = down_ref[p * piece : p * piece + piece, :]
        spread_moves = in_plane(spread, lambda w: spread_got.at[w])
        for copy in spread_moves:
            copy.start()
        spread_got[my_w] = spread[my_w]

        low = lax.rem(lax.broadcasted_iota(jnp.int32, (own_rows, 128), 1), 64) < 32
        scatter = SquareScatter(wires, parts, near, total)
        gain_sum = jnp.zeros((1, D), F32)
        for slot in (scatter.z, scatter.x, scatter.y, scatter.own):
            at = pl.ds(pl.multiple_of(slot * own_rows, 16), own_rows)
            cos_t, sin_t = c_ref[at, :], -s_ref[at, :]
            for b in range(3):
                block = q_ref[at, 128 * b : 128 * b + 128].astype(F32)
                pg[at, 128 * b : 128 * b + 128] = turn(block, cos_t, sin_t, low).astype(BF)
            summed = kv_ref[0, at, :].astype(F32)
            for c in range(1, ctx):
                summed += kv_ref[c, at, :].astype(F32)
            block = summed[:, :128].astype(BF).astype(F32)
            pg[at, 384:512] = turn(block, cos_t, sin_t, low).astype(BF)
            pg[at, 512:] = summed[:, 128:].astype(BF)
            part = dot_general(pg[at, :], w_ref[...], 1, 1)
            parts[slot] = part.astype(BF)
            gain_sum += jnp.sum(part * n_ref[at, :].astype(F32), axis=0, keepdims=True)
            if slot is scatter.z:
                scatter.send_diagonal()
            elif slot is scatter.x:
                scatter.send_x()
            elif slot is scatter.y:
                scatter.send_y()

        for copy in spread_moves:
            copy.wait()
        lane = lax.rem(my_c, wsh)
        rise, arrive = wires.used, []
        wires.used += wsh
        for p in range(wsh):
            to = (p * ctx + my_c) // wsh
            out_copy_p = pltpu.make_async_remote_copy(
                spread_got.at[p],
                risen.at[lane],
                send.at[rise + p],
                recv.at[rise + lane],
                device_id={"ctx": to},
                device_id_type=MESH,
            )

            @pl.when(to != my_c)
            def _():
                out_copy_p.start()

            @pl.when(to == my_c)
            def _():
                risen[lane] = spread_got[p]

            from_c = lax.rem(my_c, fold) * wsh + p
            in_copy_p = pltpu.make_async_remote_copy(
                spread_got.at[p],
                risen.at[p],
                send.at[rise + p],
                recv.at[rise + p],
                device_id={"ctx": to},
                device_id_type=MESH,
            )
            arrive.append((out_copy_p, to != my_c, in_copy_p, from_c != my_c))

        strip = dot_general(n_ref[...], pg[:, 384:], 0, 0).astype(BF)
        for c in range(ctx):
            kv_own[c] = strip[c * chunk : c * chunk + chunk, :]
        kv_swap = wires.copy(kv_own, kv_pair, sibling)
        begin(first, kv_swap)
        scatter.relay()
        strip = dot_general(n_ref[...], pg[:, :384], 0, 0).astype(BF)
        for c in range(ctx):
            q_own[c] = strip[c * chunk : c * chunk + chunk, :]
        q_swap = wires.copy(q_own, q_pair, sibling)
        begin(second, q_swap)
        layer = SquareScatter(wires, dp_ref, near2, total2)
        layer.send_diagonal()
        layer.send_x()
        layer.send_y()
        wide[...] = dot_general(at_ref[...], br_ref[...], 0, 0)

        def out_strips(pieces):
            at = 0
            for start, size in pieces:
                acc_rows = wide[start : start + size, :].astype(BF)
                part = jnp.concatenate([acc_rows[:, :576], jnp.zeros((size, 64), BF)], axis=1)
                out_halves[0, at : at + size, :] = part
                part = jnp.concatenate([acc_rows[:, 576:], jnp.zeros((size, 64), BF)], axis=1)
                out_halves[1, at : at + size, :] = part
                at += size

        @pl.when(odd)
        def _():
            out_strips(ODD_ROWS)

        @pl.when(jnp.logical_not(odd))
        def _():
            out_strips(EVEN_ROWS)

        out_swap = wires.start(out_halves.at[1 - core], out_pair, sibling)
        q_copies, kvg_copies, out_copies = [], [], []
        for where, index in levels:
            q_copies.append(wires.copy(q_send.at[index], q_got.at[my_c], where))
            kvg_copies.append(wires.copy(kv_go.at[index], kv_got.at[my_c], where))

        @pl.when(first)
        def _():
            q_swap.wait_recv()

            @pl.loop(0, ctx)
            def _(c):
                q_send[c] = (q_own[c].astype(F32) + q_pair[c].astype(F32)).astype(BF)

            for copy in q_copies:
                copy.start()
            q_got[my_c] = q_send[my_c]
            kv_swap.wait_send()

        @pl.when(second)
        def _():
            kv_swap.wait_recv()

            @pl.loop(0, ctx)
            def _(c):
                kv_go[c] = (kv_own[c].astype(F32) + kv_pair[c].astype(F32)).astype(BF)

            for copy in kvg_copies:
                copy.start()
            kv_got[my_c] = kv_go[my_c]
            q_swap.wait_send()

        both = jnp.concatenate([gain_sum / g_ref[...].reshape(1, D), fs_ref[...]], axis=0)
        gains[...] = jnp.zeros_like(gains)
        for s in range(shards):
            gains[s, :2, :rows] = both[:, rows * s : rows * s + rows]
        gain_copies = []
        for offset in peers[1:]:
            where, index = link.place(axes, offset)
            gain_copies.append(wires.start(gains.at[index], gains_got.at[me], where))
        gains_got[me] = gains[me]
        layer.relay()

        out_swap.wait()
        for k in range(ctx):
            strip = slice(k * rows, k * rows + rows)
            out_send[k % wsh, k // wsh] = (
                out_halves[core, strip, :].astype(F32) + out_pair[strip, :].astype(F32)
            ).astype(BF)
        out_moves = in_plane(out_send, lambda w: out_mid.at[w])
        for copy in out_moves:
            copy.start()
        out_mid[my_w] = out_send[my_w]

        grad = scatter.result()
        x = x_ref[...].astype(F32)
        factor = lax.rsqrt(jnp.mean(x * x, axis=-1, keepdims=True) + EPSILON)
        weighted = grad * g_ref[...].reshape(1, D)
        inner = jnp.mean(weighted * x, axis=-1, keepdims=True)
        ig_ref[...] = mg_ref[...] + factor * weighted - x * (factor * factor * factor) * inner
        for copy in out_moves:
            copy.wait()
        for where, index in levels:
            part = out_mid.at[index // fold, lax.rem(index, fold)]
            out_copies.append(wires.start(part, out_got.at[my_c], where))
        out_got[my_c] = out_mid[my_c // fold, lax.rem(my_c, fold)]


        for out_copy_p, goes, in_copy_p, comes in arrive:

            @pl.when(goes)
            def _():
                out_copy_p.wait_send()

            @pl.when(comes)
            def _():
                in_copy_p.wait_recv()

        land_moves = in_plane(risen, lambda w: landed.at[w])
        for copy in land_moves:
            copy.start()
        landed[my_w] = risen[my_w]
        over_ctx(gate_ref, gate_mid)
        gate_moves = in_plane(gate_mid, lambda w: gate_fin.at[core, w])
        for copy in gate_moves:
            copy.start()
        gate_fin[core, my_w] = gate_mid[my_w]
        for copy in late_copies:
            copy.wait()
        late_got[my_c] = late_ref[my_c]
        over_ctx(late_got, late_mid)
        late_moves = in_plane(late_mid, lambda w: late_fin.at[core, w])
        for copy in late_moves:
            copy.start()
        late_fin[core, my_w] = late_mid[my_w]
        act_ref[...] = (mid_ref[...] + layer.result()).astype(BF)

        q_moves = in_plane(q_mid, lambda w: q_fin.at[w])
        kv_moves = in_plane(kv_mid, lambda w: kv_fin.at[w])

        @pl.when(first)
        def _():
            for copy in q_copies:
                copy.wait()
            over_ctx(q_got, q_mid)
            for copy in q_moves:
                copy.start()
            q_fin[my_w] = q_mid[my_w]

        @pl.when(second)
        def _():
            for copy in kvg_copies:
                copy.wait()
            over_ctx(kv_got, kv_mid)
            for copy in kv_moves:
                copy.start()
            kv_fin[my_w] = kv_mid[my_w]

        for copy in land_moves:
            copy.wait()
        for p in range(wsh):
            down_fin[core, p * piece : p * piece + piece, :] = landed[p]
        down_copy = wires.start(down_fin.at[core], down_fin.at[core], sibling)
        for copy in gate_moves + late_moves:
            copy.wait()
        gate_copy = wires.start(gate_fin.at[core], gate_fin.at[core], sibling)
        late_copy = wires.start(late_fin.at[core], late_fin.at[core], sibling)
        for copy in out_copies:
            copy.wait()
        out_fin[core] = jnp.sum(out_got[...].astype(F32), axis=0).astype(BF)
        out_copy = wires.start(out_fin.at[core], out_fin.at[core], sibling)
        for copy in gain_copies:
            copy.wait()
        gains_fin[core] = jnp.sum(gains_got[...], axis=0)
        gain_copy = wires.start(gains_fin.at[core], gains_fin.at[core], sibling)
        q_final = wires.copy(q_fin, q_fin, sibling)
        kv_final = wires.copy(kv_fin, kv_fin, sibling)

        @pl.when(first)
        def _():
            for copy in q_moves:
                copy.wait()
            q_final.start()

        @pl.when(second)
        def _():
            for copy in kv_moves:
                copy.wait()
            kv_final.start()

        down_copy.wait()
        gate_copy.wait()
        late_copy.wait()
        out_copy.wait()

        @pl.when(first)
        def _():
            q_final.wait_send()
            kv_final.wait_recv()

        @pl.when(second)
        def _():
            kv_final.wait_send()
            q_final.wait_recv()

        gain_copy.wait()
        gains_out[...] = gains_fin[0] + gains_fin[1]

    operands = (
        q_grad, kv_grad, weight, cos, sin, normed, tokens, gain, middle_grad, gate_got, down_got,
        attended, branch, feed_sum, down_part, middle, gate_late,
    )
    vmem = pl.BlockSpec(memory_space=pltpu.VMEM)
    return pl.pallas_call(
        kernel,
        name="finish",
        in_specs=[vmem] * len(operands),
        out_specs=[vmem] * 9,
        out_shape=[
            jax.ShapeDtypeStruct((own_rows, D), BF),
            jax.ShapeDtypeStruct((own_rows, D), F32),
            jax.ShapeDtypeStruct((wsh, rows, 384), BF),
            jax.ShapeDtypeStruct((wsh, rows, 256), BF),
            jax.ShapeDtypeStruct((2, rows, 640), BF),
            jax.ShapeDtypeStruct((2, wsh, rows, gate_width), BF),
            jax.ShapeDtypeStruct((2, wsh, rows, late_width), BF),
            jax.ShapeDtypeStruct((2, down_rows, D), BF),
            jax.ShapeDtypeStruct((8, 128), F32),
        ],
        scratch_shapes=[
            pltpu.VMEM((plane, 640), BF),
            pltpu.VMEM((4, own_rows, D), BF),
            *square_scratch(own_rows),
            *square_scratch(own_rows),
            pltpu.VMEM((384, D), F32),
            *[pltpu.VMEM((ctx, chunk, 384), BF)] * 4,
            pltpu.VMEM((wsh, rows, 384), BF),
            *[pltpu.VMEM((ctx, chunk, 256), BF)] * 4,
            pltpu.VMEM((wsh, rows, 256), BF),
            pltpu.VMEM((wsh, rows, gate_width), BF),
            pltpu.VMEM((ctx, chunk, late_width), BF),
            pltpu.VMEM((wsh, rows, late_width), BF),
            *[pltpu.VMEM((wsh, piece, D), BF)] * 4,
            pltpu.VMEM((2, 288, 640), BF),
            pltpu.VMEM((288, 640), BF),
            pltpu.VMEM((wsh, fold, rows, 640), BF),
            pltpu.VMEM((wsh, fold, rows, 640), BF),
            pltpu.VMEM((ctx, rows, 640), BF),
            pltpu.VMEM((shards, 8, 128), F32),
            pltpu.VMEM((shards, 8, 128), F32),
            pltpu.VMEM((2, 8, 128), F32),
            pltpu.SemaphoreType.DMA((shards + 5 * ctx + 48,)),
            pltpu.SemaphoreType.DMA((shards + 5 * ctx + 48,)),
        ],
        compiler_params=pltpu.CompilerParams(
            collective_id=8, has_side_effects=True, vmem_limit_bytes=VMEM_LIMIT
        ),
    )(*operands)


def wrap(act, input_grad, q_sum, kv_sum, out_sum, gate_sum, late_sum, down_sum, gain_sum):
    wsh, rows, _ = q_sum.shape
    down_rows = down_sum.shape[1]
    width, wide = gate_sum.shape[3], late_sum.shape[3]

    def kernel(
        act_in, ig_in, q_in, kv_in, out_in, gate_in, late_in, down_in, gain_in,
        act_ref, ig_ref, qkv_ref, out_ref, gate_ref, down_ref, one_ref, two_ref,
    ):
        one_ref[...] = gain_in[0:1, :rows].reshape(rows)
        two_ref[...] = gain_in[1:2, :rows].reshape(rows)
        act_ref[...] = act_in[...]
        ig_ref[...] = ig_in[...]
        qkv_ref[...] = qkv_restore(
            [
                jnp.concatenate([q_in[w].astype(F32), kv_in[w].astype(F32)], axis=1)
                for w in range(wsh)
            ]
        )
        out_ref[...] = jnp.concatenate(
            [out_in[0, :, :576].astype(F32), out_in[1, :, :576].astype(F32)], axis=1
        )
        for half in range(2):
            for w in range(wsh):
                left = (half * wsh + w) * (width + wide)
                gate_ref[:, left : left + width] = gate_in[half, w].astype(F32)
                left += width
                gate_ref[:, left : left + wide] = late_in[half, w].astype(F32)
            down_ref[half * down_rows : half * down_rows + down_rows, :] = down_in[half].astype(
                F32
            )

    vmem = pl.BlockSpec(memory_space=pltpu.VMEM)
    return pl.pallas_call(
        kernel,
        name="wrap",
        in_specs=[vmem] * 9,
        out_specs=[vmem] * 8,
        out_shape=[
            jax.ShapeDtypeStruct(act.shape, BF),
            jax.ShapeDtypeStruct(act.shape, F32),
            jax.ShapeDtypeStruct((rows, QW + 2 * KW), F32),
            jax.ShapeDtypeStruct((rows, D), F32),
            jax.ShapeDtypeStruct((rows, 2 * FF), F32),
            jax.ShapeDtypeStruct((2 * down_rows, D), F32),
            jax.ShapeDtypeStruct((rows,), F32),
            jax.ShapeDtypeStruct((rows,), F32),
        ],
        compiler_params=pltpu.CompilerParams(vmem_limit_bytes=VMEM_LIMIT),
    )(act, input_grad, q_sum, kv_sum, out_sum, gate_sum, late_sum, down_sum, gain_sum)


def build(sizes):
    ctx, wsh = sizes["ctx"], sizes["wsh"]
    shards = ctx * wsh
    link = Exchange(sizes)

    def local(
        tokens,
        segment_ids,
        positions,
        attend_gain,
        query_key_value,
        attend_out,
        feed_gain,
        gate_up,
        down_weight,
        upstream,
    ):
        own = tokens.shape[0]
        plane = own * wsh
        group = plane * ctx
        (
            queries,
            kv_all,
            normed_all,
            w_qkv,
            k_pos,
            k_seg,
            q_marks,
            dy_all,
            cos,
            sin,
            attended,
            attended_wide,
            lse,
            w_half,
        ) = head(
            link, tokens, attend_gain, query_key_value, positions, segment_ids, upstream, gate_up
        )
        kv_all = kv_all.reshape(group, 256)
        normed_all, dy_all = normed_all.reshape(plane, D), dy_all.reshape(plane, D)
        w_qkv = w_qkv.reshape(D, 640)
        w_half = w_half.reshape(D, FF // wsh)
        (
            middle,
            middle_grad,
            branch_all,
            attended_grad,
            feed_sum,
            down_part,
            gate_send,
            gate_late,
            down_sum,
        ) = feed(link, attended, attend_out, tokens, feed_gain, w_half, down_weight, dy_all)
        q_grad, kv_grad, gate_got = attend_backward(
            link, queries, kv_all, q_marks, k_pos, k_seg, lse, attended_wide, attended_grad,
            gate_send,
        )
        sums = finish(
            link, q_grad, kv_grad, w_qkv, cos, sin, normed_all, tokens,
            attend_gain, middle_grad, gate_got, down_sum, attended,
            branch_all.reshape(plane, D), feed_sum, down_part, middle, gate_late,
        )
        return wrap(*sums)

    return local


def solution(mesh):
    whole = ("grp", "ctx", "wsh")
    in_specs = (
        P(whole, None),
        P(whole),
        P(whole),
        P(),
        P("wsh", None),
        P("wsh", None),
        P(),
        P("wsh", None),
        P("wsh", None),
        P(whole, None),
    )
    out_specs = (
        P(whole, None),
        P(whole, None),
        P(("ctx", "wsh"), None),
        P(("ctx", "wsh"), None),
        P(("ctx", "wsh"), None),
        P(("ctx", "wsh"), None),
        P(("ctx", "wsh")),
        P(("ctx", "wsh")),
    )
    return jax.shard_map(
        build(dict(mesh.shape)), mesh=mesh, in_specs=in_specs, out_specs=out_specs, check_vma=False
    )
```

```python
import itertools
import math

import jax
import jax.numpy as jnp
from jax import lax
from jax.experimental import pallas as pl
from jax.experimental.pallas import tpu as pltpu
from jax.sharding import PartitionSpec as P

HEADS = 18
KV_HEADS = 6
HEAD_DIM = 64
FF = 3072
D = 1152
QW = 1152
KW = 384
EPSILON = 1e-05
MESH = pl.DeviceIdType.MESH
F32 = jnp.float32
BF = jnp.bfloat16
VMEM_LIMIT = 56 << 20


def dot_general(a, b, ca, cb):
    return lax.dot_general(a, b, (((ca,), (cb,)), ((), ())), preferred_element_type=F32)


class Exchange:
    def __init__(self, sizes):
        self.sizes = sizes

    def place(self, axes, offset):
        where, index = {}, 0
        for axis, step in zip(axes, offset):
            size = self.sizes[axis]
            spot = lax.axis_index(axis)
            if step:
                spot = lax.rem(spot + step, size)
            where[axis] = spot
            index = index * size + spot
        return where, index

    def offsets(self, axes):
        return list(itertools.product(*[range(self.sizes[axis]) for axis in axes]))


def head_plan(w):
    pair, odd = w // 2, w % 2
    start = 9 * pair + 4 * odd
    if odd:
        f_heads, h_heads = [start + 2, start + 3, start + 4], [start, start + 1]
        f_kv, h_kv = 3 * pair + 2, 3 * pair + 1
    else:
        f_heads, h_heads = [start, start + 1, start + 2], [start + 3, start + 4]
        f_kv, h_kv = 3 * pair, 3 * pair + 1
    q_order = [f_heads[0], h_heads[0], f_heads[1], h_heads[1], f_heads[2], None]
    return q_order, [f_kv, h_kv]


def qkv_restore(parts):
    found = {}
    for w in range(4):
        q_order, kv_order = head_plan(w)
        slots = list(q_order) + [HEADS + h for h in kv_order]
        slots += [HEADS + KV_HEADS + h for h in kv_order]
        for at, head in enumerate(slots):
            if head is not None:
                found.setdefault(head, []).append(
                    parts[w][:, at * HEAD_DIM : (at + 1) * HEAD_DIM]
                )
    pieces = []
    for head in range(HEADS + 2 * KV_HEADS):
        term = found[head][0]
        for other in found[head][1:]:
            term = term + other
        pieces.append(term)
    return jnp.concatenate(pieces, axis=1)


def turn(x, cos, sin, lanes):
    swapped = jnp.where(lanes, pltpu.roll(x, 96, 1), pltpu.roll(x, 32, 1))
    return x * cos + swapped * sin


TQ = 256


def head_block(block, head):
    low = lax.broadcasted_iota(jnp.int32, block.shape, 1) < 64
    return jnp.where(low if head == 0 else jnp.logical_not(low), block, jnp.zeros_like(block))


ODD_ROWS = [(96, 32), (192, 64), (0, 64), (128, 64), (256, 64)]
EVEN_ROWS = [(0, 64), (128, 64), (256, 64), (64, 64), (192, 32)]
HEAD_SLOTS = [(0, 0), (0, 1), (1, 0), (1, 1), (2, 0)]


BK = 384
EARLY = 384


def attend_backward(
    link, q, kv, q_marks, k_pos, k_seg, lse, out, out_grad, send_rows
):
    ctx = link.sizes["ctx"]
    rows, keys = q.shape[0], kv.shape[0]
    steps = rows // TQ
    span = keys // ctx
    levels = link.offsets(("ctx",))[1:]

    def kernel(
        q_ref, kv_ref, qm_ref, kp_ref, ks_ref, lse_ref, o_ref, do_ref, rows_ref,
        dq_ref, got_kv, got_rows,
        acc, heads, grads, delta, marks, lses, k_sum, v_sum, kv_send, bounce, send, recv, kv_out, kv_in, near,
    ):
        wires = Wires(send, recv)
        my_c = lax.axis_index("ctx")
        greet([link.place(("ctx",), offset)[0] for offset in levels])
        copies = []
        for offset in levels:
            where, index = link.place(("ctx",), offset)
            copies.append(wires.start(rows_ref.at[index], got_rows.at[my_c], where))
        inward = pltpu.make_async_copy(rows_ref.at[my_c], bounce, near.at[0])
        outward = pltpu.make_async_copy(bounce, got_rows.at[my_c], near.at[0])
        inward.start()
        acc[...] = jnp.zeros_like(acc)
        delta[...] = jnp.zeros_like(delta)
        for i in range(steps):
            at = slice(i * TQ, i * TQ + TQ)
            marks[i] = qm_ref[:, at]
            lses[i] = lse_ref[:, at]
            for j, (b, h) in enumerate(HEAD_SLOTS):
                lanes = slice(128 * b, 128 * b + 128)
                heads[i, j] = head_block(q_ref[at, lanes], h)
                grad = head_block(do_ref[at, lanes], h)
                grads[i, j] = grad
                product = grad.astype(F32) * o_ref[at, lanes]
                delta[i, j : j + 1, :] = jnp.sum(product.T, axis=0, keepdims=True)
        inward.wait()
        outward.start()

        @pl.loop(0, ctx)
        def _(d):
            chunk = lax.rem(my_c + 1 + d, ctx)

            @pl.loop(0, span // BK)
            def _(t):
                inner = pl.multiple_of(t * BK, 128)
                at = pl.ds(pl.multiple_of(chunk * span + t * BK, 128), BK)
                k_tile = kv_ref[at, :128]
                v_tile = kv_ref[at, 128:]
                key_pos = jnp.tile(kp_ref[at, :], (1, TQ // 128))
                key_seg = jnp.tile(ks_ref[at, :], (1, TQ // 128))
                k_sum[...] = jnp.zeros_like(k_sum)
                v_sum[...] = jnp.zeros_like(v_sum)

                @pl.loop(0, steps)
                def _(i):
                    seen = (key_pos <= marks[i, 0:1, :]) & (
                        (key_seg == 0) | (key_seg == marks[i, 1:2, :])
                    )
                    k_part = jnp.zeros((BK, 128), F32)
                    v_part = jnp.zeros((BK, 128), F32)
                    scores = [dot_general(k_tile, heads[i, j], 1, 1) for j in range(5)]
                    back = [dot_general(v_tile, grads[i, j], 1, 1) for j in range(5)]
                    probs = [
                        jnp.where(seen, jnp.exp(scores[j] - lses[i, j : j + 1, :]), 0.0)
                        for j in range(5)
                    ]
                    score_grad = [
                        (probs[j] * (back[j] - delta[i, j : j + 1, :])).astype(BF)
                        for j in range(5)
                    ]
                    for j in range(5):
                        v_part += jnp.dot(
                            probs[j].astype(BF), grads[i, j], preferred_element_type=F32
                        )
                        k_part += jnp.dot(
                            score_grad[j], heads[i, j], preferred_element_type=F32
                        )
                        acc[i, j] += dot_general(k_tile, score_grad[j], 0, 0)
                    k_sum[...] += k_part
                    v_sum[...] += v_part

                kv_send[chunk, pl.ds(inner, BK), :128] = k_sum[...].astype(BF)
                kv_send[chunk, pl.ds(inner, BK), 128:] = v_sum[...].astype(BF)

            @pl.when(d < ctx - 1)
            def _():
                pltpu.make_async_remote_copy(
                    kv_send.at[chunk],
                    got_kv.at[my_c],
                    kv_out.at[d],
                    kv_in.at[d],
                    device_id={"ctx": chunk},
                    device_id_type=MESH,
                ).start()

        near_kv = pltpu.make_async_copy(kv_send.at[my_c], got_kv.at[my_c], near.at[1])
        near_kv.start()
        low = lax.broadcasted_iota(jnp.int32, (TQ, 128), 1) < 64
        for i in range(steps):
            for b in range(3):
                first = acc[i, 2 * b].T * 0.125
                if b < 2:
                    block = jnp.where(low, first, acc[i, 2 * b + 1].T * 0.125)
                else:
                    block = jnp.where(low, first, 0.0)
                dq_ref[i * TQ : i * TQ + TQ, 128 * b : 128 * b + 128] = block.astype(BF)

        near_kv.wait()
        outward.wait()
        for copy in copies:
            copy.wait()

        for d in range(ctx - 1):
            pltpu.make_async_remote_copy(
                kv_send.at[0],
                got_kv.at[0],
                kv_out.at[d],
                kv_in.at[d],
                device_id={"ctx": my_c},
                device_id_type=MESH,
            ).wait()

    vmem = pl.BlockSpec(memory_space=pltpu.VMEM)
    anywhere = pl.BlockSpec(memory_space=pl.ANY)
    return pl.pallas_call(
        kernel,
        name="attend_backward",
        in_specs=[vmem] * 8 + [anywhere],
        out_specs=[vmem] + [anywhere] * 2,
        out_shape=[
            jax.ShapeDtypeStruct((rows, 384), BF),
            jax.ShapeDtypeStruct((ctx, span, 256), BF),
            jax.ShapeDtypeStruct(send_rows.shape, BF),
        ],
        scratch_shapes=[
            pltpu.VMEM((steps, 5, 128, TQ), F32),
            pltpu.VMEM((steps, 5, TQ, 128), BF),
            pltpu.VMEM((steps, 5, TQ, 128), BF),
            pltpu.VMEM((steps, 8, TQ), F32),
            pltpu.VMEM((steps, 8, TQ), F32),
            pltpu.VMEM((steps, 8, TQ), F32),
            pltpu.VMEM((BK, 128), F32),
            pltpu.VMEM((BK, 128), F32),
            pltpu.VMEM((ctx, span, 256), BF),
            pltpu.VMEM(send_rows.shape[1:], BF),
            pltpu.SemaphoreType.DMA((ctx,)),
            pltpu.SemaphoreType.DMA((ctx,)),
            pltpu.SemaphoreType.DMA((ctx,)),
            pltpu.SemaphoreType.DMA((ctx,)),
            pltpu.SemaphoreType.DMA((2,)),
        ],
        compiler_params=pltpu.CompilerParams(
            collective_id=11, has_side_effects=True, vmem_limit_bytes=VMEM_LIMIT
        ),
    )(q, kv, q_marks, k_pos, k_seg, lse, out, out_grad, send_rows)


class Wires:
    def __init__(self, send, recv):
        self.send, self.recv, self.used = send, recv, 0

    def copy(self, source, target, where):
        at = self.used
        self.used += 1
        return pltpu.make_async_remote_copy(
            source,
            target,
            self.send.at[at],
            self.recv.at[at],
            device_id=where,
            device_id_type=MESH,
        )

    def start(self, source, target, where):
        copy = self.copy(source, target, where)
        copy.start()
        return copy


def greet(places):
    barrier = pltpu.get_barrier_semaphore()
    for where in places:
        pl.semaphore_signal(barrier, 1, device_id=where, device_id_type=MESH)
    pl.semaphore_wait(barrier, len(places))


def square():
    w = lax.axis_index("wsh")
    return w, w + 1 - 2 * lax.rem(w, 2), w + 2 - 4 * (w // 2), 3 - w


class SquareScatter:
    def __init__(self, wires, parts, near, total):
        self.wires, self.parts, self.near, self.total = wires, parts, near, total
        self.half = parts.shape[1] // 2
        self.a, self.b = pl.ds(0, self.half), pl.ds(self.half, self.half)
        self.own, self.x, self.y, self.z = square()
        self.pending = []

    def send_diagonal(self):
        wires, parts = self.wires, self.parts
        self.one = wires.start(parts.at[self.z, self.a], self.near.at[0], {"wsh": self.x})
        self.two = wires.start(parts.at[self.z, self.b], self.near.at[1], {"wsh": self.y})

    def send_x(self):
        self.pending.append(
            self.wires.start(
                self.parts.at[self.x, self.a], self.total.at[0, self.a], {"wsh": self.x}
            )
        )

    def send_y(self):
        self.pending.append(
            self.wires.start(
                self.parts.at[self.y, self.b], self.total.at[1, self.b], {"wsh": self.y}
            )
        )

    def relay(self):
        near, parts = self.near, self.parts
        self.one.wait()
        near[2] = (near[0].astype(F32) + parts[self.y, self.a].astype(F32)).astype(BF)
        self.pending.append(
            self.wires.start(near.at[2], self.total.at[1, self.a], {"wsh": self.y})
        )
        self.two.wait()
        near[3] = (near[1].astype(F32) + parts[self.x, self.b].astype(F32)).astype(BF)
        self.pending.append(
            self.wires.start(near.at[3], self.total.at[0, self.b], {"wsh": self.x})
        )

    def result(self):
        for copy in self.pending:
            copy.wait()
        return (
            self.parts[self.own].astype(F32)
            + self.total[0].astype(F32)
            + self.total[1].astype(F32)
        )


def square_scratch(rows):
    return [pltpu.VMEM((4, rows // 2, D), BF), pltpu.VMEM((2, rows, D), BF)]


class SquareGather:
    def __init__(self, wires, out):
        self.wires, self.out = wires, out
        half = out.shape[1] // 2
        self.a, self.b = pl.ds(0, half), pl.ds(half, half)
        self.own, self.x, self.y, self.z = square()

    def move(self, slot, part, to):
        return self.wires.start(self.out.at[slot, part], self.out.at[slot, part], {"wsh": to})

    def begin(self):
        self.xa = self.move(self.own, self.a, self.x)
        self.yb = self.move(self.own, self.b, self.y)
        self.xb = self.move(self.own, self.b, self.x)
        self.ya = self.move(self.own, self.a, self.y)

    def relay(self):
        self.xa.wait()
        self.one = self.move(self.x, self.a, self.y)
        self.yb.wait()
        self.two = self.move(self.y, self.b, self.x)

    def wait_x(self):
        self.xb.wait()

    def wait_y(self):
        self.ya.wait()

    def wait_z(self):
        self.one.wait()
        self.two.wait()


def feed(link, attended, w_out, tokens, gain, w_half, down, dy):
    ctx, wsh = link.sizes["ctx"], link.sizes["wsh"]
    own_rows = tokens.shape[0]
    plane = dy.shape[0]
    units = down.shape[0]
    chunk = D // ctx
    pick = units // ctx // 2
    early = EARLY

    def kernel(
        at_ref, ao_ref, x_ref, g_ref, wh_ref, dw_ref, dy_ref,
        mid_ref, mg_ref, br_ref, ag_ref, fs_ref, dp_ref, gs_ref, gl_ref, ds_ref,
        wo_ref, w_both, parts, near, total, near2, total2, n2, hgrad, hidden, gate_g, up_g,
        down_h, down_pair, down_send, down_got, gate_h, gate_pair, send, recv, local,
    ):
        wires = Wires(send, recv)
        core = lax.axis_index("grp")
        sibling = {"grp": 1 - core}
        my_c = lax.axis_index("ctx")
        own, x, y, z = square()
        levels = [link.place(("ctx",), offset) for offset in link.offsets(("ctx",))[1:]]
        greet([{"wsh": x}, {"wsh": y}, sibling] + [where for where, _ in levels])

        def rows_of(slot):
            return pl.ds(pl.multiple_of(slot * own_rows, 16), own_rows)

        w_copy = pltpu.make_async_copy(wh_ref, w_both.at[core], local)
        w_copy.start()

        odd = lax.rem(own, 2) == 1
        wo_ref[...] = jnp.zeros_like(wo_ref)

        def spread(pieces):
            at = 0
            for start, size in pieces:
                wo_ref[start : start + size, :] = ao_ref[at : at + size, :]
                at += size

        @pl.when(odd)
        def _():
            spread(ODD_ROWS)

        @pl.when(jnp.logical_not(odd))
        def _():
            spread(EVEN_ROWS)

        first = SquareScatter(wires, parts, near, total)
        for slot in (z, x, y, own):
            parts[slot] = jnp.dot(
                at_ref[rows_of(slot), :], wo_ref[...], preferred_element_type=F32
            ).astype(BF)
            if slot is z:
                first.send_diagonal()
            elif slot is x:
                first.send_x()
            elif slot is y:
                first.send_y()
        w_swap = wires.start(wh_ref, w_both.at[core], sibling)
        hgrad[...] = dot_general(dy_ref[...], dw_ref[...], 1, 1)
        first.relay()
        middle = x_ref[...].astype(F32) + first.result()
        mid_ref[...] = middle
        factor = lax.rsqrt(jnp.mean(middle * middle, axis=-1, keepdims=True) + EPSILON)
        n2[own] = (middle * factor * g_ref[...].reshape(1, D)).astype(BF)
        gather = SquareGather(wires, n2)
        gather.begin()
        w_copy.wait()
        w_swap.wait()

        def block(slot):
            at = rows_of(slot)
            gate = jnp.dot(n2[slot], w_both[0], preferred_element_type=F32)
            up = jnp.dot(n2[slot], w_both[1], preferred_element_type=F32)
            sigmoid = 1.0 / (1.0 + jnp.exp(-gate))
            silu = gate * sigmoid
            hidden[at, :] = (silu * up).astype(BF)
            back = hgrad[at, :]
            gate_g[at, :] = (back * up * sigmoid * (1.0 + gate * (1.0 - sigmoid))).astype(BF)
            up_g[at, :] = (back * silu).astype(BF)
            parts[slot] = (
                dot_general(gate_g[at, :], w_both[0], 1, 1)
                + dot_general(up_g[at, :], w_both[1], 1, 1)
            ).astype(BF)

        second = SquareScatter(wires, parts, near2, total2)
        block(own)
        gather.relay()
        gather.wait_x()
        block(x)
        second.send_x()
        gather.wait_y()
        block(y)
        second.send_y()
        gather.wait_z()
        block(z)
        second.send_diagonal()

        strip = dot_general(hidden[...], dy_ref[...], 0, 0).astype(BF)
        for k in range(ctx):
            for g in range(2):
                top = (2 * k + g) * pick
                down_h[g, k] = strip[top : top + pick, :]
        down_swap = wires.start(down_h.at[1 - core], down_pair, sibling)
        second.relay()
        tokens_all = n2[...].reshape(plane, D)
        for g, source in enumerate((gate_g, up_g)):
            strip = dot_general(tokens_all, source[...], 0, 0).astype(BF)
            for c in range(ctx):
                gate_h[g, c] = strip[c * chunk : c * chunk + chunk, :]
        gate_swap = wires.start(gate_h.at[1 - core], gate_pair, sibling)
        down_swap.wait()
        down_send[...] = (down_h[core].astype(F32) + down_pair[...].astype(F32)).astype(BF)
        down_copies = []
        for where, index in levels:
            down_copies.append(wires.start(down_send.at[index], down_got.at[my_c], where))
        down_got[my_c] = down_send[my_c]

        grad = second.result()
        middle = mid_ref[...]
        factor = lax.rsqrt(jnp.mean(middle * middle, axis=-1, keepdims=True) + EPSILON)
        weighted = grad * g_ref[...].reshape(1, D)
        inner = jnp.mean(weighted * middle, axis=-1, keepdims=True)
        middle_grad = (
            dy_ref[rows_of(own), :].astype(F32)
            + factor * weighted
            - middle * (factor * factor * factor) * inner
        )
        mg_ref[...] = middle_grad
        br_ref[own] = middle_grad.astype(BF)
        branch = SquareGather(wires, br_ref)
        branch.begin()
        fs_ref[...] = jnp.sum(grad * middle * factor, axis=0, keepdims=True)

        def outward(slot):
            ag_ref[rows_of(slot), :] = dot_general(br_ref[slot], wo_ref[...], 1, 1).astype(BF)

        outward(own)
        gate_swap.wait()
        for c in range(ctx):
            both = (gate_h[core, c].astype(F32) + gate_pair[c].astype(F32)).astype(BF)
            gs_ref[c] = both[:, :early]
            gl_ref[c] = both[:, early:]
        branch.relay()

        @pl.loop(0, wsh)
        def _(slot):
            dp_ref[slot] = jnp.dot(
                hidden[rows_of(slot), :], dw_ref[...], preferred_element_type=F32
            ).astype(BF)

        branch.wait_x()
        outward(x)
        branch.wait_y()
        outward(y)
        branch.wait_z()
        outward(z)
        for copy in down_copies:
            copy.wait()
        ds_ref[...] = jnp.sum(down_got[...].astype(F32), axis=0).astype(BF)

    operands = (attended, w_out, tokens, gain, w_half, down, dy)
    vmem = pl.BlockSpec(memory_space=pltpu.VMEM)
    return pl.pallas_call(
        kernel,
        name="feed",
        in_specs=[vmem] * len(operands),
        out_specs=[vmem] * 9,
        out_shape=[
            jax.ShapeDtypeStruct((own_rows, D), F32),
            jax.ShapeDtypeStruct((own_rows, D), F32),
            jax.ShapeDtypeStruct((wsh, own_rows, D), BF),
            jax.ShapeDtypeStruct((plane, 384), BF),
            jax.ShapeDtypeStruct((1, D), F32),
            jax.ShapeDtypeStruct((wsh, own_rows, D), BF),
            jax.ShapeDtypeStruct((ctx, chunk, early), BF),
            jax.ShapeDtypeStruct((ctx, chunk, units - early), BF),
            jax.ShapeDtypeStruct((pick, D), BF),
        ],
        scratch_shapes=[
            pltpu.VMEM((384, D), BF),
            pltpu.VMEM((2, D, units), BF),
            pltpu.VMEM((4, own_rows, D), BF),
            *square_scratch(own_rows),
            *square_scratch(own_rows),
            pltpu.VMEM((4, own_rows, D), BF),
            pltpu.VMEM((plane, units), F32),
            *[pltpu.VMEM((plane, units), BF)] * 3,
            pltpu.VMEM((2, ctx, pick, D), BF),
            *[pltpu.VMEM((ctx, pick, D), BF)] * 3,
            pltpu.VMEM((2, ctx, chunk, units), BF),
            pltpu.VMEM((ctx, chunk, units), BF),
            pltpu.SemaphoreType.DMA((ctx + 28,)),
            pltpu.SemaphoreType.DMA((ctx + 28,)),
            pltpu.SemaphoreType.DMA,
        ],
        compiler_params=pltpu.CompilerParams(
            collective_id=3, has_side_effects=True, vmem_limit_bytes=VMEM_LIMIT
        ),
    )(*operands)


def head(link, tokens, gain, weight, positions, segments, upstream, gate_up):
    ctx, wsh = link.sizes["ctx"], link.sizes["wsh"]
    own_rows = tokens.shape[0]
    plane, group = own_rows * wsh, own_rows * wsh * ctx
    half = weight.shape[0] // 2
    units = FF // wsh
    steps = plane // TQ

    def kernel(
        x_ref, g_ref, w_ref, pos_ref, seg_ref, up_ref, gu_ref,
        q_ref, kv_ref, n_ref, wq_ref, kpos_ref, kseg_ref, q_marks, dy_ref, c_ref, s_ref,
        a_ref, o_ref, lse_ref, wh_ref,
        cols, mine, marks_all, heads, tile_marks, acc, top, tot, bounce, send, recv, kv_out, kv_in,
        near,
    ):
        wires = Wires(send, recv)
        core = lax.axis_index("grp")
        sibling = {"grp": 1 - core}
        my_c = lax.axis_index("ctx")
        own, x, y, z = square()
        levels = [link.place(("ctx",), offset) for offset in link.offsets(("ctx",))[1:]]
        greet(
            [{"wsh": x}, {"wsh": y}, {"wsh": z}, sibling] + [where for where, _ in levels]
        )
        mine[...] = jnp.zeros_like(mine)
        mine[0:1, :own_rows] = pos_ref[...].reshape(1, own_rows).astype(F32)
        mine[1:2, :own_rows] = seg_ref[...].reshape(1, own_rows).astype(F32)
        mark_copies = []
        for p in (x, y, z):
            mark_copies.append(wires.start(mine, marks_all.at[my_c, own], {"wsh": p}))
        marks_all[my_c, own] = mine[...]
        side = pl.ds(pl.multiple_of(core * half, 16), half)

        for w in range(wsh):
            q_order, kv_order = head_plan(w)
            slots = [h for h in q_order] + [HEADS + h for h in kv_order]
            slots += [HEADS + KV_HEADS + h for h in kv_order]
            blank = jnp.zeros((w_ref.shape[0], HEAD_DIM), BF)
            for pair in range(5):
                two = [
                    blank if h is None else w_ref[:, h * HEAD_DIM : h * HEAD_DIM + HEAD_DIM]
                    for h in slots[2 * pair : 2 * pair + 2]
                ]
                cols[w, :, 128 * pair : 128 * pair + 128] = jnp.concatenate(two, axis=1)
        w_copies = []
        for p in (x, y, z):
            w_copies.append(
                wires.start(cols.at[p, side], wq_ref.at[own, side], {"wsh": p})
            )
        tokens_in = x_ref[...].astype(F32)
        factor = lax.rsqrt(jnp.mean(tokens_in * tokens_in, axis=-1, keepdims=True) + EPSILON)
        n_ref[own] = (tokens_in * factor * g_ref[...].reshape(1, D)).astype(BF)
        wq_ref[own] = cols[own]
        dy_ref[own] = up_ref[...]

        for copy in mark_copies:
            copy.wait()
        level_copies = []
        for where, _ in levels:
            level_copies.append(wires.start(marks_all.at[my_c], marks_all.at[my_c], where))
        lane = lax.broadcasted_iota(jnp.int32, (1, 128), 1)
        power = lax.rem(lane, 32).astype(F32) * (-math.log(10000.0) / 32)
        frequency = jnp.exp(power)
        sign = jnp.where(lax.rem(lane, 64) < 32, -1.0, 1.0)

        def upright(row):
            return jnp.broadcast_to(row, (128, row.shape[1])).T

        for w in range(wsh):
            at = slice(w * own_rows, w * own_rows + own_rows)
            angles = upright(marks_all[my_c, w, 0:1, :])[:own_rows] * frequency
            c_ref[at, :] = jnp.cos(angles)
            s_ref[at, :] = jnp.sin(angles) * sign
        forward = []
        for p, copy in zip((x, y, z), w_copies):
            copy.wait()
            forward.append(wires.start(wq_ref.at[p, side], wq_ref.at[p, side], sibling))
        gather = SquareGather(wires, n_ref)
        gather.begin()
        for copy in forward:
            copy.wait()

        low = lax.rem(lax.broadcasted_iota(jnp.int32, (own_rows, 128), 1), 64) < 32

        def kv_copy(slot, order, d, to):
            at = pl.ds(pl.multiple_of(slot * own_rows, 16), own_rows)
            return pltpu.make_async_remote_copy(
                kv_ref.at[my_c, at],
                kv_ref.at[my_c, at],
                kv_out.at[order, d],
                kv_in.at[order, d],
                device_id={"ctx": to},
                device_id_type=MESH,
            )

        def block(slot, order):
            at = pl.ds(pl.multiple_of(slot * own_rows, 16), own_rows)
            full = jnp.dot(
                n_ref[slot], wq_ref[...].reshape(D, 640), preferred_element_type=F32
            )
            cos_t, sin_t = c_ref[at, :], s_ref[at, :]
            for b in range(3):
                turned = turn(full[:, 128 * b : 128 * b + 128], cos_t, sin_t, low)
                q_ref[at, 128 * b : 128 * b + 128] = (
                    turned.astype(BF).astype(F32) * 0.125
                ).astype(BF)
            kv_ref[my_c, at, :128] = turn(full[:, 384:512], cos_t, sin_t, low).astype(BF)
            kv_ref[my_c, at, 128:] = full[:, 512:].astype(BF)
            for d, (_, index) in enumerate(levels):
                kv_copy(slot, order, d, index).start()

        block(own, 0)
        gather.relay()
        dy_gather = SquareGather(wires, dy_ref)
        dy_gather.begin()
        gather.wait_x()
        block(x, 1)
        gather.wait_y()
        block(y, 2)
        gather.wait_z()
        def columns(p):
            left = core * FF + p * units
            return gu_ref.at[:, pl.ds(pl.multiple_of(left, 128), units)]

        gate_copies = []
        for p in (x, y, z):
            gate_copies.append(wires.start(columns(p), wh_ref.at[own], {"wsh": p}))
        inward = pltpu.make_async_copy(columns(own), bounce, near)
        outward = pltpu.make_async_copy(bounce, wh_ref.at[own], near)
        inward.start()

        block(z, 3)
        dy_gather.relay()

        for w in range(wsh):
            q_marks[:, w * own_rows : w * own_rows + own_rows] = marks_all[my_c, w, :, :own_rows]

        for copy in level_copies:
            copy.wait()

        @pl.loop(0, ctx)
        def _(c):
            for w in range(wsh):
                at = pl.ds(pl.multiple_of(c * plane + w * own_rows, 16), own_rows)
                kpos_ref[at, :] = upright(marks_all[c, w, 0:1, :])[:own_rows]
                kseg_ref[at, :] = upright(marks_all[c, w, 1:2, :])[:own_rows]

        inward.wait()
        outward.start()

        acc[...] = jnp.zeros_like(acc)
        top[...] = jnp.full_like(top, -1e30)
        tot[...] = jnp.zeros_like(tot)
        for i in range(steps):
            at = slice(i * TQ, i * TQ + TQ)
            tile_marks[i] = q_marks[:, at]
            for j, (b, side_of) in enumerate(HEAD_SLOTS):
                heads[i, j] = head_block(q_ref[at, 128 * b : 128 * b + 128], side_of)

        @pl.loop(0, ctx)
        def _(d):
            chunk = lax.rem(my_c + ctx - d, ctx)

            @pl.when(d > 0)
            def _():
                for order in range(wsh):
                    kv_copy(0, order, d - 1, my_c).wait()

            at = pl.ds(pl.multiple_of(chunk * plane, 128), plane)
            k_tile = kv_ref[chunk, :, :128]
            v_tile = kv_ref[chunk, :, 128:]
            key_pos = jnp.tile(kpos_ref[at, :], (1, TQ // 128))
            key_seg = jnp.tile(kseg_ref[at, :], (1, TQ // 128))

            @pl.loop(0, steps)
            def _(i):
                seen = (key_pos <= tile_marks[i, 0:1, :]) & (
                    (key_seg == 0) | (key_seg == tile_marks[i, 1:2, :])
                )
                scores = [
                    jnp.where(seen, dot_general(k_tile, heads[i, j], 1, 1), -1e30)
                    for j in range(5)
                ]
                old = [top[i, j : j + 1, :] for j in range(5)]
                new = [
                    jnp.maximum(old[j], jnp.max(scores[j], axis=0, keepdims=True))
                    for j in range(5)
                ]
                expons = [jnp.exp(scores[j] - new[j]) for j in range(5)]
                shrink = [jnp.exp(old[j] - new[j]) for j in range(5)]
                mixed = [dot_general(v_tile, expons[j].astype(BF), 0, 0) for j in range(5)]
                for j in range(5):
                    tot[i, j : j + 1, :] = tot[i, j : j + 1, :] * shrink[j] + jnp.sum(
                        expons[j], axis=0, keepdims=True
                    )
                    acc[i, j] = acc[i, j] * shrink[j] + mixed[j]
                    top[i, j : j + 1, :] = new[j]

        half_lanes = lax.broadcasted_iota(jnp.int32, (TQ, 128), 1) < 64
        for i in range(steps):
            at = slice(i * TQ, i * TQ + TQ)
            lse_ref[:, at] = top[i] + jnp.log(jnp.maximum(tot[i], 1e-37))
            outs = [(acc[i, j] / tot[i, j : j + 1, :]).T for j in range(5)] + [0.0]
            for b in range(3):
                block_out = jnp.where(half_lanes, outs[2 * b], outs[2 * b + 1])
                o_ref[at, 128 * b : 128 * b + 128] = block_out
                a_ref[at, 128 * b : 128 * b + 128] = block_out.astype(BF)

        dy_gather.wait_x()
        dy_gather.wait_y()
        dy_gather.wait_z()
        for copy in gate_copies:
            copy.wait()
        outward.wait()

    operands = (tokens, gain, weight, positions, segments, upstream, gate_up)
    vmem = pl.BlockSpec(memory_space=pltpu.VMEM)
    return pl.pallas_call(
        kernel,
        name="head",
        in_specs=[vmem] * 6 + [pl.BlockSpec(memory_space=pl.ANY)],
        out_specs=[vmem] * 13 + [pl.BlockSpec(memory_space=pl.ANY)],
        out_shape=[
            jax.ShapeDtypeStruct((plane, 384), BF),
            jax.ShapeDtypeStruct((ctx, plane, 256), BF),
            jax.ShapeDtypeStruct((wsh, own_rows, D), BF),
            jax.ShapeDtypeStruct((wsh, 2 * half, 640), BF),
            jax.ShapeDtypeStruct((group, 128), F32),
            jax.ShapeDtypeStruct((group, 128), F32),
            jax.ShapeDtypeStruct((8, plane), F32),
            jax.ShapeDtypeStruct((wsh, own_rows, D), BF),
            jax.ShapeDtypeStruct((plane, 128), F32),
            jax.ShapeDtypeStruct((plane, 128), F32),
            jax.ShapeDtypeStruct((plane, 384), BF),
            jax.ShapeDtypeStruct((plane, 384), F32),
            jax.ShapeDtypeStruct((8, plane), F32),
            jax.ShapeDtypeStruct((wsh, 2 * half, units), BF),
        ],
        scratch_shapes=[
            pltpu.VMEM((wsh, 2 * half, 640), BF),
            pltpu.VMEM((8, 256), F32),
            pltpu.VMEM((ctx, wsh, 8, 256), F32),
            pltpu.VMEM((steps, 5, TQ, 128), BF),
            pltpu.VMEM((steps, 8, TQ), F32),
            pltpu.VMEM((steps, 5, 128, TQ), F32),
            pltpu.VMEM((steps, 8, TQ), F32),
            pltpu.VMEM((steps, 8, TQ), F32),
            pltpu.VMEM((2 * half, units), BF),
            pltpu.SemaphoreType.DMA((ctx + 28,)),
            pltpu.SemaphoreType.DMA((ctx + 28,)),
            pltpu.SemaphoreType.DMA((wsh, ctx)),
            pltpu.SemaphoreType.DMA((wsh, ctx)),
            pltpu.SemaphoreType.DMA,
        ],
        compiler_params=pltpu.CompilerParams(
            collective_id=1, has_side_effects=True, vmem_limit_bytes=VMEM_LIMIT
        ),
    )(*operands)


def finish(
    link, q_grad, kv_grad, weight, cos, sin, normed, tokens, gain, middle_grad, gate_got, down_got,
    attended, branch, feed_sum, down_part, middle, gate_late,
):
    ctx, wsh = link.sizes["ctx"], link.sizes["wsh"]
    shards = ctx * wsh
    rows = D // shards
    chunk = D // ctx
    fold = ctx // wsh
    own_rows = tokens.shape[0]
    plane = normed.shape[0]
    axes = ("ctx", "wsh")
    peers = link.offsets(axes)
    gate_width, late_width = gate_got.shape[2], gate_late.shape[2]
    down_rows = down_got.shape[0]
    piece = down_rows // wsh

    def kernel(
        q_ref, kv_ref, w_ref, c_ref, s_ref, n_ref, x_ref, g_ref, mg_ref, gate_ref, down_ref,
        at_ref, br_ref, fs_ref, dp_ref, mid_ref, late_ref,
        act_ref, ig_ref, q_fin, kv_fin, out_fin, gate_fin, late_fin, down_fin, gains_out,
        pg, parts, near, total, near2, total2, wide, q_own, q_pair, q_send, q_got,
        q_mid, kv_own, kv_pair, kv_go, kv_got, kv_mid, gate_mid, late_got,
        late_mid, spread, spread_got, risen, landed, out_halves,
        out_pair, out_send, out_mid, out_got, gains, gains_got, gains_fin,
        send, recv,
    ):
        wires = Wires(send, recv)
        core = lax.axis_index("grp")
        first, second = core == 0, core == 1
        sibling = {"grp": 1 - core}
        my_c, my_w = lax.axis_index("ctx"), lax.axis_index("wsh")
        odd = lax.rem(my_w, 2) == 1
        greet([link.place(axes, offset)[0] for offset in peers[1:]] + [sibling])
        _, me = link.place(axes, peers[0])

        def over_ctx(got, mid):
            for w in range(wsh):
                strip = got[0, w * rows : w * rows + rows, :].astype(F32)
                for c in range(1, ctx):
                    strip += got[c, w * rows : w * rows + rows, :].astype(F32)
                mid[w] = strip.astype(BF)

        def in_plane(mid, slot_of):
            copies = []
            for offset in link.offsets(("wsh",))[1:]:
                where, index = link.place(("wsh",), offset)
                copies.append(wires.copy(mid.at[index], slot_of(my_w), where))
            return copies

        def begin(cond, *copies):
            @pl.when(cond)
            def _():
                for copy in copies:
                    copy.start()

        levels = [link.place(("ctx",), offset) for offset in link.offsets(("ctx",))[1:]]
        late_copies = []
        for where, index in levels:
            late_copies.append(wires.start(late_ref.at[index], late_got.at[my_c], where))

        for p in range(wsh):
            spread[p] = down_ref[p * piece : p * piece + piece, :]
        spread_moves = in_plane(spread, lambda w: spread_got.at[w])
        for copy in spread_moves:
            copy.start()
        spread_got[my_w] = spread[my_w]

        low = lax.rem(lax.broadcasted_iota(jnp.int32, (own_rows, 128), 1), 64) < 32
        scatter = SquareScatter(wires, parts, near, total)
        gain_sum = jnp.zeros((1, D), F32)
        for slot in (scatter.z, scatter.x, scatter.y, scatter.own):
            at = pl.ds(pl.multiple_of(slot * own_rows, 16), own_rows)
            cos_t, sin_t = c_ref[at, :], -s_ref[at, :]
            for b in range(3):
                block = q_ref[at, 128 * b : 128 * b + 128].astype(F32)
                pg[at, 128 * b : 128 * b + 128] = turn(block, cos_t, sin_t, low).astype(BF)
            summed = kv_ref[0, at, :].astype(F32)
            for c in range(1, ctx):
                summed += kv_ref[c, at, :].astype(F32)
            block = summed[:, :128].astype(BF).astype(F32)
            pg[at, 384:512] = turn(block, cos_t, sin_t, low).astype(BF)
            pg[at, 512:] = summed[:, 128:].astype(BF)
            part = dot_general(pg[at, :], w_ref[...], 1, 1)
            parts[slot] = part.astype(BF)
            gain_sum += jnp.sum(part * n_ref[at, :].astype(F32), axis=0, keepdims=True)
            if slot is scatter.z:
                scatter.send_diagonal()
            elif slot is scatter.x:
                scatter.send_x()
            elif slot is scatter.y:
                scatter.send_y()

        for copy in spread_moves:
            copy.wait()
        lane = lax.rem(my_c, wsh)
        rise, arrive = wires.used, []
        wires.used += wsh
        for p in range(wsh):
            to = (p * ctx + my_c) // wsh
            out_copy_p = pltpu.make_async_remote_copy(
                spread_got.at[p],
                risen.at[lane],
                send.at[rise + p],
                recv.at[rise + lane],
                device_id={"ctx": to},
                device_id_type=MESH,
            )

            @pl.when(to != my_c)
            def _():
                out_copy_p.start()

            @pl.when(to == my_c)
            def _():
                risen[lane] = spread_got[p]

            from_c = lax.rem(my_c, fold) * wsh + p
            in_copy_p = pltpu.make_async_remote_copy(
                spread_got.at[p],
                risen.at[p],
                send.at[rise + p],
                recv.at[rise + p],
                device_id={"ctx": to},
                device_id_type=MESH,
            )
            arrive.append((out_copy_p, to != my_c, in_copy_p, from_c != my_c))

        strip = dot_general(n_ref[...], pg[:, 384:], 0, 0).astype(BF)
        for c in range(ctx):
            kv_own[c] = strip[c * chunk : c * chunk + chunk, :]
        kv_swap = wires.copy(kv_own, kv_pair, sibling)
        begin(first, kv_swap)
        scatter.relay()
        strip = dot_general(n_ref[...], pg[:, :384], 0, 0).astype(BF)
        for c in range(ctx):
            q_own[c] = strip[c * chunk : c * chunk + chunk, :]
        q_swap = wires.copy(q_own, q_pair, sibling)
        begin(second, q_swap)
        layer = SquareScatter(wires, dp_ref, near2, total2)
        layer.send_diagonal()
        layer.send_x()
        layer.send_y()
        wide[...] = dot_general(at_ref[...], br_ref[...], 0, 0)

        def out_strips(pieces):
            at = 0
            for start, size in pieces:
                acc_rows = wide[start : start + size, :].astype(BF)
                part = jnp.concatenate([acc_rows[:, :576], jnp.zeros((size, 64), BF)], axis=1)
                out_halves[0, at : at + size, :] = part
                part = jnp.concatenate([acc_rows[:, 576:], jnp.zeros((size, 64), BF)], axis=1)
                out_halves[1, at : at + size, :] = part
                at += size

        @pl.when(odd)
        def _():
            out_strips(ODD_ROWS)

        @pl.when(jnp.logical_not(odd))
        def _():
            out_strips(EVEN_ROWS)

        out_swap = wires.start(out_halves.at[1 - core], out_pair, sibling)
        q_copies, kvg_copies, out_copies = [], [], []
        for where, index in levels:
            q_copies.append(wires.copy(q_send.at[index], q_got.at[my_c], where))
            kvg_copies.append(wires.copy(kv_go.at[index], kv_got.at[my_c], where))

        @pl.when(first)
        def _():
            q_swap.wait_recv()

            @pl.loop(0, ctx)
            def _(c):
                q_send[c] = (q_own[c].astype(F32) + q_pair[c].astype(F32)).astype(BF)

            for copy in q_copies:
                copy.start()
            q_got[my_c] = q_send[my_c]
            kv_swap.wait_send()

        @pl.when(second)
        def _():
            kv_swap.wait_recv()

            @pl.loop(0, ctx)
            def _(c):
                kv_go[c] = (kv_own[c].astype(F32) + kv_pair[c].astype(F32)).astype(BF)

            for copy in kvg_copies:
                copy.start()
            kv_got[my_c] = kv_go[my_c]
            q_swap.wait_send()

        both = jnp.concatenate([gain_sum / g_ref[...].reshape(1, D), fs_ref[...]], axis=0)
        gains[...] = jnp.zeros_like(gains)
        for s in range(shards):
            gains[s, :2, :rows] = both[:, rows * s : rows * s + rows]
        gain_copies = []
        for offset in peers[1:]:
            where, index = link.place(axes, offset)
            gain_copies.append(wires.start(gains.at[index], gains_got.at[me], where))
        gains_got[me] = gains[me]
        layer.relay()

        out_swap.wait()
        for k in range(ctx):
            strip = slice(k * rows, k * rows + rows)
            out_send[k % wsh, k // wsh] = (
                out_halves[core, strip, :].astype(F32) + out_pair[strip, :].astype(F32)
            ).astype(BF)
        out_moves = in_plane(out_send, lambda w: out_mid.at[w])
        for copy in out_moves:
            copy.start()
        out_mid[my_w] = out_send[my_w]

        grad = scatter.result()
        x = x_ref[...].astype(F32)
        factor = lax.rsqrt(jnp.mean(x * x, axis=-1, keepdims=True) + EPSILON)
        weighted = grad * g_ref[...].reshape(1, D)
        inner = jnp.mean(weighted * x, axis=-1, keepdims=True)
        ig_ref[...] = mg_ref[...] + factor * weighted - x * (factor * factor * factor) * inner
        for copy in out_moves:
            copy.wait()
        for where, index in levels:
            part = out_mid.at[index // fold, lax.rem(index, fold)]
            out_copies.append(wires.start(part, out_got.at[my_c], where))
        out_got[my_c] = out_mid[my_c // fold, lax.rem(my_c, fold)]


        for out_copy_p, goes, in_copy_p, comes in arrive:

            @pl.when(goes)
            def _():
                out_copy_p.wait_send()

            @pl.when(comes)
            def _():
                in_copy_p.wait_recv()

        land_moves = in_plane(risen, lambda w: landed.at[w])
        for copy in land_moves:
            copy.start()
        landed[my_w] = risen[my_w]
        over_ctx(gate_ref, gate_mid)
        gate_moves = in_plane(gate_mid, lambda w: gate_fin.at[core, w])
        for copy in gate_moves:
            copy.start()
        gate_fin[core, my_w] = gate_mid[my_w]
        for copy in late_copies:
            copy.wait()
        late_got[my_c] = late_ref[my_c]
        over_ctx(late_got, late_mid)
        late_moves = in_plane(late_mid, lambda w: late_fin.at[core, w])
        for copy in late_moves:
            copy.start()
        late_fin[core, my_w] = late_mid[my_w]
        act_ref[...] = (mid_ref[...] + layer.result()).astype(BF)

        q_moves = in_plane(q_mid, lambda w: q_fin.at[w])
        kv_moves = in_plane(kv_mid, lambda w: kv_fin.at[w])

        @pl.when(first)
        def _():
            for copy in q_copies:
                copy.wait()
            over_ctx(q_got, q_mid)
            for copy in q_moves:
                copy.start()
            q_fin[my_w] = q_mid[my_w]

        @pl.when(second)
        def _():
            for copy in kvg_copies:
                copy.wait()
            over_ctx(kv_got, kv_mid)
            for copy in kv_moves:
                copy.start()
            kv_fin[my_w] = kv_mid[my_w]

        for copy in land_moves:
            copy.wait()
        for p in range(wsh):
            down_fin[core, p * piece : p * piece + piece, :] = landed[p]
        down_copy = wires.start(down_fin.at[core], down_fin.at[core], sibling)
        for copy in gate_moves + late_moves:
            copy.wait()
        gate_copy = wires.start(gate_fin.at[core], gate_fin.at[core], sibling)
        late_copy = wires.start(late_fin.at[core], late_fin.at[core], sibling)
        for copy in out_copies:
            copy.wait()
        out_fin[core] = jnp.sum(out_got[...].astype(F32), axis=0).astype(BF)
        out_copy = wires.start(out_fin.at[core], out_fin.at[core], sibling)
        for copy in gain_copies:
            copy.wait()
        gains_fin[core] = jnp.sum(gains_got[...], axis=0)
        gain_copy = wires.start(gains_fin.at[core], gains_fin.at[core], sibling)
        q_final = wires.copy(q_fin, q_fin, sibling)
        kv_final = wires.copy(kv_fin, kv_fin, sibling)

        @pl.when(first)
        def _():
            for copy in q_moves:
                copy.wait()
            q_final.start()

        @pl.when(second)
        def _():
            for copy in kv_moves:
                copy.wait()
            kv_final.start()

        down_copy.wait()
        gate_copy.wait()
        late_copy.wait()
        out_copy.wait()

        @pl.when(first)
        def _():
            q_final.wait_send()
            kv_final.wait_recv()

        @pl.when(second)
        def _():
            kv_final.wait_send()
            q_final.wait_recv()

        gain_copy.wait()
        gains_out[...] = gains_fin[0] + gains_fin[1]

    operands = (
        q_grad, kv_grad, weight, cos, sin, normed, tokens, gain, middle_grad, gate_got, down_got,
        attended, branch, feed_sum, down_part, middle, gate_late,
    )
    vmem = pl.BlockSpec(memory_space=pltpu.VMEM)
    return pl.pallas_call(
        kernel,
        name="finish",
        in_specs=[vmem] * len(operands),
        out_specs=[vmem] * 9,
        out_shape=[
            jax.ShapeDtypeStruct((own_rows, D), BF),
            jax.ShapeDtypeStruct((own_rows, D), F32),
            jax.ShapeDtypeStruct((wsh, rows, 384), BF),
            jax.ShapeDtypeStruct((wsh, rows, 256), BF),
            jax.ShapeDtypeStruct((2, rows, 640), BF),
            jax.ShapeDtypeStruct((2, wsh, rows, gate_width), BF),
            jax.ShapeDtypeStruct((2, wsh, rows, late_width), BF),
            jax.ShapeDtypeStruct((2, down_rows, D), BF),
            jax.ShapeDtypeStruct((8, 128), F32),
        ],
        scratch_shapes=[
            pltpu.VMEM((plane, 640), BF),
            pltpu.VMEM((4, own_rows, D), BF),
            *square_scratch(own_rows),
            *square_scratch(own_rows),
            pltpu.VMEM((384, D), F32),
            *[pltpu.VMEM((ctx, chunk, 384), BF)] * 4,
            pltpu.VMEM((wsh, rows, 384), BF),
            *[pltpu.VMEM((ctx, chunk, 256), BF)] * 4,
            pltpu.VMEM((wsh, rows, 256), BF),
            pltpu.VMEM((wsh, rows, gate_width), BF),
            pltpu.VMEM((ctx, chunk, late_width), BF),
            pltpu.VMEM((wsh, rows, late_width), BF),
            *[pltpu.VMEM((wsh, piece, D), BF)] * 4,
            pltpu.VMEM((2, 288, 640), BF),
            pltpu.VMEM((288, 640), BF),
            pltpu.VMEM((wsh, fold, rows, 640), BF),
            pltpu.VMEM((wsh, fold, rows, 640), BF),
            pltpu.VMEM((ctx, rows, 640), BF),
            pltpu.VMEM((shards, 8, 128), F32),
            pltpu.VMEM((shards, 8, 128), F32),
            pltpu.VMEM((2, 8, 128), F32),
            pltpu.SemaphoreType.DMA((shards + 5 * ctx + 48,)),
            pltpu.SemaphoreType.DMA((shards + 5 * ctx + 48,)),
        ],
        compiler_params=pltpu.CompilerParams(
            collective_id=8, has_side_effects=True, vmem_limit_bytes=VMEM_LIMIT
        ),
    )(*operands)


def wrap(act, input_grad, q_sum, kv_sum, out_sum, gate_sum, late_sum, down_sum, gain_sum):
    wsh, rows, _ = q_sum.shape
    down_rows = down_sum.shape[1]
    width, wide = gate_sum.shape[3], late_sum.shape[3]

    def kernel(
        act_in, ig_in, q_in, kv_in, out_in, gate_in, late_in, down_in, gain_in,
        act_ref, ig_ref, qkv_ref, out_ref, gate_ref, down_ref, one_ref, two_ref,
    ):
        one_ref[...] = gain_in[0:1, :rows].reshape(rows)
        two_ref[...] = gain_in[1:2, :rows].reshape(rows)
        act_ref[...] = act_in[...]
        ig_ref[...] = ig_in[...]
        qkv_ref[...] = qkv_restore(
            [
                jnp.concatenate([q_in[w].astype(F32), kv_in[w].astype(F32)], axis=1)
                for w in range(wsh)
            ]
        )
        out_ref[...] = jnp.concatenate(
            [out_in[0, :, :576].astype(F32), out_in[1, :, :576].astype(F32)], axis=1
        )
        for half in range(2):
            for w in range(wsh):
                left = (half * wsh + w) * (width + wide)
                gate_ref[:, left : left + width] = gate_in[half, w].astype(F32)
                left += width
                gate_ref[:, left : left + wide] = late_in[half, w].astype(F32)
            down_ref[half * down_rows : half * down_rows + down_rows, :] = down_in[half].astype(
                F32
            )

    vmem = pl.BlockSpec(memory_space=pltpu.VMEM)
    return pl.pallas_call(
        kernel,
        name="wrap",
        in_specs=[vmem] * 9,
        out_specs=[vmem] * 8,
        out_shape=[
            jax.ShapeDtypeStruct(act.shape, BF),
            jax.ShapeDtypeStruct(act.shape, F32),
            jax.ShapeDtypeStruct((rows, QW + 2 * KW), F32),
            jax.ShapeDtypeStruct((rows, D), F32),
            jax.ShapeDtypeStruct((rows, 2 * FF), F32),
            jax.ShapeDtypeStruct((2 * down_rows, D), F32),
            jax.ShapeDtypeStruct((rows,), F32),
            jax.ShapeDtypeStruct((rows,), F32),
        ],
        compiler_params=pltpu.CompilerParams(vmem_limit_bytes=VMEM_LIMIT),
    )(act, input_grad, q_sum, kv_sum, out_sum, gate_sum, late_sum, down_sum, gain_sum)


def build(sizes):
    ctx, wsh = sizes["ctx"], sizes["wsh"]
    shards = ctx * wsh
    link = Exchange(sizes)

    def local(
        tokens,
        segment_ids,
        positions,
        attend_gain,
        query_key_value,
        attend_out,
        feed_gain,
        gate_up,
        down_weight,
        upstream,
    ):
        own = tokens.shape[0]
        plane = own * wsh
        group = plane * ctx
        (
            queries,
            kv_all,
            normed_all,
            w_qkv,
            k_pos,
            k_seg,
            q_marks,
            dy_all,
            cos,
            sin,
            attended,
            attended_wide,
            lse,
            w_half,
        ) = head(
            link, tokens, attend_gain, query_key_value, positions, segment_ids, upstream, gate_up
        )
        kv_all = kv_all.reshape(group, 256)
        normed_all, dy_all = normed_all.reshape(plane, D), dy_all.reshape(plane, D)
        w_qkv = w_qkv.reshape(D, 640)
        w_half = w_half.reshape(D, FF // wsh)
        (
            middle,
            middle_grad,
            branch_all,
            attended_grad,
            feed_sum,
            down_part,
            gate_send,
            gate_late,
            down_sum,
        ) = feed(link, attended, attend_out, tokens, feed_gain, w_half, down_weight, dy_all)
        q_grad, kv_grad, gate_got = attend_backward(
            link, queries, kv_all, q_marks, k_pos, k_seg, lse, attended_wide, attended_grad,
            gate_send,
        )
        sums = finish(
            link, q_grad, kv_grad, w_qkv, cos, sin, normed_all, tokens,
            attend_gain, middle_grad, gate_got, down_sum, attended,
            branch_all.reshape(plane, D), feed_sum, down_part, middle, gate_late,
        )
        return wrap(*sums)

    return local


def solution(mesh):
    whole = ("grp", "ctx", "wsh")
    in_specs = (
        P(whole, None),
        P(whole),
        P(whole),
        P(),
        P("wsh", None),
        P("wsh", None),
        P(),
        P("wsh", None),
        P("wsh", None),
        P(whole, None),
    )
    out_specs = (
        P(whole, None),
        P(whole, None),
        P(("ctx", "wsh"), None),
        P(("ctx", "wsh"), None),
        P(("ctx", "wsh"), None),
        P(("ctx", "wsh"), None),
        P(("ctx", "wsh")),
        P(("ctx", "wsh")),
    )
    return jax.shard_map(
        build(dict(mesh.shape)), mesh=mesh, in_specs=in_specs, out_specs=out_specs, check_vma=False
    )
```
